32 devices in a mesh: dp: 8 (over z, y), tensor: 4 (over x, core).
Axes of the slice: x: 2, y: 2, z: 4, core: 2. Of those that a mesh axis runs over, the one named last changes fastest.
Arguments:
- block_input: bfloat16 [2048, 2560], P('dp'), may hold values from -6 to 6
- cotangent: bfloat16 [2048, 2560], P('dp'), may hold values from -6 to 6
- seq_lengths: int32 [8, 8], P('dp'), may hold values from 1 to 128, 256 in all within a row
- norm_gain: float32 [2560], replicated, may hold values from 0.5 to 1.5
- gate_weight: bfloat16 [2560, 5120], P(None, 'tensor'), may hold values from -0.125 to 0.125
- inner_weight: bfloat16 [2560, 5120], P(None, 'tensor'), may hold values from -0.125 to 0.125
- step_weight: bfloat16 [2560, 80], P(None, 'tensor'), may hold values from -0.125 to 0.125
- state_weight: bfloat16 [2560, 256], replicated, may hold values from -0.125 to 0.125
- inner_kernel: float32 [4, 5120], P(None, 'tensor'), may hold values from -3 to 3
- inner_bias: float32 [5120], P('tensor'), may hold values from -3 to 3
- state_kernel: float32 [4, 256], replicated, may hold values from -3 to 3
- state_bias: float32 [256], replicated, may hold values from -3 to 3
- step_bias: float32 [80], P('tensor'), may hold values from -5 to -2
- decay_log: float32 [80], P('tensor'), may hold values from -2.5 to 1.5
- skip_scale: float32 [80], P('tensor'), may hold values from 0.5 to 1.5
- gate_gain: float32 [5120], P('tensor'), may hold values from 0.5 to 1.5
- output_weight: bfloat16 [5120, 2560], P('tensor'), may hold values from -0.078125 to 0.078125
Outputs:
- block_output: bfloat16 [2048, 2560], P('dp', 'tensor')
- input_gradient: float32 [2048, 2560], P('dp', 'tensor')
- norm_gain_gradient: float32 [2560], P('tensor')
- gate_weight_gradient: float32 [2560, 5120], P('dp', 'tensor')
- inner_weight_gradient: float32 [2560, 5120], P('dp', 'tensor')
- step_weight_gradient: float32 [2560, 80], P('dp', 'tensor')
- state_weight_gradient: float32 [2560, 256], P('dp')
- inner_kernel_gradient: float32 [4, 5120], P(None, 'tensor')
- inner_bias_gradient: float32 [5120], P('tensor')
- state_kernel_gradient: float32 [4, 256], replicated
- state_bias_gradient: float32 [256], replicated
- step_bias_gradient: float32 [80], P('tensor')
- decay_log_gradient: float32 [80], P('tensor')
- skip_scale_gradient: float32 [80], P('tensor')
- gate_gain_gradient: float32 [5120], P('tensor')
- output_weight_gradient: float32 [5120, 2560], P('tensor', 'dp')
The draws below stay inside these ranges and needn't reach their ends.
Inputs may be any that keep to these rules, and one draw needn't show every extreme that they name: `seq_lengths`: each row holds the lengths of the 8 sequences of one data shard; they sum to 256 and the longest is exactly 128.
All inputs are finite; a program needn't handle non-finite values.
Results may differ from the reference program's by a relative error of at most 0.0081.
Values sent between devices are 32-bit elements; how exact they have to be, the bound alone decides.
A program may use at most 192 MiB of HBM per device.

```python
import math
from functools import partial
import jax
import jax.numpy as jnp
import numpy as np
from jax import lax

D = 2560
HEADS = 80
HEAD_DIM = 64
STATE = 128
CONV = 4
GROUP = 256
TOK_DEV = 256
SEQS = 8
INNER = 5120
LMAX = 128
TOKENS = 2048
N_DP = 8


def raised(values, key, source, target, blocks, factor):
    owner, partner = [(jnp.arange(values.shape[axis_at]) // (values.shape[axis_at] // blocks)).reshape([-1 if axis == axis_at else 1 for axis in range(values.ndim)]) for axis_at in (source, target)]
    chosen = jax.random.permutation(key, blocks)[partner]
    strong = (owner == chosen) | (owner == (partner + blocks // 2) % blocks)
    return jnp.where(strong, factor * values, values)


def levels(own_key, shape, shards, smallest, top_value):
    def one(dim, parts):
        steps = jax.random.uniform(jax.random.fold_in(jax.random.fold_in(own_key, 6), dim), (parts,), jnp.float32, smallest / len(shards), top_value / len(shards))
        return jnp.repeat(jnp.exp(steps), shape[dim] // parts).reshape((-1,) + (1,) * (len(shape) - dim - 1))

    factor_of = one(*shards[0])
    for cut in shards[1:]:
        factor_of = factor_of * one(*cut)
    return factor_of


def length_profile(amount, total, bound, slope):
    portions = [(1 << 20) // math.isqrt(grade ** slope) + 1 for grade in range(2, amount + 1)]
    spare, given = total - bound - (amount - 1), [1] * (amount - 1)
    while spare > 0:
        movable = [i for i in range(amount - 1) if given[i] < bound]
        whole, left = sum([portions[i] for i in movable]), spare
        for i in movable:
            addition = min(bound - given[i], max(1, left * portions[i] // whole), spare)
            given[i] = given[i] + addition
            spare = spare - addition
    return np.array([bound] + given)


def ragged(key, count, total, reach, slope):
    if count == 2:
        one = jax.random.randint(key, (), max(1, total - reach), min(reach, total - 1) + 1)
        return jnp.stack([one, total - one])
    tallies = jnp.asarray(length_profile(count, total, reach, slope), jnp.int32)
    pairs = (count - 1) // 2
    source_of, receiver = tallies[1:1 + 2 * pairs:2], tallies[2:2 + 2 * pairs:2]
    slack = jnp.minimum(source_of - 1, reach - receiver)
    passed = jax.random.randint(jax.random.fold_in(key, 1), (pairs,), 0, 1 << 20) % (slack + 1)
    tallies = tallies.at[1:1 + 2 * pairs:2].set(source_of - passed).at[2:2 + 2 * pairs:2].set(receiver + passed)
    return tallies[jax.random.permutation(jax.random.fold_in(key, 2), count)]


def normal_values(key, dims, spread, limit, split=(), kind=jnp.bfloat16):
    drawn = jax.random.normal(key, dims, jnp.float32) * spread
    if len(split) > 0:
        drawn = levels(key, dims, split, -0.22, 0.18) * drawn
    return jnp.clip(drawn, min=-limit, max=limit).astype(kind)


def heavy_noise(rng, extent, scale, most, cuts, heavy, kind=jnp.bfloat16):
    entries = scale * jax.random.normal(rng, extent, jnp.float32)
    if cuts:
        entries = entries * levels(rng, extent, cuts, -0.22, 0.18)
    return jnp.clip(raised(entries, jax.random.fold_in(rng, 3), *heavy), -most, most).astype(kind)


def setup_inputs(seed: int = 0) -> dict:
    streams_of = jax.random.split(jax.random.key(seed), 18)
    block_input = heavy_noise(streams_of[0], (TOKENS, D), 1.0, 6.0, ((0, 8),), (0, 1, 8, 2.0))
    cotangent = normal_values(streams_of[1], (TOKENS, D), 1.0, 6.0, ((0, 8),))
    seq_lengths = jax.vmap(lambda own: ragged(own, SEQS, TOK_DEV, LMAX, 2))(jax.random.split(streams_of[2], N_DP)).reshape((N_DP, SEQS)).astype(jnp.int32)
    norm_gain = jnp.clip(1.0 + 0.1 * jax.random.normal(streams_of[3], (D,), jnp.float32), 0.5, 1.5)
    gate_weight = normal_values(streams_of[4], (D, INNER), D ** -0.5, 0.125, ((1, 4),))
    inner_weight = normal_values(streams_of[5], (D, INNER), D ** -0.5, 0.125, ((1, 4),))
    step_weight = normal_values(streams_of[6], (D, HEADS), D ** -0.5, 0.125, ((1, 4),))
    state_weight = normal_values(streams_of[7], (D, 2 * STATE), D ** -0.5, 0.125)
    inner_kernel = normal_values(streams_of[8], (CONV, INNER), CONV ** -0.5, 3.0, ((1, 4),), jnp.float32)
    inner_bias = normal_values(streams_of[9], (INNER,), 0.5, 3.0, ((0, 4),), jnp.float32)
    state_kernel = normal_values(streams_of[10], (CONV, 2 * STATE), CONV ** -0.5, 3.0, (), jnp.float32)
    state_bias = normal_values(streams_of[11], (2 * STATE,), 0.5, 3.0, (), jnp.float32)
    step_bias = jnp.clip(-5.0 + 3.0 * jax.random.uniform(streams_of[12], (HEADS,), jnp.float32) ** levels(streams_of[12], (HEADS,), ((0, 4),), -0.2, 0.2), -5.0, -2.0)
    decay_log = jnp.clip(-2.5 + 4.0 * jax.random.uniform(streams_of[13], (HEADS,), jnp.float32) ** levels(streams_of[13], (HEADS,), ((0, 4),), -0.2, 0.2), -2.5, 1.5)
    skip_scale = jnp.clip(0.5 + 1.0 * jax.random.uniform(streams_of[14], (HEADS,), jnp.float32) ** levels(streams_of[14], (HEADS,), ((0, 4),), -0.2, 0.2), 0.5, 1.5)
    gate_gain = jnp.clip(1.0 + 0.1 * jax.random.normal(streams_of[15], (INNER,), jnp.float32), 0.5, 1.5)
    output_weight = normal_values(streams_of[16], (INNER, D), INNER ** -0.5, 0.078125, ((0, 4),))
    return {"block_input": block_input, "cotangent": cotangent, "seq_lengths": seq_lengths, "norm_gain": norm_gain, "gate_weight": gate_weight, "inner_weight": inner_weight, "step_weight": step_weight, "state_weight": state_weight, "inner_kernel": inner_kernel, "inner_bias": inner_bias, "state_kernel": state_kernel, "state_bias": state_bias, "step_bias": step_bias, "decay_log": decay_log, "skip_scale": skip_scale, "gate_gain": gate_gain, "output_weight": output_weight}


norm_eps = 1e-05

def segment_ids(lengths, count):
    ends = jnp.cumsum(lengths)
    places = jnp.arange(count, dtype=jnp.int32)
    return lax.optimization_barrier(jnp.sum((places[:, None] >= ends[None, :]).astype(jnp.int32), axis=1)).astype(jnp.int32)

def causal_conv(values, kernel, bias, segment):
    width = kernel.shape[0]
    result = bias[None, :] + kernel[width - 1][None, :] * values
    for back in range(1, width):
        shifted = jnp.concatenate([jnp.zeros((back, values.shape[1]), values.dtype), values[:-back]], axis=0)
        earlier = jnp.concatenate([jnp.full((back,), -1, jnp.int32), segment[:-back]], axis=0)
        keep = (earlier == segment).astype(values.dtype)
        result = result + kernel[width - 1 - back][None, :] * shifted * keep[:, None]
    return result

def block_scan(inner, step, rate, bmat, cmat, segment):
    length = inner.shape[0]
    heads = inner.shape[1]
    count = length // GROUP
    blocks = (inner.reshape(count, GROUP, heads, HEAD_DIM), step.reshape(count, GROUP, heads), bmat.reshape(count, GROUP, STATE), cmat.reshape(count, GROUP, STATE), segment.reshape(count, GROUP))
    lower = jnp.tril(jnp.ones((GROUP, GROUP), dtype=bool))
    highest = lax.Precision.HIGHEST

    def advance(carry, block):
        state, before = carry
        values, steps, keys, queries, labels = block
        logs = jnp.cumsum(steps * rate[None, :], axis=0)
        same = (labels[:, None] == labels[None, :]) & lower
        gaps = logs[:, None, :] - logs[None, :, :]
        decay = jnp.exp(jnp.where(same[:, :, None], gaps, -jnp.inf))
        scores = jnp.dot(queries, keys.T, precision=highest)
        mixing = scores[:, :, None] * decay * steps[None, :, :]
        within = jnp.einsum('ijh,jhp->ihp', mixing, values, precision=highest)
        entering = (labels == before).astype(values.dtype)
        carried = jnp.einsum('in,hpn->ihp', queries, state, precision=highest) * (jnp.exp(logs) * entering[:, None])[:, :, None]
        final = labels[GROUP - 1].astype(jnp.int32)
        ending = jnp.exp(logs[GROUP - 1][None, :] - logs) * (labels == final).astype(values.dtype)[:, None] * steps
        keeping = jnp.exp(logs[GROUP - 1]) * (final == before).astype(values.dtype)
        update = jnp.einsum('jh,jhp,jn->hpn', ending, values, keys, precision=highest)
        return ((state * keeping[:, None, None] + update, final), within + carried)
    start = (jnp.zeros((heads, HEAD_DIM, STATE), inner.dtype), jnp.array(-1, dtype=jnp.int32))
    _, outputs = lax.scan(advance, start, blocks)
    return outputs.reshape(length, heads, HEAD_DIM)

def mixer(inner_raw, step_raw, state_act, inner_kernel, inner_bias, step_bias, decay_log, skip_scale, segment):
    inner_act = jax.nn.silu(causal_conv(inner_raw, inner_kernel, inner_bias, segment))
    step = jax.nn.softplus(step_raw + step_bias[None, :])
    rate = -jnp.exp(decay_log)
    length = inner_raw.shape[0]
    heads = step.shape[1]
    shaped = inner_act.reshape(length, heads, HEAD_DIM)
    scanned = block_scan(shaped, step, rate, state_act[:, :STATE], state_act[:, STATE:], segment)
    return (scanned + skip_scale[None, :, None] * shaped).reshape(length, heads * HEAD_DIM)

def state_path(state_raw, state_kernel, state_bias, segment):
    return jax.nn.silu(causal_conv(state_raw, state_kernel, state_bias, segment))

def layer_rows(rows, cot_rows, lengths, norm_gain, gate_weight, inner_weight, step_weight, state_weight, inner_kernel, inner_bias, state_kernel, state_bias, step_bias, decay_log, skip_scale, gate_gain, output_weight):
    f32 = jnp.float32
    segment = segment_ids(lengths, rows.shape[0])
    hidden = rows.astype(f32)
    inv_in = lax.rsqrt(lax.optimization_barrier(jnp.sum(hidden * hidden, axis=1, keepdims=True)) / D + norm_eps)
    normed = hidden * inv_in
    normed_in = (normed * norm_gain[None, :]).astype(jnp.bfloat16)
    gate_pre = jnp.dot(normed_in, gate_weight, preferred_element_type=f32)
    inner_raw = jnp.dot(normed_in, inner_weight, preferred_element_type=f32)
    step_raw = jnp.dot(normed_in, step_weight, preferred_element_type=f32)
    state_raw = jnp.dot(normed_in, state_weight, preferred_element_type=f32)
    state_act = state_path(state_raw, state_kernel, state_bias, segment=segment)
    mixed = mixer(inner_raw, step_raw, state_act, inner_kernel, inner_bias, step_bias, decay_log, skip_scale, segment=segment)
    gate_act = jax.nn.silu(gate_pre)
    gated = mixed * gate_act
    inv_gate = lax.rsqrt(lax.optimization_barrier(jnp.sum(gated * gated, axis=1, keepdims=True)) / INNER + norm_eps)
    unit = gated * inv_gate
    unit_out = (unit * gate_gain[None, :]).astype(jnp.bfloat16)
    block_output = (jnp.dot(unit_out, output_weight, preferred_element_type=f32) + hidden).astype(jnp.bfloat16)
    output_gradient = jnp.dot(unit_out.T, cot_rows, preferred_element_type=f32)
    scaled_back = jnp.dot(cot_rows, output_weight.T, preferred_element_type=f32)
    gate_gain_grad = lax.optimization_barrier(jnp.sum(scaled_back * unit, axis=0))
    d_unit = scaled_back * gate_gain[None, :]
    unit_dot = lax.optimization_barrier(jnp.sum(d_unit * unit, axis=1, keepdims=True))
    d_gated = inv_gate * (d_unit - unit * unit_dot / INNER)
    d_mixed = d_gated * gate_act
    sigmoid_gate = jax.nn.sigmoid(gate_pre)
    d_gate = d_gated * mixed * sigmoid_gate * (1.0 + gate_pre * (1.0 - sigmoid_gate))
    _, mixer_back = jax.vjp(partial(mixer, segment=segment), inner_raw, step_raw, state_act, inner_kernel, inner_bias, step_bias, decay_log, skip_scale)
    d_inner_raw, d_step_raw, d_state_act, kernel_grad, bias_grad, step_bias_grad, decay_grad, skip_grad = mixer_back(d_mixed)
    _, state_backward = jax.vjp(partial(state_path, segment=segment), state_raw, state_kernel, state_bias)
    d_state_raw, state_kernel_grad, state_bias_grad = state_backward(d_state_act)
    gate_back = d_gate.astype(jnp.bfloat16)
    inner_back = d_inner_raw.astype(jnp.bfloat16)
    step_back = d_step_raw.astype(jnp.bfloat16)
    state_back = d_state_raw.astype(jnp.bfloat16)
    gate_gradient = jnp.dot(normed_in.T, gate_back, preferred_element_type=f32)
    inner_gradient = jnp.dot(normed_in.T, inner_back, preferred_element_type=f32)
    step_gradient = jnp.dot(normed_in.T, step_back, preferred_element_type=f32)
    states_gradient = jnp.dot(normed_in.T, state_back, preferred_element_type=f32)
    d_normed = jnp.dot(gate_back, gate_weight.T, preferred_element_type=f32) + jnp.dot(inner_back, inner_weight.T, preferred_element_type=f32) + jnp.dot(step_back, step_weight.T, preferred_element_type=f32) + jnp.dot(state_back, state_weight.T, preferred_element_type=f32)
    norm_gain_grad = lax.optimization_barrier(jnp.sum(d_normed * normed, axis=0))
    d_hat = d_normed * norm_gain[None, :]
    hat_dot = lax.optimization_barrier(jnp.sum(d_hat * normed, axis=1, keepdims=True)) / D
    input_gradient = inv_in * (d_hat - normed * hat_dot) + cot_rows.astype(f32)
    grads = (norm_gain_grad, gate_gradient, inner_gradient, step_gradient, states_gradient, kernel_grad, bias_grad, state_kernel_grad, state_bias_grad, step_bias_grad, decay_grad, skip_grad, gate_gain_grad, output_gradient)
    return ((block_output, input_gradient), grads)

def reference(block_input, cotangent, seq_lengths, norm_gain, gate_weight, inner_weight, step_weight, state_weight, inner_kernel, inner_bias, state_kernel, state_bias, step_bias, decay_log, skip_scale, gate_gain, output_weight):
    f32 = jnp.float32
    blocks_in = block_input.reshape(N_DP, TOK_DEV, D)
    blocks_cot = cotangent.reshape(N_DP, TOK_DEV, D)

    def visit(totals, item):
        rows, cot_rows, lengths = item
        results, grads = layer_rows(rows, cot_rows, lengths, norm_gain, gate_weight, inner_weight, step_weight, state_weight, inner_kernel, inner_bias, state_kernel, state_bias, step_bias, decay_log, skip_scale, gate_gain, output_weight)
        return (tuple((total + grad for total, grad in zip(totals, grads))), results)
    zeros = (jnp.zeros((D,), f32), jnp.zeros((D, INNER), f32), jnp.zeros((D, INNER), f32), jnp.zeros((D, HEADS), f32), jnp.zeros((D, 2 * STATE), f32), jnp.zeros((CONV, INNER), f32), jnp.zeros((INNER,), f32), jnp.zeros((CONV, 2 * STATE), f32), jnp.zeros((2 * STATE,), f32), jnp.zeros((HEADS,), f32), jnp.zeros((HEADS,), f32), jnp.zeros((HEADS,), f32), jnp.zeros((INNER,), f32), jnp.zeros((INNER, D), f32))
    totals, (out_blocks, grad_blocks) = lax.scan(visit, zeros, (blocks_in, blocks_cot, seq_lengths))
    block_output = out_blocks.reshape(TOKENS, D)
    input_gradient = grad_blocks.reshape(TOKENS, D)
    return (block_output, input_gradient, totals[0], totals[1], totals[2], totals[3], totals[4], totals[5], totals[6], totals[7], totals[8], totals[9], totals[10], totals[11], totals[12], totals[13])
```

```python
from functools import partial

import jax
import jax.numpy as jnp
from jax import lax
from jax.experimental import pallas as pl
from jax.experimental.pallas import tpu as pltpu
from jax.sharding import PartitionSpec as P

HEAD_DIM = 64
STATE = 128
CONV = 4
BLK = 256
HPB = BLK // HEAD_DIM
eps = 1e-05
NEG = -1e30
f32 = jnp.float32
bf16 = jnp.bfloat16
HIGH = lax.Precision.HIGHEST
NN = (((1,), (0,)), ((), ()))
NT = (((1,), (1,)), ((), ()))
TN = (((0,), (0,)), ((), ()))


def mm(a, b, dims=NN, precision=None):
    return lax.dot_general(a, b, dims, precision=precision, preferred_element_type=f32)


def sigmoid(x):
    return 1.0 / (1.0 + jnp.exp(-x))


def softplus(x):
    return jnp.maximum(x, 0.0) + jnp.log1p(jnp.exp(-jnp.abs(x)))


def seg_of(places, lengths):
    total = jnp.zeros(places.shape, jnp.int32)
    end = jnp.int32(0)
    for s in range(lengths.shape[1]):
        end = end + lengths[0, s]
        total = total + (places >= end).astype(jnp.int32)
    return total


def keeps(lengths, count):
    t = lax.broadcasted_iota(jnp.int32, (count, 1), 0)
    own = seg_of(t, lengths)
    out = [None]
    for back in range(1, CONV):
        out.append(((seg_of(t - back, lengths) == own) & (t >= back)).astype(f32))
    return out


def down(x, back):
    return pltpu.roll(x, back, 0)


def up(x, back):
    return pltpu.roll(x, x.shape[0] - back, 0)


def conv(u, kernel, bias, keep):
    out = bias + kernel[CONV - 1 : CONV, :] * u
    for back in range(1, CONV):
        out = out + kernel[CONV - 1 - back : CONV - back, :] * (down(u, back) * keep[back])
    return out


def conv_back(dc, u, kernel, keep):
    du = kernel[CONV - 1 : CONV, :] * dc
    rows = [jnp.sum(dc * u, axis=0, keepdims=True)]
    for back in range(1, CONV):
        kept = dc * keep[back]
        du = du + kernel[CONV - 1 - back : CONV - back, :] * up(kept, back)
        rows.append(jnp.sum(kept * down(u, back), axis=0, keepdims=True))
    return du, rows[::-1] + [jnp.sum(dc, axis=0, keepdims=True)]


def lanes_first(shape):
    return lax.broadcasted_iota(jnp.int32, shape, 1) < HEAD_DIM


def norm_kernel(x_ref, gain_ref, nb_ref, inv_ref):
    x = x_ref[...].astype(f32)
    inv = lax.rsqrt(jnp.sum(x * x, axis=1, keepdims=True) / x.shape[1] + eps)
    nb_ref[...] = (x * inv * gain_ref[...]).astype(bf16)
    inv_ref[...] = jnp.broadcast_to(inv, inv_ref.shape)


def forward_kernel(
    lengths, nb_ref, cot_ref, wg_ref, wi_ref, wo_ref, ws_ref, wst_ref, ik_ref, ib_ref, sk_ref, sb_ref,
    stepb_ref, decay_ref, skipc_ref, gain_ref,
    graw_ref, iraw_ref, cv_ref, mixed_ref, scaled_ref, sums_ref, sraw_ref, sact_ref, state_ref, hc_ref, lsr_ref,
    addm_ref, g_ref, acc,
):
    j = pl.program_id(0)
    count = nb_ref.shape[0]
    nb = nb_ref[...]

    @pl.when(j == 0)
    def _():
        i0 = lax.broadcasted_iota(jnp.int32, (count, count), 0)
        j0 = lax.broadcasted_iota(jnp.int32, (count, count), 1)
        same = (seg_of(i0, lengths) == seg_of(j0, lengths)) & (j0 <= i0)
        addm_ref[...] = jnp.where(same, 0.0, NEG)
        state = mm(nb, wst_ref[...])
        state_ref[...] = state
        cv = conv(state, sk_ref[...], sb_ref[...], keeps(lengths, count))
        act = cv * sigmoid(cv)
        sact_ref[...] = act
        g_ref[...] = mm(act[:, STATE:], act[:, :STATE], NT, HIGH)
        raw = mm(nb, ws_ref[...]) + stepb_ref[...]
        sraw_ref[...] = raw
        step = softplus(raw)
        logs = mm(same.astype(f32), step * (-jnp.exp(decay_ref[...])), NN, HIGH)
        lsr_ref[...] = jnp.transpose(logs)
        for k in range(hc_ref.shape[0]):
            hc_ref[k, :, 0:HPB] = logs[:, HPB * k : HPB * (k + 1)]
            hc_ref[k, :, HPB : 2 * HPB] = step[:, HPB * k : HPB * (k + 1)]
        acc[...] = jnp.zeros_like(acc)

    gate = mm(nb, wg_ref[...])
    inner = mm(nb, wi_ref[...])
    scaled = mm(cot_ref[...], wo_ref[...], NT)
    graw_ref[...] = gate
    iraw_ref[...] = inner
    scaled_ref[...] = scaled
    cv = conv(inner, ik_ref[...], ib_ref[...], keeps(lengths, count))
    cv_ref[...] = cv
    v = cv * sigmoid(cv)
    first = lanes_first((count, 2 * HEAD_DIM))
    addm = addm_ref[...]
    g = g_ref[...]
    parts = []
    for pair in range(BLK // (2 * HEAD_DIM)):
        vp = v[:, 2 * HEAD_DIM * pair : 2 * HEAD_DIM * (pair + 1)]
        k = 2 * pair
        steps = jnp.where(first, hc_ref[j, :, HPB + k : HPB + k + 1], hc_ref[j, :, HPB + k + 1 : HPB + k + 2])
        vs = (vp * steps).astype(bf16)
        ys = []
        for h in (k, k + 1):
            gaps = hc_ref[j, :, h : h + 1] - lsr_ref[pl.ds(HPB * j + h, 1), :] + addm
            ys.append(mm((g * jnp.exp(gaps)).astype(bf16), vs))
        parts.append(jnp.where(first, ys[0], ys[1]))
    mixed = jnp.concatenate(parts, axis=1) + skipc_ref[...] * v
    mixed_ref[...] = mixed
    gated = mixed * (gate * sigmoid(gate))
    acc[:, 0:1] += jnp.sum(gated * gated, axis=1, keepdims=True)
    acc[:, 1:2] += jnp.sum(scaled * gain_ref[...] * gated, axis=1, keepdims=True)

    @pl.when(j == pl.num_programs(0) - 1)
    def _():
        sums_ref[...] = jnp.transpose(acc[...])[0:8, :]


def unit_kernel(width, s_ref, graw_ref, mixed_ref, scaled_ref, gain_ref, uo_ref, gb_ref, dm_ref, gg_ref):
    sums = jnp.sum(s_ref[...], axis=0)
    cols = jnp.transpose(sums)
    inv = lax.rsqrt(cols[:, 0:1] / width + eps)
    dot = inv * cols[:, 1:2]
    gate, mixed, scaled, gain = graw_ref[...], mixed_ref[...], scaled_ref[...], gain_ref[...]
    s = sigmoid(gate)
    act = gate * s
    unit = mixed * act * inv
    uo_ref[...] = (unit * gain).astype(bf16).astype(f32)
    gg_ref[...] = jnp.broadcast_to(jnp.sum(scaled * unit, axis=0, keepdims=True), gg_ref.shape)
    d_gated = inv * (scaled * gain - unit * (dot / width))
    dm_ref[...] = d_gated * act
    gb_ref[...] = (d_gated * mixed * s * (1.0 + gate * (1.0 - s))).astype(bf16).astype(f32)


def backward_kernel(
    lengths, dm_ref, cv_ref, iraw_ref, mixed_ref, hc_ref, lsr_ref, addm_ref, g_ref, sraw_ref, sact_ref,
    ik_ref, skipc_ref, decay_ref,
    back_ref, rows_ref, sback_ref, hrows_ref, dstate_ref, dg, dlogs, dstep,
):
    j = pl.program_id(0)
    count = dm_ref.shape[0]

    @pl.when(j == 0)
    def _():
        dg[...] = jnp.zeros_like(dg)
        dlogs[...] = jnp.zeros_like(dlogs)
        dstep[...] = jnp.zeros_like(dstep)

    cv, dm, skipc = cv_ref[...], dm_ref[...], skipc_ref[...]
    s = sigmoid(cv)
    v = cv * s
    within = mixed_ref[...] - skipc * v
    first = lanes_first((count, 2 * HEAD_DIM))
    addm = addm_ref[...]
    g = g_ref[...]
    us, vss, dyb, stepm = [], [], [], []
    total = dg[...]
    for pair in range(BLK // (2 * HEAD_DIM)):
        cols = slice(2 * HEAD_DIM * pair, 2 * HEAD_DIM * (pair + 1))
        k = 2 * pair
        steps = jnp.where(first, hc_ref[0, :, HPB + k : HPB + k + 1], hc_ref[0, :, HPB + k + 1 : HPB + k + 2])
        vs = (v[:, cols] * steps).astype(bf16)
        dy = dm[:, cols].astype(bf16)
        both = []
        for h in (k, k + 1):
            gaps = hc_ref[0, :, h : h + 1] - lsr_ref[pl.ds(HPB * j + h, 1), :] + addm
            decay = jnp.exp(gaps)
            both.append(mm((g * decay).astype(bf16), dy, TN))
            mine = first if h == k else jnp.logical_not(first)
            total = total + decay * mm(jnp.where(mine, dy, jnp.zeros_like(dy)), vs, NT)
        us.append(jnp.where(first, both[0], both[1]))
        vss.append(vs.astype(f32))
        dyb.append(dy.astype(f32))
        stepm.append(steps)
    dg[...] = total
    u = jnp.concatenate(us, axis=1)
    vs = jnp.concatenate(vss, axis=1)
    dy = jnp.concatenate(dyb, axis=1)
    steps = jnp.concatenate(stepm, axis=1)
    c0 = lax.broadcasted_iota(jnp.int32, (BLK, 128), 0) // HEAD_DIM
    l0 = lax.broadcasted_iota(jnp.int32, (BLK, 128), 1)
    pick = (l0 == c0 + HPB * j).astype(f32)
    dlogs[...] += mm(dy * within - vs * u, pick, NN, HIGH)
    dstep[...] += mm(v * u, pick, NN, HIGH)
    dv = steps * u + skipc * dm
    dc = dv * (s * (1.0 + cv * (1.0 - s)))
    du, rows = conv_back(dc, iraw_ref[...], ik_ref[...], keeps(lengths, count))
    back_ref[...] = du.astype(bf16).astype(f32)
    rows_ref[...] = jnp.concatenate(rows + [jnp.sum(dm * v, axis=0, keepdims=True)] + [jnp.zeros((2, BLK), f32)], axis=0)

    @pl.when(j == pl.num_programs(0) - 1)
    def _():
        mask = (addm > -1.0).astype(f32)
        q = mm(mask, dlogs[...], TN, HIGH)
        raw = sraw_ref[...]
        step = softplus(raw)
        rate = -jnp.exp(decay_ref[...])
        draw = (dstep[...] + rate * q) * sigmoid(raw)
        sback_ref[...] = draw.astype(bf16).astype(f32)
        hrows_ref[...] = jnp.concatenate(
            [jnp.sum(draw, axis=0, keepdims=True), rate * jnp.sum(step * q, axis=0, keepdims=True), jnp.zeros((6, 128), f32)],
            axis=0,
        )
        act = sact_ref[...]
        d_b = mm(dg[...], act[:, STATE:], TN, HIGH)
        d_c = mm(dg[...], act[:, :STATE], NN, HIGH)
        both = jnp.concatenate([d_b, d_c], axis=1)
        span = dstate_ref.shape[2]
        for t in range(dstate_ref.shape[0]):
            dstate_ref[t] = both[:, span * t : span * (t + 1)]


def state_kernel(lengths, parts_ref, u_ref, sk_ref, sb_ref, back_ref, rows_ref):
    keep = keeps(lengths, u_ref.shape[0])
    cv = conv(u_ref[...], sk_ref[...], sb_ref[...], keep)
    s = sigmoid(cv)
    dc = jnp.sum(parts_ref[...], axis=0) * (s * (1.0 + cv * (1.0 - s)))
    du, rows = conv_back(dc, u_ref[...], sk_ref[...], keep)
    back_ref[...] = du.astype(bf16).astype(f32)
    rows_ref[...] = jnp.concatenate(rows + [jnp.zeros((3, du.shape[1]), f32)], axis=0)


def gather_kernel(slots, nb_ref, cot_ref, own_ref, across_ref, pair_ref, out_ref):
    count, piece = nb_ref.shape[0], own_ref.shape[2]
    out_ref[0, 0:count, :] = nb_ref[...]
    out_ref[1, 0:count, :] = cot_ref[...]
    for shard in range(3):
        for family in range(2):
            for k, ref in enumerate((own_ref.at[shard, family], pair_ref.at[0, shard, family],
                                     across_ref.at[shard, family], pair_ref.at[1, shard, family])):
                at = pl.multiple_of(count * (shard + 1) + piece * slots[k], piece)
                out_ref[family, pl.ds(at, piece), :] = ref[...].astype(bf16)


def grad_kernel(f_ref, a_ref, b_ref, c_ref, d_ref, out_ref):
    count = a_ref.shape[0]
    total = None
    for k, ref in enumerate((a_ref, b_ref, c_ref, d_ref)):
        one = mm(f_ref[0, pl.ds(count * k, count), :], ref[...].astype(bf16), TN)
        total = one if total is None else total + one
    out_ref[0] = total


def whole(shape):
    return pl.BlockSpec(shape, lambda *_: (0,) * len(shape))


def columns(rows):
    return pl.BlockSpec((rows, BLK), lambda j, *_: (0, j))


SMEM = pl.BlockSpec(memory_space=pltpu.SMEM)
VM = pltpu.CompilerParams(vmem_limit_bytes=56 << 20)
VMS = pltpu.CompilerParams(vmem_limit_bytes=56 << 20, dimension_semantics=("arbitrary",))


def struct(shape, dtype=f32):
    return jax.ShapeDtypeStruct(shape, dtype)


def cost(flops, moved):
    return pl.CostEstimate(flops=int(flops), bytes_accessed=int(moved), transcendentals=0)


def on_device(
    block_input, cotangent, seq_lengths, norm_gain, gate_weight, inner_weight, step_weight, state_weight,
    inner_kernel, inner_bias, state_kernel_, state_bias, step_bias, decay_log, skip_scale, gate_gain, output_weight,
):
    parts = lax.axis_size("tensor")
    shards = lax.axis_size("dp")
    t = lax.axis_index("tensor")
    count, width = block_input.shape
    inner = gate_weight.shape[1]
    heads = step_bias.shape[0]
    share = width // parts
    span = 2 * STATE // parts
    steps = inner // BLK
    pad = ((0, 0), (0, 128 - heads))
    row = lambda x: x.reshape(1, -1)

    def swap(x, k):
        return lax.ppermute(x, "tensor", [(i, i ^ k) for i in range(parts)])

    nb, inv = pl.pallas_call(
        norm_kernel,
        out_shape=(struct((count, width), bf16), struct((count, 128))),
        compiler_params=VM,
        name="norm_in",
    )(block_input, row(norm_gain))

    hub_plan = shards == 8 and parts == 4
    if hub_plan:
        d = lax.axis_index("dp")
        z, y = d // 2, d % 2
        half, side = z // 2, z % 2
        hub = (z == 1) | (z == 2)
        to_hub = [(0, 2), (1, 3), (6, 4), (7, 5)]
        hubs = [(2, 4), (4, 2), (3, 5), (5, 3)]
        to_edge = [(b, a) for a, b in to_hub]
        lines = [(i, i ^ 1) for i in range(8)]
        near, far = half * (width // 2), (1 - half) * (width // 2)
        piece = count // parts
        cut = lambda x: lax.dynamic_slice_in_dim(x, t * piece, piece, 0)
        mine = jnp.stack([cut(nb), cut(cotangent)]).astype(f32)
        side_of = lambda x, at: lax.dynamic_slice_in_dim(x, at, width // 2, x.ndim - 1)
        from_edge = lax.ppermute(mine, "dp", to_hub)
        from_hub = lax.ppermute(side_of(mine, far), "dp", hubs)
        from_far = lax.ppermute(side_of(from_edge, far), "dp", hubs)
        own = jnp.stack([side_of(from_edge, near), from_hub, from_far])
        across = swap(own, 2)
        pair = swap(jnp.stack([own, across]), 1)
        slots = jnp.stack([t, t ^ 1, t ^ 2, t ^ 3]).astype(jnp.int32)
        features = pl.pallas_call(
            gather_kernel,
            in_specs=[SMEM] + [pl.BlockSpec(memory_space=pltpu.VMEM)] * 5,
            out_shape=struct((2, 4 * count, width // 2), bf16),
            compiler_params=VM,
            name="features",
        )(slots, side_of(nb, near), side_of(cotangent, near), own, across, pair)

    padded_step = jnp.pad(step_weight, pad)
    stepb, decay = jnp.pad(row(step_bias), pad), jnp.pad(row(decay_log), pad)
    skipc = jnp.repeat(skip_scale, HEAD_DIM).reshape(1, -1)
    ik, ib, gain = inner_kernel, row(inner_bias), row(gate_gain)
    full = struct((count, inner))
    graw, iraw, cv, mixed, scaled, sums, sraw, sact, state_raw, hc, lsr, addm, g = pl.pallas_call(
        forward_kernel,
        grid=(steps,),
        in_specs=[
            SMEM, whole((count, width)), whole((count, width)), columns(width), columns(width),
            pl.BlockSpec((BLK, width), lambda j: (j, 0)), whole((width, 128)), whole((width, 2 * STATE)),
            columns(CONV), columns(1), whole((CONV, 2 * STATE)), whole((1, 2 * STATE)), whole((1, 128)), whole((1, 128)),
            columns(1), columns(1),
        ],
        out_specs=(
            [columns(count)] * 5
            + [whole((8, count)), whole((count, 128)), whole((count, 2 * STATE)), whole((count, 2 * STATE)),
               whole((steps, count, 128)), whole((128, count)), whole((count, count)), whole((count, count))]
        ),
        out_shape=(
            [full] * 5
            + [struct((8, count)), struct((count, 128)), struct((count, 2 * STATE)), struct((count, 2 * STATE)),
               struct((steps, count, 128)), struct((128, count)), struct((count, count)), struct((count, count))]
        ),
        scratch_shapes=[pltpu.VMEM((count, 128), f32)],
        compiler_params=VMS,
        cost_estimate=cost(6 * count * width * inner, 6 * width * inner + 20 * count * inner),
        name="forward",
    )(
        seq_lengths, nb, cotangent, gate_weight, inner_weight, output_weight, padded_step, state_weight, ik, ib,
        state_kernel_, row(state_bias), stepb, decay, skipc, gain,
    )

    all_sums = jnp.stack([sums] + [swap(sums, k) for k in range(1, parts)])
    uo, gb, dm, gg = pl.pallas_call(
        partial(unit_kernel, float(inner * parts)),
        grid=(steps,),
        in_specs=[whole((parts, 8, count)), columns(count), columns(count), columns(count), columns(1)],
        out_specs=[columns(count)] * 3 + [columns(8)],
        out_shape=[full] * 3 + [struct((8, inner))],
        compiler_params=VMS,
        cost_estimate=cost(0, 24 * count * inner),
        name="unit",
    )(all_sums, graw, mixed, scaled, gain)

    back, rows, sback, hrows, dstate = pl.pallas_call(
        backward_kernel,
        grid=(steps,),
        in_specs=[
            SMEM, columns(count), columns(count), columns(count), columns(count),
            pl.BlockSpec((1, count, 128), lambda j: (j, 0, 0)), whole((128, count)), whole((count, count)),
            whole((count, count)), whole((count, 128)), whole((count, 2 * STATE)), columns(CONV), columns(1), whole((1, 128)),
        ],
        out_specs=[columns(count), columns(8), whole((count, 128)), whole((8, 128)), whole((parts, count, span))],
        out_shape=[full, struct((8, inner)), struct((count, 128)), struct((8, 128)), struct((parts, count, span))],
        scratch_shapes=[pltpu.VMEM((count, count), f32), pltpu.VMEM((count, 128), f32), pltpu.VMEM((count, 128), f32)],
        compiler_params=VMS,
        cost_estimate=cost(40 * count * count * inner // 64 * 4, 24 * count * inner),
        name="backward",
    )(seq_lengths, dm, cv, iraw, mixed, hc, lsr, addm, g, sraw, sact, ik, skipc, decay)

    def to_parts(x, axis):
        size = x.shape[axis] // parts
        block = lambda i: lax.dynamic_slice_in_dim(x, i * size, size, axis)
        got = [swap(block(t ^ k), k) for k in range(1, parts)]
        return [block(t)] + got

    def from_parts(x):
        got = jnp.stack([x] + [swap(x, k) for k in range(1, parts)])
        return jnp.stack([lax.dynamic_index_in_dim(got, t ^ i, 0, False) for i in range(parts)])

    state_parts = jnp.concatenate(to_parts(dstate, 0), axis=0)
    slab = lambda x, size: lax.dynamic_slice_in_dim(x, t * size, size, x.ndim - 1)
    sq, srows = pl.pallas_call(
        state_kernel,
        in_specs=[SMEM] + [pl.BlockSpec(memory_space=pltpu.VMEM)] * 4,
        out_shape=(struct((count, span)), struct((8, span))),
        compiler_params=VM,
        name="state_back",
    )(seq_lengths, state_parts, slab(state_raw, span), slab(state_kernel_, span), row(slab(state_bias, span)))

    hidden = slab(block_input, share).astype(f32)
    cot_share = slab(cotangent, share).astype(f32)
    out_parts = to_parts(mm(uo.astype(bf16), output_weight), 1)
    block_output = (sum(out_parts[1:], out_parts[0]) + hidden).astype(bf16)

    gbb, ibb, sbb, qb = (x.astype(bf16) for x in (gb, back, sback[:, :heads], sq))
    partial_in = (
        mm(gbb, gate_weight, NT) + mm(ibb, inner_weight, NT) + mm(sbb, step_weight, NT)
        + mm(qb, slab(state_weight, span), NT)
    )
    in_parts = to_parts(partial_in, 1)
    d_normed = sum(in_parts[1:], in_parts[0])
    inv_in = inv[:, 0:1]
    normed = hidden * inv_in
    gain_share = row(slab(norm_gain, share))
    d_hat = d_normed * gain_share
    dot = jnp.sum(d_hat * normed, axis=1).reshape(-1, 128)
    dot = sum((swap(dot, k) for k in range(1, parts)), dot).reshape(-1, 1) / width
    input_gradient = inv_in * (d_hat - normed * dot) + cot_share
    norm_gain_grad = jnp.sum(d_normed * normed, axis=0)

    extra = jnp.concatenate([sq, sback[:, :heads], jnp.zeros((count, 128 - span - heads), f32)], axis=1)
    if hub_plan:
        zero = jnp.int32(0)

        def exchange(x):
            edge = lax.ppermute(x, "dp", to_hub)
            return x, edge, lax.ppermute(x, "dp", hubs), lax.ppermute(edge, "dp", hubs)

        def gradient(family, xs, first_y):
            cols = xs[0].shape[1]
            block = 256 if cols % 256 == 0 else 128
            rows_of = width // 2
            order = jnp.stack([side, 1 - side]).astype(jnp.int32)
            blocks = [
                pl.BlockSpec((1, 4 * count, rows_of // 2), lambda r, j, o: (family, 0, o[r])),
            ] + [pl.BlockSpec((count, block), lambda r, j, o: (0, j))] * 4
            sums_ = pl.pallas_call(
                lambda o, *refs: grad_kernel(*refs),
                grid_spec=pltpu.PrefetchScalarGridSpec(
                    num_scalar_prefetch=1, grid=(2, cols // block), in_specs=blocks,
                    out_specs=pl.BlockSpec((1, rows_of // 2, block), lambda r, j, o: (r, 0, j)),
                ),
                out_shape=struct((2, rows_of // 2, cols)),
                compiler_params=pltpu.CompilerParams(vmem_limit_bytes=56 << 20),
                cost_estimate=cost(8 * count * rows_of * cols, 16 * count * cols + 4 * rows_of * cols),
                name="gradient",
            )(order, features, *xs)
            both = sums_.reshape(2, 2, rows_of // 4, cols)
            pick = lambda x, i: lax.dynamic_index_in_dim(x, i, x.ndim - 3, False)
            if first_y:
                got = lax.ppermute(pick(both, 1 - y), "dp", lines)
                ready = pick(both, y) + got
                return jnp.where(hub, ready[0], lax.ppermute(ready[1], "dp", to_edge))
            taken = jnp.where(hub, both[0], lax.ppermute(both[1], "dp", to_edge))
            return pick(taken, y) + lax.ppermute(pick(taken, 1 - y), "dp", lines)

        output_grad = gradient(1, exchange(uo), True).T
        gate_grad = gradient(0, exchange(gb), False)
        mix = gradient(0, exchange(jnp.concatenate([back, extra], axis=1)), True)
        inner_grad, extra_grad = mix[:, :inner], mix[:, inner:]

        def over_dp(x):
            for k in (1, 2, 4):
                x = x + lax.ppermute(x, "dp", [(i, i ^ k) for i in range(8)])
            return x
    else:
        def scatter(a, b):
            return lax.psum_scatter(mm(a, b.astype(bf16), TN), "dp", scatter_dimension=0, tiled=True)

        output_grad = scatter(cotangent, uo).T
        gate_grad, inner_grad, extra_grad = scatter(nb, gb), scatter(nb, back), scatter(nb, extra)

        def over_dp(x):
            return lax.psum(x, "dp")

    step_grad = extra_grad[:, span : span + heads]
    state_grad = jnp.swapaxes(from_parts(extra_grad[:, :span]), 0, 1).reshape(-1, 2 * STATE)
    misc = jnp.concatenate([hrows[0], hrows[1], srows[: CONV + 1].reshape(-1), norm_gain_grad])
    misc = jnp.pad(misc, (0, -misc.shape[0] % 1024)).reshape(8, -1)
    smalls = over_dp(jnp.concatenate([rows, gg], axis=0))
    misc = over_dp(misc).reshape(-1)
    step_bias_grad, decay_grad = misc[:heads], misc[128 : 128 + heads]
    state_rows = from_parts(misc[256 : 256 + (CONV + 1) * span].reshape(CONV + 1, span))
    state_rows = jnp.swapaxes(state_rows, 0, 1).reshape(CONV + 1, 2 * STATE)
    at = 256 + (CONV + 1) * span
    skip_grad = jnp.sum(smalls[CONV + 1].reshape(heads, HEAD_DIM), axis=1)
    return (
        block_output,
        input_gradient,
        misc[at : at + share],
        gate_grad,
        inner_grad,
        step_grad,
        state_grad,
        smalls[:CONV],
        smalls[CONV],
        state_rows[:CONV],
        state_rows[CONV],
        step_bias_grad,
        decay_grad,
        skip_grad,
        smalls[8],
        output_grad,
    )


def solution(mesh):
    return jax.shard_map(
        on_device,
        mesh=mesh,
        in_specs=(
            P("dp", None), P("dp", None), P("dp", None), P(), P(None, "tensor"), P(None, "tensor"), P(None, "tensor"), P(),
            P(None, "tensor"), P("tensor"), P(), P(), P("tensor"), P("tensor"), P("tensor"), P("tensor"), P("tensor", None),
        ),
        out_specs=(
            P("dp", "tensor"), P("dp", "tensor"), P("tensor"), P("dp", "tensor"), P("dp", "tensor"), P("dp", "tensor"),
            P("dp", None), P(None, "tensor"), P("tensor"), P(), P(), P("tensor"), P("tensor"), P("tensor"), P("tensor"),
            P("tensor", "dp"),
        ),
        check_vma=False,
    )
```

```python
from functools import partial

import jax
import jax.numpy as jnp
from jax import lax
from jax.experimental import pallas as pl
from jax.experimental.pallas import tpu as pltpu
from jax.sharding import PartitionSpec as P

HEAD_DIM = 64
STATE = 128
CONV = 4
BLK = 256
HPB = BLK // HEAD_DIM
eps = 1e-05
NEG = -1e30
f32 = jnp.float32
bf16 = jnp.bfloat16
HIGH = lax.Precision.HIGHEST
NN = (((1,), (0,)), ((), ()))
NT = (((1,), (1,)), ((), ()))
TN = (((0,), (0,)), ((), ()))


def mm(a, b, dims=NN, precision=None):
    return lax.dot_general(a, b, dims, precision=precision, preferred_element_type=f32)


def sigmoid(x):
    return 1.0 / (1.0 + jnp.exp(-x))


def softplus(x):
    return jnp.maximum(x, 0.0) + jnp.log1p(jnp.exp(-jnp.abs(x)))


def seg_of(places, lengths):
    total = jnp.zeros(places.shape, jnp.int32)
    end = jnp.int32(0)
    for s in range(lengths.shape[1]):
        end = end + lengths[0, s]
        total = total + (places >= end).astype(jnp.int32)
    return total


def keeps(lengths, count):
    t = lax.broadcasted_iota(jnp.int32, (count, 1), 0)
    own = seg_of(t, lengths)
    out = [None]
    for back in range(1, CONV):
        out.append(((seg_of(t - back, lengths) == own) & (t >= back)).astype(f32))
    return out


def down(x, back):
    return pltpu.roll(x, back, 0)


def up(x, back):
    return pltpu.roll(x, x.shape[0] - back, 0)


def conv(u, kernel, bias, keep):
    out = bias + kernel[CONV - 1 : CONV, :] * u
    for back in range(1, CONV):
        out = out + kernel[CONV - 1 - back : CONV - back, :] * (down(u, back) * keep[back])
    return out


def conv_back(dc, u, kernel, keep):
    du = kernel[CONV - 1 : CONV, :] * dc
    rows = [jnp.sum(dc * u, axis=0, keepdims=True)]
    for back in range(1, CONV):
        kept = dc * keep[back]
        du = du + kernel[CONV - 1 - back : CONV - back, :] * up(kept, back)
        rows.append(jnp.sum(kept * down(u, back), axis=0, keepdims=True))
    return du, rows[::-1] + [jnp.sum(dc, axis=0, keepdims=True)]


def lanes_first(shape):
    return lax.broadcasted_iota(jnp.int32, shape, 1) < HEAD_DIM


def norm_kernel(x_ref, gain_ref, nb_ref, inv_ref):
    x = x_ref[...].astype(f32)
    inv = lax.rsqrt(jnp.sum(x * x, axis=1, keepdims=True) / x.shape[1] + eps)
    nb_ref[...] = (x * inv * gain_ref[...]).astype(bf16)
    inv_ref[...] = jnp.broadcast_to(inv, inv_ref.shape)


def forward_kernel(
    lengths, nb_ref, cot_ref, wg_ref, wi_ref, wo_ref, ws_ref, wst_ref, ik_ref, ib_ref, sk_ref, sb_ref,
    stepb_ref, decay_ref, skipc_ref, gain_ref,
    graw_ref, iraw_ref, cv_ref, mixed_ref, scaled_ref, sums_ref, sraw_ref, sact_ref, state_ref, hc_ref, lsr_ref,
    addm_ref, g_ref, keep_ref, acc,
):
    j = pl.program_id(0)
    count = nb_ref.shape[0]
    nb = nb_ref[...]

    @pl.when(j == 0)
    def _():
        i0 = lax.broadcasted_iota(jnp.int32, (count, count), 0)
        j0 = lax.broadcasted_iota(jnp.int32, (count, count), 1)
        same = (seg_of(i0, lengths) == seg_of(j0, lengths)) & (j0 <= i0)
        addm_ref[...] = jnp.where(same, 0.0, NEG)
        state = mm(nb, wst_ref[...])
        state_ref[...] = state
        keep = keeps(lengths, count)
        for back in range(1, CONV):
            keep_ref[:, back : back + 1] = keep[back]
        cv = conv(state, sk_ref[...], sb_ref[...], keep)
        act = cv * sigmoid(cv)
        sact_ref[...] = act
        g_ref[...] = mm(act[:, STATE:], act[:, :STATE], NT, HIGH)
        raw = mm(nb, ws_ref[...]) + stepb_ref[...]
        sraw_ref[...] = raw
        step = softplus(raw)
        logs = mm(same.astype(f32), step * (-jnp.exp(decay_ref[...])), NN, HIGH)
        lsr_ref[...] = jnp.transpose(logs)
        for k in range(hc_ref.shape[0]):
            hc_ref[k, :, 0:HPB] = logs[:, HPB * k : HPB * (k + 1)]
            hc_ref[k, :, HPB : 2 * HPB] = step[:, HPB * k : HPB * (k + 1)]
        acc[...] = jnp.zeros_like(acc)

    gate = mm(nb, wg_ref[...])
    inner = mm(nb, wi_ref[...])
    scaled = mm(cot_ref[...], wo_ref[...], NT)
    graw_ref[...] = gate
    iraw_ref[...] = inner
    scaled_ref[...] = scaled
    cv = conv(inner, ik_ref[...], ib_ref[...], keeps(lengths, count))
    cv_ref[...] = cv
    v = cv * sigmoid(cv)
    first = lanes_first((count, 2 * HEAD_DIM))
    addm = addm_ref[...]
    g = g_ref[...]
    parts = []
    for pair in range(BLK // (2 * HEAD_DIM)):
        vp = v[:, 2 * HEAD_DIM * pair : 2 * HEAD_DIM * (pair + 1)]
        k = 2 * pair
        steps = jnp.where(first, hc_ref[j, :, HPB + k : HPB + k + 1], hc_ref[j, :, HPB + k + 1 : HPB + k + 2])
        vs = (vp * steps).astype(bf16)
        ys = []
        for h in (k, k + 1):
            gaps = hc_ref[j, :, h : h + 1] - lsr_ref[pl.ds(HPB * j + h, 1), :] + addm
            ys.append(mm((g * jnp.exp(gaps)).astype(bf16), vs))
        parts.append(jnp.where(first, ys[0], ys[1]))
    mixed = jnp.concatenate(parts, axis=1) + skipc_ref[...] * v
    mixed_ref[...] = mixed
    gated = mixed * (gate * sigmoid(gate))
    acc[:, 0:1] += jnp.sum(gated * gated, axis=1, keepdims=True)
    acc[:, 1:2] += jnp.sum(scaled * gain_ref[...] * gated, axis=1, keepdims=True)

    @pl.when(j == pl.num_programs(0) - 1)
    def _():
        sums_ref[...] = jnp.transpose(acc[...])[0:8, :]


def unit_kernel(width, s_ref, graw_ref, mixed_ref, scaled_ref, gain_ref, x_ref, dm_ref, gg_ref):
    sums = jnp.sum(s_ref[...], axis=0)
    cols = jnp.transpose(sums)
    inv = lax.rsqrt(cols[:, 0:1] / width + eps)
    dot = inv * cols[:, 1:2]
    gate, mixed, scaled, gain = graw_ref[...], mixed_ref[...], scaled_ref[...], gain_ref[...]
    s = sigmoid(gate)
    act = gate * s
    unit = mixed * act * inv
    x_ref[0, 0] = (unit * gain).astype(bf16).astype(f32)
    gg_ref[...] = jnp.broadcast_to(jnp.sum(scaled * unit, axis=0, keepdims=True), gg_ref.shape)
    d_gated = inv * (scaled * gain - unit * (dot / width))
    dm_ref[...] = d_gated * act
    x_ref[1, 0] = (d_gated * mixed * s * (1.0 + gate * (1.0 - s))).astype(bf16).astype(f32)


def backward_kernel(
    lengths, dm_ref, cv_ref, iraw_ref, mixed_ref, hc_ref, lsr_ref, addm_ref, g_ref, sraw_ref, sact_ref,
    ik_ref, skipc_ref, decay_ref, _,
    back_ref, rows_ref, sback_ref, hrows_ref, dstate_ref, dg, dlogs, dstep,
):
    j = pl.program_id(0)
    count = dm_ref.shape[0]

    @pl.when(j == 0)
    def _():
        dg[...] = jnp.zeros_like(dg)
        dlogs[...] = jnp.zeros_like(dlogs)
        dstep[...] = jnp.zeros_like(dstep)

    cv, dm, skipc = cv_ref[...], dm_ref[...], skipc_ref[...]
    s = sigmoid(cv)
    v = cv * s
    within = mixed_ref[...] - skipc * v
    first = lanes_first((count, 2 * HEAD_DIM))
    addm = addm_ref[...]
    g = g_ref[...]
    us, vss, dyb, stepm = [], [], [], []
    total = dg[...]
    for pair in range(BLK // (2 * HEAD_DIM)):
        cols = slice(2 * HEAD_DIM * pair, 2 * HEAD_DIM * (pair + 1))
        k = 2 * pair
        steps = jnp.where(first, hc_ref[0, :, HPB + k : HPB + k + 1], hc_ref[0, :, HPB + k + 1 : HPB + k + 2])
        vs = (v[:, cols] * steps).astype(bf16)
        dy = dm[:, cols].astype(bf16)
        both = []
        for h in (k, k + 1):
            gaps = hc_ref[0, :, h : h + 1] - lsr_ref[pl.ds(HPB * j + h, 1), :] + addm
            decay = jnp.exp(gaps)
            both.append(mm((g * decay).astype(bf16), dy, TN))
            mine = first if h == k else jnp.logical_not(first)
            total = total + decay * mm(jnp.where(mine, dy, jnp.zeros_like(dy)), vs, NT)
        us.append(jnp.where(first, both[0], both[1]))
        vss.append(vs.astype(f32))
        dyb.append(dy.astype(f32))
        stepm.append(steps)
    dg[...] = total
    u = jnp.concatenate(us, axis=1)
    vs = jnp.concatenate(vss, axis=1)
    dy = jnp.concatenate(dyb, axis=1)
    steps = jnp.concatenate(stepm, axis=1)
    c0 = lax.broadcasted_iota(jnp.int32, (BLK, 128), 0) // HEAD_DIM
    l0 = lax.broadcasted_iota(jnp.int32, (BLK, 128), 1)
    pick = (l0 == c0 + HPB * j).astype(f32)
    dlogs[...] += mm(dy * within - vs * u, pick, NN, HIGH)
    dstep[...] += mm(v * u, pick, NN, HIGH)
    dv = steps * u + skipc * dm
    dc = dv * (s * (1.0 + cv * (1.0 - s)))
    du, rows = conv_back(dc, iraw_ref[...], ik_ref[...], keeps(lengths, count))
    back_ref[0, 0] = du.astype(bf16).astype(f32)
    rows_ref[...] = jnp.concatenate(rows + [jnp.sum(dm * v, axis=0, keepdims=True)] + [jnp.zeros((2, BLK), f32)], axis=0)

    @pl.when(j == pl.num_programs(0) - 1)
    def _():
        mask = (addm > -1.0).astype(f32)
        q = mm(mask, dlogs[...], TN, HIGH)
        raw = sraw_ref[...]
        step = softplus(raw)
        rate = -jnp.exp(decay_ref[...])
        draw = (dstep[...] + rate * q) * sigmoid(raw)
        sback_ref[...] = draw.astype(bf16).astype(f32)
        hrows_ref[...] = jnp.concatenate(
            [jnp.sum(draw, axis=0, keepdims=True), rate * jnp.sum(step * q, axis=0, keepdims=True), jnp.zeros((6, 128), f32)],
            axis=0,
        )
        act = sact_ref[...]
        d_b = mm(dg[...], act[:, STATE:], TN, HIGH)
        d_c = mm(dg[...], act[:, :STATE], NN, HIGH)
        both = jnp.concatenate([d_b, d_c], axis=1)
        span = dstate_ref.shape[2]
        for t in range(dstate_ref.shape[0]):
            dstate_ref[t] = both[:, span * t : span * (t + 1)]


def state_kernel(lengths, parts_ref, u_ref, sk_ref, sb_ref, back_ref, rows_ref):
    keep = keeps(lengths, u_ref.shape[0])
    cv = conv(u_ref[...], sk_ref[...], sb_ref[...], keep)
    s = sigmoid(cv)
    dc = jnp.sum(parts_ref[...], axis=0) * (s * (1.0 + cv * (1.0 - s)))
    du, rows = conv_back(dc, u_ref[...], sk_ref[...], keep)
    back_ref[...] = du.astype(bf16).astype(f32)
    rows_ref[...] = jnp.concatenate(rows + [jnp.zeros((3, du.shape[1]), f32)], axis=0)


MESH = pl.DeviceIdType.MESH


def features_kernel(slots, nb_ref, cot_ref, own_ref, across_ref, pair_ref, out_ref):
    count, piece = nb_ref.shape[0], own_ref.shape[2]
    out_ref[0, :, 0:count] = nb_ref[...].T
    out_ref[1, :, 0:count] = cot_ref[...].T

    def fill(tmp):
        for shard in range(3):
            for family in range(2):
                for k, ref in enumerate((own_ref.at[shard, family], pair_ref.at[0, shard, family],
                                         across_ref.at[shard, family], pair_ref.at[1, shard, family])):
                    at = pl.multiple_of(piece * slots[k], piece)
                    tmp[pl.ds(at, piece), :] = ref[...].astype(bf16)
                out_ref[family, :, count * (shard + 1) : count * (shard + 2)] = tmp[...].T

    pl.run_scoped(fill, pltpu.VMEM((count, nb_ref.shape[1]), bf16))


def exchange_kernel(
    x_ref, ft_ref, sback_ref, dstate_ref, rows_ref, gg_ref, hrows_ref, ustate_ref, kstate_ref, bstate_ref, keep_ref, wx_ref,
    hidden_ref, cot_ref, inv_ref, gain_ref, wg_ref, wi_ref, wo_ref,
    out_ref, din_ref, gate_out, inner_out, state_out, step_out, turned_out, smalls_ref,
    big, yra, yrb, r, ea, fin, turned, xb, wro, wri, po, por, pir, dsr, srr, sm, smr, ex, exr, rx, exe, yrx, exg, dots, dotr,
    p1s, p1r, p2s, p2r, p3s, p3r, es, er, yas, yar, ybs, ybr, fas, far, fins, wsem, pos, porr, pis, pirr,
    dss, dsrr, srs, srrr, dts, dtr, sms, smrr, exs, exrr, yxs, yxr, exgs, exgr,
):
    d, t = lax.axis_index("dp"), lax.axis_index("tensor")
    y, z = d % 2, d // 2
    side = z % 2
    hub = (z == 1) | (z == 2)
    edge = jnp.logical_not(hub)
    chunks, count, wide = x_ref.shape
    each = chunks // 3
    lanes = wide // 2
    part = ft_ref.shape[1] // 2
    own = part // 2
    share = hidden_ref.shape[1]
    span = dsr.shape[2]
    inner = each * wide
    pair, peer, line = d ^ 2, d ^ 6, d ^ 1
    mine, other = pl.multiple_of(own * y, own), pl.multiple_of(own * (1 - y), own)
    mine_part, pair_part = pl.multiple_of(part * side, part), pl.multiple_of(part * (1 - side), part)

    def send(src, dst, ssem, rsem, dev):
        return pltpu.make_async_remote_copy(
            src_ref=src, dst_ref=dst, send_sem=ssem, recv_sem=rsem, device_id=dev, device_id_type=MESH
        )

    def p1(q):
        return send(x_ref.at[q], big.at[q, pl.ds(0, count)], p1s.at[q], p1r.at[q], (pair, t))

    def p2(q):
        return send(x_ref.at[q], big.at[q, pl.ds(count, count)], p2s.at[q], p2r.at[q], (peer, t))

    def p3(q):
        return send(big.at[q, pl.ds(0, count)], big.at[q, pl.ds(2 * count, count)], p3s.at[q], p3r.at[q], (peer, t))

    def e(q):
        return send(
            r.at[q % 2, 0, :, pl.ds(lanes, lanes)], big.at[q, pl.ds(0, part), pl.ds(0, lanes)], es.at[q], er.at[q], (pair, t)
        )

    def ya(q, k):
        return send(
            r.at[q % 2, k, pl.ds(other, own), pl.ds(0, lanes)], yra.at[q, k], yas.at[q, k], yar.at[q, k], (line, t)
        )

    def yb_hub(q):
        return send(r.at[q % 2, 1, pl.ds(other, own), pl.ds(lanes, lanes)], yrb.at[q], ybs.at[q], ybr.at[q], (line, t))

    def yb_edge(q):
        return send(big.at[q, pl.ds(other, own), pl.ds(0, lanes)], yrb.at[q], ybs.at[q], ybr.at[q], (line, t))

    def fa(q):
        return send(ea.at[q % 2], yra.at[q, 0], fas.at[q], far.at[q], (pair, t))

    p1x = send(ex, exr.at[0], exs.at[0], exrr.at[0], (pair, t))
    p2x = send(ex, exr.at[1], exs.at[1], exrr.at[1], (peer, t))
    p3x = send(exr.at[0], exr.at[2], exs.at[2], exrr.at[2], (peer, t))
    e_x = send(rx.at[0], exe, exs.at[3], exrr.at[3], (pair, t))
    yx_hub = send(rx.at[1, pl.ds(other, own)], yrx, yxs.at[0], yxr.at[0], (line, t))
    yx_edge = send(exe.at[pl.ds(other, own)], yrx, yxs.at[0], yxr.at[0], (line, t))

    def over_tensor(src, dst, ssem, rsem):
        return [send(src(k), dst(k), ssem.at[k - 1], rsem.at[k - 1], (d, t ^ k)) for k in range(1, 4)]

    state_copies = over_tensor(lambda k: dstate_ref.at[t ^ k], lambda k: dsr.at[k - 1], dss, dsrr)
    row_copies = over_tensor(lambda k: srr.at[t], lambda k: srr.at[t], srs, srrr)
    po_copies = over_tensor(lambda k: po.at[k], lambda k: por.at[k - 1], pos, porr)
    pi_copies = over_tensor(lambda k: po.at[k], lambda k: pir.at[k - 1], pis, pirr)
    dot_copies = over_tensor(lambda k: dots, lambda k: dotr.at[k - 1], dts, dtr)
    ex_copies = over_tensor(lambda k: exg.at[t], lambda k: exg.at[t], exgs, exgr)
    small_copies = [send(sm, smr.at[k], sms.at[k], smrr.at[k], (d ^ (1 << k), t)) for k in range(3)]

    def started(copies):
        for c in copies:
            c.start()

    def waited(copies):
        for c in copies:
            c.wait()

    barrier = pltpu.get_barrier_semaphore()
    for dev in ((pair, t), (peer, t), (line, t), (d ^ 4, t), (d, t ^ 1), (d, t ^ 2), (d, t ^ 3)):
        pl.semaphore_signal(barrier, inc=1, device_id=dev, device_id_type=MESH)
    pl.semaphore_wait(barrier, 7)

    @pl.when(hub)
    def _():
        for q in range(each):
            p2(q).start()

    @pl.when(edge)
    def _():
        for q in range(each):
            p1(q).start()

    started(state_copies)

    order = [1, 2, 3, 0]
    ats = [pl.multiple_of((t ^ k) * share, share) for k in range(4)]

    def load_out(i):
        return pltpu.make_async_copy(wo_ref.at[:, pl.ds(ats[order[i]], share)], wro.at[i % 2], wsem.at[0, i])

    def load_in(i, k):
        ref = wi_ref if k else wg_ref
        return pltpu.make_async_copy(ref.at[pl.ds(ats[order[i]], share), :], wri.at[i % 2, k], wsem.at[1 + k, i])

    for i in range(2):
        load_out(i).start()
        load_in(i, 0).start()
        load_in(i, 1).start()

    def states():
        waited(state_copies)
        total = dstate_ref[t] + dsr[0] + dsr[1] + dsr[2]
        keep = [None] + [keep_ref[:, b : b + 1] for b in range(1, CONV)]
        u, kernel = ustate_ref[...], kstate_ref[...]
        cv = conv(u, kernel, bstate_ref[...], keep)
        s = sigmoid(cv)
        du, rows = conv_back(total * (s * (1.0 + cv * (1.0 - s))), u, kernel, keep)
        ex[:, 0:span] = du.astype(bf16).astype(f32)
        ex[:, span : 2 * span] = sback_ref[:, 0:span]
        srr[t] = jnp.concatenate(rows + [jnp.zeros((3, span), f32)], axis=0)
        started(row_copies)

        @pl.when(hub)
        def _():
            p2x.start()

        @pl.when(edge)
        def _():
            p1x.start()

    def out_parts():
        for i, k in enumerate(order):
            load_out(i).wait()
            total = None
            for c in range(each):
                one = mm(x_ref[c].astype(bf16), wro[i % 2, c * wide : (c + 1) * wide, :])
                total = one if total is None else total + one
            po[k] = total
            if i + 2 < 4:
                load_out(i + 2).start()
            if k:
                po_copies[k - 1].start()

    def out_sum():
        waited(po_copies)
        out_ref[...] = (po[0] + por[0] + por[1] + por[2] + hidden_ref[...].astype(f32)).astype(bf16)

    def in_parts():
        extra = ex[...].astype(bf16)
        for i, k in enumerate(order):
            load_in(i, 0).wait()
            load_in(i, 1).wait()
            total = mm(extra, wx_ref[pl.ds(ats[k], share), :], NT)
            for c in range(each):
                cols = slice(c * wide, (c + 1) * wide)
                total = total + mm(x_ref[each + c].astype(bf16), wri[i % 2, 0, :, cols], NT)
                total = total + mm(x_ref[2 * each + c].astype(bf16), wri[i % 2, 1, :, cols], NT)
            po[k] = total
            if i + 2 < 4:
                load_in(i + 2, 0).start()
                load_in(i + 2, 1).start()
            if k:
                pi_copies[k - 1].start()

    def normed():
        return hidden_ref[...].astype(f32) * inv_ref[:, 0:1]

    def in_sum():
        waited(pi_copies)
        d_normed = po[0] + pir[0] + pir[1] + pir[2]
        po[0] = d_normed
        dot = jnp.sum(d_normed * gain_ref[...] * normed(), axis=1, keepdims=True)
        dots[...] = jnp.transpose(jnp.broadcast_to(dot, (count, 128)))[0:8, :]
        started(dot_copies)

    def finish():
        waited(dot_copies)
        waited(row_copies)
        d_normed, n = po[0], normed()
        dot = jnp.transpose(dots[...] + dotr[0] + dotr[1] + dotr[2])[:, 0:1] / (4 * share)
        din_ref[...] = inv_ref[:, 0:1] * (d_normed * gain_ref[...] - n * dot) + cot_ref[...].astype(f32)
        sm[0:8, :] = rows_ref[...]
        sm[8:16, :] = jnp.zeros((8, inner), f32)
        sm[8:9, :] = gg_ref[0:1, :]
        sm[9:10, 0:share] = jnp.sum(d_normed * n, axis=0, keepdims=True)
        for i in range(4):
            sm[10:15, span * i : span * (i + 1)] = srr[i][0:5, :]
        sm[15:16, 0:128] = hrows_ref[0:1, :]
        sm[15:16, 128:256] = hrows_ref[1:2, :]
        small_copies[0].start()

    def small(k):
        small_copies[k].wait()
        sm[...] = sm[...] + smr[k]
        if k < 2:
            small_copies[k + 1].start()
        else:
            smalls_ref[...] = sm[...]

    def extra_hub():
        p2x.wait_recv()
        p3x.wait_recv()
        for k, ref in enumerate((ex, exr.at[0], exr.at[1], exr.at[2])):
            xb[k * count : (k + 1) * count, 0:128] = ref[...].astype(bf16)
        rx[0] = mm(ft_ref[0, pl.ds(pair_part, part), :], xb[:, 0:128])
        rx[1] = mm(ft_ref[0, pl.ds(mine_part, part), :], xb[:, 0:128])
        e_x.start()
        yx_hub.start()

    def process(q):
        p2(q).wait_recv()
        p3(q).wait_recv()

        @pl.when(q >= 2)
        def _():
            e(q - 2).wait_send()
            ya(q - 2, 0).wait_send()
            ya(q - 2, 1).wait_send()
            yb_hub(q - 2).wait_send()

        xb[0:count, :] = x_ref[q].astype(bf16)
        xb[count:, :] = big[q].astype(bf16)
        family = jnp.where(q < each, 1, 0)
        slot = q % 2
        r[slot, 0] = mm(ft_ref[family, pl.ds(pair_part, part), :], xb[...])
        e(q).start()
        ya(q, 0).start()
        r[slot, 1] = mm(ft_ref[family, pl.ds(mine_part, part), :], xb[...])
        ya(q, 1).start()
        yb_hub(q).start()

    def stored(q):
        slot = q % 2
        c = q % each
        at = pl.multiple_of(c * wide, wide)
        return (
            pltpu.make_async_copy(turned.at[slot], turned_out.at[pl.ds(at, wide), :], fins.at[q]),
            pltpu.make_async_copy(fin.at[slot], gate_out.at[:, pl.ds(at, wide)], fins.at[q]),
            pltpu.make_async_copy(fin.at[slot], inner_out.at[:, pl.ds(at, wide)], fins.at[q]),
        )

    def store(q, left, right):
        slot = q % 2

        def waiting(p):
            for k in range(3):
                @pl.when((p >= k * each) & (p < (k + 1) * each))
                def _():
                    stored(p)[k].wait()

        @pl.when(q >= 2)
        def _():
            waiting(q - 2)

        fin[slot, :, 0:lanes] = left
        fin[slot, :, lanes:] = right

        @pl.when(q < each)
        def _():
            turned[slot] = jnp.transpose(fin[slot])

        for k in range(3):
            @pl.when((q >= k * each) & (q < (k + 1) * each))
            def _():
                stored(q)[k].start()

    def finalize_hub(q):
        slot = q % 2
        ya(q, 0).wait_recv()
        ya(q, 1).wait_recv()
        yb_hub(q).wait_recv()

        @pl.when(q >= 2)
        def _():
            fa(q - 2).wait_send()

        ea[slot] = r[slot, 0, pl.ds(mine, own), 0:lanes] + yra[q, 0]
        fa(q).start()
        store(
            q,
            r[slot, 1, pl.ds(mine, own), 0:lanes] + yra[q, 1],
            r[slot, 1, pl.ds(mine, own), lanes:] + yrb[q],
        )

    def finalize_edge(q):
        yb_edge(q).wait_recv()
        fa(q).wait_recv()
        store(q, yra[q, 0], big[q, pl.ds(mine, own), 0:lanes] + yrb[q])

    def extra_sent():
        started(ex_copies)

    def extra_done():
        waited(ex_copies)
        for i in range(4):
            state_out[:, span * i : span * (i + 1)] = exg[i, :, 0:span]

    pieces = {
        1: states, 2: out_parts, 3: out_sum, 4: in_parts, 6: in_sum, 7: finish,
        9: lambda: small(0), 12: lambda: small(1), 15: lambda: small(2), 14: extra_sent, 16: extra_done,
    }

    def body(q, carry):
        @pl.when(hub)
        def _():
            @pl.when(q < chunks)
            def _():
                p1(q).wait_recv()
                p3(q).start()

            @pl.when(q + each < chunks)
            def _():
                p2(q + each).start()

            @pl.when((q >= 1) & (q <= chunks))
            def _():
                process(q - 1)

            @pl.when(q >= 2)
            def _():
                finalize_hub(q - 2)

            @pl.when(q == 5)
            def _():
                p1x.wait_recv()
                p3x.start()

            @pl.when(q == 9)
            def _():
                extra_hub()

            @pl.when(q == 14)
            def _():
                yx_hub.wait_recv()
                exg[t] = rx[1, pl.ds(mine, own), :] + yrx[...]
                step_out[...] = exg[t]

        @pl.when(edge)
        def _():
            @pl.when(q < chunks)
            def _():
                e(q).wait_recv()
                yb_edge(q).start()

            @pl.when(q + each < chunks)
            def _():
                p1(q + each).start()

            @pl.when((q >= 1) & (q <= chunks))
            def _():
                finalize_edge(q - 1)

            @pl.when(q == 11)
            def _():
                e_x.wait_recv()
                yx_edge.start()

            @pl.when(q == 14)
            def _():
                yx_edge.wait_recv()
                exg[t] = exe[pl.ds(mine, own), :] + yrx[...]
                step_out[...] = exg[t]

        for at, piece in pieces.items():
            pl.when(q == at)(piece)
        return carry

    lax.fori_loop(0, chunks + 2, body, 0)

    stored(chunks - 2)[2].wait()
    stored(chunks - 1)[2].wait()

    @pl.when(hub)
    def _():
        def drain(q, carry):
            p2(q).wait_send()
            p3(q).wait_send()
            return carry

        lax.fori_loop(0, chunks, drain, 0)
        for q in (chunks - 2, chunks - 1):
            e(q).wait_send()
            ya(q, 0).wait_send()
            ya(q, 1).wait_send()
            yb_hub(q).wait_send()
            fa(q).wait_send()
        p2x.wait_send()
        p3x.wait_send()
        e_x.wait_send()
        yx_hub.wait_send()

    @pl.when(edge)
    def _():
        def drain(q, carry):
            p1(q).wait_send()
            yb_edge(q).wait_send()
            return carry

        lax.fori_loop(0, chunks, drain, 0)
        p1x.wait_send()
        yx_edge.wait_send()


def whole(shape):
    return pl.BlockSpec(shape, lambda *_: (0,) * len(shape))


def columns(rows):
    return pl.BlockSpec((rows, BLK), lambda j, *_: (0, j))


SMEM = pl.BlockSpec(memory_space=pltpu.SMEM)
VM = pltpu.CompilerParams(vmem_limit_bytes=56 << 20)
VMS = pltpu.CompilerParams(vmem_limit_bytes=56 << 20, dimension_semantics=("arbitrary",))


def struct(shape, dtype=f32):
    return jax.ShapeDtypeStruct(shape, dtype)


def cost(flops, moved):
    return pl.CostEstimate(flops=int(flops), bytes_accessed=int(moved), transcendentals=0)


def on_device(
    block_input, cotangent, seq_lengths, norm_gain, gate_weight, inner_weight, step_weight, state_weight,
    inner_kernel, inner_bias, state_kernel_, state_bias, step_bias, decay_log, skip_scale, gate_gain, output_weight,
):
    parts = lax.axis_size("tensor")
    shards = lax.axis_size("dp")
    t = lax.axis_index("tensor")
    count, width = block_input.shape
    inner = gate_weight.shape[1]
    heads = step_bias.shape[0]
    share = width // parts
    span = 2 * STATE // parts
    steps = inner // BLK
    pad = ((0, 0), (0, 128 - heads))
    row = lambda x: x.reshape(1, -1)

    def swap(x, k):
        return lax.ppermute(x, "tensor", [(i, i ^ k) for i in range(parts)])

    nb, inv = pl.pallas_call(
        norm_kernel,
        out_shape=(struct((count, width), bf16), struct((count, 128))),
        compiler_params=VM,
        name="norm_in",
    )(block_input, row(norm_gain))

    hub_plan = shards == 8 and parts == 4
    if hub_plan:
        d = lax.axis_index("dp")
        z, y = d // 2, d % 2
        half, side = z // 2, z % 2
        hub = (z == 1) | (z == 2)
        to_hub = [(0, 2), (1, 3), (6, 4), (7, 5)]
        hubs = [(2, 4), (4, 2), (3, 5), (5, 3)]
        to_edge = [(b, a) for a, b in to_hub]
        lines = [(i, i ^ 1) for i in range(8)]
        near, far = half * (width // 2), (1 - half) * (width // 2)
        piece = count // parts
        cut = lambda x: lax.dynamic_slice_in_dim(x, t * piece, piece, 0)
        mine = jnp.stack([cut(nb), cut(cotangent)]).astype(f32)
        side_of = lambda x, at: lax.dynamic_slice_in_dim(x, at, width // 2, x.ndim - 1)
        from_edge = lax.ppermute(mine, "dp", to_hub)
        from_hub = lax.ppermute(side_of(mine, far), "dp", hubs)
        from_far = lax.ppermute(side_of(from_edge, far), "dp", hubs)
        own = jnp.stack([side_of(from_edge, near), from_hub, from_far])
        across = swap(own, 2)
        pair = swap(jnp.stack([own, across]), 1)
        slots = jnp.stack([t, t ^ 1, t ^ 2, t ^ 3]).astype(jnp.int32)
        features = pl.pallas_call(
            features_kernel,
            in_specs=[SMEM] + [pl.BlockSpec(memory_space=pltpu.VMEM)] * 5,
            out_shape=struct((2, width // 2, 4 * count), bf16),
            compiler_params=VM,
            name="features",
        )(slots, side_of(nb, near), side_of(cotangent, near), own, across, pair)

    padded_step = jnp.pad(step_weight, pad)
    stepb, decay = jnp.pad(row(step_bias), pad), jnp.pad(row(decay_log), pad)
    skipc = jnp.repeat(skip_scale, HEAD_DIM).reshape(1, -1)
    ik, ib, gain = inner_kernel, row(inner_bias), row(gate_gain)
    full = struct((count, inner))
    graw, iraw, cv, mixed, scaled, sums, sraw, sact, state_raw, hc, lsr, addm, g, keep = pl.pallas_call(
        forward_kernel,
        grid=(steps,),
        in_specs=[
            SMEM, whole((count, width)), whole((count, width)), columns(width), columns(width),
            pl.BlockSpec((BLK, width), lambda j: (j, 0)), whole((width, 128)), whole((width, 2 * STATE)),
            columns(CONV), columns(1), whole((CONV, 2 * STATE)), whole((1, 2 * STATE)), whole((1, 128)), whole((1, 128)),
            columns(1), columns(1),
        ],
        out_specs=(
            [columns(count)] * 5
            + [whole((8, count)), whole((count, 128)), whole((count, 2 * STATE)), whole((count, 2 * STATE)),
               whole((steps, count, 128)), whole((128, count)), whole((count, count)), whole((count, count)),
               whole((count, 128))]
        ),
        out_shape=(
            [full] * 5
            + [struct((8, count)), struct((count, 128)), struct((count, 2 * STATE)), struct((count, 2 * STATE)),
               struct((steps, count, 128)), struct((128, count)), struct((count, count)), struct((count, count)),
               struct((count, 128))]
        ),
        scratch_shapes=[pltpu.VMEM((count, 128), f32)],
        compiler_params=VMS,
        cost_estimate=cost(6 * count * width * inner, 6 * width * inner + 20 * count * inner),
        name="forward",
    )(
        seq_lengths, nb, cotangent, gate_weight, inner_weight, output_weight, padded_step, state_weight, ik, ib,
        state_kernel_, row(state_bias), stepb, decay, skipc, gain,
    )

    all_sums = jnp.stack([sums] + [swap(sums, k) for k in range(1, parts)])
    x, dm, gg = pl.pallas_call(
        partial(unit_kernel, float(inner * parts)),
        grid=(steps,),
        in_specs=[whole((parts, 8, count)), columns(count), columns(count), columns(count), columns(1)],
        out_specs=[pl.BlockSpec((2, 1, count, BLK), lambda j: (0, j, 0, 0)), columns(count), columns(8)],
        out_shape=[struct((3, steps, count, BLK)), full, struct((8, inner))],
        compiler_params=VMS,
        cost_estimate=cost(0, 24 * count * inner),
        name="unit",
    )(all_sums, graw, mixed, scaled, gain)

    x, rows, sback, hrows, dstate = pl.pallas_call(
        backward_kernel,
        grid=(steps,),
        in_specs=[
            SMEM, columns(count), columns(count), columns(count), columns(count),
            pl.BlockSpec((1, count, 128), lambda j: (j, 0, 0)), whole((128, count)), whole((count, count)),
            whole((count, count)), whole((count, 128)), whole((count, 2 * STATE)), columns(CONV), columns(1), whole((1, 128)),
            pl.BlockSpec(memory_space=pl.ANY),
        ],
        input_output_aliases={14: 0},
        out_specs=[pl.BlockSpec((1, 1, count, BLK), lambda j: (2, j, 0, 0)), columns(8), whole((count, 128)), whole((8, 128)), whole((parts, count, span))],
        out_shape=[struct((3, steps, count, BLK)), struct((8, inner)), struct((count, 128)), struct((8, 128)), struct((parts, count, span))],
        scratch_shapes=[pltpu.VMEM((count, count), f32), pltpu.VMEM((count, 128), f32), pltpu.VMEM((count, 128), f32)],
        compiler_params=VMS,
        cost_estimate=cost(40 * count * count * inner // 64 * 4, 24 * count * inner),
        name="backward",
    )(seq_lengths, dm, cv, iraw, mixed, hc, lsr, addm, g, sraw, sact, ik, skipc, decay, x)

    slab = lambda x, size: lax.dynamic_slice_in_dim(x, t * size, size, x.ndim - 1)
    if hub_plan:
        weight_x = jnp.concatenate(
            [slab(state_weight, span), step_weight, jnp.zeros((width, 128 - span - heads), bf16)], axis=1
        )
        chunks = 3 * steps
        own = width // 8
        half_blk = BLK // 2
        dma = pltpu.SemaphoreType.DMA
        vmem, hbm = pl.BlockSpec(memory_space=pltpu.VMEM), pl.BlockSpec(memory_space=pl.ANY)
        block_output, input_gradient, gate_grad, inner_grad, state_grad, extra_grad, output_grad, smalls = pl.pallas_call(
            exchange_kernel,
            in_specs=[vmem] * 16 + [hbm] * 3,
            out_specs=[vmem, vmem, hbm, hbm, vmem, vmem, hbm, vmem],
            out_shape=[
                struct((count, share), bf16), struct((count, share)), struct((2 * own // 2, inner)), struct((own, inner)),
                struct((own, 2 * STATE)), struct((own, 128)), struct((inner, own)), struct((16, inner)),
            ],
            scratch_shapes=[
                pltpu.VMEM((chunks, 3 * count, BLK), f32), pltpu.VMEM((chunks, 2, own, half_blk), f32),
                pltpu.VMEM((chunks, own, half_blk), f32), pltpu.VMEM((2, 2, 2 * own, BLK), f32),
                pltpu.VMEM((2, own, half_blk), f32), pltpu.VMEM((2, own, BLK), f32), pltpu.VMEM((2, BLK, own), f32),
                pltpu.VMEM((4 * count, BLK), bf16), pltpu.VMEM((2, inner, share), bf16), pltpu.VMEM((2, 2, share, inner), bf16),
                pltpu.VMEM((4, count, share), f32), pltpu.VMEM((3, count, share), f32), pltpu.VMEM((3, count, share), f32),
                pltpu.VMEM((3, count, span), f32), pltpu.VMEM((4, 8, span), f32), pltpu.VMEM((16, inner), f32),
                pltpu.VMEM((3, 16, inner), f32), pltpu.VMEM((count, 128), f32), pltpu.VMEM((3, count, 128), f32),
                pltpu.VMEM((2, 2 * own, 128), f32), pltpu.VMEM((2 * own, 128), f32), pltpu.VMEM((own, 128), f32),
                pltpu.VMEM((4, own, 128), f32), pltpu.VMEM((8, count), f32), pltpu.VMEM((3, 8, count), f32),
            ]
            + [dma((chunks,))] * 8 + [dma((chunks, 2))] * 2 + [dma((chunks,))] * 5 + [dma((3, 4))] + [dma((3,))] * 12
            + [dma((4,))] * 2 + [dma((1,))] * 2 + [dma((3,))] * 2,
            compiler_params=pltpu.CompilerParams(collective_id=1, has_side_effects=True, vmem_limit_bytes=62 << 20),
            name="exchange",
        )(
            x.reshape(chunks, count, BLK), features, sback, dstate, rows, gg, hrows, slab(state_raw, span),
            slab(state_kernel_, span), row(slab(state_bias, span)), keep, weight_x, slab(block_input, share),
            slab(cotangent, share), inv, row(slab(norm_gain, share)), gate_weight, inner_weight, output_weight,
        )
        return (
            block_output, input_gradient, smalls[9, :share], gate_grad, inner_grad, extra_grad[:, span : span + heads],
            state_grad, smalls[:CONV], smalls[CONV], smalls[10 : 10 + CONV, : 2 * STATE], smalls[10 + CONV, : 2 * STATE],
            smalls[15, :heads], smalls[15, 128 : 128 + heads],
            jnp.sum(smalls[CONV + 1].reshape(heads, HEAD_DIM), axis=1), smalls[8], output_grad,
        )

    uo, gb, back = (jnp.swapaxes(x[i], 0, 1).reshape(count, inner) for i in range(3))

    def to_parts(x, axis):
        size = x.shape[axis] // parts
        block = lambda i: lax.dynamic_slice_in_dim(x, i * size, size, axis)
        got = [swap(block(t ^ k), k) for k in range(1, parts)]
        return [block(t)] + got

    def from_parts(x):
        got = jnp.stack([x] + [swap(x, k) for k in range(1, parts)])
        return jnp.stack([lax.dynamic_index_in_dim(got, t ^ i, 0, False) for i in range(parts)])

    state_parts = jnp.concatenate(to_parts(dstate, 0), axis=0)
    sq, srows = pl.pallas_call(
        state_kernel,
        in_specs=[SMEM] + [pl.BlockSpec(memory_space=pltpu.VMEM)] * 4,
        out_shape=(struct((count, span)), struct((8, span))),
        compiler_params=VM,
        name="state_back",
    )(seq_lengths, state_parts, slab(state_raw, span), slab(state_kernel_, span), row(slab(state_bias, span)))

    hidden = slab(block_input, share).astype(f32)
    cot_share = slab(cotangent, share).astype(f32)
    out_parts = to_parts(mm(uo.astype(bf16), output_weight), 1)
    block_output = (sum(out_parts[1:], out_parts[0]) + hidden).astype(bf16)

    gbb, ibb, sbb, qb = (x.astype(bf16) for x in (gb, back, sback[:, :heads], sq))
    partial_in = (
        mm(gbb, gate_weight, NT) + mm(ibb, inner_weight, NT) + mm(sbb, step_weight, NT)
        + mm(qb, slab(state_weight, span), NT)
    )
    in_parts = to_parts(partial_in, 1)
    d_normed = sum(in_parts[1:], in_parts[0])
    inv_in = inv[:, 0:1]
    normed = hidden * inv_in
    gain_share = row(slab(norm_gain, share))
    d_hat = d_normed * gain_share
    dot = jnp.sum(d_hat * normed, axis=1).reshape(-1, 128)
    dot = sum((swap(dot, k) for k in range(1, parts)), dot).reshape(-1, 1) / width
    input_gradient = inv_in * (d_hat - normed * dot) + cot_share
    norm_gain_grad = jnp.sum(d_normed * normed, axis=0)

    extra = jnp.concatenate([sq, sback[:, :heads], jnp.zeros((count, 128 - span - heads), f32)], axis=1)

    def scatter(a, b):
        return lax.psum_scatter(mm(a, b.astype(bf16), TN), "dp", scatter_dimension=0, tiled=True)

    output_grad = scatter(cotangent, uo).T
    gate_grad, inner_grad, extra_grad = scatter(nb, gb), scatter(nb, back), scatter(nb, extra)

    def over_dp(x):
        return lax.psum(x, "dp")

    step_grad = extra_grad[:, span : span + heads]
    state_grad = jnp.swapaxes(from_parts(extra_grad[:, :span]), 0, 1).reshape(-1, 2 * STATE)
    misc = jnp.concatenate([hrows[0], hrows[1], srows[: CONV + 1].reshape(-1), norm_gain_grad])
    misc = jnp.pad(misc, (0, -misc.shape[0] % 1024)).reshape(8, -1)
    smalls = over_dp(jnp.concatenate([rows, gg], axis=0))
    misc = over_dp(misc).reshape(-1)
    step_bias_grad, decay_grad = misc[:heads], misc[128 : 128 + heads]
    state_rows = from_parts(misc[256 : 256 + (CONV + 1) * span].reshape(CONV + 1, span))
    state_rows = jnp.swapaxes(state_rows, 0, 1).reshape(CONV + 1, 2 * STATE)
    at = 256 + (CONV + 1) * span
    skip_grad = jnp.sum(smalls[CONV + 1].reshape(heads, HEAD_DIM), axis=1)
    return (
        block_output,
        input_gradient,
        misc[at : at + share],
        gate_grad,
        inner_grad,
        step_grad,
        state_grad,
        smalls[:CONV],
        smalls[CONV],
        state_rows[:CONV],
        state_rows[CONV],
        step_bias_grad,
        decay_grad,
        skip_grad,
        smalls[8],
        output_grad,
    )


def solution(mesh):
    return jax.shard_map(
        on_device,
        mesh=mesh,
        in_specs=(
            P("dp", None), P("dp", None), P("dp", None), P(), P(None, "tensor"), P(None, "tensor"), P(None, "tensor"), P(),
            P(None, "tensor"), P("tensor"), P(), P(), P("tensor"), P("tensor"), P("tensor"), P("tensor"), P("tensor", None),
        ),
        out_specs=(
            P("dp", "tensor"), P("dp", "tensor"), P("tensor"), P("dp", "tensor"), P("dp", "tensor"), P("dp", "tensor"),
            P("dp", None), P(None, "tensor"), P("tensor"), P(), P(), P("tensor"), P("tensor"), P("tensor"), P("tensor"),
            P("tensor", "dp"),
        ),
        check_vma=False,
    )
```

```python
from functools import partial

import jax
import jax.numpy as jnp
from jax import lax
from jax.experimental import pallas as pl
from jax.experimental.pallas import tpu as pltpu
from jax.sharding import PartitionSpec as P

HEAD_DIM = 64
STATE = 128
CONV = 4
BLK = 256
HPB = BLK // HEAD_DIM
eps = 1e-05
NEG = -1e30
f32 = jnp.float32
bf16 = jnp.bfloat16
HIGH = lax.Precision.HIGHEST
NN = (((1,), (0,)), ((), ()))
NT = (((1,), (1,)), ((), ()))
TN = (((0,), (0,)), ((), ()))


def mm(a, b, dims=NN, precision=None):
    return lax.dot_general(a, b, dims, precision=precision, preferred_element_type=f32)


def sigmoid(x):
    return 1.0 / (1.0 + jnp.exp(-x))


def softplus(x):
    return jnp.maximum(x, 0.0) + jnp.log1p(jnp.exp(-jnp.abs(x)))


def seg_of(places, lengths):
    total = jnp.zeros(places.shape, jnp.int32)
    end = jnp.int32(0)
    for s in range(lengths.shape[1]):
        end = end + lengths[0, s]
        total = total + (places >= end).astype(jnp.int32)
    return total


def keeps(lengths, count):
    t = lax.broadcasted_iota(jnp.int32, (count, 1), 0)
    own = seg_of(t, lengths)
    out = [None]
    for back in range(1, CONV):
        out.append(((seg_of(t - back, lengths) == own) & (t >= back)).astype(f32))
    return out


def down(x, back):
    return pltpu.roll(x, back, 0)


def up(x, back):
    return pltpu.roll(x, x.shape[0] - back, 0)


def conv(u, kernel, bias, keep):
    out = bias + kernel[CONV - 1 : CONV, :] * u
    for back in range(1, CONV):
        out = out + kernel[CONV - 1 - back : CONV - back, :] * (down(u, back) * keep[back])
    return out


def conv_back(dc, u, kernel, keep):
    du = kernel[CONV - 1 : CONV, :] * dc
    rows = [jnp.sum(dc * u, axis=0, keepdims=True)]
    for back in range(1, CONV):
        kept = dc * keep[back]
        du = du + kernel[CONV - 1 - back : CONV - back, :] * up(kept, back)
        rows.append(jnp.sum(kept * down(u, back), axis=0, keepdims=True))
    return du, rows[::-1] + [jnp.sum(dc, axis=0, keepdims=True)]


def lanes_first(shape):
    return lax.broadcasted_iota(jnp.int32, shape, 1) < HEAD_DIM


def norm_kernel(x_ref, gain_ref, nb_ref, inv_ref):
    x = x_ref[...].astype(f32)
    inv = lax.rsqrt(jnp.sum(x * x, axis=1, keepdims=True) / x.shape[1] + eps)
    nb_ref[...] = (x * inv * gain_ref[...]).astype(bf16)
    inv_ref[...] = jnp.broadcast_to(inv, inv_ref.shape)


def forward_kernel(
    lengths, nb_ref, cot_ref, wg_ref, wi_ref, wo_ref, ws_ref, wst_ref, ik_ref, ib_ref, sk_ref, sb_ref,
    stepb_ref, decay_ref, skipc_ref, gain_ref,
    graw_ref, iraw_ref, cv_ref, mixed_ref, scaled_ref, sums_ref, sraw_ref, sact_ref, state_ref, hc_ref, lsr_ref,
    addm_ref, g_ref, keep_ref, acc,
):
    j = pl.program_id(0)
    count = nb_ref.shape[0]
    nb = nb_ref[...]

    @pl.when(j == 0)
    def _():
        i0 = lax.broadcasted_iota(jnp.int32, (count, count), 0)
        j0 = lax.broadcasted_iota(jnp.int32, (count, count), 1)
        same = (seg_of(i0, lengths) == seg_of(j0, lengths)) & (j0 <= i0)
        addm_ref[...] = jnp.where(same, 0.0, NEG)
        state = mm(nb, wst_ref[...])
        state_ref[...] = state
        keep = keeps(lengths, count)
        for back in range(1, CONV):
            keep_ref[:, back : back + 1] = keep[back]
        cv = conv(state, sk_ref[...], sb_ref[...], keep)
        act = cv * sigmoid(cv)
        sact_ref[...] = act
        g_ref[...] = mm(act[:, STATE:], act[:, :STATE], NT, HIGH)
        raw = mm(nb, ws_ref[...]) + stepb_ref[...]
        sraw_ref[...] = raw
        step = softplus(raw)
        logs = mm(same.astype(f32), step * (-jnp.exp(decay_ref[...])), NN, HIGH)
        lsr_ref[...] = jnp.transpose(logs)
        for k in range(hc_ref.shape[0]):
            hc_ref[k, :, 0:HPB] = logs[:, HPB * k : HPB * (k + 1)]
            hc_ref[k, :, HPB : 2 * HPB] = step[:, HPB * k : HPB * (k + 1)]
        acc[...] = jnp.zeros_like(acc)

    gate = mm(nb, wg_ref[...])
    inner = mm(nb, wi_ref[...])
    scaled = mm(cot_ref[...], wo_ref[...], NT)
    graw_ref[...] = gate
    iraw_ref[...] = inner
    scaled_ref[...] = scaled
    cv = conv(inner, ik_ref[...], ib_ref[...], keeps(lengths, count))
    cv_ref[...] = cv
    v = cv * sigmoid(cv)
    first = lanes_first((count, 2 * HEAD_DIM))
    addm = addm_ref[...]
    g = g_ref[...]
    parts = []
    for pair in range(BLK // (2 * HEAD_DIM)):
        vp = v[:, 2 * HEAD_DIM * pair : 2 * HEAD_DIM * (pair + 1)]
        k = 2 * pair
        steps = jnp.where(first, hc_ref[j, :, HPB + k : HPB + k + 1], hc_ref[j, :, HPB + k + 1 : HPB + k + 2])
        vs = (vp * steps).astype(bf16)
        ys = []
        for h in (k, k + 1):
            gaps = hc_ref[j, :, h : h + 1] - lsr_ref[pl.ds(HPB * j + h, 1), :] + addm
            ys.append(mm((g * jnp.exp(gaps)).astype(bf16), vs))
        parts.append(jnp.where(first, ys[0], ys[1]))
    mixed = jnp.concatenate(parts, axis=1) + skipc_ref[...] * v
    mixed_ref[...] = mixed
    gated = mixed * (gate * sigmoid(gate))
    acc[:, 0:1] += jnp.sum(gated * gated, axis=1, keepdims=True)
    acc[:, 1:2] += jnp.sum(scaled * gain_ref[...] * gated, axis=1, keepdims=True)

    @pl.when(j == pl.num_programs(0) - 1)
    def _():
        sums_ref[...] = jnp.transpose(acc[...])[0:8, :]


def unit_kernel(width, s_ref, graw_ref, mixed_ref, scaled_ref, gain_ref, x_ref, dm_ref, gg_ref):
    sums = jnp.sum(s_ref[...], axis=0)
    cols = jnp.transpose(sums)
    inv = lax.rsqrt(cols[:, 0:1] / width + eps)
    dot = inv * cols[:, 1:2]
    gate, mixed, scaled, gain = graw_ref[...], mixed_ref[...], scaled_ref[...], gain_ref[...]
    s = sigmoid(gate)
    act = gate * s
    unit = mixed * act * inv
    x_ref[0, 0] = (unit * gain).astype(bf16).astype(f32)
    gg_ref[...] = jnp.broadcast_to(jnp.sum(scaled * unit, axis=0, keepdims=True), gg_ref.shape)
    d_gated = inv * (scaled * gain - unit * (dot / width))
    dm_ref[...] = d_gated * act
    x_ref[1, 0] = (d_gated * mixed * s * (1.0 + gate * (1.0 - s))).astype(bf16).astype(f32)


def backward_kernel(
    lengths, dm_ref, cv_ref, iraw_ref, mixed_ref, hc_ref, lsr_ref, addm_ref, g_ref, sraw_ref, sact_ref,
    ik_ref, skipc_ref, decay_ref, _,
    back_ref, rows_ref, sback_ref, hrows_ref, dstate_ref, dg, dlogs, dstep,
):
    j = pl.program_id(0)
    count = dm_ref.shape[0]

    @pl.when(j == 0)
    def _():
        dg[...] = jnp.zeros_like(dg)
        dlogs[...] = jnp.zeros_like(dlogs)
        dstep[...] = jnp.zeros_like(dstep)

    cv, dm, skipc = cv_ref[...], dm_ref[...], skipc_ref[...]
    s = sigmoid(cv)
    v = cv * s
    within = mixed_ref[...] - skipc * v
    first = lanes_first((count, 2 * HEAD_DIM))
    addm = addm_ref[...]
    g = g_ref[...]
    us, vss, dyb, stepm = [], [], [], []
    total = dg[...]
    for pair in range(BLK // (2 * HEAD_DIM)):
        cols = slice(2 * HEAD_DIM * pair, 2 * HEAD_DIM * (pair + 1))
        k = 2 * pair
        steps = jnp.where(first, hc_ref[0, :, HPB + k : HPB + k + 1], hc_ref[0, :, HPB + k + 1 : HPB + k + 2])
        vs = (v[:, cols] * steps).astype(bf16)
        dy = dm[:, cols].astype(bf16)
        both = []
        for h in (k, k + 1):
            gaps = hc_ref[0, :, h : h + 1] - lsr_ref[pl.ds(HPB * j + h, 1), :] + addm
            decay = jnp.exp(gaps)
            both.append(mm((g * decay).astype(bf16), dy, TN))
            mine = first if h == k else jnp.logical_not(first)
            total = total + decay * mm(jnp.where(mine, dy, jnp.zeros_like(dy)), vs, NT)
        us.append(jnp.where(first, both[0], both[1]))
        vss.append(vs.astype(f32))
        dyb.append(dy.astype(f32))
        stepm.append(steps)
    dg[...] = total
    u = jnp.concatenate(us, axis=1)
    vs = jnp.concatenate(vss, axis=1)
    dy = jnp.concatenate(dyb, axis=1)
    steps = jnp.concatenate(stepm, axis=1)
    c0 = lax.broadcasted_iota(jnp.int32, (BLK, 128), 0) // HEAD_DIM
    l0 = lax.broadcasted_iota(jnp.int32, (BLK, 128), 1)
    pick = (l0 == c0 + HPB * j).astype(f32)
    dlogs[...] += mm(dy * within - vs * u, pick, NN, HIGH)
    dstep[...] += mm(v * u, pick, NN, HIGH)
    dv = steps * u + skipc * dm
    dc = dv * (s * (1.0 + cv * (1.0 - s)))
    du, rows = conv_back(dc, iraw_ref[...], ik_ref[...], keeps(lengths, count))
    back_ref[0, 0] = du.astype(bf16).astype(f32)
    rows_ref[...] = jnp.concatenate(rows + [jnp.sum(dm * v, axis=0, keepdims=True)] + [jnp.zeros((2, BLK), f32)], axis=0)

    @pl.when(j == pl.num_programs(0) - 1)
    def _():
        mask = (addm > -1.0).astype(f32)
        q = mm(mask, dlogs[...], TN, HIGH)
        raw = sraw_ref[...]
        step = softplus(raw)
        rate = -jnp.exp(decay_ref[...])
        draw = (dstep[...] + rate * q) * sigmoid(raw)
        sback_ref[...] = draw.astype(bf16).astype(f32)
        hrows_ref[...] = jnp.concatenate(
            [jnp.sum(draw, axis=0, keepdims=True), rate * jnp.sum(step * q, axis=0, keepdims=True), jnp.zeros((6, 128), f32)],
            axis=0,
        )
        act = sact_ref[...]
        d_b = mm(dg[...], act[:, STATE:], TN, HIGH)
        d_c = mm(dg[...], act[:, :STATE], NN, HIGH)
        both = jnp.concatenate([d_b, d_c], axis=1)
        span = dstate_ref.shape[2]
        for t in range(dstate_ref.shape[0]):
            dstate_ref[t] = both[:, span * t : span * (t + 1)]


def state_kernel(lengths, parts_ref, u_ref, sk_ref, sb_ref, back_ref, rows_ref):
    keep = keeps(lengths, u_ref.shape[0])
    cv = conv(u_ref[...], sk_ref[...], sb_ref[...], keep)
    s = sigmoid(cv)
    dc = jnp.sum(parts_ref[...], axis=0) * (s * (1.0 + cv * (1.0 - s)))
    du, rows = conv_back(dc, u_ref[...], sk_ref[...], keep)
    back_ref[...] = du.astype(bf16).astype(f32)
    rows_ref[...] = jnp.concatenate(rows + [jnp.zeros((3, du.shape[1]), f32)], axis=0)


MESH = pl.DeviceIdType.MESH
RING = 6
VMEM_LIMIT = 64 << 20
LEAD = 4


def layer_kernel(
    lengths, xin, cot, gain_in, ws, wst, ik, ib, sk, sb, stepb, decay, skipc, gain, wg_hbm, wi_hbm, wo_hbm,
    out_ref, din_ref, gate_out, inner_out, state_out, step_out, turned_out, smalls_ref,
    x, mixb, cvb, dmb, nb, inv, fs, f1, f2, f3, fx, fc, ft, big, yra, yrb, r, ea, fin, turned, xb, xbr, wring, woring, po, por,
    addm, g, hc, lsr, sact, state_raw, sraw, keep_ref, dg, dlogs, dstep, hsum, acc, sums, sumr, dstate, dsr, srr, sm, smr,
    ex, exr, rx, exe, yrx, exg, dots, dotr,
    p1s, p1v, p2s, p2v, p3s, p3v, es, ev, yas, yav, ybs, ybv, fas, fav, fins, wsem, pos, pov, pis, piv,
    dss, dsv, srs, srv, dts, dtv, sus, suv, sms, smv, exs, exv, yxs, yxv, exgs, exgv,
    f1s, f1v, f2s, f2v, f3s, f3v, fxs, fxv, fcs, fcv, credit, por_free, fc_free,
):
    d, t = lax.axis_index("dp"), lax.axis_index("tensor")
    y, z = d % 2, d // 2
    side, half = z % 2, z // 2
    hub = (z == 1) | (z == 2)
    edge = jnp.logical_not(hub)
    chunks, count, wide = x.shape
    each = chunks // 3
    lanes = wide // 2
    width = xin.shape[1]
    part = width // 4
    own = part // 2
    share = width // 4
    span = dsr.shape[2]
    inner = each * wide
    piece = f1.shape[1]
    pair, peer, line = d ^ 2, d ^ 6, d ^ 1
    mine, other = pl.multiple_of(own * y, own), pl.multiple_of(own * (1 - y), own)
    mine_part, pair_part = pl.multiple_of(part * side, part), pl.multiple_of(part * (1 - side), part)
    near, far = pl.multiple_of(half * 2 * part, 2 * part), pl.multiple_of((1 - half) * 2 * part, 2 * part)
    my_rows = pl.multiple_of(t * piece, piece)
    my_share = pl.multiple_of(t * share, share)

    def send(src, dst, ssem, rsem, dev):
        return pltpu.make_async_remote_copy(
            src_ref=src, dst_ref=dst, send_sem=ssem, recv_sem=rsem, device_id=dev, device_id_type=MESH
        )

    def p1(q):
        return send(x.at[q], big.at[q % RING, pl.ds(0, count)], p1s.at[q], p1v.at[q], (pair, t))

    def p2(q):
        return send(x.at[q], big.at[q % RING, pl.ds(count, count)], p2s.at[q], p2v.at[q], (peer, t))

    def p3(q):
        slot = q % RING
        return send(
            big.at[slot, pl.ds(0, count)], big.at[slot, pl.ds(2 * count, count)], p3s.at[q], p3v.at[q], (peer, t)
        )

    def e(q):
        return send(
            r.at[q % 2, 0, :, pl.ds(lanes, lanes)], big.at[q % RING, pl.ds(0, part), pl.ds(0, lanes)], es.at[q], ev.at[q],
            (pair, t),
        )

    def ya(q, k):
        return send(
            r.at[q % 2, k, pl.ds(other, own), pl.ds(0, lanes)], yra.at[q % RING, k], yas.at[q, k], yav.at[q, k], (line, t)
        )

    def yb_hub(q):
        return send(
            r.at[q % 2, 1, pl.ds(other, own), pl.ds(lanes, lanes)], yrb.at[q % LEAD], ybs.at[q], ybv.at[q], (line, t)
        )

    def yb_edge(q):
        return send(
            big.at[q % RING, pl.ds(other, own), pl.ds(0, lanes)], yrb.at[q % LEAD], ybs.at[q], ybv.at[q], (line, t)
        )

    def fa(q):
        return send(ea.at[q % 2], yra.at[q % RING, 0], fas.at[q], fav.at[q], (pair, t))

    def feature1(f):
        return send(f1.at[f], f1.at[f], f1s.at[f], f1v.at[f], (pair, t))

    def feature2(f):
        return send(fs.at[f], f2.at[f], f2s.at[f], f2v.at[f], (peer, t))

    def feature3(f):
        return send(f1.at[f, :, pl.ds(far, 2 * part)], f3.at[f], f3s.at[f], f3v.at[f], (peer, t))

    def feature(f, shard):
        return (f1.at[f, :, pl.ds(near, 2 * part)], f2.at[f], f3.at[f])[shard]

    def across(f, shard):
        return send(feature(f, shard), fx.at[f, shard], fxs.at[f, shard], fxv.at[f, shard], (d, t ^ 2))

    def sibling(f, shard, k):
        src = fx.at[f, shard] if k else feature(f, shard)
        return send(src, fc.at[k, shard], fcs.at[k, f, shard], fcv.at[k, f, shard], (d, t ^ 1))

    def spread(f, shard):
        across(f, shard).start()
        if f:
            sibling(f, shard, 0).start()

    p1x = lambda: send(ex, exr.at[0], exs.at[0], exv.at[0], (pair, t))
    p2x = lambda: send(ex, exr.at[1], exs.at[1], exv.at[1], (peer, t))
    p3x = lambda: send(exr.at[0], exr.at[2], exs.at[2], exv.at[2], (peer, t))
    e_x = lambda: send(rx.at[0], exe, exs.at[3], exv.at[3], (pair, t))
    yx_hub = lambda: send(rx.at[1, pl.ds(other, own)], yrx, yxs.at[0], yxv.at[0], (line, t))
    yx_edge = lambda: send(exe.at[pl.ds(other, own)], yrx, yxs.at[0], yxv.at[0], (line, t))

    def over_tensor(src, dst, ssem, rsem):
        return lambda k: send(src(k), dst(k), ssem.at[k - 1], rsem.at[k - 1], (d, t ^ k))

    sum_copy = over_tensor(lambda k: sums, lambda k: sumr.at[k - 1], sus, suv)
    state_copy = over_tensor(lambda k: dstate.at[t ^ k], lambda k: dsr.at[k - 1], dss, dsv)
    row_copy = over_tensor(lambda k: srr.at[t], lambda k: srr.at[t], srs, srv)
    out_copy = over_tensor(lambda k: po.at[t ^ k], lambda k: por.at[k - 1], pos, pov)
    in_copy = over_tensor(lambda k: po.at[t ^ k], lambda k: por.at[k - 1], pis, piv)
    dot_copy = over_tensor(lambda k: dots, lambda k: dotr.at[k - 1], dts, dtv)
    extra_copy = over_tensor(lambda k: exg.at[t], lambda k: exg.at[t], exgs, exgv)
    small_copy = lambda k: send(sm, smr.at[k], sms.at[k], smv.at[k], (d ^ (1 << k), t))

    def started(copy):
        for k in range(1, 4):
            copy(k).start()

    def waited(copy):
        for k in range(1, 4):
            copy(k).wait()

    def load(n, kind):
        at = pl.multiple_of((n % each) * wide, wide)
        if kind == 2:
            return pltpu.make_async_copy(wo_hbm.at[pl.ds(at, wide), :], woring.at[n % 2], wsem.at[kind, n % 2])
        ref = (wg_hbm, wi_hbm)[kind]
        return pltpu.make_async_copy(ref.at[:, pl.ds(at, wide)], wring.at[n % 2, kind], wsem.at[kind, n % 2])

    for n in range(2):
        for kind in range(3):
            load(n, kind).start()

    barrier = pltpu.get_barrier_semaphore()
    for dev in ((pair, t), (peer, t), (line, t), (d ^ 4, t), (d, t ^ 1), (d, t ^ 2), (d, t ^ 3)):
        pl.semaphore_signal(barrier, inc=1, device_id=dev, device_id_type=MESH)
    pl.semaphore_wait(barrier, 7)

    def begin_features(f):
        ref = cot if f else nb

        @pl.when(edge)
        def _():
            f1[f] = ref[pl.ds(my_rows, piece), :].astype(f32)
            feature1(f).start()

        @pl.when(hub)
        def _():
            fs[f] = ref[pl.ds(my_rows, piece), pl.ds(far, 2 * part)].astype(f32)
            feature2(f).start()

    begin_features(1)
    xv = xin[...].astype(f32)
    scale = lax.rsqrt(jnp.sum(xv * xv, axis=1, keepdims=True) / width + eps)
    nb[...] = (xv * scale * gain_in[...]).astype(bf16)
    inv[...] = jnp.broadcast_to(scale, inv.shape)
    begin_features(0)

    i0 = lax.broadcasted_iota(jnp.int32, (count, count), 0)
    j0 = lax.broadcasted_iota(jnp.int32, (count, count), 1)
    same = (seg_of(i0, lengths) == seg_of(j0, lengths)) & (j0 <= i0)
    addm[...] = jnp.where(same, 0.0, NEG)
    keep = keeps(lengths, count)
    for back in range(1, CONV):
        keep_ref[:, back : back + 1] = keep[back]
    state = mm(nb[...], wst[...])
    state_raw[...] = state
    cv = conv(state, sk[...], sb[...], keep)
    act = cv * sigmoid(cv)
    sact[...] = act
    g[...] = mm(act[:, STATE:], act[:, :STATE], NT, HIGH)
    raw = mm(nb[...], ws[...]) + stepb[...]
    sraw[...] = raw
    step = softplus(raw)
    logs = mm(same.astype(f32), step * (-jnp.exp(decay[...])), NN, HIGH)
    lsr[...] = jnp.transpose(logs)
    for k in range(each):
        hc[k, :, 0:HPB] = logs[:, HPB * k : HPB * (k + 1)]
        hc[k, :, HPB : 2 * HPB] = step[:, HPB * k : HPB * (k + 1)]
    for ref in (acc, dg, dlogs, dstep, hsum, sm):
        ref[...] = jnp.zeros_like(ref)

    first = lanes_first((count, 2 * HEAD_DIM))

    def kept():
        return [None] + [keep_ref[:, b : b + 1] for b in range(1, CONV)]

    def steps_of(j, k):
        return jnp.where(first, hc[j, :, HPB + k : HPB + k + 1], hc[j, :, HPB + k + 1 : HPB + k + 2])

    def decay_of(j, h):
        return jnp.exp(hc[j, :, h : h + 1] - lsr[pl.ds(HPB * j + h, 1), :] + addm[...])

    def forward_block(j, carry):
        slot = j % 2
        cols = pl.ds(pl.multiple_of(j * wide, wide), wide)
        for kind in range(3):
            load(j, kind).wait()
        gate = mm(nb[...], wring[slot, 0])
        raw = mm(nb[...], wring[slot, 1])
        scaled = mm(cot[...], woring[slot], NT)
        for kind in range(3):
            load(j + 2, kind).start()
        x[j] = scaled
        x[each + j] = gate
        x[2 * each + j] = raw
        cv = conv(raw, ik[:, cols], ib[:, cols], kept())
        cvb[j] = cv
        v = cv * sigmoid(cv)
        parts = []
        for k in range(0, HPB, 2):
            vs = (v[:, HEAD_DIM * k : HEAD_DIM * (k + 2)] * steps_of(j, k)).astype(bf16)
            ys = [mm((g[...] * decay_of(j, h)).astype(bf16), vs) for h in (k, k + 1)]
            parts.append(jnp.where(first, ys[0], ys[1]))
        mixed = jnp.concatenate(parts, axis=1) + skipc[:, cols] * v
        mixb[j] = mixed
        gated = mixed * (gate * sigmoid(gate))
        acc[:, 0:1] += jnp.sum(gated * gated, axis=1, keepdims=True)
        acc[:, 1:2] += jnp.sum(scaled * gain[:, cols] * gated, axis=1, keepdims=True)

        @pl.when(hub & (j == 1))
        def _():
            feature1(1).wait_recv()
            feature3(1).start()
            spread(1, 0)

        @pl.when(hub & (j == 2))
        def _():
            feature2(1).wait_recv()
            spread(1, 1)

        return carry

    lax.fori_loop(0, each, forward_block, 0)
    sums[...] = jnp.transpose(acc[...])[0:8, :]
    started(sum_copy)

    @pl.when(hub)
    def _():
        feature3(1).wait_recv()
        spread(1, 2)

    waited(sum_copy)
    total = jnp.transpose(sums[...] + sumr[0] + sumr[1] + sumr[2])
    acc[:, 0:1] = lax.rsqrt(total[:, 0:1] / (4 * inner) + eps)
    acc[:, 1:2] = acc[:, 0:1] * total[:, 1:2] / (4 * inner)

    def unit_block(j, carry):
        cols = pl.ds(pl.multiple_of(j * wide, wide), wide)
        scaled, gate, mixed = x[j], x[each + j], mixb[j]
        inv_gate, dot = acc[:, 0:1], acc[:, 1:2]
        s = sigmoid(gate)
        act = gate * s
        unit = mixed * act * inv_gate
        weights = gain[:, cols]
        x[j] = (unit * weights).astype(bf16).astype(f32)
        sm[8:9, cols] = jnp.sum(scaled * unit, axis=0, keepdims=True)
        d_gated = inv_gate * (scaled * weights - unit * dot)
        dmb[j] = d_gated * act
        x[each + j] = (d_gated * mixed * s * (1.0 + gate * (1.0 - s))).astype(bf16).astype(f32)

        @pl.when(hub & (j < LEAD))
        def _():
            p2(j).start()

        @pl.when(edge & (j < LEAD))
        def _():
            p1(j).start()

        return carry

    lax.fori_loop(0, each, unit_block, 0)

    @pl.when(hub)
    def _():
        feature1(0).wait_recv()
        feature3(0).start()
        spread(0, 0)
        feature2(0).wait_recv()
        spread(0, 1)

    def forward_features(f):
        if not f:
            pl.semaphore_wait(fc_free, 1)
        for shard in range(3):
            if not f:
                sibling(f, shard, 0).start()
            across(f, shard).wait_recv()
            sibling(f, shard, 1).start()

    def assemble(f):
        own_rows = (cot if f else nb)[:, pl.ds(near, 2 * part)]
        ft[f, :, 0:count] = own_rows.T
        for shard in range(3):
            sibling(f, shard, 0).wait_recv()
            sibling(f, shard, 1).wait_recv()
            for k, ref in enumerate((feature(f, shard), fc.at[0, shard], fx.at[f, shard], fc.at[1, shard])):
                xbr[pl.ds(pl.multiple_of((t ^ k) * piece, piece), piece), :] = ref[...].astype(bf16)
            ft[f, :, count * (shard + 1) : count * (shard + 2)] = xbr[...].T
        if f:
            pl.semaphore_signal(fc_free, inc=1, device_id=(d, t ^ 1), device_id_type=MESH)

    def backward_block(j):
        cols = pl.ds(pl.multiple_of(j * wide, wide), wide)
        cv, dm = cvb[j], dmb[j]
        s = sigmoid(cv)
        v = cv * s
        within = mixb[j] - skipc[:, cols] * v
        us, vss, dys, stepm = [], [], [], []
        for k in range(0, HPB, 2):
            lane = slice(HEAD_DIM * k, HEAD_DIM * (k + 2))
            steps = steps_of(j, k)
            vs = (v[:, lane] * steps).astype(bf16)
            dy = dm[:, lane].astype(bf16)
            both = []
            for h in (k, k + 1):
                ratio = decay_of(j, h)
                both.append(mm((g[...] * ratio).astype(bf16), dy, TN))
                part_of = first if h == k else jnp.logical_not(first)
                dg[...] += ratio * mm(jnp.where(part_of, dy, jnp.zeros_like(dy)), vs, NT)
            us.append(jnp.where(first, both[0], both[1]))
            vss.append(vs.astype(f32))
            dys.append(dy.astype(f32))
            stepm.append(steps)
        u, vs, dy, steps = (jnp.concatenate(p, axis=1) for p in (us, vss, dys, stepm))
        c0 = lax.broadcasted_iota(jnp.int32, (wide, 128), 0) // HEAD_DIM
        l0 = lax.broadcasted_iota(jnp.int32, (wide, 128), 1)
        pick = (l0 == c0 + HPB * j).astype(f32)
        dlogs[...] += mm(dy * within - vs * u, pick, NN, HIGH)
        dstep[...] += mm(v * u, pick, NN, HIGH)
        per_lane = jnp.sum(dm * v, axis=0, keepdims=True)
        hsum[...] += mm(jnp.broadcast_to(per_lane, (8, wide)), pick, NN, HIGH)
        dc = (steps * u + skipc[:, cols] * dm) * (s * (1.0 + cv * (1.0 - s)))
        du, rows = conv_back(dc, x[2 * each + j], ik[:, cols], kept())
        x[2 * each + j] = du.astype(bf16).astype(f32)
        sm[0:5, cols] = jnp.concatenate(rows, axis=0)

    def backward_end():
        mask = (addm[...] > -1.0).astype(f32)
        q = mm(mask, dlogs[...], TN, HIGH)
        raw = sraw[...]
        step = softplus(raw)
        rate = -jnp.exp(decay[...])
        draw = (dstep[...] + rate * q) * sigmoid(raw)
        dstep[...] = draw.astype(bf16).astype(f32)
        sm[15:16, 0:128] = jnp.sum(draw, axis=0, keepdims=True)
        sm[15:16, 128:256] = rate * jnp.sum(step * q, axis=0, keepdims=True)
        sm[15:16, 256:384] = hsum[0:1, :]
        d_b = mm(dg[...], sact[:, STATE:], TN, HIGH)
        d_c = mm(dg[...], sact[:, :STATE], NN, HIGH)
        both = jnp.concatenate([d_b, d_c], axis=1)
        for i in range(4):
            dstate[i] = both[:, span * i : span * (i + 1)]
        started(state_copy)

    def slab(ref):
        out = None
        for i in range(4):
            one = jnp.where(t == i, ref[:, span * i : span * (i + 1)], 0.0)
            out = one if out is None else out + one
        return out

    def states():
        waited(state_copy)
        total = dstate[t] + dsr[0] + dsr[1] + dsr[2]
        u, kernel = slab(state_raw), slab(sk)
        cv = conv(u, kernel, slab(sb), kept())
        s = sigmoid(cv)
        du, rows = conv_back(total * (s * (1.0 + cv * (1.0 - s))), u, kernel, kept())
        ex[:, 0:span] = du.astype(bf16).astype(f32)
        ex[:, span : 2 * span] = dstep[:, 0:span]
        srr[t] = jnp.concatenate(rows + [jnp.zeros((3, span), f32)], axis=0)
        started(row_copy)

        @pl.when(hub)
        def _():
            p2x().start()

        @pl.when(edge)
        def _():
            p1x().start()

    def out_parts():
        for c in range(each):
            n = each + c
            load(n, 2).wait()
            xc = x[c].astype(bf16)
            for i in range(4):
                one = mm(xc, woring[n % 2, :, share * i : share * (i + 1)])
                po[i] = one if c == 0 else po[i] + one
            if c + 2 < each:
                load(n + 2, 2).start()
        started(out_copy)

    def out_sum():
        waited(out_copy)
        hidden = xin[:, pl.ds(my_share, share)].astype(f32)
        out_ref[...] = (po[t] + por[0] + por[1] + por[2] + hidden).astype(bf16)
        for k in range(1, 4):
            pl.semaphore_signal(por_free, inc=1, device_id=(d, t ^ k), device_id_type=MESH)

    def in_parts():
        lane = lax.broadcasted_iota(jnp.int32, (count, 4 * span), 1) // span
        own_state = ex[:, 0:span]
        states4 = jnp.where(lane == t, jnp.concatenate([own_state] * 4, axis=1), 0.0).astype(bf16)
        steps_back = dstep[...].astype(bf16)
        for i in range(4):
            rows = slice(share * i, share * (i + 1))
            po[i] = mm(states4, wst[rows, :], NT) + mm(steps_back, ws[rows, :], NT)
        for c in range(each):
            n = each + c
            load(n, 0).wait()
            load(n, 1).wait()
            gc, ic = x[each + c].astype(bf16), x[2 * each + c].astype(bf16)
            for i in range(4):
                rows = slice(share * i, share * (i + 1))
                po[i] = po[i] + (mm(gc, wring[n % 2, 0, rows, :], NT) + mm(ic, wring[n % 2, 1, rows, :], NT))
            if c + 2 < each:
                load(n + 2, 0).start()
                load(n + 2, 1).start()
        pl.semaphore_wait(por_free, 3)
        started(in_copy)

    def normed():
        return xin[:, pl.ds(my_share, share)].astype(f32) * inv[:, 0:1]

    def in_sum():
        waited(in_copy)
        d_normed = po[t] + por[0] + por[1] + por[2]
        po[0] = d_normed
        dot = jnp.sum(d_normed * gain_in[:, pl.ds(my_share, share)] * normed(), axis=1, keepdims=True)
        dots[...] = jnp.transpose(jnp.broadcast_to(dot, (count, 128)))[0:8, :]
        started(dot_copy)

    def finish():
        waited(dot_copy)
        waited(row_copy)
        d_normed, n = po[0], normed()
        dot = jnp.transpose(dots[...] + dotr[0] + dotr[1] + dotr[2])[:, 0:1] / width
        d_hat = d_normed * gain_in[:, pl.ds(my_share, share)]
        din_ref[...] = inv[:, 0:1] * (d_hat - n * dot) + cot[:, pl.ds(my_share, share)].astype(f32)
        sm[9:10, 0:share] = jnp.sum(d_normed * n, axis=0, keepdims=True)
        for i in range(4):
            sm[10:15, span * i : span * (i + 1)] = srr[i][0:5, :]
        small_copy(0).start()

    def small(k):
        small_copy(k).wait()
        sm[...] = sm[...] + smr[k]
        if k < 2:
            small_copy(k + 1).start()
        else:
            smalls_ref[...] = sm[...]

    def extra_hub():
        p2x().wait_recv()
        p3x().wait_recv()
        for k, ref in enumerate((ex, exr.at[0], exr.at[1], exr.at[2])):
            xb[k * count : (k + 1) * count, 0:128] = ref[...].astype(bf16)
        rx[0] = mm(ft[0, pl.ds(pair_part, part), :], xb[:, 0:128])
        rx[1] = mm(ft[0, pl.ds(mine_part, part), :], xb[:, 0:128])
        e_x().start()
        yx_hub().start()

    def extra_spread(rows):
        exg[t] = rows + yrx[...]
        step_out[...] = exg[t]
        started(extra_copy)

    def extra_end():
        waited(extra_copy)
        for i in range(4):
            state_out[:, span * i : span * (i + 1)] = exg[i, :, 0:span]

    def process(q):
        p2(q).wait_recv()
        p3(q).wait_recv()
        p3(q).wait_send()

        @pl.when(q >= 2)
        def _():
            e(q - 2).wait_send()
            ya(q - 2, 0).wait_send()
            ya(q - 2, 1).wait_send()
            yb_hub(q - 2).wait_send()

        xb[0:count, :] = x[q].astype(bf16)
        xb[count:, :] = big[q % RING].astype(bf16)

        @pl.when(q + RING < chunks)
        def _():
            pl.semaphore_signal(credit, inc=1, device_id=(peer, t), device_id_type=MESH)

        family = jnp.where(q < each, 1, 0)
        slot = q % 2
        r[slot, 0] = mm(ft[family, pl.ds(pair_part, part), :], xb[...])
        e(q).start()
        ya(q, 0).start()
        r[slot, 1] = mm(ft[family, pl.ds(mine_part, part), :], xb[...])
        ya(q, 1).start()
        yb_hub(q).start()

    def stored(q, k):
        at = pl.multiple_of((q % each) * wide, wide)
        if k == 0:
            return pltpu.make_async_copy(turned.at[q % 2], turned_out.at[pl.ds(at, wide), :], fins.at[q])
        return pltpu.make_async_copy(fin.at[q % 2], (gate_out, inner_out)[k - 1].at[:, pl.ds(at, wide)], fins.at[q])

    def store(q, left, right):
        slot = q % 2
        for k in range(3):
            @pl.when((q >= k * each + 2) & (q < (k + 1) * each + 2))
            def _():
                stored(q - 2, k).wait()

        fin[slot, :, 0:lanes] = left
        fin[slot, :, lanes:] = right

        @pl.when(q < each)
        def _():
            turned[slot] = jnp.transpose(fin[slot])

        for k in range(3):
            @pl.when((q >= k * each) & (q < (k + 1) * each))
            def _():
                stored(q, k).start()

    def finalize_hub(q):
        slot = q % 2
        ya(q, 0).wait_recv()
        ya(q, 1).wait_recv()
        yb_hub(q).wait_recv()

        @pl.when(q >= 2)
        def _():
            fa(q - 2).wait_send()

        got = yra.at[q % RING]
        ea[slot] = r[slot, 0, pl.ds(mine, own), 0:lanes] + got[0]
        fa(q).start()
        store(
            q,
            r[slot, 1, pl.ds(mine, own), 0:lanes] + got[1],
            r[slot, 1, pl.ds(mine, own), lanes:] + yrb[q % LEAD],
        )

    def finalize_edge(q):
        yb_edge(q).wait_recv()
        fa(q).wait_recv()
        store(q, yra[q % RING, 0], big[q % RING, pl.ds(mine, own), 0:lanes] + yrb[q % LEAD])

    pieces = {
        each - 1: backward_end, 5: states, 6: out_parts, 7: out_sum, 8: in_parts, 9: in_sum, 10: finish,
        11: lambda: small(0), 13: lambda: small(1), 16: lambda: small(2), 15: extra_end,
    }

    def body(q, carry):
        @pl.when(hub)
        def _():
            @pl.when(q < chunks)
            def _():
                p1(q).wait_recv()
                p3(q).start()

            @pl.when(q + LEAD < chunks)
            def _():
                @pl.when(q + LEAD >= RING)
                def _():
                    pl.semaphore_wait(credit, 1)

                p2(q + LEAD).start()

            @pl.when(q == 0)
            def _():
                forward_features(1)
                assemble(1)

            @pl.when((q >= 1) & (q <= chunks))
            def _():
                process(q - 1)

            @pl.when(q >= 2)
            def _():
                finalize_hub(q - 2)

            @pl.when(q == 1)
            def _():
                feature3(0).wait_recv()
                spread(0, 2)

            @pl.when(q == 3)
            def _():
                forward_features(0)

            @pl.when(q == 4)
            def _():
                assemble(0)

            @pl.when(q == 8)
            def _():
                p1x().wait_recv()
                p3x().start()

            @pl.when(q == 10)
            def _():
                extra_hub()

            @pl.when(q == 14)
            def _():
                yx_hub().wait_recv()
                extra_spread(rx[1, pl.ds(mine, own), :])

        @pl.when(q < each)
        def _():
            backward_block(q)

        for at, job in pieces.items():
            pl.when(q == at)(job)

        @pl.when(edge)
        def _():
            @pl.when(q < chunks)
            def _():
                e(q).wait_recv()
                yb_edge(q).start()

            @pl.when(q + LEAD < chunks)
            def _():
                @pl.when(q >= 2)
                def _():
                    yb_edge(q - 2).wait_send()

                p1(q + LEAD).start()

            @pl.when((q >= 1) & (q <= chunks))
            def _():
                finalize_edge(q - 1)

            @pl.when(q == 12)
            def _():
                e_x().wait_recv()
                yx_edge().start()

            @pl.when(q == 14)
            def _():
                yx_edge().wait_recv()
                extra_spread(exe[pl.ds(mine, own), :])

        return carry

    lax.fori_loop(0, chunks + 2, body, 0)

    stored(chunks - 2, 2).wait()
    stored(chunks - 1, 2).wait()

    @pl.when(hub)
    def _():
        def drain(q, carry):
            p2(q).wait_send()
            return carry

        lax.fori_loop(0, chunks, drain, 0)
        for q in (chunks - 2, chunks - 1):
            e(q).wait_send()
            ya(q, 0).wait_send()
            ya(q, 1).wait_send()
            yb_hub(q).wait_send()
            fa(q).wait_send()
        for f in range(2):
            feature2(f).wait_send()
            feature3(f).wait_send()
            for shard in range(3):
                across(f, shard).wait_send()
                sibling(f, shard, 0).wait_send()
                sibling(f, shard, 1).wait_send()
        p2x().wait_send()
        p3x().wait_send()
        e_x().wait_send()
        yx_hub().wait_send()

    @pl.when(edge)
    def _():
        def drain(q, carry):
            p1(q).wait_send()
            return carry

        lax.fori_loop(0, chunks, drain, 0)
        for q in range(chunks - LEAD - 2, chunks):
            yb_edge(q).wait_send()
        for f in range(2):
            feature1(f).wait_send()
        p1x().wait_send()
        yx_edge().wait_send()


def whole(shape):
    return pl.BlockSpec(shape, lambda *_: (0,) * len(shape))


def columns(rows):
    return pl.BlockSpec((rows, BLK), lambda j, *_: (0, j))


SMEM = pl.BlockSpec(memory_space=pltpu.SMEM)
VM = pltpu.CompilerParams(vmem_limit_bytes=56 << 20)
VMS = pltpu.CompilerParams(vmem_limit_bytes=56 << 20, dimension_semantics=("arbitrary",))


def struct(shape, dtype=f32):
    return jax.ShapeDtypeStruct(shape, dtype)


def cost(flops, moved):
    return pl.CostEstimate(flops=int(flops), bytes_accessed=int(moved), transcendentals=0)


def on_device(
    block_input, cotangent, seq_lengths, norm_gain, gate_weight, inner_weight, step_weight, state_weight,
    inner_kernel, inner_bias, state_kernel_, state_bias, step_bias, decay_log, skip_scale, gate_gain, output_weight,
):
    parts = lax.axis_size("tensor")
    shards = lax.axis_size("dp")
    t = lax.axis_index("tensor")
    count, width = block_input.shape
    inner = gate_weight.shape[1]
    heads = step_bias.shape[0]
    share = width // parts
    span = 2 * STATE // parts
    steps = inner // BLK
    pad = ((0, 0), (0, 128 - heads))
    row = lambda x: x.reshape(1, -1)

    def swap(x, k):
        return lax.ppermute(x, "tensor", [(i, i ^ k) for i in range(parts)])

    padded_step = jnp.pad(step_weight, pad)
    stepb, decay = jnp.pad(row(step_bias), pad), jnp.pad(row(decay_log), pad)
    skipc = jnp.repeat(skip_scale, HEAD_DIM).reshape(1, -1)
    ik, ib, gain = inner_kernel, row(inner_bias), row(gate_gain)
    chunks = 3 * steps
    slab = lambda x, size: lax.dynamic_slice_in_dim(x, t * size, size, x.ndim - 1)
    if shards == 8 and parts == 4:
        own, half_blk, piece, near = width // 8, BLK // 2, count // parts, width // 2
        dma, v = pltpu.SemaphoreType.DMA, lambda *shape: pltpu.VMEM(shape, f32)
        vb = lambda *shape: pltpu.VMEM(shape, bf16)
        vmem, hbm = pl.BlockSpec(memory_space=pltpu.VMEM), pl.BlockSpec(memory_space=pl.ANY)
        scratch = [
            v(chunks, count, BLK), v(steps, count, BLK), v(steps, count, BLK), v(steps, count, BLK), vb(count, width),
            v(count, 128), v(2, piece, near), v(2, piece, width), v(2, piece, near), v(2, piece, near),
            v(2, 3, piece, near), v(2, 3, piece, near), vb(2, near, 4 * count), v(RING, 3 * count, BLK),
            v(RING, 2, own, half_blk), v(LEAD, own, half_blk), v(2, 2, 2 * own, BLK), v(2, own, half_blk), v(2, own, BLK),
            v(2, BLK, own), vb(4 * count, BLK), vb(count, near), vb(2, 2, width, BLK), vb(2, BLK, width),
            v(4, count, share), v(3, count, share),
            v(count, count), v(count, count), v(steps, count, 128), v(128, count), v(count, 2 * STATE), v(count, 2 * STATE),
            v(count, 128), v(count, 128), v(count, count), v(count, 128), v(count, 128), v(8, 128), v(count, 128),
            v(8, count), v(3, 8, count), v(4, count, span), v(3, count, span), v(4, 8, span), v(16, inner), v(3, 16, inner),
            v(count, 128), v(3, count, 128), v(2, 2 * own, 128), v(2 * own, 128), v(own, 128), v(4, own, 128),
            v(8, count), v(3, 8, count),
        ]
        scratch += [dma((chunks,))] * 8 + [dma((chunks, 2))] * 2 + [dma((chunks,))] * 5 + [dma((3, 2))] + [dma((3,))] * 14
        scratch += [dma((4,))] * 2 + [dma((1,))] * 2 + [dma((3,))] * 2 + [dma((2,))] * 6 + [dma((2, 3))] * 2
        scratch += [dma((2, 2, 3))] * 2 + [pltpu.SemaphoreType.REGULAR] * 3
        block_output, input_gradient, gate_grad, inner_grad, state_grad, extra_grad, output_grad, smalls = pl.pallas_call(
            layer_kernel,
            in_specs=[SMEM] + [vmem] * 13 + [hbm] * 3,
            out_specs=[vmem, vmem, hbm, hbm, vmem, vmem, hbm, vmem],
            out_shape=[
                struct((count, share), bf16), struct((count, share)), struct((own, inner)), struct((own, inner)),
                struct((own, 2 * STATE)), struct((own, 128)), struct((inner, own)), struct((16, inner)),
            ],
            scratch_shapes=scratch,
            compiler_params=pltpu.CompilerParams(collective_id=1, has_side_effects=True, vmem_limit_bytes=VMEM_LIMIT),
            name="layer",
        )(
            seq_lengths, block_input, cotangent, row(norm_gain), padded_step, state_weight, ik, ib, state_kernel_,
            row(state_bias), stepb, decay, skipc, gain, gate_weight, inner_weight, output_weight,
        )
        return (
            block_output, input_gradient, smalls[9, :share], gate_grad, inner_grad, extra_grad[:, span : span + heads],
            state_grad, smalls[:CONV], smalls[CONV], smalls[10 : 10 + CONV, : 2 * STATE], smalls[10 + CONV, : 2 * STATE],
            smalls[15, :heads], smalls[15, 128 : 128 + heads], smalls[15, 256 : 256 + heads], smalls[8], output_grad,
        )

    nb, inv = pl.pallas_call(
        norm_kernel,
        out_shape=(struct((count, width), bf16), struct((count, 128))),
        compiler_params=VM,
        name="norm_in",
    )(block_input, row(norm_gain))

    full = struct((count, inner))
    graw, iraw, cv, mixed, scaled, sums, sraw, sact, state_raw, hc, lsr, addm, g, keep = pl.pallas_call(
        forward_kernel,
        grid=(steps,),
        in_specs=[
            SMEM, whole((count, width)), whole((count, width)), columns(width), columns(width),
            pl.BlockSpec((BLK, width), lambda j: (j, 0)), whole((width, 128)), whole((width, 2 * STATE)),
            columns(CONV), columns(1), whole((CONV, 2 * STATE)), whole((1, 2 * STATE)), whole((1, 128)), whole((1, 128)),
            columns(1), columns(1),
        ],
        out_specs=(
            [columns(count)] * 5
            + [whole((8, count)), whole((count, 128)), whole((count, 2 * STATE)), whole((count, 2 * STATE)),
               whole((steps, count, 128)), whole((128, count)), whole((count, count)), whole((count, count)),
               whole((count, 128))]
        ),
        out_shape=(
            [full] * 5
            + [struct((8, count)), struct((count, 128)), struct((count, 2 * STATE)), struct((count, 2 * STATE)),
               struct((steps, count, 128)), struct((128, count)), struct((count, count)), struct((count, count)),
               struct((count, 128))]
        ),
        scratch_shapes=[pltpu.VMEM((count, 128), f32)],
        compiler_params=VMS,
        cost_estimate=cost(6 * count * width * inner, 6 * width * inner + 20 * count * inner),
        name="forward",
    )(
        seq_lengths, nb, cotangent, gate_weight, inner_weight, output_weight, padded_step, state_weight, ik, ib,
        state_kernel_, row(state_bias), stepb, decay, skipc, gain,
    )

    all_sums = jnp.stack([sums] + [swap(sums, k) for k in range(1, parts)])
    x, dm, gg = pl.pallas_call(
        partial(unit_kernel, float(inner * parts)),
        grid=(steps,),
        in_specs=[whole((parts, 8, count)), columns(count), columns(count), columns(count), columns(1)],
        out_specs=[pl.BlockSpec((2, 1, count, BLK), lambda j: (0, j, 0, 0)), columns(count), columns(8)],
        out_shape=[struct((3, steps, count, BLK)), full, struct((8, inner))],
        compiler_params=VMS,
        cost_estimate=cost(0, 24 * count * inner),
        name="unit",
    )(all_sums, graw, mixed, scaled, gain)

    x, rows, sback, hrows, dstate = pl.pallas_call(
        backward_kernel,
        grid=(steps,),
        in_specs=[
            SMEM, columns(count), columns(count), columns(count), columns(count),
            pl.BlockSpec((1, count, 128), lambda j: (j, 0, 0)), whole((128, count)), whole((count, count)),
            whole((count, count)), whole((count, 128)), whole((count, 2 * STATE)), columns(CONV), columns(1), whole((1, 128)),
            pl.BlockSpec(memory_space=pl.ANY),
        ],
        input_output_aliases={14: 0},
        out_specs=[pl.BlockSpec((1, 1, count, BLK), lambda j: (2, j, 0, 0)), columns(8), whole((count, 128)), whole((8, 128)), whole((parts, count, span))],
        out_shape=[struct((3, steps, count, BLK)), struct((8, inner)), struct((count, 128)), struct((8, 128)), struct((parts, count, span))],
        scratch_shapes=[pltpu.VMEM((count, count), f32), pltpu.VMEM((count, 128), f32), pltpu.VMEM((count, 128), f32)],
        compiler_params=VMS,
        cost_estimate=cost(40 * count * count * inner // 64 * 4, 24 * count * inner),
        name="backward",
    )(seq_lengths, dm, cv, iraw, mixed, hc, lsr, addm, g, sraw, sact, ik, skipc, decay, x)

    uo, gb, back = (jnp.swapaxes(x[i], 0, 1).reshape(count, inner) for i in range(3))

    def to_parts(x, axis):
        size = x.shape[axis] // parts
        block = lambda i: lax.dynamic_slice_in_dim(x, i * size, size, axis)
        got = [swap(block(t ^ k), k) for k in range(1, parts)]
        return [block(t)] + got

    def from_parts(x):
        got = jnp.stack([x] + [swap(x, k) for k in range(1, parts)])
        return jnp.stack([lax.dynamic_index_in_dim(got, t ^ i, 0, False) for i in range(parts)])

    state_parts = jnp.concatenate(to_parts(dstate, 0), axis=0)
    sq, srows = pl.pallas_call(
        state_kernel,
        in_specs=[SMEM] + [pl.BlockSpec(memory_space=pltpu.VMEM)] * 4,
        out_shape=(struct((count, span)), struct((8, span))),
        compiler_params=VM,
        name="state_back",
    )(seq_lengths, state_parts, slab(state_raw, span), slab(state_kernel_, span), row(slab(state_bias, span)))

    hidden = slab(block_input, share).astype(f32)
    cot_share = slab(cotangent, share).astype(f32)
    out_parts = to_parts(mm(uo.astype(bf16), output_weight), 1)
    block_output = (sum(out_parts[1:], out_parts[0]) + hidden).astype(bf16)

    gbb, ibb, sbb, qb = (x.astype(bf16) for x in (gb, back, sback[:, :heads], sq))
    partial_in = (
        mm(gbb, gate_weight, NT) + mm(ibb, inner_weight, NT) + mm(sbb, step_weight, NT)
        + mm(qb, slab(state_weight, span), NT)
    )
    in_parts = to_parts(partial_in, 1)
    d_normed = sum(in_parts[1:], in_parts[0])
    inv_in = inv[:, 0:1]
    normed = hidden * inv_in
    gain_share = row(slab(norm_gain, share))
    d_hat = d_normed * gain_share
    dot = jnp.sum(d_hat * normed, axis=1).reshape(-1, 128)
    dot = sum((swap(dot, k) for k in range(1, parts)), dot).reshape(-1, 1) / width
    input_gradient = inv_in * (d_hat - normed * dot) + cot_share
    norm_gain_grad = jnp.sum(d_normed * normed, axis=0)

    extra = jnp.concatenate([sq, sback[:, :heads], jnp.zeros((count, 128 - span - heads), f32)], axis=1)

    def scatter(a, b):
        return lax.psum_scatter(mm(a, b.astype(bf16), TN), "dp", scatter_dimension=0, tiled=True)

    output_grad = scatter(cotangent, uo).T
    gate_grad, inner_grad, extra_grad = scatter(nb, gb), scatter(nb, back), scatter(nb, extra)

    def over_dp(x):
        return lax.psum(x, "dp")

    step_grad = extra_grad[:, span : span + heads]
    state_grad = jnp.swapaxes(from_parts(extra_grad[:, :span]), 0, 1).reshape(-1, 2 * STATE)
    misc = jnp.concatenate([hrows[0], hrows[1], srows[: CONV + 1].reshape(-1), norm_gain_grad])
    misc = jnp.pad(misc, (0, -misc.shape[0] % 1024)).reshape(8, -1)
    smalls = over_dp(jnp.concatenate([rows, gg], axis=0))
    misc = over_dp(misc).reshape(-1)
    step_bias_grad, decay_grad = misc[:heads], misc[128 : 128 + heads]
    state_rows = from_parts(misc[256 : 256 + (CONV + 1) * span].reshape(CONV + 1, span))
    state_rows = jnp.swapaxes(state_rows, 0, 1).reshape(CONV + 1, 2 * STATE)
    at = 256 + (CONV + 1) * span
    skip_grad = jnp.sum(smalls[CONV + 1].reshape(heads, HEAD_DIM), axis=1)
    return (
        block_output,
        input_gradient,
        misc[at : at + share],
        gate_grad,
        inner_grad,
        step_grad,
        state_grad,
        smalls[:CONV],
        smalls[CONV],
        state_rows[:CONV],
        state_rows[CONV],
        step_bias_grad,
        decay_grad,
        skip_grad,
        smalls[8],
        output_grad,
    )


def solution(mesh):
    return jax.shard_map(
        on_device,
        mesh=mesh,
        in_specs=(
            P("dp", None), P("dp", None), P("dp", None), P(), P(None, "tensor"), P(None, "tensor"), P(None, "tensor"), P(),
            P(None, "tensor"), P("tensor"), P(), P(), P("tensor"), P("tensor"), P("tensor"), P("tensor"), P("tensor", None),
        ),
        out_specs=(
            P("dp", "tensor"), P("dp", "tensor"), P("tensor"), P("dp", "tensor"), P("dp", "tensor"), P("dp", "tensor"),
            P("dp", None), P(None, "tensor"), P("tensor"), P(), P(), P("tensor"), P("tensor"), P("tensor"), P("tensor"),
            P("tensor", "dp"),
        ),
        check_vma=False,
    )
```

```python
from functools import partial

import jax
import jax.numpy as jnp
from jax import lax
from jax.experimental import pallas as pl
from jax.experimental.pallas import tpu as pltpu
from jax.sharding import PartitionSpec as P

HEAD_DIM = 64
STATE = 128
CONV = 4
BLK = 256
HPB = BLK // HEAD_DIM
eps = 1e-05
NEG = -1e30
f32 = jnp.float32
bf16 = jnp.bfloat16
HIGH = lax.Precision.HIGHEST
NN = (((1,), (0,)), ((), ()))
NT = (((1,), (1,)), ((), ()))
TN = (((0,), (0,)), ((), ()))


def mm(a, b, dims=NN, precision=None):
    return lax.dot_general(a, b, dims, precision=precision, preferred_element_type=f32)


def sigmoid(x):
    return 1.0 / (1.0 + jnp.exp(-x))


def softplus(x):
    return jnp.maximum(x, 0.0) + jnp.log1p(jnp.exp(-jnp.abs(x)))


def seg_of(places, lengths):
    total = jnp.zeros(places.shape, jnp.int32)
    end = jnp.int32(0)
    for s in range(lengths.shape[1]):
        end = end + lengths[0, s]
        total = total + (places >= end).astype(jnp.int32)
    return total


def keeps(lengths, count):
    t = lax.broadcasted_iota(jnp.int32, (count, 1), 0)
    own = seg_of(t, lengths)
    out = [None]
    for back in range(1, CONV):
        out.append(((seg_of(t - back, lengths) == own) & (t >= back)).astype(f32))
    return out


def down(x, back):
    return pltpu.roll(x, back, 0)


def up(x, back):
    return pltpu.roll(x, x.shape[0] - back, 0)


def conv(u, kernel, bias, keep):
    out = bias + kernel[CONV - 1 : CONV, :] * u
    for back in range(1, CONV):
        out = out + kernel[CONV - 1 - back : CONV - back, :] * (down(u, back) * keep[back])
    return out


def conv_back(dc, u, kernel, keep):
    du = kernel[CONV - 1 : CONV, :] * dc
    rows = [jnp.sum(dc * u, axis=0, keepdims=True)]
    for back in range(1, CONV):
        kept = dc * keep[back]
        du = du + kernel[CONV - 1 - back : CONV - back, :] * up(kept, back)
        rows.append(jnp.sum(kept * down(u, back), axis=0, keepdims=True))
    return du, rows[::-1] + [jnp.sum(dc, axis=0, keepdims=True)]


def lanes_first(shape):
    return lax.broadcasted_iota(jnp.int32, shape, 1) < HEAD_DIM


def norm_kernel(x_ref, gain_ref, nb_ref, inv_ref):
    x = x_ref[...].astype(f32)
    inv = lax.rsqrt(jnp.sum(x * x, axis=1, keepdims=True) / x.shape[1] + eps)
    nb_ref[...] = (x * inv * gain_ref[...]).astype(bf16)
    inv_ref[...] = jnp.broadcast_to(inv, inv_ref.shape)


def forward_kernel(
    lengths, nb_ref, cot_ref, wg_ref, wi_ref, wo_ref, ws_ref, wst_ref, ik_ref, ib_ref, sk_ref, sb_ref,
    stepb_ref, decay_ref, skipc_ref, gain_ref,
    graw_ref, iraw_ref, cv_ref, mixed_ref, scaled_ref, sums_ref, sraw_ref, sact_ref, state_ref, hc_ref, lsr_ref,
    addm_ref, g_ref, keep_ref, acc,
):
    j = pl.program_id(0)
    count = nb_ref.shape[0]
    nb = nb_ref[...]

    @pl.when(j == 0)
    def _():
        i0 = lax.broadcasted_iota(jnp.int32, (count, count), 0)
        j0 = lax.broadcasted_iota(jnp.int32, (count, count), 1)
        same = (seg_of(i0, lengths) == seg_of(j0, lengths)) & (j0 <= i0)
        addm_ref[...] = jnp.where(same, 0.0, NEG)
        state = mm(nb, wst_ref[...])
        state_ref[...] = state
        keep = keeps(lengths, count)
        for back in range(1, CONV):
            keep_ref[:, back : back + 1] = keep[back]
        cv = conv(state, sk_ref[...], sb_ref[...], keep)
        act = cv * sigmoid(cv)
        sact_ref[...] = act
        g_ref[...] = mm(act[:, STATE:], act[:, :STATE], NT, HIGH)
        raw = mm(nb, ws_ref[...]) + stepb_ref[...]
        sraw_ref[...] = raw
        step = softplus(raw)
        logs = mm(same.astype(f32), step * (-jnp.exp(decay_ref[...])), NN, HIGH)
        lsr_ref[...] = jnp.transpose(logs)
        for k in range(hc_ref.shape[0]):
            hc_ref[k, :, 0:HPB] = logs[:, HPB * k : HPB * (k + 1)]
            hc_ref[k, :, HPB : 2 * HPB] = step[:, HPB * k : HPB * (k + 1)]
        acc[...] = jnp.zeros_like(acc)

    gate = mm(nb, wg_ref[...])
    inner = mm(nb, wi_ref[...])
    scaled = mm(cot_ref[...], wo_ref[...], NT)
    graw_ref[...] = gate
    iraw_ref[...] = inner
    scaled_ref[...] = scaled
    cv = conv(inner, ik_ref[...], ib_ref[...], keeps(lengths, count))
    cv_ref[...] = cv
    v = cv * sigmoid(cv)
    first = lanes_first((count, 2 * HEAD_DIM))
    addm = addm_ref[...]
    g = g_ref[...]
    parts = []
    for pair in range(BLK // (2 * HEAD_DIM)):
        vp = v[:, 2 * HEAD_DIM * pair : 2 * HEAD_DIM * (pair + 1)]
        k = 2 * pair
        steps = jnp.where(first, hc_ref[j, :, HPB + k : HPB + k + 1], hc_ref[j, :, HPB + k + 1 : HPB + k + 2])
        vs = (vp * steps).astype(bf16)
        ys = []
        for h in (k, k + 1):
            gaps = hc_ref[j, :, h : h + 1] - lsr_ref[pl.ds(HPB * j + h, 1), :] + addm
            ys.append(mm((g * jnp.exp(gaps)).astype(bf16), vs))
        parts.append(jnp.where(first, ys[0], ys[1]))
    mixed = jnp.concatenate(parts, axis=1) + skipc_ref[...] * v
    mixed_ref[...] = mixed
    gated = mixed * (gate * sigmoid(gate))
    acc[:, 0:1] += jnp.sum(gated * gated, axis=1, keepdims=True)
    acc[:, 1:2] += jnp.sum(scaled * gain_ref[...] * gated, axis=1, keepdims=True)

    @pl.when(j == pl.num_programs(0) - 1)
    def _():
        sums_ref[...] = jnp.transpose(acc[...])[0:8, :]


def unit_kernel(width, s_ref, graw_ref, mixed_ref, scaled_ref, gain_ref, x_ref, dm_ref, gg_ref):
    sums = jnp.sum(s_ref[...], axis=0)
    cols = jnp.transpose(sums)
    inv = lax.rsqrt(cols[:, 0:1] / width + eps)
    dot = inv * cols[:, 1:2]
    gate, mixed, scaled, gain = graw_ref[...], mixed_ref[...], scaled_ref[...], gain_ref[...]
    s = sigmoid(gate)
    act = gate * s
    unit = mixed * act * inv
    x_ref[0, 0] = (unit * gain).astype(bf16).astype(f32)
    gg_ref[...] = jnp.broadcast_to(jnp.sum(scaled * unit, axis=0, keepdims=True), gg_ref.shape)
    d_gated = inv * (scaled * gain - unit * (dot / width))
    dm_ref[...] = d_gated * act
    x_ref[1, 0] = (d_gated * mixed * s * (1.0 + gate * (1.0 - s))).astype(bf16).astype(f32)


def backward_kernel(
    lengths, dm_ref, cv_ref, iraw_ref, mixed_ref, hc_ref, lsr_ref, addm_ref, g_ref, sraw_ref, sact_ref,
    ik_ref, skipc_ref, decay_ref, _,
    back_ref, rows_ref, sback_ref, hrows_ref, dstate_ref, dg, dlogs, dstep,
):
    j = pl.program_id(0)
    count = dm_ref.shape[0]

    @pl.when(j == 0)
    def _():
        dg[...] = jnp.zeros_like(dg)
        dlogs[...] = jnp.zeros_like(dlogs)
        dstep[...] = jnp.zeros_like(dstep)

    cv, dm, skipc = cv_ref[...], dm_ref[...], skipc_ref[...]
    s = sigmoid(cv)
    v = cv * s
    within = mixed_ref[...] - skipc * v
    first = lanes_first((count, 2 * HEAD_DIM))
    addm = addm_ref[...]
    g = g_ref[...]
    us, vss, dyb, stepm = [], [], [], []
    total = dg[...]
    for pair in range(BLK // (2 * HEAD_DIM)):
        cols = slice(2 * HEAD_DIM * pair, 2 * HEAD_DIM * (pair + 1))
        k = 2 * pair
        steps = jnp.where(first, hc_ref[0, :, HPB + k : HPB + k + 1], hc_ref[0, :, HPB + k + 1 : HPB + k + 2])
        vs = (v[:, cols] * steps).astype(bf16)
        dy = dm[:, cols].astype(bf16)
        both = []
        for h in (k, k + 1):
            gaps = hc_ref[0, :, h : h + 1] - lsr_ref[pl.ds(HPB * j + h, 1), :] + addm
            decay = jnp.exp(gaps)
            both.append(mm((g * decay).astype(bf16), dy, TN))
            mine = first if h == k else jnp.logical_not(first)
            total = total + decay * mm(jnp.where(mine, dy, jnp.zeros_like(dy)), vs, NT)
        us.append(jnp.where(first, both[0], both[1]))
        vss.append(vs.astype(f32))
        dyb.append(dy.astype(f32))
        stepm.append(steps)
    dg[...] = total
    u = jnp.concatenate(us, axis=1)
    vs = jnp.concatenate(vss, axis=1)
    dy = jnp.concatenate(dyb, axis=1)
    steps = jnp.concatenate(stepm, axis=1)
    c0 = lax.broadcasted_iota(jnp.int32, (BLK, 128), 0) // HEAD_DIM
    l0 = lax.broadcasted_iota(jnp.int32, (BLK, 128), 1)
    pick = (l0 == c0 + HPB * j).astype(f32)
    dlogs[...] += mm(dy * within - vs * u, pick, NN, HIGH)
    dstep[...] += mm(v * u, pick, NN, HIGH)
    dv = steps * u + skipc * dm
    dc = dv * (s * (1.0 + cv * (1.0 - s)))
    du, rows = conv_back(dc, iraw_ref[...], ik_ref[...], keeps(lengths, count))
    back_ref[0, 0] = du.astype(bf16).astype(f32)
    rows_ref[...] = jnp.concatenate(rows + [jnp.sum(dm * v, axis=0, keepdims=True)] + [jnp.zeros((2, BLK), f32)], axis=0)

    @pl.when(j == pl.num_programs(0) - 1)
    def _():
        mask = (addm > -1.0).astype(f32)
        q = mm(mask, dlogs[...], TN, HIGH)
        raw = sraw_ref[...]
        step = softplus(raw)
        rate = -jnp.exp(decay_ref[...])
        draw = (dstep[...] + rate * q) * sigmoid(raw)
        sback_ref[...] = draw.astype(bf16).astype(f32)
        hrows_ref[...] = jnp.concatenate(
            [jnp.sum(draw, axis=0, keepdims=True), rate * jnp.sum(step * q, axis=0, keepdims=True), jnp.zeros((6, 128), f32)],
            axis=0,
        )
        act = sact_ref[...]
        d_b = mm(dg[...], act[:, STATE:], TN, HIGH)
        d_c = mm(dg[...], act[:, :STATE], NN, HIGH)
        both = jnp.concatenate([d_b, d_c], axis=1)
        span = dstate_ref.shape[2]
        for t in range(dstate_ref.shape[0]):
            dstate_ref[t] = both[:, span * t : span * (t + 1)]


def state_kernel(lengths, parts_ref, u_ref, sk_ref, sb_ref, back_ref, rows_ref):
    keep = keeps(lengths, u_ref.shape[0])
    cv = conv(u_ref[...], sk_ref[...], sb_ref[...], keep)
    s = sigmoid(cv)
    dc = jnp.sum(parts_ref[...], axis=0) * (s * (1.0 + cv * (1.0 - s)))
    du, rows = conv_back(dc, u_ref[...], sk_ref[...], keep)
    back_ref[...] = du.astype(bf16).astype(f32)
    rows_ref[...] = jnp.concatenate(rows + [jnp.zeros((3, du.shape[1]), f32)], axis=0)


MESH = pl.DeviceIdType.MESH
RING = 6
VMEM_LIMIT = 64 << 20
LEAD = 4
LEAD2 = 2


def layer_kernel(
    lengths, xin, cot, gain_in1, ws, wst, ik, ib1, sk, sb1, stepb1, decay1, skip1, gain1, wg_hbm, wi_hbm, wo_hbm,
    out_ref, din_ref, gate_out, inner_out, state_out, step_out, turned_out, smalls_ref,
    x, act, dmb, nb, inv, gain_in, ib, sb, heads_in, skipc, gain, fs, f1, f2, f3, fx, fc, ft, big, yra, yrb, r, ea, fin, xb, xbr, wring, woring, po, por, pir, addm, g, hc, lsr, sact, state_raw, sraw, keep_ref, dg, dlogs, dstep, hsum, acc, sums, sumr, dstate, dsr, srr, sm, smr,
    ex, exr, rx, exe, yrx, exg, dots, dotr,
    p1s, p1v, p2s, p2v, p3s, p3v, es, ev, yas, yav, ybs, ybv, fas, fav, fins, wsem, pos, pov, pis, piv,
    dss, dsv, srs, srv, dts, dtv, sus, suv, sms, smv, exs, exv, yxs, yxv, exgs, exgv,
    f1s, f1v, f2s, f2v, f3s, f3v, fxs, fxv, fcs, fcv, credit, fc_free,
):
    d, t = lax.axis_index("dp"), lax.axis_index("tensor")
    y, z = d % 2, d // 2
    side, half = z % 2, z // 2
    hub = (z == 1) | (z == 2)
    edge = jnp.logical_not(hub)
    chunks, count, wide = x.shape
    each = chunks // 3
    lanes = wide // 2
    width = xin.shape[1]
    part = width // 4
    own = part // 2
    share = width // 4
    span = dsr.shape[2]
    inner = each * wide
    piece = f1.shape[1]
    pair, peer, line = d ^ 2, d ^ 6, d ^ 1
    mine, other = pl.multiple_of(own * y, own), pl.multiple_of(own * (1 - y), own)
    mine_part, pair_part = pl.multiple_of(part * side, part), pl.multiple_of(part * (1 - side), part)
    near, far = pl.multiple_of(half * 2 * part, 2 * part), pl.multiple_of((1 - half) * 2 * part, 2 * part)
    my_rows = pl.multiple_of(t * piece, piece)
    my_share = pl.multiple_of(t * share, share)

    def send(src, dst, ssem, rsem, dev):
        return pltpu.make_async_remote_copy(
            src_ref=src, dst_ref=dst, send_sem=ssem, recv_sem=rsem, device_id=dev, device_id_type=MESH
        )

    def p1(q):
        return send(x.at[q], big.at[q % RING, pl.ds(0, count)], p1s.at[q], p1v.at[q], (pair, t))

    def p2(q):
        return send(x.at[q], big.at[q % RING, pl.ds(count, count)], p2s.at[q], p2v.at[q], (peer, t))

    def p3(q):
        slot = q % RING
        return send(
            big.at[slot, pl.ds(0, count)], big.at[slot, pl.ds(2 * count, count)], p3s.at[q], p3v.at[q], (peer, t)
        )

    def e(q):
        return send(
            r.at[q % 2, 0, :, pl.ds(lanes, lanes)], big.at[q % RING, pl.ds(0, part), pl.ds(0, lanes)], es.at[q], ev.at[q],
            (pair, t),
        )

    def ya(q, k):
        return send(
            r.at[q % 2, k, pl.ds(other, own), pl.ds(0, lanes)], yra.at[q % RING, k], yas.at[q, k], yav.at[q, k], (line, t)
        )

    def yb_hub(q):
        return send(
            r.at[q % 2, 1, pl.ds(other, own), pl.ds(lanes, lanes)], yrb.at[q % LEAD], ybs.at[q], ybv.at[q], (line, t)
        )

    def yb_edge(q):
        return send(
            big.at[q % RING, pl.ds(other, own), pl.ds(0, lanes)], yrb.at[q % LEAD], ybs.at[q], ybv.at[q], (line, t)
        )

    def fa(q):
        return send(ea.at[q % 2], yra.at[q % RING, 0], fas.at[q], fav.at[q], (pair, t))

    def feature1(f):
        return send(f1.at[f], f1.at[f], f1s.at[f], f1v.at[f], (pair, t))

    def feature2(f):
        return send(fs.at[f], f2.at[f], f2s.at[f], f2v.at[f], (peer, t))

    def feature3(f):
        return send(f1.at[f, :, pl.ds(far, 2 * part)], f3.at[f], f3s.at[f], f3v.at[f], (peer, t))

    def feature(f, shard):
        return (f1.at[f, :, pl.ds(near, 2 * part)], f2.at[f], f3.at[f])[shard]

    def across(f, shard):
        return send(feature(f, shard), fx.at[f, shard], fxs.at[f, shard], fxv.at[f, shard], (d, t ^ 2))

    def sibling(f, shard, k):
        src = fx.at[f, shard] if k else feature(f, shard)
        return send(src, fc.at[k, shard], fcs.at[k, f, shard], fcv.at[k, f, shard], (d, t ^ 1))

    def spread(f, shard):
        across(f, shard).start()
        if f:
            sibling(f, shard, 0).start()

    p1x = lambda: send(ex, exr.at[0], exs.at[0], exv.at[0], (pair, t))
    p2x = lambda: send(ex, exr.at[1], exs.at[1], exv.at[1], (peer, t))
    p3x = lambda: send(exr.at[0], exr.at[2], exs.at[2], exv.at[2], (peer, t))
    e_x = lambda: send(rx.at[0], exe, exs.at[3], exv.at[3], (pair, t))
    yx_hub = lambda: send(rx.at[1, pl.ds(other, own)], yrx, yxs.at[0], yxv.at[0], (line, t))
    yx_edge = lambda: send(exe.at[pl.ds(other, own)], yrx, yxs.at[0], yxv.at[0], (line, t))

    def over_tensor(src, dst, ssem, rsem):
        return lambda k: send(src(k), dst(k), ssem.at[k - 1], rsem.at[k - 1], (d, t ^ k))

    sum_copy = over_tensor(lambda k: sums, lambda k: sumr.at[k - 1], sus, suv)
    state_copy = over_tensor(lambda k: dstate.at[t ^ k], lambda k: dsr.at[k - 1], dss, dsv)
    row_copy = over_tensor(lambda k: srr.at[t], lambda k: srr.at[t], srs, srv)
    out_near = lambda n: send(po.at[t ^ (1 + 2 * n)], por.at[n], pos.at[n], pov.at[n], (d, t ^ 1))
    out_far = lambda: send(po.at[t ^ 2], por.at[2], pos.at[2], pov.at[2], (d, t ^ 2))
    tiles = share // lanes
    block = lambda i: act.at[pl.ds(tiles * i, tiles)]
    in_near = lambda n: send(block(t ^ (1 + 2 * n)), pir.at[n], pis.at[n], piv.at[n], (d, t ^ 1))
    in_far = lambda: send(block(t ^ 2), pir.at[2], pis.at[2], piv.at[2], (d, t ^ 2))
    dot_copy = over_tensor(lambda k: dots, lambda k: dotr.at[k - 1], dts, dtv)
    extra_copy = over_tensor(lambda k: exg.at[t], lambda k: exg.at[t], exgs, exgv)
    small_copy = lambda k: send(sm, smr.at[k], sms.at[k], smv.at[k], (d ^ (1 << k), t))

    def started(copy):
        for k in range(1, 4):
            copy(k).start()

    def waited(copy):
        for k in range(1, 4):
            copy(k).wait()

    def load(n, kind):
        at = pl.multiple_of((n % each) * wide, wide)
        if kind == 2:
            return pltpu.make_async_copy(wo_hbm.at[pl.ds(at, wide), :], woring.at[n % 2], wsem.at[kind, n % 2])
        ref = (wg_hbm, wi_hbm)[kind]
        return pltpu.make_async_copy(ref.at[:, pl.ds(at, wide)], wring.at[n % 2, kind], wsem.at[kind, n % 2])

    for n in range(2):
        for kind in range(3):
            load(n, kind).start()

    barrier = pltpu.get_barrier_semaphore()
    for dev in ((pair, t), (peer, t), (line, t), (d ^ 4, t), (d, t ^ 1), (d, t ^ 2), (d, t ^ 3)):
        pl.semaphore_signal(barrier, inc=1, device_id=dev, device_id_type=MESH)
    pl.semaphore_wait(barrier, 7)

    heads = ws.shape[0]
    gain_in[...] = gain_in1[...].reshape(1, width)
    ib[...] = ib1[...].reshape(1, inner)
    gain[...] = gain1[...].reshape(1, inner)
    sb[...] = sb1[...].reshape(1, 4 * span)
    heads_in[...] = jnp.zeros_like(heads_in)
    for n, ref in enumerate((stepb1, decay1, skip1)):
        heads_in[8 * n : 8 * n + 8, 0:heads] = jnp.broadcast_to(ref[...].reshape(1, heads), (8, heads))
    h0 = lax.broadcasted_iota(jnp.int32, (128, inner), 0)
    spread_heads = (h0 == lax.broadcasted_iota(jnp.int32, (128, inner), 1) // HEAD_DIM).astype(f32)
    skipc[...] = mm(heads_in[16:24, :], spread_heads, NN, HIGH)[0:1, :]
    rate_row = -jnp.exp(heads_in[8:9, :])

    def begin_features(f):
        ref = cot if f else nb

        @pl.when(edge)
        def _():
            f1[f] = ref[pl.ds(my_rows, piece), :].astype(f32)
            feature1(f).start()

        @pl.when(hub)
        def _():
            fs[f] = ref[pl.ds(my_rows, piece), pl.ds(far, 2 * part)].astype(f32)
            feature2(f).start()

    begin_features(1)
    xv = xin[...].astype(f32)
    scale = lax.rsqrt(jnp.sum(xv * xv, axis=1, keepdims=True) / width + eps)
    nb[...] = (xv * scale * gain_in[...]).astype(bf16)
    inv[...] = jnp.broadcast_to(scale, inv.shape)
    begin_features(0)

    i0 = lax.broadcasted_iota(jnp.int32, (count, count), 0)
    j0 = lax.broadcasted_iota(jnp.int32, (count, count), 1)
    same = (seg_of(i0, lengths) == seg_of(j0, lengths)) & (j0 <= i0)
    addm[...] = jnp.where(same, 0.0, NEG)
    keep = keeps(lengths, count)
    for back in range(1, CONV):
        keep_ref[:, back : back + 1] = keep[back]
    state = mm(nb[...], wst[...])
    state_raw[...] = state
    cv = conv(state, sk[...], sb[...], keep)
    sact[...] = cv * sigmoid(cv)
    g[...] = mm(sact[:, STATE:], sact[:, :STATE], NT, HIGH)
    sraw[...] = jnp.zeros_like(sraw)
    sraw[:, 0:heads] = mm(nb[...], ws[...], NT) + heads_in[0:1, 0:heads]
    step = softplus(sraw[...])
    logs = mm(same.astype(f32), step * rate_row, NN, HIGH)
    lsr[...] = jnp.transpose(logs)
    for k in range(each):
        hc[k, :, 0:HPB] = logs[:, HPB * k : HPB * (k + 1)]
        hc[k, :, HPB : 2 * HPB] = step[:, HPB * k : HPB * (k + 1)]
    for ref in (acc, dg, dlogs, dstep, hsum, sm):
        ref[...] = jnp.zeros_like(ref)

    first = lanes_first((count, 2 * HEAD_DIM))

    def kept():
        return [None] + [keep_ref[:, b : b + 1] for b in range(1, CONV)]

    def steps_of(j, k):
        return jnp.where(first, hc[j, :, HPB + k : HPB + k + 1], hc[j, :, HPB + k + 1 : HPB + k + 2])

    def decay_of(j, h):
        return jnp.exp(hc[j, :, h : h + 1] - lsr[pl.ds(HPB * j + h, 1), :] + addm[...])

    def put(base, j, value):
        for half_block in range(2):
            act[base + 2 * j + half_block] = value[:, lanes * half_block : lanes * (half_block + 1)]

    def take(base, j):
        return jnp.concatenate([act[base + 2 * j], act[base + 2 * j + 1]], axis=1)

    def forward_block(j, carry):
        slot = j % 2
        cols = pl.ds(pl.multiple_of(j * wide, wide), wide)
        for kind in range(3):
            load(j, kind).wait()
        gate = mm(nb[...], wring[slot, 0])
        raw = mm(nb[...], wring[slot, 1])
        scaled = mm(cot[...], woring[slot], NT)
        for kind in range(3):
            load(j + 2, kind).start()
        x[j] = scaled
        x[each + j] = gate
        x[2 * each + j] = raw
        cv = conv(raw, ik[:, cols], ib[:, cols], kept())
        put(2 * each, j, cv)
        v = cv * sigmoid(cv)
        parts = []
        for k in range(0, HPB, 2):
            vs = (v[:, HEAD_DIM * k : HEAD_DIM * (k + 2)] * steps_of(j, k)).astype(bf16)
            ys = [mm((g[...] * decay_of(j, h)).astype(bf16), vs) for h in (k, k + 1)]
            parts.append(jnp.where(first, ys[0], ys[1]))
        mixed = jnp.concatenate(parts, axis=1) + skipc[:, cols] * v
        put(0, j, mixed)
        gated = mixed * (gate * sigmoid(gate))
        acc[:, 0:1] += jnp.sum(gated * gated, axis=1, keepdims=True)
        acc[:, 1:2] += jnp.sum(scaled * gain[:, cols] * gated, axis=1, keepdims=True)

        @pl.when(hub & (j == 1))
        def _():
            feature1(1).wait_recv()
            feature3(1).start()
            spread(1, 0)

        @pl.when(hub & (j == 2))
        def _():
            feature2(1).wait_recv()
            spread(1, 1)

        return carry

    lax.fori_loop(0, each, forward_block, 0)
    sums[...] = jnp.transpose(acc[...])[0:8, :]
    started(sum_copy)

    @pl.when(hub)
    def _():
        feature3(1).wait_recv()
        spread(1, 2)

    waited(sum_copy)
    total = jnp.transpose(sums[...] + sumr[0] + sumr[1] + sumr[2])
    acc[:, 0:1] = lax.rsqrt(total[:, 0:1] / (4 * inner) + eps)
    acc[:, 1:2] = acc[:, 0:1] * total[:, 1:2] / (4 * inner)

    def unit_block(j, carry):
        cols = pl.ds(pl.multiple_of(j * wide, wide), wide)
        scaled, gate, mixed = x[j], x[each + j], take(0, j)
        inv_gate, dot = acc[:, 0:1], acc[:, 1:2]
        s = sigmoid(gate)
        gate_act = gate * s
        unit = mixed * gate_act * inv_gate
        weights = gain[:, cols]
        x[j] = (unit * weights).astype(bf16).astype(f32)
        sm[8:9, cols] = jnp.sum(scaled * unit, axis=0, keepdims=True)
        d_gated = inv_gate * (scaled * weights - unit * dot)
        dmb[j] = d_gated * gate_act
        x[each + j] = (d_gated * mixed * s * (1.0 + gate * (1.0 - s))).astype(bf16).astype(f32)

        @pl.when(hub & (j < LEAD2))
        def _():
            p2(j).start()

        @pl.when(edge & (j < 2))
        def _():
            p1(j).start()

        return carry

    lax.fori_loop(0, each, unit_block, 0)

    @pl.when(hub)
    def _():
        feature1(0).wait_recv()
        feature3(0).start()
        spread(0, 0)
        feature2(0).wait_recv()
        spread(0, 1)

    @pl.when(edge)
    def _():
        for n in range(2, LEAD):
            p1(n - 2).wait_send()
            p1(n).start()

    def forward_features(f):
        if not f:
            pl.semaphore_wait(fc_free, 1)
        for shard in range(3):
            if not f:
                sibling(f, shard, 0).start()
            across(f, shard).wait_recv()
            sibling(f, shard, 1).start()

    def assemble(f):
        own_rows = (cot if f else nb)[:, pl.ds(near, 2 * part)]
        ft[f, :, 0:count] = own_rows.T
        for shard in range(3):
            sibling(f, shard, 0).wait_recv()
            sibling(f, shard, 1).wait_recv()
            for k, ref in enumerate((feature(f, shard), fc.at[0, shard], fx.at[f, shard], fc.at[1, shard])):
                xbr[pl.ds(pl.multiple_of((t ^ k) * piece, piece), piece), :] = ref[...].astype(bf16)
            ft[f, :, count * (shard + 1) : count * (shard + 2)] = xbr[...].T
        if f:
            pl.semaphore_signal(fc_free, inc=1, device_id=(d, t ^ 1), device_id_type=MESH)

    def backward_block(j, carry):
        cols = pl.ds(pl.multiple_of(j * wide, wide), wide)
        cv, dm = take(2 * each, j), dmb[j]
        s = sigmoid(cv)
        v = cv * s
        within = take(0, j) - skipc[:, cols] * v
        us, vss, dys, stepm = [], [], [], []
        for k in range(0, HPB, 2):
            lane = slice(HEAD_DIM * k, HEAD_DIM * (k + 2))
            steps = steps_of(j, k)
            vs = (v[:, lane] * steps).astype(bf16)
            dy = dm[:, lane].astype(bf16)
            both = []
            for h in (k, k + 1):
                ratio = decay_of(j, h)
                both.append(mm((g[...] * ratio).astype(bf16), dy, TN))
                part_of = first if h == k else jnp.logical_not(first)
                dg[...] += ratio * mm(jnp.where(part_of, dy, jnp.zeros_like(dy)), vs, NT)
            us.append(jnp.where(first, both[0], both[1]))
            vss.append(vs.astype(f32))
            dys.append(dy.astype(f32))
            stepm.append(steps)
        u, vs, dy, steps = (jnp.concatenate(p, axis=1) for p in (us, vss, dys, stepm))
        c0 = lax.broadcasted_iota(jnp.int32, (wide, 128), 0) // HEAD_DIM
        l0 = lax.broadcasted_iota(jnp.int32, (wide, 128), 1)
        pick = (l0 == c0 + HPB * j).astype(f32)
        dlogs[...] += mm(dy * within - vs * u, pick, NN, HIGH)
        dstep[...] += mm(v * u, pick, NN, HIGH)
        per_lane = jnp.sum(dm * v, axis=0, keepdims=True)
        hsum[...] += mm(jnp.broadcast_to(per_lane, (8, wide)), pick, NN, HIGH)
        dc = (steps * u + skipc[:, cols] * dm) * (s * (1.0 + cv * (1.0 - s)))
        du, rows = conv_back(dc, x[2 * each + j], ik[:, cols], kept())
        x[2 * each + j] = du.astype(bf16).astype(f32)
        sm[0:5, cols] = jnp.concatenate(rows, axis=0)
        return carry

    def backward_end():
        mask = (addm[...] > -1.0).astype(f32)
        q = mm(mask, dlogs[...], TN, HIGH)
        raw = sraw[...]
        step = softplus(raw)
        rate = -jnp.exp(heads_in[8:9, :])
        draw = (dstep[...] + rate * q) * sigmoid(raw)
        dstep[...] = draw.astype(bf16).astype(f32)
        sm[15:16, 0:128] = jnp.sum(draw, axis=0, keepdims=True)
        sm[15:16, 128:256] = rate * jnp.sum(step * q, axis=0, keepdims=True)
        sm[15:16, 256:384] = hsum[0:1, :]
        d_b = mm(dg[...], sact[:, STATE:], TN, HIGH)
        d_c = mm(dg[...], sact[:, :STATE], NN, HIGH)
        both = jnp.concatenate([d_b, d_c], axis=1)
        for i in range(4):
            dstate[i] = both[:, span * i : span * (i + 1)]
        started(state_copy)

    def slab(ref):
        out = None
        for i in range(4):
            one = jnp.where(t == i, ref[:, span * i : span * (i + 1)], 0.0)
            out = one if out is None else out + one
        return out

    def states():
        waited(state_copy)
        total = dstate[t] + dsr[0] + dsr[1] + dsr[2]
        u, kernel = slab(state_raw), slab(sk)
        cv = conv(u, kernel, slab(sb), kept())
        s = sigmoid(cv)
        du, rows = conv_back(total * (s * (1.0 + cv * (1.0 - s))), u, kernel, kept())
        ex[:, 0:span] = du.astype(bf16).astype(f32)
        ex[:, span : 2 * span] = dstep[:, 0:span]
        srr[t] = jnp.concatenate(rows + [jnp.zeros((3, span), f32)], axis=0)
        started(row_copy)

        @pl.when(hub)
        def _():
            p2x().start()

        @pl.when(edge)
        def _():
            p1x().start()

    def out_parts():
        for c in range(each):
            n = each + c
            load(n, 2).wait()
            xc = x[c].astype(bf16)
            for i in range(4):
                one = mm(xc, woring[n % 2, :, share * i : share * (i + 1)])
                po[i] = one if c == 0 else po[i] + one
            if c + 2 < each:
                load(n + 2, 2).start()
        for n in range(2):
            out_near(n).start()

    def out_across():
        for n in range(2):
            out_near(n).wait()
        po[t ^ 2] = po[t ^ 2] + por[1]
        out_far().start()

    def out_sum():
        out_far().wait()
        hidden = xin[:, pl.ds(my_share, share)].astype(f32)
        out_ref[...] = (po[t] + por[0] + por[2] + hidden).astype(bf16)

    def in_parts():
        lane = lax.broadcasted_iota(jnp.int32, (count, 4 * span), 1) // span
        own_state = ex[:, 0:span]
        states4 = jnp.where(lane == t, jnp.concatenate([own_state] * 4, axis=1), 0.0).astype(bf16)
        steps_back = dstep[:, 0:heads].astype(bf16)
        for i in range(4 * tiles):
            rows = slice(lanes * i, lanes * (i + 1))
            act[i] = mm(states4, wst[rows, :], NT) + mm(steps_back, ws[:, rows])
        for c in range(each):
            n = each + c
            load(n, 0).wait()
            load(n, 1).wait()
            gc, ic = x[each + c].astype(bf16), x[2 * each + c].astype(bf16)
            for i in range(2 * tiles):
                rows = slice(2 * lanes * i, 2 * lanes * (i + 1))
                one = mm(gc, wring[n % 2, 0, rows, :], NT) + mm(ic, wring[n % 2, 1, rows, :], NT)
                act[2 * i] = act[2 * i] + one[:, 0:lanes]
                act[2 * i + 1] = act[2 * i + 1] + one[:, lanes:]
            if c + 2 < each:
                load(n + 2, 0).start()
                load(n + 2, 1).start()
        for n in range(2):
            in_near(n).start()

    def in_across():
        for n in range(2):
            in_near(n).wait()
        for i in range(tiles):
            act[tiles * (t ^ 2) + i] = act[tiles * (t ^ 2) + i] + pir[1, i]
        in_far().start()

    def normed():
        return xin[:, pl.ds(my_share, share)].astype(f32) * inv[:, 0:1]

    def in_sum():
        in_far().wait()
        for i in range(tiles):
            po[0, :, lanes * i : lanes * (i + 1)] = act[tiles * t + i] + pir[0, i] + pir[2, i]
        d_normed = po[0]
        dot = jnp.sum(d_normed * gain_in[:, pl.ds(my_share, share)] * normed(), axis=1, keepdims=True)
        dots[...] = jnp.transpose(jnp.broadcast_to(dot, (count, 128)))[0:8, :]
        started(dot_copy)

    def finish():
        waited(dot_copy)
        waited(row_copy)
        d_normed, n = po[0], normed()
        dot = jnp.transpose(dots[...] + dotr[0] + dotr[1] + dotr[2])[:, 0:1] / width
        d_hat = d_normed * gain_in[:, pl.ds(my_share, share)]
        din_ref[...] = inv[:, 0:1] * (d_hat - n * dot) + cot[:, pl.ds(my_share, share)].astype(f32)
        sm[9:10, 0:share] = jnp.sum(d_normed * n, axis=0, keepdims=True)
        for i in range(4):
            sm[10:15, span * i : span * (i + 1)] = srr[i][0:5, :]
        small_copy(0).start()

    def small(k):
        small_copy(k).wait()
        sm[...] = sm[...] + smr[k]
        if k < 2:
            small_copy(k + 1).start()
        else:
            smalls_ref[...] = sm[...]

    def extra_hub():
        p2x().wait_recv()
        p3x().wait_recv()
        for k, ref in enumerate((ex, exr.at[0], exr.at[1], exr.at[2])):
            xb[k * count : (k + 1) * count, 0:128] = ref[...].astype(bf16)
        rx[0] = mm(ft[0, pl.ds(pair_part, part), :], xb[:, 0:128])
        rx[1] = mm(ft[0, pl.ds(mine_part, part), :], xb[:, 0:128])
        e_x().start()
        yx_hub().start()

    def extra_spread(rows):
        exg[t] = rows + yrx[...]
        step_out[...] = jnp.transpose(exg[t])[span : span + heads, :]
        started(extra_copy)

    def extra_end():
        waited(extra_copy)
        for i in range(4):
            state_out[:, span * i : span * (i + 1)] = exg[i, :, 0:span]

    def process(q):
        p2(q).wait_recv()
        p3(q).wait_recv()
        p3(q).wait_send()

        @pl.when(q >= 2)
        def _():
            e(q - 2).wait_send()
            ya(q - 2, 0).wait_send()
            ya(q - 2, 1).wait_send()
            yb_hub(q - 2).wait_send()

        xb[0:count, :] = x[q].astype(bf16)
        xb[count:, :] = big[q % RING].astype(bf16)

        @pl.when(q + RING < chunks)
        def _():
            pl.semaphore_signal(credit, inc=1, device_id=(peer, t), device_id_type=MESH)

        family = jnp.where(q < each, 1, 0)
        slot = q % 2
        r[slot, 0] = mm(ft[family, pl.ds(pair_part, part), :], xb[...])
        e(q).start()
        ya(q, 0).start()
        r[slot, 1] = mm(ft[family, pl.ds(mine_part, part), :], xb[...])
        ya(q, 1).start()
        yb_hub(q).start()

    def stored(q, k):
        at = pl.multiple_of((q % each) * wide, wide)
        out = (turned_out, gate_out, inner_out)[k]
        return pltpu.make_async_copy(fin.at[q % 2], out.at[:, pl.ds(at, wide)], fins.at[q])

    def store(q, left, right):
        slot = q % 2
        for k in range(3):
            @pl.when((q >= k * each + 2) & (q < (k + 1) * each + 2))
            def _():
                stored(q - 2, k).wait()

        fin[slot, :, 0:lanes] = left
        fin[slot, :, lanes:] = right

        for k in range(3):
            @pl.when((q >= k * each) & (q < (k + 1) * each))
            def _():
                stored(q, k).start()

    def finalize_hub(q):
        slot = q % 2
        ya(q, 0).wait_recv()
        ya(q, 1).wait_recv()
        yb_hub(q).wait_recv()

        @pl.when(q >= 2)
        def _():
            fa(q - 2).wait_send()

        got = yra.at[q % RING]
        ea[slot] = r[slot, 0, pl.ds(mine, own), 0:lanes] + got[0]
        fa(q).start()
        store(
            q,
            r[slot, 1, pl.ds(mine, own), 0:lanes] + got[1],
            r[slot, 1, pl.ds(mine, own), lanes:] + yrb[q % LEAD],
        )

    def finalize_edge(q):
        yb_edge(q).wait_recv()
        fa(q).wait_recv()
        store(q, yra[q % RING, 0], big[q % RING, pl.ds(mine, own), 0:lanes] + yrb[q % LEAD])

    pieces = {
        2: backward_end, 3: out_parts, 4: [out_across, states], 5: in_parts, 6: out_sum, 7: in_across, 9: in_sum,
        10: finish, 11: lambda: small(0), 13: lambda: small(1), 16: lambda: small(2), 15: extra_end,
    }

    def body(q, carry):
        @pl.when(hub)
        def _():
            @pl.when(q < chunks)
            def _():
                p1(q).wait_recv()
                p3(q).start()

            @pl.when(q + LEAD2 < chunks)
            def _():
                @pl.when(q + LEAD2 >= RING)
                def _():
                    pl.semaphore_wait(credit, 1)

                p2(q + LEAD2).start()

            @pl.when(q == 0)
            def _():
                forward_features(1)
                assemble(1)

            @pl.when((q >= 1) & (q <= chunks))
            def _():
                process(q - 1)

            @pl.when(q >= 2)
            def _():
                finalize_hub(q - 2)

            @pl.when(q == 1)
            def _():
                feature3(0).wait_recv()
                spread(0, 2)

            @pl.when(q == 3)
            def _():
                forward_features(0)

            @pl.when(q == 4)
            def _():
                assemble(0)

            @pl.when(q == 8)
            def _():
                p1x().wait_recv()
                p3x().start()

            @pl.when(q == 10)
            def _():
                extra_hub()

            @pl.when(q == 14)
            def _():
                yx_hub().wait_recv()
                extra_spread(rx[1, pl.ds(mine, own), :])

        @pl.when(q < (each + 1) // 2)
        def _():
            lax.fori_loop(2 * q, jnp.minimum(2 * q + 2, each), backward_block, 0)

        for at, jobs in pieces.items():
            for job in jobs if isinstance(jobs, list) else [jobs]:
                pl.when(q == at)(job)

        @pl.when(edge)
        def _():
            @pl.when(q < chunks)
            def _():
                e(q).wait_recv()
                yb_edge(q).start()

            @pl.when(q + LEAD < chunks)
            def _():
                @pl.when(q >= 2)
                def _():
                    yb_edge(q - 2).wait_send()

                p1(q + LEAD).start()

            @pl.when((q >= 1) & (q <= chunks))
            def _():
                finalize_edge(q - 1)

            @pl.when(q == 12)
            def _():
                e_x().wait_recv()
                yx_edge().start()

            @pl.when(q == 14)
            def _():
                yx_edge().wait_recv()
                extra_spread(exe[pl.ds(mine, own), :])

        return carry

    lax.fori_loop(0, chunks + 2, body, 0)

    stored(chunks - 2, 2).wait()
    stored(chunks - 1, 2).wait()

    @pl.when(hub)
    def _():
        def drain(q, carry):
            p2(q).wait_send()
            return carry

        lax.fori_loop(0, chunks, drain, 0)
        for q in (chunks - 2, chunks - 1):
            e(q).wait_send()
            ya(q, 0).wait_send()
            ya(q, 1).wait_send()
            yb_hub(q).wait_send()
            fa(q).wait_send()
        for f in range(2):
            feature2(f).wait_send()
            feature3(f).wait_send()
            for shard in range(3):
                across(f, shard).wait_send()
                sibling(f, shard, 0).wait_send()
                sibling(f, shard, 1).wait_send()
        p2x().wait_send()
        p3x().wait_send()
        e_x().wait_send()
        yx_hub().wait_send()

    @pl.when(edge)
    def _():
        def drain(q, carry):
            p1(q).wait_send()
            return carry

        lax.fori_loop(LEAD - 2, chunks, drain, 0)
        for q in range(chunks - LEAD - 2, chunks):
            yb_edge(q).wait_send()
        for f in range(2):
            feature1(f).wait_send()
        p1x().wait_send()
        yx_edge().wait_send()


def outputs_kernel(
    smalls, a, b, c, d, e, f, g,
    norm_gain, inner_kernel, inner_bias, state_kernel_out, state_bias, step_bias, decay, skip, gate_gain,
    ao, bo, co, do, eo, fo, go, at_, bt, ct, dt, et, ft, gt, loads, stores,
):
    through = list(zip((a, b, c, d, e, f, g), (at_, bt, ct, dt, et, ft, gt), (ao, bo, co, do, eo, fo, go)))
    load = lambda n: pltpu.make_async_copy(through[n][0], through[n][1], loads.at[n])
    keep = lambda n: pltpu.make_async_copy(through[n][1], through[n][2], stores.at[n])
    for n in range(len(through)):
        load(n).start()
    for ref, at, lane in (
        (norm_gain, 9, 0), (inner_bias, CONV, 0), (state_bias, 10 + CONV, 0), (step_bias, 15, 0), (decay, 15, 128),
        (skip, 15, 256), (gate_gain, 8, 0),
    ):
        ref[...] = smalls[at : at + 1, lane : lane + ref.shape[0]].reshape(ref.shape)
    inner_kernel[...] = smalls[0:CONV, :]
    state_kernel_out[...] = smalls[10 : 10 + CONV, 0 : state_kernel_out.shape[1]]
    for n in range(len(through)):
        load(n).wait()
        keep(n).start()
    for n in range(len(through)):
        keep(n).wait()


def whole(shape):
    return pl.BlockSpec(shape, lambda *_: (0,) * len(shape))


def columns(rows):
    return pl.BlockSpec((rows, BLK), lambda j, *_: (0, j))


SMEM = pl.BlockSpec(memory_space=pltpu.SMEM)
VM = pltpu.CompilerParams(vmem_limit_bytes=56 << 20)
VMS = pltpu.CompilerParams(vmem_limit_bytes=56 << 20, dimension_semantics=("arbitrary",))


def struct(shape, dtype=f32):
    return jax.ShapeDtypeStruct(shape, dtype)


def cost(flops, moved):
    return pl.CostEstimate(flops=int(flops), bytes_accessed=int(moved), transcendentals=0)


def on_device(
    block_input, cotangent, seq_lengths, norm_gain, gate_weight, inner_weight, step_weight, state_weight,
    inner_kernel, inner_bias, state_kernel_, state_bias, step_bias, decay_log, skip_scale, gate_gain, output_weight,
):
    parts = lax.axis_size("tensor")
    shards = lax.axis_size("dp")
    t = lax.axis_index("tensor")
    count, width = block_input.shape
    inner = gate_weight.shape[1]
    heads = step_bias.shape[0]
    share = width // parts
    span = 2 * STATE // parts
    steps = inner // BLK
    pad = ((0, 0), (0, 128 - heads))
    row = lambda x: x.reshape(1, -1)

    def swap(x, k):
        return lax.ppermute(x, "tensor", [(i, i ^ k) for i in range(parts)])

    chunks = 3 * steps
    slab = lambda x, size: lax.dynamic_slice_in_dim(x, t * size, size, x.ndim - 1)
    if shards == 8 and parts == 4:
        own, half_blk, piece, near = width // 8, BLK // 2, count // parts, width // 2
        dma, v = pltpu.SemaphoreType.DMA, lambda *shape: pltpu.VMEM(shape, f32)
        vb = lambda *shape: pltpu.VMEM(shape, bf16)
        vmem, hbm = pl.BlockSpec(memory_space=pltpu.VMEM), pl.BlockSpec(memory_space=pl.ANY)
        scratch = [
            v(chunks, count, BLK), v(4 * steps, count, half_blk), v(steps, count, BLK), vb(count, width),
            v(count, 128), v(1, width), v(1, inner), v(1, 2 * STATE), v(24, 128), v(1, inner), v(1, inner), v(2, piece, near), v(2, piece, width), v(2, piece, near), v(2, piece, near),
            v(2, 3, piece, near), v(2, 3, piece, near), vb(2, near, 4 * count), v(RING, 3 * count, BLK),
            v(RING, 2, own, half_blk), v(LEAD, own, half_blk), v(2, 2, 2 * own, BLK), v(2, own, half_blk), v(2, own, BLK),
            vb(4 * count, BLK), vb(count, near), vb(2, 2, width, BLK), vb(2, BLK, width),
            v(4, count, share), v(3, count, share), v(3, share // half_blk, count, half_blk),
            v(count, count), v(count, count), v(steps, count, 128), v(128, count), v(count, 2 * STATE), v(count, 2 * STATE),
            v(count, 128), v(count, 128), v(count, count), v(count, 128), v(count, 128), v(8, 128), v(count, 128),
            v(8, count), v(3, 8, count), v(4, count, span), v(3, count, span), v(4, 8, span), v(16, inner), v(3, 16, inner),
            v(count, 128), v(3, count, 128), v(2, 2 * own, 128), v(2 * own, 128), v(own, 128), v(4, own, 128),
            v(8, count), v(3, 8, count),
        ]
        scratch += [dma((chunks,))] * 8 + [dma((chunks, 2))] * 2 + [dma((chunks,))] * 5 + [dma((3, 2))] + [dma((3,))] * 14
        scratch += [dma((4,))] * 2 + [dma((1,))] * 2 + [dma((3,))] * 2 + [dma((2,))] * 6 + [dma((2, 3))] * 2
        scratch += [dma((2, 2, 3))] * 2 + [pltpu.SemaphoreType.REGULAR] * 2
        shapes = [
            struct((count, share), bf16), struct((count, share)), struct((own, inner)), struct((own, inner)),
            struct((own, 2 * STATE)), struct((heads, own)), struct((own, inner)),
        ]
        *large, smalls = pl.pallas_call(
            layer_kernel,
            in_specs=[SMEM] + [vmem] * 13 + [hbm] * 3,
            out_specs=[vmem, vmem, hbm, hbm, vmem, vmem, hbm, vmem],
            out_shape=shapes + [struct((16, inner))],
            scratch_shapes=scratch,
            compiler_params=pltpu.CompilerParams(collective_id=1, has_side_effects=True, vmem_limit_bytes=VMEM_LIMIT),
            name="layer",
        )(
            seq_lengths, block_input, cotangent, norm_gain, step_weight.T, state_weight, inner_kernel, inner_bias,
            state_kernel_, state_bias, step_bias, decay_log, skip_scale, gate_gain, gate_weight, inner_weight, output_weight,
        )
        cut = [
            struct((share,)), struct((CONV, inner)), struct((inner,)), struct((CONV, 2 * STATE)), struct((2 * STATE,)),
            struct((heads,)), struct((heads,)), struct((heads,)), struct((inner,)),
        ]
        *smalls, out, into, gate_grad, inner_grad, state_grad, step_grad, output_grad = pl.pallas_call(
            outputs_kernel,
            in_specs=[vmem] + [hbm] * 7,
            out_specs=[vmem] * 9 + [hbm] * 7,
            out_shape=cut + shapes,
            scratch_shapes=[pltpu.VMEM(a.shape, a.dtype) for a in shapes] + [dma((7,)), dma((7,))],
            compiler_params=VM,
            name="outputs",
        )(smalls, *large)
        return (
            out, into, smalls[0], gate_grad, inner_grad, step_grad.T, state_grad, *smalls[1:9], output_grad.T,
        )

    padded_step = jnp.pad(step_weight, pad)
    stepb, decay = jnp.pad(row(step_bias), pad), jnp.pad(row(decay_log), pad)
    skipc = jnp.repeat(skip_scale, HEAD_DIM).reshape(1, -1)
    ik, ib, gain = inner_kernel, row(inner_bias), row(gate_gain)
    full = struct((count, inner))
    nb, inv = pl.pallas_call(
        norm_kernel,
        out_shape=(struct((count, width), bf16), struct((count, 128))),
        compiler_params=VM,
        name="norm_in",
    )(block_input, row(norm_gain))

    graw, iraw, cv, mixed, scaled, sums, sraw, sact, state_raw, hc, lsr, addm, g, keep = pl.pallas_call(
        forward_kernel,
        grid=(steps,),
        in_specs=[
            SMEM, whole((count, width)), whole((count, width)), columns(width), columns(width),
            pl.BlockSpec((BLK, width), lambda j: (j, 0)), whole((width, 128)), whole((width, 2 * STATE)),
            columns(CONV), columns(1), whole((CONV, 2 * STATE)), whole((1, 2 * STATE)), whole((1, 128)), whole((1, 128)),
            columns(1), columns(1),
        ],
        out_specs=(
            [columns(count)] * 5
            + [whole((8, count)), whole((count, 128)), whole((count, 2 * STATE)), whole((count, 2 * STATE)),
               whole((steps, count, 128)), whole((128, count)), whole((count, count)), whole((count, count)),
               whole((count, 128))]
        ),
        out_shape=(
            [full] * 5
            + [struct((8, count)), struct((count, 128)), struct((count, 2 * STATE)), struct((count, 2 * STATE)),
               struct((steps, count, 128)), struct((128, count)), struct((count, count)), struct((count, count)),
               struct((count, 128))]
        ),
        scratch_shapes=[pltpu.VMEM((count, 128), f32)],
        compiler_params=VMS,
        cost_estimate=cost(6 * count * width * inner, 6 * width * inner + 20 * count * inner),
        name="forward",
    )(
        seq_lengths, nb, cotangent, gate_weight, inner_weight, output_weight, padded_step, state_weight, ik, ib,
        state_kernel_, row(state_bias), stepb, decay, skipc, gain,
    )

    all_sums = jnp.stack([sums] + [swap(sums, k) for k in range(1, parts)])
    x, dm, gg = pl.pallas_call(
        partial(unit_kernel, float(inner * parts)),
        grid=(steps,),
        in_specs=[whole((parts, 8, count)), columns(count), columns(count), columns(count), columns(1)],
        out_specs=[pl.BlockSpec((2, 1, count, BLK), lambda j: (0, j, 0, 0)), columns(count), columns(8)],
        out_shape=[struct((3, steps, count, BLK)), full, struct((8, inner))],
        compiler_params=VMS,
        cost_estimate=cost(0, 24 * count * inner),
        name="unit",
    )(all_sums, graw, mixed, scaled, gain)

    x, rows, sback, hrows, dstate = pl.pallas_call(
        backward_kernel,
        grid=(steps,),
        in_specs=[
            SMEM, columns(count), columns(count), columns(count), columns(count),
            pl.BlockSpec((1, count, 128), lambda j: (j, 0, 0)), whole((128, count)), whole((count, count)),
            whole((count, count)), whole((count, 128)), whole((count, 2 * STATE)), columns(CONV), columns(1), whole((1, 128)),
            pl.BlockSpec(memory_space=pl.ANY),
        ],
        input_output_aliases={14: 0},
        out_specs=[pl.BlockSpec((1, 1, count, BLK), lambda j: (2, j, 0, 0)), columns(8), whole((count, 128)), whole((8, 128)), whole((parts, count, span))],
        out_shape=[struct((3, steps, count, BLK)), struct((8, inner)), struct((count, 128)), struct((8, 128)), struct((parts, count, span))],
        scratch_shapes=[pltpu.VMEM((count, count), f32), pltpu.VMEM((count, 128), f32), pltpu.VMEM((count, 128), f32)],
        compiler_params=VMS,
        cost_estimate=cost(40 * count * count * inner // 64 * 4, 24 * count * inner),
        name="backward",
    )(seq_lengths, dm, cv, iraw, mixed, hc, lsr, addm, g, sraw, sact, ik, skipc, decay, x)

    uo, gb, back = (jnp.swapaxes(x[i], 0, 1).reshape(count, inner) for i in range(3))

    def to_parts(x, axis):
        size = x.shape[axis] // parts
        block = lambda i: lax.dynamic_slice_in_dim(x, i * size, size, axis)
        got = [swap(block(t ^ k), k) for k in range(1, parts)]
        return [block(t)] + got

    def from_parts(x):
        got = jnp.stack([x] + [swap(x, k) for k in range(1, parts)])
        return jnp.stack([lax.dynamic_index_in_dim(got, t ^ i, 0, False) for i in range(parts)])

    state_parts = jnp.concatenate(to_parts(dstate, 0), axis=0)
    sq, srows = pl.pallas_call(
        state_kernel,
        in_specs=[SMEM] + [pl.BlockSpec(memory_space=pltpu.VMEM)] * 4,
        out_shape=(struct((count, span)), struct((8, span))),
        compiler_params=VM,
        name="state_back",
    )(seq_lengths, state_parts, slab(state_raw, span), slab(state_kernel_, span), row(slab(state_bias, span)))

    hidden = slab(block_input, share).astype(f32)
    cot_share = slab(cotangent, share).astype(f32)
    out_parts = to_parts(mm(uo.astype(bf16), output_weight), 1)
    block_output = (sum(out_parts[1:], out_parts[0]) + hidden).astype(bf16)

    gbb, ibb, sbb, qb = (x.astype(bf16) for x in (gb, back, sback[:, :heads], sq))
    partial_in = (
        mm(gbb, gate_weight, NT) + mm(ibb, inner_weight, NT) + mm(sbb, step_weight, NT)
        + mm(qb, slab(state_weight, span), NT)
    )
    in_parts = to_parts(partial_in, 1)
    d_normed = sum(in_parts[1:], in_parts[0])
    inv_in = inv[:, 0:1]
    normed = hidden * inv_in
    gain_share = row(slab(norm_gain, share))
    d_hat = d_normed * gain_share
    dot = jnp.sum(d_hat * normed, axis=1).reshape(-1, 128)
    dot = sum((swap(dot, k) for k in range(1, parts)), dot).reshape(-1, 1) / width
    input_gradient = inv_in * (d_hat - normed * dot) + cot_share
    norm_gain_grad = jnp.sum(d_normed * normed, axis=0)

    extra = jnp.concatenate([sq, sback[:, :heads], jnp.zeros((count, 128 - span - heads), f32)], axis=1)

    def scatter(a, b):
        return lax.psum_scatter(mm(a, b.astype(bf16), TN), "dp", scatter_dimension=0, tiled=True)

    output_grad = scatter(cotangent, uo).T
    gate_grad, inner_grad, extra_grad = scatter(nb, gb), scatter(nb, back), scatter(nb, extra)

    def over_dp(x):
        return lax.psum(x, "dp")

    step_grad = extra_grad[:, span : span + heads]
    state_grad = jnp.swapaxes(from_parts(extra_grad[:, :span]), 0, 1).reshape(-1, 2 * STATE)
    misc = jnp.concatenate([hrows[0], hrows[1], srows[: CONV + 1].reshape(-1), norm_gain_grad])
    misc = jnp.pad(misc, (0, -misc.shape[0] % 1024)).reshape(8, -1)
    smalls = over_dp(jnp.concatenate([rows, gg], axis=0))
    misc = over_dp(misc).reshape(-1)
    step_bias_grad, decay_grad = misc[:heads], misc[128 : 128 + heads]
    state_rows = from_parts(misc[256 : 256 + (CONV + 1) * span].reshape(CONV + 1, span))
    state_rows = jnp.swapaxes(state_rows, 0, 1).reshape(CONV + 1, 2 * STATE)
    at = 256 + (CONV + 1) * span
    skip_grad = jnp.sum(smalls[CONV + 1].reshape(heads, HEAD_DIM), axis=1)
    return (
        block_output,
        input_gradient,
        misc[at : at + share],
        gate_grad,
        inner_grad,
        step_grad,
        state_grad,
        smalls[:CONV],
        smalls[CONV],
        state_rows[:CONV],
        state_rows[CONV],
        step_bias_grad,
        decay_grad,
        skip_grad,
        smalls[8],
        output_grad,
    )


def solution(mesh):
    return jax.shard_map(
        on_device,
        mesh=mesh,
        in_specs=(
            P("dp", None), P("dp", None), P("dp", None), P(), P(None, "tensor"), P(None, "tensor"), P(None, "tensor"), P(),
            P(None, "tensor"), P("tensor"), P(), P(), P("tensor"), P("tensor"), P("tensor"), P("tensor"), P("tensor", None),
        ),
        out_specs=(
            P("dp", "tensor"), P("dp", "tensor"), P("tensor"), P("dp", "tensor"), P("dp", "tensor"), P("dp", "tensor"),
            P("dp", None), P(None, "tensor"), P("tensor"), P(), P(), P("tensor"), P("tensor"), P("tensor"), P("tensor"),
            P("tensor", "dp"),
        ),
        check_vma=False,
    )
```

```python
from functools import partial

import jax
import jax.numpy as jnp
from jax import lax
from jax.experimental import pallas as pl
from jax.experimental.pallas import tpu as pltpu
from jax.sharding import PartitionSpec as P

HEAD_DIM = 64
STATE = 128
CONV = 4
BLK = 256
HPB = BLK // HEAD_DIM
eps = 1e-05
NEG = -1e30
f32 = jnp.float32
bf16 = jnp.bfloat16
HIGH = lax.Precision.HIGHEST
NN = (((1,), (0,)), ((), ()))
NT = (((1,), (1,)), ((), ()))
TN = (((0,), (0,)), ((), ()))


def mm(a, b, dims=NN, precision=None):
    return lax.dot_general(a, b, dims, precision=precision, preferred_element_type=f32)


def sigmoid(x):
    return 1.0 / (1.0 + jnp.exp(-x))


def softplus(x):
    return jnp.maximum(x, 0.0) + jnp.log1p(jnp.exp(-jnp.abs(x)))


def seg_of(places, lengths):
    total = jnp.zeros(places.shape, jnp.int32)
    end = jnp.int32(0)
    for s in range(lengths.shape[1]):
        end = end + lengths[0, s]
        total = total + (places >= end).astype(jnp.int32)
    return total


def keeps(lengths, count):
    t = lax.broadcasted_iota(jnp.int32, (count, 1), 0)
    own = seg_of(t, lengths)
    out = [None]
    for back in range(1, CONV):
        out.append(((seg_of(t - back, lengths) == own) & (t >= back)).astype(f32))
    return out


def down(x, back):
    return pltpu.roll(x, back, 0)


def up(x, back):
    return pltpu.roll(x, x.shape[0] - back, 0)


def conv(u, kernel, bias, keep):
    out = bias + kernel[CONV - 1 : CONV, :] * u
    for back in range(1, CONV):
        out = out + kernel[CONV - 1 - back : CONV - back, :] * (down(u, back) * keep[back])
    return out


def conv_back(dc, u, kernel, keep):
    du = kernel[CONV - 1 : CONV, :] * dc
    rows = [jnp.sum(dc * u, axis=0, keepdims=True)]
    for back in range(1, CONV):
        kept = dc * keep[back]
        du = du + kernel[CONV - 1 - back : CONV - back, :] * up(kept, back)
        rows.append(jnp.sum(kept * down(u, back), axis=0, keepdims=True))
    return du, rows[::-1] + [jnp.sum(dc, axis=0, keepdims=True)]


def lanes_first(shape):
    return lax.broadcasted_iota(jnp.int32, shape, 1) < HEAD_DIM


def norm_kernel(x_ref, gain_ref, nb_ref, inv_ref):
    x = x_ref[...].astype(f32)
    inv = lax.rsqrt(jnp.sum(x * x, axis=1, keepdims=True) / x.shape[1] + eps)
    nb_ref[...] = (x * inv * gain_ref[...]).astype(bf16)
    inv_ref[...] = jnp.broadcast_to(inv, inv_ref.shape)


def forward_kernel(
    lengths, nb_ref, cot_ref, wg_ref, wi_ref, wo_ref, ws_ref, wst_ref, ik_ref, ib_ref, sk_ref, sb_ref,
    stepb_ref, decay_ref, skipc_ref, gain_ref,
    graw_ref, iraw_ref, cv_ref, mixed_ref, scaled_ref, sums_ref, sraw_ref, sact_ref, state_ref, hc_ref, lsr_ref,
    addm_ref, g_ref, keep_ref, acc,
):
    j = pl.program_id(0)
    count = nb_ref.shape[0]
    nb = nb_ref[...]

    @pl.when(j == 0)
    def _():
        i0 = lax.broadcasted_iota(jnp.int32, (count, count), 0)
        j0 = lax.broadcasted_iota(jnp.int32, (count, count), 1)
        same = (seg_of(i0, lengths) == seg_of(j0, lengths)) & (j0 <= i0)
        addm_ref[...] = jnp.where(same, 0.0, NEG)
        state = mm(nb, wst_ref[...])
        state_ref[...] = state
        keep = keeps(lengths, count)
        for back in range(1, CONV):
            keep_ref[:, back : back + 1] = keep[back]
        cv = conv(state, sk_ref[...], sb_ref[...], keep)
        act = cv * sigmoid(cv)
        sact_ref[...] = act
        g_ref[...] = mm(act[:, STATE:], act[:, :STATE], NT, HIGH)
        raw = mm(nb, ws_ref[...]) + stepb_ref[...]
        sraw_ref[...] = raw
        step = softplus(raw)
        logs = mm(same.astype(f32), step * (-jnp.exp(decay_ref[...])), NN, HIGH)
        lsr_ref[...] = jnp.transpose(logs)
        for k in range(hc_ref.shape[0]):
            hc_ref[k, :, 0:HPB] = logs[:, HPB * k : HPB * (k + 1)]
            hc_ref[k, :, HPB : 2 * HPB] = step[:, HPB * k : HPB * (k + 1)]
        acc[...] = jnp.zeros_like(acc)

    gate = mm(nb, wg_ref[...])
    inner = mm(nb, wi_ref[...])
    scaled = mm(cot_ref[...], wo_ref[...], NT)
    graw_ref[...] = gate
    iraw_ref[...] = inner
    scaled_ref[...] = scaled
    cv = conv(inner, ik_ref[...], ib_ref[...], keeps(lengths, count))
    cv_ref[...] = cv
    v = cv * sigmoid(cv)
    first = lanes_first((count, 2 * HEAD_DIM))
    addm = addm_ref[...]
    g = g_ref[...]
    parts = []
    for pair in range(BLK // (2 * HEAD_DIM)):
        vp = v[:, 2 * HEAD_DIM * pair : 2 * HEAD_DIM * (pair + 1)]
        k = 2 * pair
        steps = jnp.where(first, hc_ref[j, :, HPB + k : HPB + k + 1], hc_ref[j, :, HPB + k + 1 : HPB + k + 2])
        vs = (vp * steps).astype(bf16)
        ys = []
        for h in (k, k + 1):
            gaps = hc_ref[j, :, h : h + 1] - lsr_ref[pl.ds(HPB * j + h, 1), :] + addm
            ys.append(mm((g * jnp.exp(gaps)).astype(bf16), vs))
        parts.append(jnp.where(first, ys[0], ys[1]))
    mixed = jnp.concatenate(parts, axis=1) + skipc_ref[...] * v
    mixed_ref[...] = mixed
    gated = mixed * (gate * sigmoid(gate))
    acc[:, 0:1] += jnp.sum(gated * gated, axis=1, keepdims=True)
    acc[:, 1:2] += jnp.sum(scaled * gain_ref[...] * gated, axis=1, keepdims=True)

    @pl.when(j == pl.num_programs(0) - 1)
    def _():
        sums_ref[...] = jnp.transpose(acc[...])[0:8, :]


def unit_kernel(width, s_ref, graw_ref, mixed_ref, scaled_ref, gain_ref, x_ref, dm_ref, gg_ref):
    sums = jnp.sum(s_ref[...], axis=0)
    cols = jnp.transpose(sums)
    inv = lax.rsqrt(cols[:, 0:1] / width + eps)
    dot = inv * cols[:, 1:2]
    gate, mixed, scaled, gain = graw_ref[...], mixed_ref[...], scaled_ref[...], gain_ref[...]
    s = sigmoid(gate)
    act = gate * s
    unit = mixed * act * inv
    x_ref[0, 0] = (unit * gain).astype(bf16).astype(f32)
    gg_ref[...] = jnp.broadcast_to(jnp.sum(scaled * unit, axis=0, keepdims=True), gg_ref.shape)
    d_gated = inv * (scaled * gain - unit * (dot / width))
    dm_ref[...] = d_gated * act
    x_ref[1, 0] = (d_gated * mixed * s * (1.0 + gate * (1.0 - s))).astype(bf16).astype(f32)


def backward_kernel(
    lengths, dm_ref, cv_ref, iraw_ref, mixed_ref, hc_ref, lsr_ref, addm_ref, g_ref, sraw_ref, sact_ref,
    ik_ref, skipc_ref, decay_ref, _,
    back_ref, rows_ref, sback_ref, hrows_ref, dstate_ref, dg, dlogs, dstep,
):
    j = pl.program_id(0)
    count = dm_ref.shape[0]

    @pl.when(j == 0)
    def _():
        dg[...] = jnp.zeros_like(dg)
        dlogs[...] = jnp.zeros_like(dlogs)
        dstep[...] = jnp.zeros_like(dstep)

    cv, dm, skipc = cv_ref[...], dm_ref[...], skipc_ref[...]
    s = sigmoid(cv)
    v = cv * s
    within = mixed_ref[...] - skipc * v
    first = lanes_first((count, 2 * HEAD_DIM))
    addm = addm_ref[...]
    g = g_ref[...]
    us, vss, dyb, stepm = [], [], [], []
    total = dg[...]
    for pair in range(BLK // (2 * HEAD_DIM)):
        cols = slice(2 * HEAD_DIM * pair, 2 * HEAD_DIM * (pair + 1))
        k = 2 * pair
        steps = jnp.where(first, hc_ref[0, :, HPB + k : HPB + k + 1], hc_ref[0, :, HPB + k + 1 : HPB + k + 2])
        vs = (v[:, cols] * steps).astype(bf16)
        dy = dm[:, cols].astype(bf16)
        both = []
        for h in (k, k + 1):
            gaps = hc_ref[0, :, h : h + 1] - lsr_ref[pl.ds(HPB * j + h, 1), :] + addm
            decay = jnp.exp(gaps)
            both.append(mm((g * decay).astype(bf16), dy, TN))
            mine = first if h == k else jnp.logical_not(first)
            total = total + decay * mm(jnp.where(mine, dy, jnp.zeros_like(dy)), vs, NT)
        us.append(jnp.where(first, both[0], both[1]))
        vss.append(vs.astype(f32))
        dyb.append(dy.astype(f32))
        stepm.append(steps)
    dg[...] = total
    u = jnp.concatenate(us, axis=1)
    vs = jnp.concatenate(vss, axis=1)
    dy = jnp.concatenate(dyb, axis=1)
    steps = jnp.concatenate(stepm, axis=1)
    c0 = lax.broadcasted_iota(jnp.int32, (BLK, 128), 0) // HEAD_DIM
    l0 = lax.broadcasted_iota(jnp.int32, (BLK, 128), 1)
    pick = (l0 == c0 + HPB * j).astype(f32)
    dlogs[...] += mm(dy * within - vs * u, pick, NN, HIGH)
    dstep[...] += mm(v * u, pick, NN, HIGH)
    dv = steps * u + skipc * dm
    dc = dv * (s * (1.0 + cv * (1.0 - s)))
    du, rows = conv_back(dc, iraw_ref[...], ik_ref[...], keeps(lengths, count))
    back_ref[0, 0] = du.astype(bf16).astype(f32)
    rows_ref[...] = jnp.concatenate(rows + [jnp.sum(dm * v, axis=0, keepdims=True)] + [jnp.zeros((2, BLK), f32)], axis=0)

    @pl.when(j == pl.num_programs(0) - 1)
    def _():
        mask = (addm > -1.0).astype(f32)
        q = mm(mask, dlogs[...], TN, HIGH)
        raw = sraw_ref[...]
        step = softplus(raw)
        rate = -jnp.exp(decay_ref[...])
        draw = (dstep[...] + rate * q) * sigmoid(raw)
        sback_ref[...] = draw.astype(bf16).astype(f32)
        hrows_ref[...] = jnp.concatenate(
            [jnp.sum(draw, axis=0, keepdims=True), rate * jnp.sum(step * q, axis=0, keepdims=True), jnp.zeros((6, 128), f32)],
            axis=0,
        )
        act = sact_ref[...]
        d_b = mm(dg[...], act[:, STATE:], TN, HIGH)
        d_c = mm(dg[...], act[:, :STATE], NN, HIGH)
        both = jnp.concatenate([d_b, d_c], axis=1)
        span = dstate_ref.shape[2]
        for t in range(dstate_ref.shape[0]):
            dstate_ref[t] = both[:, span * t : span * (t + 1)]


def state_kernel(lengths, parts_ref, u_ref, sk_ref, sb_ref, back_ref, rows_ref):
    keep = keeps(lengths, u_ref.shape[0])
    cv = conv(u_ref[...], sk_ref[...], sb_ref[...], keep)
    s = sigmoid(cv)
    dc = jnp.sum(parts_ref[...], axis=0) * (s * (1.0 + cv * (1.0 - s)))
    du, rows = conv_back(dc, u_ref[...], sk_ref[...], keep)
    back_ref[...] = du.astype(bf16).astype(f32)
    rows_ref[...] = jnp.concatenate(rows + [jnp.zeros((3, du.shape[1]), f32)], axis=0)


MESH = pl.DeviceIdType.MESH
RING = 6
VMEM_LIMIT = 64 << 20
LEAD = 4
LEAD2 = 1


def layer_kernel(
    lengths, xin, cot, gain_in1, ws, wst, ik, ib1, sk, sb1, stepb1, decay1, skip1, gain1, wg_hbm, wi_hbm, wo_hbm,
    out_ref, din_ref, gate_out, inner_out, state_out, step_out, turned_out, smalls_ref,
    x, act, dmb, nb, inv, gain_in, ib, sb, heads_in, skipc, gain, fs, f1, f2, f3, fx, fc, ft, big, yra, yrb, r, ea, fin, xb, xbr, wring, woring, po, por, pir, addm, g, hc, lsr, sact, state_raw, sraw, keep_ref, dg, dlogs, dstep, hsum, acc, sums, sumr, dstate, dsr, srr, sm, smr,
    ex, exr, rx, exe, yrx, exg, dots, dotr,
    p1s, p1v, p2s, p2v, p3s, p3v, es, ev, yas, yav, ybs, ybv, fas, fav, fins, wsem, pos, pov, pis, piv,
    dss, dsv, srs, srv, dts, dtv, sus, suv, sms, smv, exs, exv, yxs, yxv, exgs, exgv,
    f1s, f1v, f2s, f2v, f3s, f3v, fxs, fxv, fcs, fcv, credit, fc_free,
):
    d, t = lax.axis_index("dp"), lax.axis_index("tensor")
    y, z = d % 2, d // 2
    side, half = z % 2, z // 2
    hub = (z == 1) | (z == 2)
    edge = jnp.logical_not(hub)
    chunks, count, wide = x.shape
    each = chunks // 3
    lanes = wide // 2
    width = xin.shape[1]
    part = width // 4
    own = part // 2
    share = width // 4
    span = dsr.shape[2]
    inner = each * wide
    piece = f1.shape[1]
    pair, peer, line = d ^ 2, d ^ 6, d ^ 1
    mine, other = pl.multiple_of(own * y, own), pl.multiple_of(own * (1 - y), own)
    mine_part, pair_part = pl.multiple_of(part * side, part), pl.multiple_of(part * (1 - side), part)
    near, far = pl.multiple_of(half * 2 * part, 2 * part), pl.multiple_of((1 - half) * 2 * part, 2 * part)
    my_rows = pl.multiple_of(t * piece, piece)
    my_share = pl.multiple_of(t * share, share)

    def send(src, dst, ssem, rsem, dev):
        return pltpu.make_async_remote_copy(
            src_ref=src, dst_ref=dst, send_sem=ssem, recv_sem=rsem, device_id=dev, device_id_type=MESH
        )

    def p1(q):
        return send(x.at[q], big.at[q % RING, pl.ds(0, count)], p1s.at[q], p1v.at[q], (pair, t))

    def p2(q):
        return send(x.at[q], big.at[q % RING, pl.ds(count, count)], p2s.at[q], p2v.at[q], (peer, t))

    def p3(q):
        slot = q % RING
        return send(
            big.at[slot, pl.ds(0, count)], big.at[slot, pl.ds(2 * count, count)], p3s.at[q], p3v.at[q], (peer, t)
        )

    def e(q):
        return send(
            r.at[q % 2, 0, :, pl.ds(lanes, lanes)], big.at[q % RING, pl.ds(0, part), pl.ds(0, lanes)], es.at[q], ev.at[q],
            (pair, t),
        )

    def ya(q, k):
        return send(
            r.at[q % 2, k, pl.ds(other, own), pl.ds(0, lanes)], yra.at[q % RING, k], yas.at[q, k], yav.at[q, k], (line, t)
        )

    def yb_hub(q):
        return send(
            r.at[q % 2, 1, pl.ds(other, own), pl.ds(lanes, lanes)], yrb.at[q % LEAD], ybs.at[q], ybv.at[q], (line, t)
        )

    def yb_edge(q):
        return send(
            big.at[q % RING, pl.ds(other, own), pl.ds(0, lanes)], yrb.at[q % LEAD], ybs.at[q], ybv.at[q], (line, t)
        )

    def fa(q):
        return send(ea.at[q % 2], yra.at[q % RING, 0], fas.at[q], fav.at[q], (pair, t))

    def feature1(f, k):
        half_row = f1.at[f, :, pl.ds((near, far)[k], 2 * part)]
        return send(half_row, half_row, f1s.at[f, k], f1v.at[f, k], (pair, t))

    def feature2(f):
        return send(fs.at[f], f2.at[f], f2s.at[f], f2v.at[f], (peer, t))

    def feature3(f):
        return send(f1.at[f, :, pl.ds(far, 2 * part)], f3.at[f], f3s.at[f], f3v.at[f], (peer, t))

    def feature(f, shard):
        return (f1.at[f, :, pl.ds(near, 2 * part)], f2.at[f], f3.at[f])[shard]

    def across(f, shard):
        return send(feature(f, shard), fx.at[f, shard], fxs.at[f, shard], fxv.at[f, shard], (d, t ^ 2))

    def sibling(f, shard, k):
        src = fx.at[f, shard] if k else feature(f, shard)
        return send(src, fc.at[k, shard], fcs.at[k, f, shard], fcv.at[k, f, shard], (d, t ^ 1))

    def spread(f, shard):
        across(f, shard).start()
        if f:
            sibling(f, shard, 0).start()

    p1x = lambda: send(ex, exr.at[0], exs.at[0], exv.at[0], (pair, t))
    p2x = lambda: send(ex, exr.at[1], exs.at[1], exv.at[1], (peer, t))
    p3x = lambda: send(exr.at[0], exr.at[2], exs.at[2], exv.at[2], (peer, t))
    e_x = lambda: send(rx.at[0], exe, exs.at[3], exv.at[3], (pair, t))
    yx_hub = lambda: send(rx.at[1, pl.ds(other, own)], yrx, yxs.at[0], yxv.at[0], (line, t))
    yx_edge = lambda: send(exe.at[pl.ds(other, own)], yrx, yxs.at[0], yxv.at[0], (line, t))

    def over_tensor(src, dst, ssem, rsem):
        return lambda k: send(src(k), dst(k), ssem.at[k - 1], rsem.at[k - 1], (d, t ^ k))

    sum_copy = over_tensor(lambda k: sums, lambda k: sumr.at[k - 1], sus, suv)
    state_copy = over_tensor(lambda k: dstate.at[t ^ k], lambda k: dsr.at[k - 1], dss, dsv)
    row_copy = over_tensor(lambda k: srr.at[t], lambda k: srr.at[t], srs, srv)
    out_near = lambda n: send(po.at[t ^ (1 + 2 * n)], por.at[n], pos.at[n], pov.at[n], (d, t ^ 1))
    out_far = lambda: send(po.at[t ^ 2], por.at[2], pos.at[2], pov.at[2], (d, t ^ 2))
    tiles = share // lanes
    block = lambda i: act.at[pl.ds(tiles * i, tiles)]
    in_near = lambda n: send(block(t ^ (1 + 2 * n)), pir.at[n], pis.at[n], piv.at[n], (d, t ^ 1))
    in_far = lambda: send(block(t ^ 2), pir.at[2], pis.at[2], piv.at[2], (d, t ^ 2))
    dot_copy = over_tensor(lambda k: dots, lambda k: dotr.at[k - 1], dts, dtv)
    extra_copy = over_tensor(lambda k: exg.at[t], lambda k: exg.at[t], exgs, exgv)
    small_copy = lambda k: send(sm, smr.at[k], sms.at[k], smv.at[k], (d ^ (1 << k), t))

    def started(copy):
        for k in range(1, 4):
            copy(k).start()

    def waited(copy):
        for k in range(1, 4):
            copy(k).wait()

    def load(n, kind):
        at = pl.multiple_of((n % each) * wide, wide)
        if kind == 2:
            return pltpu.make_async_copy(wo_hbm.at[pl.ds(at, wide), :], woring.at[n % 2], wsem.at[kind, n % 2])
        ref = (wg_hbm, wi_hbm)[kind]
        return pltpu.make_async_copy(ref.at[:, pl.ds(at, wide)], wring.at[n % 2, kind], wsem.at[kind, n % 2])

    for n in range(2):
        for kind in range(3):
            load(n, kind).start()

    barrier = pltpu.get_barrier_semaphore()
    for dev in ((pair, t), (peer, t), (line, t), (d ^ 4, t), (d, t ^ 1), (d, t ^ 2), (d, t ^ 3)):
        pl.semaphore_signal(barrier, inc=1, device_id=dev, device_id_type=MESH)
    pl.semaphore_wait(barrier, 7)

    heads = ws.shape[0]
    gain_in[...] = gain_in1[...].reshape(1, width)
    ib[...] = ib1[...].reshape(1, inner)
    gain[...] = gain1[...].reshape(1, inner)
    sb[...] = sb1[...].reshape(1, 4 * span)
    heads_in[...] = jnp.zeros_like(heads_in)
    for n, ref in enumerate((stepb1, decay1, skip1)):
        heads_in[8 * n : 8 * n + 8, 0:heads] = jnp.broadcast_to(ref[...].reshape(1, heads), (8, heads))
    h0 = lax.broadcasted_iota(jnp.int32, (128, inner), 0)
    spread_heads = (h0 == lax.broadcasted_iota(jnp.int32, (128, inner), 1) // HEAD_DIM).astype(f32)
    skipc[...] = mm(heads_in[16:24, :], spread_heads, NN, HIGH)[0:1, :]
    rate_row = -jnp.exp(heads_in[8:9, :])

    def begin_features(f):
        ref = cot if f else nb

        @pl.when(edge)
        def _():
            f1[f] = ref[pl.ds(my_rows, piece), :].astype(f32)
            if f:
                feature1(f, 1).start()

        @pl.when(hub)
        def _():
            fs[f] = ref[pl.ds(my_rows, piece), pl.ds(far, 2 * part)].astype(f32)
            if f:
                feature2(f).start()

    begin_features(1)
    xv = xin[...].astype(f32)
    scale = lax.rsqrt(jnp.sum(xv * xv, axis=1, keepdims=True) / width + eps)
    nb[...] = (xv * scale * gain_in[...]).astype(bf16)
    inv[...] = jnp.broadcast_to(scale, inv.shape)
    begin_features(0)

    i0 = lax.broadcasted_iota(jnp.int32, (count, count), 0)
    j0 = lax.broadcasted_iota(jnp.int32, (count, count), 1)
    same = (seg_of(i0, lengths) == seg_of(j0, lengths)) & (j0 <= i0)
    addm[...] = jnp.where(same, 0.0, NEG)
    keep = keeps(lengths, count)
    for back in range(1, CONV):
        keep_ref[:, back : back + 1] = keep[back]
    state = mm(nb[...], wst[...])
    state_raw[...] = state
    cv = conv(state, sk[...], sb[...], keep)
    sact[...] = cv * sigmoid(cv)
    g[...] = mm(sact[:, STATE:], sact[:, :STATE], NT, HIGH)
    sraw[...] = jnp.zeros_like(sraw)
    sraw[:, 0:heads] = mm(nb[...], ws[...], NT) + heads_in[0:1, 0:heads]
    step = softplus(sraw[...])
    logs = mm(same.astype(f32), step * rate_row, NN, HIGH)
    lsr[...] = jnp.transpose(logs)
    for k in range(each):
        hc[k, :, 0:HPB] = logs[:, HPB * k : HPB * (k + 1)]
        hc[k, :, HPB : 2 * HPB] = step[:, HPB * k : HPB * (k + 1)]
    for ref in (acc, dg, dlogs, dstep, hsum, sm):
        ref[...] = jnp.zeros_like(ref)

    first = lanes_first((count, 2 * HEAD_DIM))

    def kept():
        return [None] + [keep_ref[:, b : b + 1] for b in range(1, CONV)]

    def steps_of(j, k):
        return jnp.where(first, hc[j, :, HPB + k : HPB + k + 1], hc[j, :, HPB + k + 1 : HPB + k + 2])

    def decay_of(j, h):
        return jnp.exp(hc[j, :, h : h + 1] - lsr[pl.ds(HPB * j + h, 1), :] + addm[...])

    def put(base, j, value):
        for half_block in range(2):
            act[base + 2 * j + half_block] = value[:, lanes * half_block : lanes * (half_block + 1)]

    def take(base, j):
        return jnp.concatenate([act[base + 2 * j], act[base + 2 * j + 1]], axis=1)

    def forward_block(j, carry):
        slot = j % 2
        cols = pl.ds(pl.multiple_of(j * wide, wide), wide)
        for kind in range(3):
            load(j, kind).wait()
        gate = mm(nb[...], wring[slot, 0])
        raw = mm(nb[...], wring[slot, 1])
        scaled = mm(cot[...], woring[slot], NT)
        for kind in range(3):
            load(j + 2, kind).start()
        x[j] = scaled
        x[each + j] = gate
        x[2 * each + j] = raw
        cv = conv(raw, ik[:, cols], ib[:, cols], kept())
        put(2 * each, j, cv)
        v = cv * sigmoid(cv)
        parts = []
        for k in range(0, HPB, 2):
            vs = (v[:, HEAD_DIM * k : HEAD_DIM * (k + 2)] * steps_of(j, k)).astype(bf16)
            ys = [mm((g[...] * decay_of(j, h)).astype(bf16), vs) for h in (k, k + 1)]
            parts.append(jnp.where(first, ys[0], ys[1]))
        mixed = jnp.concatenate(parts, axis=1) + skipc[:, cols] * v
        put(0, j, mixed)
        gated = mixed * (gate * sigmoid(gate))
        acc[:, 0:1] += jnp.sum(gated * gated, axis=1, keepdims=True)
        acc[:, 1:2] += jnp.sum(scaled * gain[:, cols] * gated, axis=1, keepdims=True)

        @pl.when(edge & (j == 2))
        def _():
            feature1(1, 1).wait_send()
            feature1(1, 0).start()

        @pl.when(hub & (j == 2))
        def _():
            feature1(1, 1).wait_recv()
            feature3(1).start()
            feature2(1).wait_recv()
            spread(1, 1)

        @pl.when(hub & (j == 3))
        def _():
            feature2(0).start()

        return carry

    lax.fori_loop(0, each, forward_block, 0)
    sums[...] = jnp.transpose(acc[...])[0:8, :]
    started(sum_copy)

    @pl.when(hub)
    def _():
        feature1(1, 0).wait_recv()
        spread(1, 0)

    waited(sum_copy)
    total = jnp.transpose(sums[...] + sumr[0] + sumr[1] + sumr[2])
    acc[:, 0:1] = lax.rsqrt(total[:, 0:1] / (4 * inner) + eps)
    acc[:, 1:2] = acc[:, 0:1] * total[:, 1:2] / (4 * inner)

    def unit_block(j, carry):
        cols = pl.ds(pl.multiple_of(j * wide, wide), wide)
        scaled, gate, mixed = x[j], x[each + j], take(0, j)
        inv_gate, dot = acc[:, 0:1], acc[:, 1:2]
        s = sigmoid(gate)
        gate_act = gate * s
        unit = mixed * gate_act * inv_gate
        weights = gain[:, cols]
        x[j] = (unit * weights).astype(bf16).astype(f32)
        sm[8:9, cols] = jnp.sum(scaled * unit, axis=0, keepdims=True)
        d_gated = inv_gate * (scaled * weights - unit * dot)
        dmb[j] = d_gated * gate_act
        x[each + j] = (d_gated * mixed * s * (1.0 + gate * (1.0 - s))).astype(bf16).astype(f32)

        @pl.when(hub & (j < LEAD2))
        def _():
            p2(j).start()

        @pl.when(edge & (j < 2))
        def _():
            p1(j).start()

        return carry

    lax.fori_loop(0, each, unit_block, 0)

    @pl.when(hub)
    def _():
        feature3(1).wait_recv()
        spread(1, 2)

    @pl.when(edge)
    def _():
        for n in range(2, LEAD):
            p1(n - 2).wait_send()
            p1(n).start()
        feature1(0, 1).start()
        feature1(0, 0).start()

    def forward_features(f):
        if not f:
            pl.semaphore_wait(fc_free, 1)
        for shard in (1, 0, 2):
            if not f:
                sibling(f, shard, 0).start()
            across(f, shard).wait_recv()
            sibling(f, shard, 1).start()

    def assemble(f):
        own_rows = (cot if f else nb)[:, pl.ds(near, 2 * part)]
        ft[f, :, 0:count] = own_rows.T
        for shard in (1, 0, 2):
            sibling(f, shard, 0).wait_recv()
            sibling(f, shard, 1).wait_recv()
            for k, ref in enumerate((feature(f, shard), fc.at[0, shard], fx.at[f, shard], fc.at[1, shard])):
                xbr[pl.ds(pl.multiple_of((t ^ k) * piece, piece), piece), :] = ref[...].astype(bf16)
            ft[f, :, count * (shard + 1) : count * (shard + 2)] = xbr[...].T
        if f:
            pl.semaphore_signal(fc_free, inc=1, device_id=(d, t ^ 1), device_id_type=MESH)

    def backward_block(j, carry):
        cols = pl.ds(pl.multiple_of(j * wide, wide), wide)
        cv, dm = take(2 * each, j), dmb[j]
        s = sigmoid(cv)
        v = cv * s
        within = take(0, j) - skipc[:, cols] * v
        us, vss, dys, stepm = [], [], [], []
        for k in range(0, HPB, 2):
            lane = slice(HEAD_DIM * k, HEAD_DIM * (k + 2))
            steps = steps_of(j, k)
            vs = (v[:, lane] * steps).astype(bf16)
            dy = dm[:, lane].astype(bf16)
            both = []
            for h in (k, k + 1):
                ratio = decay_of(j, h)
                both.append(mm((g[...] * ratio).astype(bf16), dy, TN))
                part_of = first if h == k else jnp.logical_not(first)
                dg[...] += ratio * mm(jnp.where(part_of, dy, jnp.zeros_like(dy)), vs, NT)
            us.append(jnp.where(first, both[0], both[1]))
            vss.append(vs.astype(f32))
            dys.append(dy.astype(f32))
            stepm.append(steps)
        u, vs, dy, steps = (jnp.concatenate(p, axis=1) for p in (us, vss, dys, stepm))
        c0 = lax.broadcasted_iota(jnp.int32, (wide, 128), 0) // HEAD_DIM
        l0 = lax.broadcasted_iota(jnp.int32, (wide, 128), 1)
        pick = (l0 == c0 + HPB * j).astype(f32)
        dlogs[...] += mm(dy * within - vs * u, pick, NN, HIGH)
        dstep[...] += mm(v * u, pick, NN, HIGH)
        per_lane = jnp.sum(dm * v, axis=0, keepdims=True)
        hsum[...] += mm(jnp.broadcast_to(per_lane, (8, wide)), pick, NN, HIGH)
        dc = (steps * u + skipc[:, cols] * dm) * (s * (1.0 + cv * (1.0 - s)))
        du, rows = conv_back(dc, x[2 * each + j], ik[:, cols], kept())
        x[2 * each + j] = du.astype(bf16).astype(f32)
        sm[0:5, cols] = jnp.concatenate(rows, axis=0)
        return carry

    def backward_end():
        mask = (addm[...] > -1.0).astype(f32)
        q = mm(mask, dlogs[...], TN, HIGH)
        raw = sraw[...]
        step = softplus(raw)
        rate = -jnp.exp(heads_in[8:9, :])
        draw = (dstep[...] + rate * q) * sigmoid(raw)
        dstep[...] = draw.astype(bf16).astype(f32)
        sm[15:16, 0:128] = jnp.sum(draw, axis=0, keepdims=True)
        sm[15:16, 128:256] = rate * jnp.sum(step * q, axis=0, keepdims=True)
        sm[15:16, 256:384] = hsum[0:1, :]
        d_b = mm(dg[...], sact[:, STATE:], TN, HIGH)
        d_c = mm(dg[...], sact[:, :STATE], NN, HIGH)
        both = jnp.concatenate([d_b, d_c], axis=1)
        for i in range(4):
            dstate[i] = both[:, span * i : span * (i + 1)]
        started(state_copy)

    def slab(ref):
        out = None
        for i in range(4):
            one = jnp.where(t == i, ref[:, span * i : span * (i + 1)], 0.0)
            out = one if out is None else out + one
        return out

    def states():
        waited(state_copy)
        total = dstate[t] + dsr[0] + dsr[1] + dsr[2]
        u, kernel = slab(state_raw), slab(sk)
        cv = conv(u, kernel, slab(sb), kept())
        s = sigmoid(cv)
        du, rows = conv_back(total * (s * (1.0 + cv * (1.0 - s))), u, kernel, kept())
        ex[:, 0:span] = du.astype(bf16).astype(f32)
        ex[:, span : 2 * span] = dstep[:, 0:span]
        srr[t] = jnp.concatenate(rows + [jnp.zeros((3, span), f32)], axis=0)
        started(row_copy)

        @pl.when(hub)
        def _():
            p2x().start()

        @pl.when(edge)
        def _():
            p1x().start()

    def out_parts():
        for c in range(each):
            n = each + c
            load(n, 2).wait()
            xc = x[c].astype(bf16)
            for i in range(4):
                one = mm(xc, woring[n % 2, :, share * i : share * (i + 1)])
                po[i] = one if c == 0 else po[i] + one
            if c + 2 < each:
                load(n + 2, 2).start()
        for n in range(2):
            out_near(n).start()

    def out_across():
        for n in range(2):
            out_near(n).wait()
        po[t ^ 2] = po[t ^ 2] + por[1]
        out_far().start()

    def out_sum():
        out_far().wait()
        hidden = xin[:, pl.ds(my_share, share)].astype(f32)
        out_ref[...] = (po[t] + por[0] + por[2] + hidden).astype(bf16)

    def in_parts():
        lane = lax.broadcasted_iota(jnp.int32, (count, 4 * span), 1) // span
        own_state = ex[:, 0:span]
        states4 = jnp.where(lane == t, jnp.concatenate([own_state] * 4, axis=1), 0.0).astype(bf16)
        steps_back = dstep[:, 0:heads].astype(bf16)
        for i in range(4 * tiles):
            rows = slice(lanes * i, lanes * (i + 1))
            act[i] = mm(states4, wst[rows, :], NT) + mm(steps_back, ws[:, rows])
        for c in range(each):
            n = each + c
            load(n, 0).wait()
            load(n, 1).wait()
            gc, ic = x[each + c].astype(bf16), x[2 * each + c].astype(bf16)
            for i in range(2 * tiles):
                rows = slice(2 * lanes * i, 2 * lanes * (i + 1))
                one = mm(gc, wring[n % 2, 0, rows, :], NT) + mm(ic, wring[n % 2, 1, rows, :], NT)
                act[2 * i] = act[2 * i] + one[:, 0:lanes]
                act[2 * i + 1] = act[2 * i + 1] + one[:, lanes:]
            if c + 2 < each:
                load(n + 2, 0).start()
                load(n + 2, 1).start()
        for n in range(2):
            in_near(n).start()

    def in_across():
        for n in range(2):
            in_near(n).wait()
        for i in range(tiles):
            act[tiles * (t ^ 2) + i] = act[tiles * (t ^ 2) + i] + pir[1, i]
        in_far().start()

    def normed():
        return xin[:, pl.ds(my_share, share)].astype(f32) * inv[:, 0:1]

    def in_sum():
        in_far().wait()
        for i in range(tiles):
            po[0, :, lanes * i : lanes * (i + 1)] = act[tiles * t + i] + pir[0, i] + pir[2, i]
        d_normed = po[0]
        dot = jnp.sum(d_normed * gain_in[:, pl.ds(my_share, share)] * normed(), axis=1, keepdims=True)
        dots[...] = jnp.transpose(jnp.broadcast_to(dot, (count, 128)))[0:8, :]
        started(dot_copy)

    def finish():
        waited(dot_copy)
        waited(row_copy)
        d_normed, n = po[0], normed()
        dot = jnp.transpose(dots[...] + dotr[0] + dotr[1] + dotr[2])[:, 0:1] / width
        d_hat = d_normed * gain_in[:, pl.ds(my_share, share)]
        din_ref[...] = inv[:, 0:1] * (d_hat - n * dot) + cot[:, pl.ds(my_share, share)].astype(f32)
        sm[9:10, 0:share] = jnp.sum(d_normed * n, axis=0, keepdims=True)
        for i in range(4):
            sm[10:15, span * i : span * (i + 1)] = srr[i][0:5, :]
        small_copy(0).start()

    def small(k):
        small_copy(k).wait()
        sm[...] = sm[...] + smr[k]
        if k < 2:
            small_copy(k + 1).start()
        else:
            smalls_ref[...] = sm[...]

    def extra_hub():
        p2x().wait_recv()
        p3x().wait_recv()
        for k, ref in enumerate((ex, exr.at[0], exr.at[1], exr.at[2])):
            xb[k * count : (k + 1) * count, 0:128] = ref[...].astype(bf16)
        rx[0] = mm(ft[0, pl.ds(pair_part, part), :], xb[:, 0:128])
        rx[1] = mm(ft[0, pl.ds(mine_part, part), :], xb[:, 0:128])
        e_x().start()
        yx_hub().start()

    def extra_spread(rows):
        exg[t] = rows + yrx[...]
        step_out[...] = jnp.transpose(exg[t])[span : span + heads, :]
        started(extra_copy)

    def extra_end():
        waited(extra_copy)
        for i in range(4):
            state_out[:, span * i : span * (i + 1)] = exg[i, :, 0:span]

    def process(q):
        p2(q).wait_recv()
        p3(q).wait_recv()
        p3(q).wait_send()

        @pl.when(q >= 2)
        def _():
            e(q - 2).wait_send()
            ya(q - 2, 0).wait_send()
            ya(q - 2, 1).wait_send()
            yb_hub(q - 2).wait_send()

        xb[0:count, :] = x[q].astype(bf16)
        xb[count:, :] = big[q % RING].astype(bf16)

        @pl.when(q + RING < chunks)
        def _():
            pl.semaphore_signal(credit, inc=1, device_id=(peer, t), device_id_type=MESH)

        family = jnp.where(q < each, 1, 0)
        slot = q % 2
        r[slot, 0] = mm(ft[family, pl.ds(pair_part, part), :], xb[...])
        e(q).start()
        ya(q, 0).start()
        r[slot, 1] = mm(ft[family, pl.ds(mine_part, part), :], xb[...])
        ya(q, 1).start()
        yb_hub(q).start()

    def stored(q, k):
        at = pl.multiple_of((q % each) * wide, wide)
        out = (turned_out, gate_out, inner_out)[k]
        return pltpu.make_async_copy(fin.at[q % 2], out.at[:, pl.ds(at, wide)], fins.at[q])

    def store(q, left, right):
        slot = q % 2
        for k in range(3):
            @pl.when((q >= k * each + 2) & (q < (k + 1) * each + 2))
            def _():
                stored(q - 2, k).wait()

        fin[slot, :, 0:lanes] = left
        fin[slot, :, lanes:] = right

        for k in range(3):
            @pl.when((q >= k * each) & (q < (k + 1) * each))
            def _():
                stored(q, k).start()

    def finalize_hub(q):
        slot = q % 2
        ya(q, 0).wait_recv()
        ya(q, 1).wait_recv()
        yb_hub(q).wait_recv()

        @pl.when(q >= 2)
        def _():
            fa(q - 2).wait_send()

        got = yra.at[q % RING]
        ea[slot] = r[slot, 0, pl.ds(mine, own), 0:lanes] + got[0]
        fa(q).start()
        store(
            q,
            r[slot, 1, pl.ds(mine, own), 0:lanes] + got[1],
            r[slot, 1, pl.ds(mine, own), lanes:] + yrb[q % LEAD],
        )

    def finalize_edge(q):
        yb_edge(q).wait_recv()
        fa(q).wait_recv()
        store(q, yra[q % RING, 0], big[q % RING, pl.ds(mine, own), 0:lanes] + yrb[q % LEAD])

    pieces = {
        2: backward_end, 3: [out_parts, states], 4: out_across, 5: in_parts, 6: out_sum, 7: in_across, 8: in_sum,
        9: finish, 10: lambda: small(0), 12: lambda: small(1), 15: lambda: small(2), 14: extra_end,
    }

    def body(q, carry):
        @pl.when(hub)
        def _():
            @pl.when(q < chunks)
            def _():
                p1(q).wait_recv()
                p3(q).start()

            @pl.when(q + LEAD2 < chunks)
            def _():
                @pl.when(q + LEAD2 >= RING)
                def _():
                    pl.semaphore_wait(credit, 1)

                p2(q + LEAD2).start()

            @pl.when(q == 0)
            def _():
                forward_features(1)
                assemble(1)

            @pl.when((q >= 1) & (q <= chunks))
            def _():
                process(q - 1)

            @pl.when(q >= 2)
            def _():
                finalize_hub(q - 2)

            @pl.when(q == 2)
            def _():
                feature1(0, 1).wait_recv()
                feature3(0).start()
                feature1(0, 0).wait_recv()
                spread(0, 0)
                feature2(0).wait_recv()
                spread(0, 1)

            @pl.when(q == 3)
            def _():
                feature3(0).wait_recv()
                spread(0, 2)

            @pl.when(q == 4)
            def _():
                forward_features(0)

            @pl.when(q == 5)
            def _():
                assemble(0)

            @pl.when(q == 7)
            def _():
                p1x().wait_recv()
                p3x().start()

            @pl.when(q == 8)
            def _():
                extra_hub()

            @pl.when(q == 11)
            def _():
                yx_hub().wait_recv()
                extra_spread(rx[1, pl.ds(mine, own), :])

        @pl.when(q < (each + 1) // 2)
        def _():
            lax.fori_loop(2 * q, jnp.minimum(2 * q + 2, each), backward_block, 0)

        for at, jobs in pieces.items():
            for job in jobs if isinstance(jobs, list) else [jobs]:
                pl.when(q == at)(job)

        @pl.when(edge)
        def _():
            @pl.when(q < chunks)
            def _():
                e(q).wait_recv()
                yb_edge(q).start()

            @pl.when(q + LEAD < chunks)
            def _():
                @pl.when(q >= 2)
                def _():
                    yb_edge(q - 2).wait_send()

                p1(q + LEAD).start()

            @pl.when((q >= 1) & (q <= chunks))
            def _():
                finalize_edge(q - 1)

            @pl.when(q == 9)
            def _():
                e_x().wait_recv()
                yx_edge().start()

            @pl.when(q == 11)
            def _():
                yx_edge().wait_recv()
                extra_spread(exe[pl.ds(mine, own), :])

        return carry

    lax.fori_loop(0, chunks + 2, body, 0)

    stored(chunks - 2, 2).wait()
    stored(chunks - 1, 2).wait()

    @pl.when(hub)
    def _():
        def drain(q, carry):
            p2(q).wait_send()
            return carry

        lax.fori_loop(0, chunks, drain, 0)
        for q in (chunks - 2, chunks - 1):
            e(q).wait_send()
            ya(q, 0).wait_send()
            ya(q, 1).wait_send()
            yb_hub(q).wait_send()
            fa(q).wait_send()
        for f in range(2):
            feature2(f).wait_send()
            feature3(f).wait_send()
            for shard in range(3):
                across(f, shard).wait_send()
                sibling(f, shard, 0).wait_send()
                sibling(f, shard, 1).wait_send()
        p2x().wait_send()
        p3x().wait_send()
        e_x().wait_send()
        yx_hub().wait_send()

    @pl.when(edge)
    def _():
        def drain(q, carry):
            p1(q).wait_send()
            return carry

        lax.fori_loop(LEAD - 2, chunks, drain, 0)
        for q in range(chunks - LEAD - 2, chunks):
            yb_edge(q).wait_send()
        feature1(1, 0).wait_send()
        feature1(0, 0).wait_send()
        feature1(0, 1).wait_send()
        p1x().wait_send()
        yx_edge().wait_send()


def outputs_kernel(
    smalls, a, b, c, d, e, f, g,
    norm_gain, inner_kernel, inner_bias, state_kernel_out, state_bias, step_bias, decay, skip, gate_gain,
    ao, bo, co, do, eo, fo, go, at_, bt, ct, dt, et, ft, gt, loads, stores,
):
    through = list(zip((a, b, c, d, e, f, g), (at_, bt, ct, dt, et, ft, gt), (ao, bo, co, do, eo, fo, go)))
    load = lambda n: pltpu.make_async_copy(through[n][0], through[n][1], loads.at[n])
    keep = lambda n: pltpu.make_async_copy(through[n][1], through[n][2], stores.at[n])
    for n in range(len(through)):
        load(n).start()
    for ref, at, lane in (
        (norm_gain, 9, 0), (inner_bias, CONV, 0), (state_bias, 10 + CONV, 0), (step_bias, 15, 0), (decay, 15, 128),
        (skip, 15, 256), (gate_gain, 8, 0),
    ):
        ref[...] = smalls[at : at + 1, lane : lane + ref.shape[0]].reshape(ref.shape)
    inner_kernel[...] = smalls[0:CONV, :]
    state_kernel_out[...] = smalls[10 : 10 + CONV, 0 : state_kernel_out.shape[1]]
    for n in range(len(through)):
        load(n).wait()
        keep(n).start()
    for n in range(len(through)):
        keep(n).wait()


def whole(shape):
    return pl.BlockSpec(shape, lambda *_: (0,) * len(shape))


def columns(rows):
    return pl.BlockSpec((rows, BLK), lambda j, *_: (0, j))


SMEM = pl.BlockSpec(memory_space=pltpu.SMEM)
VM = pltpu.CompilerParams(vmem_limit_bytes=56 << 20)
VMS = pltpu.CompilerParams(vmem_limit_bytes=56 << 20, dimension_semantics=("arbitrary",))


def struct(shape, dtype=f32):
    return jax.ShapeDtypeStruct(shape, dtype)


def cost(flops, moved):
    return pl.CostEstimate(flops=int(flops), bytes_accessed=int(moved), transcendentals=0)


def on_device(
    block_input, cotangent, seq_lengths, norm_gain, gate_weight, inner_weight, step_weight, state_weight,
    inner_kernel, inner_bias, state_kernel_, state_bias, step_bias, decay_log, skip_scale, gate_gain, output_weight,
):
    parts = lax.axis_size("tensor")
    shards = lax.axis_size("dp")
    t = lax.axis_index("tensor")
    count, width = block_input.shape
    inner = gate_weight.shape[1]
    heads = step_bias.shape[0]
    share = width // parts
    span = 2 * STATE // parts
    steps = inner // BLK
    pad = ((0, 0), (0, 128 - heads))
    row = lambda x: x.reshape(1, -1)

    def swap(x, k):
        return lax.ppermute(x, "tensor", [(i, i ^ k) for i in range(parts)])

    chunks = 3 * steps
    slab = lambda x, size: lax.dynamic_slice_in_dim(x, t * size, size, x.ndim - 1)
    if shards == 8 and parts == 4:
        own, half_blk, piece, near = width // 8, BLK // 2, count // parts, width // 2
        dma, v = pltpu.SemaphoreType.DMA, lambda *shape: pltpu.VMEM(shape, f32)
        vb = lambda *shape: pltpu.VMEM(shape, bf16)
        vmem, hbm = pl.BlockSpec(memory_space=pltpu.VMEM), pl.BlockSpec(memory_space=pl.ANY)
        scratch = [
            v(chunks, count, BLK), v(4 * steps, count, half_blk), v(steps, count, BLK), vb(count, width),
            v(count, 128), v(1, width), v(1, inner), v(1, 2 * STATE), v(24, 128), v(1, inner), v(1, inner), v(2, piece, near), v(2, piece, width), v(2, piece, near), v(2, piece, near),
            v(2, 3, piece, near), v(2, 3, piece, near), vb(2, near, 4 * count), v(RING, 3 * count, BLK),
            v(RING, 2, own, half_blk), v(LEAD, own, half_blk), v(2, 2, 2 * own, BLK), v(2, own, half_blk), v(2, own, BLK),
            vb(4 * count, BLK), vb(count, near), vb(2, 2, width, BLK), vb(2, BLK, width),
            v(4, count, share), v(3, count, share), v(3, share // half_blk, count, half_blk),
            v(count, count), v(count, count), v(steps, count, 128), v(128, count), v(count, 2 * STATE), v(count, 2 * STATE),
            v(count, 128), v(count, 128), v(count, count), v(count, 128), v(count, 128), v(8, 128), v(count, 128),
            v(8, count), v(3, 8, count), v(4, count, span), v(3, count, span), v(4, 8, span), v(16, inner), v(3, 16, inner),
            v(count, 128), v(3, count, 128), v(2, 2 * own, 128), v(2 * own, 128), v(own, 128), v(4, own, 128),
            v(8, count), v(3, 8, count),
        ]
        scratch += [dma((chunks,))] * 8 + [dma((chunks, 2))] * 2 + [dma((chunks,))] * 5 + [dma((3, 2))] + [dma((3,))] * 14
        scratch += [dma((4,))] * 2 + [dma((1,))] * 2 + [dma((3,))] * 2 + [dma((2, 2))] * 2 + [dma((2,))] * 4 + [dma((2, 3))] * 2
        scratch += [dma((2, 2, 3))] * 2 + [pltpu.SemaphoreType.REGULAR] * 2
        shapes = [
            struct((count, share), bf16), struct((count, share)), struct((own, inner)), struct((own, inner)),
            struct((own, 2 * STATE)), struct((heads, own)), struct((own, inner)),
        ]
        *large, smalls = pl.pallas_call(
            layer_kernel,
            in_specs=[SMEM] + [vmem] * 13 + [hbm] * 3,
            out_specs=[vmem, vmem, hbm, hbm, vmem, vmem, hbm, vmem],
            out_shape=shapes + [struct((16, inner))],
            scratch_shapes=scratch,
            compiler_params=pltpu.CompilerParams(collective_id=1, has_side_effects=True, vmem_limit_bytes=VMEM_LIMIT),
            name="layer",
        )(
            seq_lengths, block_input, cotangent, norm_gain, step_weight.T, state_weight, inner_kernel, inner_bias,
            state_kernel_, state_bias, step_bias, decay_log, skip_scale, gate_gain, gate_weight, inner_weight, output_weight,
        )
        cut = [
            struct((share,)), struct((CONV, inner)), struct((inner,)), struct((CONV, 2 * STATE)), struct((2 * STATE,)),
            struct((heads,)), struct((heads,)), struct((heads,)), struct((inner,)),
        ]
        *smalls, out, into, gate_grad, inner_grad, state_grad, step_grad, output_grad = pl.pallas_call(
            outputs_kernel,
            in_specs=[vmem] + [hbm] * 7,
            out_specs=[vmem] * 9 + [hbm] * 7,
            out_shape=cut + shapes,
            scratch_shapes=[pltpu.VMEM(a.shape, a.dtype) for a in shapes] + [dma((7,)), dma((7,))],
            compiler_params=VM,
            name="outputs",
        )(smalls, *large)
        return (
            out, into, smalls[0], gate_grad, inner_grad, step_grad.T, state_grad, *smalls[1:9], output_grad.T,
        )

    padded_step = jnp.pad(step_weight, pad)
    stepb, decay = jnp.pad(row(step_bias), pad), jnp.pad(row(decay_log), pad)
    skipc = jnp.repeat(skip_scale, HEAD_DIM).reshape(1, -1)
    ik, ib, gain = inner_kernel, row(inner_bias), row(gate_gain)
    full = struct((count, inner))
    nb, inv = pl.pallas_call(
        norm_kernel,
        out_shape=(struct((count, width), bf16), struct((count, 128))),
        compiler_params=VM,
        name="norm_in",
    )(block_input, row(norm_gain))

    graw, iraw, cv, mixed, scaled, sums, sraw, sact, state_raw, hc, lsr, addm, g, keep = pl.pallas_call(
        forward_kernel,
        grid=(steps,),
        in_specs=[
            SMEM, whole((count, width)), whole((count, width)), columns(width), columns(width),
            pl.BlockSpec((BLK, width), lambda j: (j, 0)), whole((width, 128)), whole((width, 2 * STATE)),
            columns(CONV), columns(1), whole((CONV, 2 * STATE)), whole((1, 2 * STATE)), whole((1, 128)), whole((1, 128)),
            columns(1), columns(1),
        ],
        out_specs=(
            [columns(count)] * 5
            + [whole((8, count)), whole((count, 128)), whole((count, 2 * STATE)), whole((count, 2 * STATE)),
               whole((steps, count, 128)), whole((128, count)), whole((count, count)), whole((count, count)),
               whole((count, 128))]
        ),
        out_shape=(
            [full] * 5
            + [struct((8, count)), struct((count, 128)), struct((count, 2 * STATE)), struct((count, 2 * STATE)),
               struct((steps, count, 128)), struct((128, count)), struct((count, count)), struct((count, count)),
               struct((count, 128))]
        ),
        scratch_shapes=[pltpu.VMEM((count, 128), f32)],
        compiler_params=VMS,
        cost_estimate=cost(6 * count * width * inner, 6 * width * inner + 20 * count * inner),
        name="forward",
    )(
        seq_lengths, nb, cotangent, gate_weight, inner_weight, output_weight, padded_step, state_weight, ik, ib,
        state_kernel_, row(state_bias), stepb, decay, skipc, gain,
    )

    all_sums = jnp.stack([sums] + [swap(sums, k) for k in range(1, parts)])
    x, dm, gg = pl.pallas_call(
        partial(unit_kernel, float(inner * parts)),
        grid=(steps,),
        in_specs=[whole((parts, 8, count)), columns(count), columns(count), columns(count), columns(1)],
        out_specs=[pl.BlockSpec((2, 1, count, BLK), lambda j: (0, j, 0, 0)), columns(count), columns(8)],
        out_shape=[struct((3, steps, count, BLK)), full, struct((8, inner))],
        compiler_params=VMS,
        cost_estimate=cost(0, 24 * count * inner),
        name="unit",
    )(all_sums, graw, mixed, scaled, gain)

    x, rows, sback, hrows, dstate = pl.pallas_call(
        backward_kernel,
        grid=(steps,),
        in_specs=[
            SMEM, columns(count), columns(count), columns(count), columns(count),
            pl.BlockSpec((1, count, 128), lambda j: (j, 0, 0)), whole((128, count)), whole((count, count)),
            whole((count, count)), whole((count, 128)), whole((count, 2 * STATE)), columns(CONV), columns(1), whole((1, 128)),
            pl.BlockSpec(memory_space=pl.ANY),
        ],
        input_output_aliases={14: 0},
        out_specs=[pl.BlockSpec((1, 1, count, BLK), lambda j: (2, j, 0, 0)), columns(8), whole((count, 128)), whole((8, 128)), whole((parts, count, span))],
        out_shape=[struct((3, steps, count, BLK)), struct((8, inner)), struct((count, 128)), struct((8, 128)), struct((parts, count, span))],
        scratch_shapes=[pltpu.VMEM((count, count), f32), pltpu.VMEM((count, 128), f32), pltpu.VMEM((count, 128), f32)],
        compiler_params=VMS,
        cost_estimate=cost(40 * count * count * inner // 64 * 4, 24 * count * inner),
        name="backward",
    )(seq_lengths, dm, cv, iraw, mixed, hc, lsr, addm, g, sraw, sact, ik, skipc, decay, x)

    uo, gb, back = (jnp.swapaxes(x[i], 0, 1).reshape(count, inner) for i in range(3))

    def to_parts(x, axis):
        size = x.shape[axis] // parts
        block = lambda i: lax.dynamic_slice_in_dim(x, i * size, size, axis)
        got = [swap(block(t ^ k), k) for k in range(1, parts)]
        return [block(t)] + got

    def from_parts(x):
        got = jnp.stack([x] + [swap(x, k) for k in range(1, parts)])
        return jnp.stack([lax.dynamic_index_in_dim(got, t ^ i, 0, False) for i in range(parts)])

    state_parts = jnp.concatenate(to_parts(dstate, 0), axis=0)
    sq, srows = pl.pallas_call(
        state_kernel,
        in_specs=[SMEM] + [pl.BlockSpec(memory_space=pltpu.VMEM)] * 4,
        out_shape=(struct((count, span)), struct((8, span))),
        compiler_params=VM,
        name="state_back",
    )(seq_lengths, state_parts, slab(state_raw, span), slab(state_kernel_, span), row(slab(state_bias, span)))

    hidden = slab(block_input, share).astype(f32)
    cot_share = slab(cotangent, share).astype(f32)
    out_parts = to_parts(mm(uo.astype(bf16), output_weight), 1)
    block_output = (sum(out_parts[1:], out_parts[0]) + hidden).astype(bf16)

    gbb, ibb, sbb, qb = (x.astype(bf16) for x in (gb, back, sback[:, :heads], sq))
    partial_in = (
        mm(gbb, gate_weight, NT) + mm(ibb, inner_weight, NT) + mm(sbb, step_weight, NT)
        + mm(qb, slab(state_weight, span), NT)
    )
    in_parts = to_parts(partial_in, 1)
    d_normed = sum(in_parts[1:], in_parts[0])
    inv_in = inv[:, 0:1]
    normed = hidden * inv_in
    gain_share = row(slab(norm_gain, share))
    d_hat = d_normed * gain_share
    dot = jnp.sum(d_hat * normed, axis=1).reshape(-1, 128)
    dot = sum((swap(dot, k) for k in range(1, parts)), dot).reshape(-1, 1) / width
    input_gradient = inv_in * (d_hat - normed * dot) + cot_share
    norm_gain_grad = jnp.sum(d_normed * normed, axis=0)

    extra = jnp.concatenate([sq, sback[:, :heads], jnp.zeros((count, 128 - span - heads), f32)], axis=1)

    def scatter(a, b):
        return lax.psum_scatter(mm(a, b.astype(bf16), TN), "dp", scatter_dimension=0, tiled=True)

    output_grad = scatter(cotangent, uo).T
    gate_grad, inner_grad, extra_grad = scatter(nb, gb), scatter(nb, back), scatter(nb, extra)

    def over_dp(x):
        return lax.psum(x, "dp")

    step_grad = extra_grad[:, span : span + heads]
    state_grad = jnp.swapaxes(from_parts(extra_grad[:, :span]), 0, 1).reshape(-1, 2 * STATE)
    misc = jnp.concatenate([hrows[0], hrows[1], srows[: CONV + 1].reshape(-1), norm_gain_grad])
    misc = jnp.pad(misc, (0, -misc.shape[0] % 1024)).reshape(8, -1)
    smalls = over_dp(jnp.concatenate([rows, gg], axis=0))
    misc = over_dp(misc).reshape(-1)
    step_bias_grad, decay_grad = misc[:heads], misc[128 : 128 + heads]
    state_rows = from_parts(misc[256 : 256 + (CONV + 1) * span].reshape(CONV + 1, span))
    state_rows = jnp.swapaxes(state_rows, 0, 1).reshape(CONV + 1, 2 * STATE)
    at = 256 + (CONV + 1) * span
    skip_grad = jnp.sum(smalls[CONV + 1].reshape(heads, HEAD_DIM), axis=1)
    return (
        block_output,
        input_gradient,
        misc[at : at + share],
        gate_grad,
        inner_grad,
        step_grad,
        state_grad,
        smalls[:CONV],
        smalls[CONV],
        state_rows[:CONV],
        state_rows[CONV],
        step_bias_grad,
        decay_grad,
        skip_grad,
        smalls[8],
        output_grad,
    )


def solution(mesh):
    return jax.shard_map(
        on_device,
        mesh=mesh,
        in_specs=(
            P("dp", None), P("dp", None), P("dp", None), P(), P(None, "tensor"), P(None, "tensor"), P(None, "tensor"), P(),
            P(None, "tensor"), P("tensor"), P(), P(), P("tensor"), P("tensor"), P("tensor"), P("tensor"), P("tensor", None),
        ),
        out_specs=(
            P("dp", "tensor"), P("dp", "tensor"), P("tensor"), P("dp", "tensor"), P("dp", "tensor"), P("dp", "tensor"),
            P("dp", None), P(None, "tensor"), P("tensor"), P(), P(), P("tensor"), P("tensor"), P("tensor"), P("tensor"),
            P("tensor", "dp"),
        ),
        check_vma=False,
    )
```

```python
from functools import partial

import jax
import jax.numpy as jnp
from jax import lax
from jax.experimental import pallas as pl
from jax.experimental.pallas import tpu as pltpu
from jax.sharding import PartitionSpec as P

HEAD_DIM = 64
STATE = 128
CONV = 4
BLK = 256
HPB = BLK // HEAD_DIM
eps = 1e-05
NEG = -1e30
f32 = jnp.float32
bf16 = jnp.bfloat16
HIGH = lax.Precision.HIGHEST
NN = (((1,), (0,)), ((), ()))
NT = (((1,), (1,)), ((), ()))
TN = (((0,), (0,)), ((), ()))


def mm(a, b, dims=NN, precision=None):
    return lax.dot_general(a, b, dims, precision=precision, preferred_element_type=f32)


def sigmoid(x):
    return 1.0 / (1.0 + jnp.exp(-x))


def softplus(x):
    return jnp.maximum(x, 0.0) + jnp.log1p(jnp.exp(-jnp.abs(x)))


def seg_of(places, lengths):
    total = jnp.zeros(places.shape, jnp.int32)
    end = jnp.int32(0)
    for s in range(lengths.shape[1]):
        end = end + lengths[0, s]
        total = total + (places >= end).astype(jnp.int32)
    return total


def keeps(lengths, count):
    t = lax.broadcasted_iota(jnp.int32, (count, 1), 0)
    own = seg_of(t, lengths)
    out = [None]
    for back in range(1, CONV):
        out.append(((seg_of(t - back, lengths) == own) & (t >= back)).astype(f32))
    return out


def down(x, back):
    return pltpu.roll(x, back, 0)


def up(x, back):
    return pltpu.roll(x, x.shape[0] - back, 0)


def conv(u, kernel, bias, keep):
    out = bias + kernel[CONV - 1 : CONV, :] * u
    for back in range(1, CONV):
        out = out + kernel[CONV - 1 - back : CONV - back, :] * (down(u, back) * keep[back])
    return out


def conv_back(dc, u, kernel, keep):
    du = kernel[CONV - 1 : CONV, :] * dc
    rows = [jnp.sum(dc * u, axis=0, keepdims=True)]
    for back in range(1, CONV):
        kept = dc * keep[back]
        du = du + kernel[CONV - 1 - back : CONV - back, :] * up(kept, back)
        rows.append(jnp.sum(kept * down(u, back), axis=0, keepdims=True))
    return du, rows[::-1] + [jnp.sum(dc, axis=0, keepdims=True)]


def lanes_first(shape):
    return lax.broadcasted_iota(jnp.int32, shape, 1) < HEAD_DIM


def norm_kernel(x_ref, gain_ref, nb_ref, inv_ref):
    x = x_ref[...].astype(f32)
    inv = lax.rsqrt(jnp.sum(x * x, axis=1, keepdims=True) / x.shape[1] + eps)
    nb_ref[...] = (x * inv * gain_ref[...]).astype(bf16)
    inv_ref[...] = jnp.broadcast_to(inv, inv_ref.shape)


def forward_kernel(
    lengths, nb_ref, cot_ref, wg_ref, wi_ref, wo_ref, ws_ref, wst_ref, ik_ref, ib_ref, sk_ref, sb_ref,
    stepb_ref, decay_ref, skipc_ref, gain_ref,
    graw_ref, iraw_ref, cv_ref, mixed_ref, scaled_ref, sums_ref, sraw_ref, sact_ref, state_ref, hc_ref, lsr_ref,
    addm_ref, g_ref, keep_ref, acc,
):
    j = pl.program_id(0)
    count = nb_ref.shape[0]
    nb = nb_ref[...]

    @pl.when(j == 0)
    def _():
        i0 = lax.broadcasted_iota(jnp.int32, (count, count), 0)
        j0 = lax.broadcasted_iota(jnp.int32, (count, count), 1)
        same = (seg_of(i0, lengths) == seg_of(j0, lengths)) & (j0 <= i0)
        addm_ref[...] = jnp.where(same, 0.0, NEG)
        state = mm(nb, wst_ref[...])
        state_ref[...] = state
        keep = keeps(lengths, count)
        for back in range(1, CONV):
            keep_ref[:, back : back + 1] = keep[back]
        cv = conv(state, sk_ref[...], sb_ref[...], keep)
        act = cv * sigmoid(cv)
        sact_ref[...] = act
        g_ref[...] = mm(act[:, STATE:], act[:, :STATE], NT, HIGH)
        raw = mm(nb, ws_ref[...]) + stepb_ref[...]
        sraw_ref[...] = raw
        step = softplus(raw)
        logs = mm(same.astype(f32), step * (-jnp.exp(decay_ref[...])), NN, HIGH)
        lsr_ref[...] = jnp.transpose(logs)
        for k in range(hc_ref.shape[0]):
            hc_ref[k, :, 0:HPB] = logs[:, HPB * k : HPB * (k + 1)]
            hc_ref[k, :, HPB : 2 * HPB] = step[:, HPB * k : HPB * (k + 1)]
        acc[...] = jnp.zeros_like(acc)

    gate = mm(nb, wg_ref[...])
    inner = mm(nb, wi_ref[...])
    scaled = mm(cot_ref[...], wo_ref[...], NT)
    graw_ref[...] = gate
    iraw_ref[...] = inner
    scaled_ref[...] = scaled
    cv = conv(inner, ik_ref[...], ib_ref[...], keeps(lengths, count))
    cv_ref[...] = cv
    v = cv * sigmoid(cv)
    first = lanes_first((count, 2 * HEAD_DIM))
    addm = addm_ref[...]
    g = g_ref[...]
    parts = []
    for pair in range(BLK // (2 * HEAD_DIM)):
        vp = v[:, 2 * HEAD_DIM * pair : 2 * HEAD_DIM * (pair + 1)]
        k = 2 * pair
        steps = jnp.where(first, hc_ref[j, :, HPB + k : HPB + k + 1], hc_ref[j, :, HPB + k + 1 : HPB + k + 2])
        vs = (vp * steps).astype(bf16)
        ys = []
        for h in (k, k + 1):
            gaps = hc_ref[j, :, h : h + 1] - lsr_ref[pl.ds(HPB * j + h, 1), :] + addm
            ys.append(mm((g * jnp.exp(gaps)).astype(bf16), vs))
        parts.append(jnp.where(first, ys[0], ys[1]))
    mixed = jnp.concatenate(parts, axis=1) + skipc_ref[...] * v
    mixed_ref[...] = mixed
    gated = mixed * (gate * sigmoid(gate))
    acc[:, 0:1] += jnp.sum(gated * gated, axis=1, keepdims=True)
    acc[:, 1:2] += jnp.sum(scaled * gain_ref[...] * gated, axis=1, keepdims=True)

    @pl.when(j == pl.num_programs(0) - 1)
    def _():
        sums_ref[...] = jnp.transpose(acc[...])[0:8, :]


def unit_kernel(width, s_ref, graw_ref, mixed_ref, scaled_ref, gain_ref, x_ref, dm_ref, gg_ref):
    sums = jnp.sum(s_ref[...], axis=0)
    cols = jnp.transpose(sums)
    inv = lax.rsqrt(cols[:, 0:1] / width + eps)
    dot = inv * cols[:, 1:2]
    gate, mixed, scaled, gain = graw_ref[...], mixed_ref[...], scaled_ref[...], gain_ref[...]
    s = sigmoid(gate)
    act = gate * s
    unit = mixed * act * inv
    x_ref[0, 0] = (unit * gain).astype(bf16).astype(f32)
    gg_ref[...] = jnp.broadcast_to(jnp.sum(scaled * unit, axis=0, keepdims=True), gg_ref.shape)
    d_gated = inv * (scaled * gain - unit * (dot / width))
    dm_ref[...] = d_gated * act
    x_ref[1, 0] = (d_gated * mixed * s * (1.0 + gate * (1.0 - s))).astype(bf16).astype(f32)


def backward_kernel(
    lengths, dm_ref, cv_ref, iraw_ref, mixed_ref, hc_ref, lsr_ref, addm_ref, g_ref, sraw_ref, sact_ref,
    ik_ref, skipc_ref, decay_ref, _,
    back_ref, rows_ref, sback_ref, hrows_ref, dstate_ref, dg, dlogs, dstep,
):
    j = pl.program_id(0)
    count = dm_ref.shape[0]

    @pl.when(j == 0)
    def _():
        dg[...] = jnp.zeros_like(dg)
        dlogs[...] = jnp.zeros_like(dlogs)
        dstep[...] = jnp.zeros_like(dstep)

    cv, dm, skipc = cv_ref[...], dm_ref[...], skipc_ref[...]
    s = sigmoid(cv)
    v = cv * s
    within = mixed_ref[...] - skipc * v
    first = lanes_first((count, 2 * HEAD_DIM))
    addm = addm_ref[...]
    g = g_ref[...]
    us, vss, dyb, stepm = [], [], [], []
    total = dg[...]
    for pair in range(BLK // (2 * HEAD_DIM)):
        cols = slice(2 * HEAD_DIM * pair, 2 * HEAD_DIM * (pair + 1))
        k = 2 * pair
        steps = jnp.where(first, hc_ref[0, :, HPB + k : HPB + k + 1], hc_ref[0, :, HPB + k + 1 : HPB + k + 2])
        vs = (v[:, cols] * steps).astype(bf16)
        dy = dm[:, cols].astype(bf16)
        both = []
        for h in (k, k + 1):
            gaps = hc_ref[0, :, h : h + 1] - lsr_ref[pl.ds(HPB * j + h, 1), :] + addm
            decay = jnp.exp(gaps)
            both.append(mm((g * decay).astype(bf16), dy, TN))
            mine = first if h == k else jnp.logical_not(first)
            total = total + decay * mm(jnp.where(mine, dy, jnp.zeros_like(dy)), vs, NT)
        us.append(jnp.where(first, both[0], both[1]))
        vss.append(vs.astype(f32))
        dyb.append(dy.astype(f32))
        stepm.append(steps)
    dg[...] = total
    u = jnp.concatenate(us, axis=1)
    vs = jnp.concatenate(vss, axis=1)
    dy = jnp.concatenate(dyb, axis=1)
    steps = jnp.concatenate(stepm, axis=1)
    c0 = lax.broadcasted_iota(jnp.int32, (BLK, 128), 0) // HEAD_DIM
    l0 = lax.broadcasted_iota(jnp.int32, (BLK, 128), 1)
    pick = (l0 == c0 + HPB * j).astype(f32)
    dlogs[...] += mm(dy * within - vs * u, pick, NN, HIGH)
    dstep[...] += mm(v * u, pick, NN, HIGH)
    dv = steps * u + skipc * dm
    dc = dv * (s * (1.0 + cv * (1.0 - s)))
    du, rows = conv_back(dc, iraw_ref[...], ik_ref[...], keeps(lengths, count))
    back_ref[0, 0] = du.astype(bf16).astype(f32)
    rows_ref[...] = jnp.concatenate(rows + [jnp.sum(dm * v, axis=0, keepdims=True)] + [jnp.zeros((2, BLK), f32)], axis=0)

    @pl.when(j == pl.num_programs(0) - 1)
    def _():
        mask = (addm > -1.0).astype(f32)
        q = mm(mask, dlogs[...], TN, HIGH)
        raw = sraw_ref[...]
        step = softplus(raw)
        rate = -jnp.exp(decay_ref[...])
        draw = (dstep[...] + rate * q) * sigmoid(raw)
        sback_ref[...] = draw.astype(bf16).astype(f32)
        hrows_ref[...] = jnp.concatenate(
            [jnp.sum(draw, axis=0, keepdims=True), rate * jnp.sum(step * q, axis=0, keepdims=True), jnp.zeros((6, 128), f32)],
            axis=0,
        )
        act = sact_ref[...]
        d_b = mm(dg[...], act[:, STATE:], TN, HIGH)
        d_c = mm(dg[...], act[:, :STATE], NN, HIGH)
        both = jnp.concatenate([d_b, d_c], axis=1)
        span = dstate_ref.shape[2]
        for t in range(dstate_ref.shape[0]):
            dstate_ref[t] = both[:, span * t : span * (t + 1)]


def state_kernel(lengths, parts_ref, u_ref, sk_ref, sb_ref, back_ref, rows_ref):
    keep = keeps(lengths, u_ref.shape[0])
    cv = conv(u_ref[...], sk_ref[...], sb_ref[...], keep)
    s = sigmoid(cv)
    dc = jnp.sum(parts_ref[...], axis=0) * (s * (1.0 + cv * (1.0 - s)))
    du, rows = conv_back(dc, u_ref[...], sk_ref[...], keep)
    back_ref[...] = du.astype(bf16).astype(f32)
    rows_ref[...] = jnp.concatenate(rows + [jnp.zeros((3, du.shape[1]), f32)], axis=0)


MESH = pl.DeviceIdType.MESH
RING = 6
VMEM_LIMIT = 64 << 20
LEAD = 4
LEAD2 = 1


def layer_kernel(
    lengths, xin, cot, gain_in1, ws, wst, ik, ib1, sk, sb1, stepb1, decay1, skip1, gain1, wg_hbm, wi_hbm, wo_hbm,
    out_ref, din_ref, gate_out, inner_out, state_out, step_out, turned_out, smalls_ref,
    x, act, dmb, nb, inv, gain_in, ib, sb, heads_in, skipc, gain, fs, f1, f2, f3, fx, fc, ft, big, yra, yrb, r, ea, fin, xb, xbr, wring, woring, po, por, pir, addm, g, hc, lsr, sact, state_raw, sraw, keep_ref, dg, dlogs, dstep, hsum, acc, sums, sumr, dstate, dsr, srr, sm, smr,
    ex, exr, rx, exe, yrx, exg, dots, dotr,
    p1s, p1v, p2s, p2v, p3s, p3v, es, ev, yas, yav, ybs, ybv, fas, fav, fins, wsem, pos, pov, pis, piv,
    dss, dsv, srs, srv, dts, dtv, sus, suv, sms, smv, exs, exv, yxs, yxv, exgs, exgv,
    f1s, f1v, f2s, f2v, f3s, f3v, fxs, fxv, fcs, fcv, credit, fc_free,
):
    d, t = lax.axis_index("dp"), lax.axis_index("tensor")
    y, z = d % 2, d // 2
    side, half = z % 2, z // 2
    hub = (z == 1) | (z == 2)
    edge = jnp.logical_not(hub)
    chunks, count, wide = x.shape
    each = chunks // 3
    lanes = wide // 2
    width = xin.shape[1]
    part = width // 4
    own = part // 2
    share = width // 4
    span = dsr.shape[2]
    inner = each * wide
    piece = f1.shape[1]
    pair, peer, line = d ^ 2, d ^ 6, d ^ 1
    mine, other = pl.multiple_of(own * y, own), pl.multiple_of(own * (1 - y), own)
    mine_part, pair_part = pl.multiple_of(part * side, part), pl.multiple_of(part * (1 - side), part)
    near, far = pl.multiple_of(half * 2 * part, 2 * part), pl.multiple_of((1 - half) * 2 * part, 2 * part)
    my_rows = pl.multiple_of(t * piece, piece)
    my_share = pl.multiple_of(t * share, share)

    def send(src, dst, ssem, rsem, dev):
        return pltpu.make_async_remote_copy(
            src_ref=src, dst_ref=dst, send_sem=ssem, recv_sem=rsem, device_id=dev, device_id_type=MESH
        )

    def p1(q):
        return send(x.at[q], big.at[q % RING, pl.ds(0, count)], p1s.at[q], p1v.at[q], (pair, t))

    def p2(q):
        return send(x.at[q], big.at[q % RING, pl.ds(count, count)], p2s.at[q], p2v.at[q], (peer, t))

    def p3(q):
        slot = q % RING
        return send(
            big.at[slot, pl.ds(0, count)], big.at[slot, pl.ds(2 * count, count)], p3s.at[q], p3v.at[q], (peer, t)
        )

    def e(q):
        return send(
            r.at[q % 2, 0, :, pl.ds(lanes, lanes)], big.at[q % RING, pl.ds(0, part), pl.ds(0, lanes)], es.at[q], ev.at[q],
            (pair, t),
        )

    def ya(q, k):
        return send(
            r.at[q % 2, k, pl.ds(other, own), pl.ds(0, lanes)], yra.at[q % RING, k], yas.at[q, k], yav.at[q, k], (line, t)
        )

    def yb_hub(q):
        return send(
            r.at[q % 2, 1, pl.ds(other, own), pl.ds(lanes, lanes)], yrb.at[q % LEAD], ybs.at[q], ybv.at[q], (line, t)
        )

    def yb_edge(q):
        return send(
            big.at[q % RING, pl.ds(other, own), pl.ds(0, lanes)], yrb.at[q % LEAD], ybs.at[q], ybv.at[q], (line, t)
        )

    def fa(q):
        return send(ea.at[q % 2], yra.at[q % RING, 0], fas.at[q], fav.at[q], (pair, t))

    def feature1(f, k):
        half_row = f1.at[f, :, pl.ds((near, far)[k], 2 * part)]
        return send(half_row, half_row, f1s.at[f, k], f1v.at[f, k], (pair, t))

    def feature2(f):
        return send(fs.at[f], f2.at[f], f2s.at[f], f2v.at[f], (peer, t))

    def feature3(f):
        return send(f1.at[f, :, pl.ds(far, 2 * part)], f3.at[f], f3s.at[f], f3v.at[f], (peer, t))

    def feature(f, shard):
        return (f1.at[f, :, pl.ds(near, 2 * part)], f2.at[f], f3.at[f])[shard]

    def across(f, shard):
        return send(feature(f, shard), fx.at[f, shard], fxs.at[f, shard], fxv.at[f, shard], (d, t ^ 2))

    def sibling(f, shard, k):
        src = fx.at[f, shard] if k else feature(f, shard)
        return send(src, fc.at[k, shard], fcs.at[k, f, shard], fcv.at[k, f, shard], (d, t ^ 1))

    def spread(f, shard):
        across(f, shard).start()
        if f:
            sibling(f, shard, 0).start()

    p1x = lambda: send(ex, exr.at[0], exs.at[0], exv.at[0], (pair, t))
    p2x = lambda: send(ex, exr.at[1], exs.at[1], exv.at[1], (peer, t))
    p3x = lambda: send(exr.at[0], exr.at[2], exs.at[2], exv.at[2], (peer, t))
    e_x = lambda: send(rx.at[0], exe, exs.at[3], exv.at[3], (pair, t))
    yx_hub = lambda: send(rx.at[1, pl.ds(other, own)], yrx, yxs.at[0], yxv.at[0], (line, t))
    yx_edge = lambda: send(exe.at[pl.ds(other, own)], yrx, yxs.at[0], yxv.at[0], (line, t))

    def over_tensor(src, dst, ssem, rsem):
        return lambda k: send(src(k), dst(k), ssem.at[k - 1], rsem.at[k - 1], (d, t ^ k))

    sum_copy = over_tensor(lambda k: sums, lambda k: sumr.at[k - 1], sus, suv)
    state_copy = over_tensor(lambda k: dstate.at[t ^ k], lambda k: dsr.at[k - 1], dss, dsv)
    row_copy = over_tensor(lambda k: srr.at[t], lambda k: srr.at[t], srs, srv)
    out_near = lambda n: send(po.at[t ^ (1 + 2 * n)], por.at[n], pos.at[n], pov.at[n], (d, t ^ 1))
    out_far = lambda: send(po.at[t ^ 2], por.at[2], pos.at[2], pov.at[2], (d, t ^ 2))
    tiles = share // lanes
    block = lambda i: act.at[pl.ds(tiles * i, tiles)]
    in_near = lambda n: send(block(t ^ (1 + 2 * n)), pir.at[n], pis.at[n], piv.at[n], (d, t ^ 1))
    in_far = lambda: send(block(t ^ 2), pir.at[2], pis.at[2], piv.at[2], (d, t ^ 2))
    dot_copy = over_tensor(lambda k: dots, lambda k: dotr.at[k - 1], dts, dtv)
    extra_copy = over_tensor(lambda k: exg.at[t], lambda k: exg.at[t], exgs, exgv)
    small_copy = lambda k: send(sm, smr.at[k], sms.at[k], smv.at[k], (d ^ (1 << k), t))

    def started(copy):
        for k in range(1, 4):
            copy(k).start()

    def waited(copy):
        for k in range(1, 4):
            copy(k).wait()

    def load(n, kind):
        at = pl.multiple_of((n % each) * wide, wide)
        if kind == 2:
            return pltpu.make_async_copy(wo_hbm.at[pl.ds(at, wide), :], woring.at[n % 2], wsem.at[kind, n % 2])
        ref = (wg_hbm, wi_hbm)[kind]
        return pltpu.make_async_copy(ref.at[:, pl.ds(at, wide)], wring.at[n % 2, kind], wsem.at[kind, n % 2])

    for n in range(2):
        for kind in range(3):
            load(n, kind).start()

    barrier = pltpu.get_barrier_semaphore()
    for dev in ((pair, t), (peer, t), (line, t), (d ^ 4, t), (d, t ^ 1), (d, t ^ 2), (d, t ^ 3)):
        pl.semaphore_signal(barrier, inc=1, device_id=dev, device_id_type=MESH)
    pl.semaphore_wait(barrier, 7)

    heads = ws.shape[0]
    gain_in[...] = gain_in1[...].reshape(1, width)
    ib[...] = ib1[...].reshape(1, inner)
    gain[...] = gain1[...].reshape(1, inner)
    sb[...] = sb1[...].reshape(1, 4 * span)
    heads_in[...] = jnp.zeros_like(heads_in)
    for n, ref in enumerate((stepb1, decay1, skip1)):
        heads_in[8 * n : 8 * n + 8, 0:heads] = jnp.broadcast_to(ref[...].reshape(1, heads), (8, heads))
    h0 = lax.broadcasted_iota(jnp.int32, (128, inner), 0)
    spread_heads = (h0 == lax.broadcasted_iota(jnp.int32, (128, inner), 1) // HEAD_DIM).astype(f32)
    skipc[...] = mm(heads_in[16:24, :], spread_heads, NN, HIGH)[0:1, :]
    rate_row = -jnp.exp(heads_in[8:9, :])

    def begin_features(f):
        ref = cot if f else nb

        @pl.when(edge)
        def _():
            f1[f] = ref[pl.ds(my_rows, piece), :].astype(f32)
            if f:
                feature1(f, 1).start()

        @pl.when(hub)
        def _():
            fs[f] = ref[pl.ds(my_rows, piece), pl.ds(far, 2 * part)].astype(f32)
            feature2(f).start()

    begin_features(1)
    xv = xin[...].astype(f32)
    scale = lax.rsqrt(jnp.sum(xv * xv, axis=1, keepdims=True) / width + eps)
    nb[...] = (xv * scale * gain_in[...]).astype(bf16)
    inv[...] = jnp.broadcast_to(scale, inv.shape)
    begin_features(0)

    i0 = lax.broadcasted_iota(jnp.int32, (count, count), 0)
    j0 = lax.broadcasted_iota(jnp.int32, (count, count), 1)
    same = (seg_of(i0, lengths) == seg_of(j0, lengths)) & (j0 <= i0)
    addm[...] = jnp.where(same, 0.0, NEG)
    keep = keeps(lengths, count)
    for back in range(1, CONV):
        keep_ref[:, back : back + 1] = keep[back]
    state = mm(nb[...], wst[...])
    state_raw[...] = state
    cv = conv(state, sk[...], sb[...], keep)
    sact[...] = cv * sigmoid(cv)
    g[...] = mm(sact[:, STATE:], sact[:, :STATE], NT, HIGH)
    sraw[...] = jnp.zeros_like(sraw)
    sraw[:, 0:heads] = mm(nb[...], ws[...], NT) + heads_in[0:1, 0:heads]
    step = softplus(sraw[...])
    logs = mm(same.astype(f32), step * rate_row, NN, HIGH)
    lsr[...] = jnp.transpose(logs)
    for k in range(each):
        hc[k, :, 0:HPB] = logs[:, HPB * k : HPB * (k + 1)]
        hc[k, :, HPB : 2 * HPB] = step[:, HPB * k : HPB * (k + 1)]
    for ref in (acc, dg, dlogs, dstep, hsum, sm):
        ref[...] = jnp.zeros_like(ref)

    first = lanes_first((count, 2 * HEAD_DIM))

    def kept():
        return [None] + [keep_ref[:, b : b + 1] for b in range(1, CONV)]

    def steps_of(j, k):
        return jnp.where(first, hc[j, :, HPB + k : HPB + k + 1], hc[j, :, HPB + k + 1 : HPB + k + 2])

    def decay_of(j, h):
        return jnp.exp(hc[j, :, h : h + 1] - lsr[pl.ds(HPB * j + h, 1), :] + addm[...])

    def put(base, j, value):
        for half_block in range(2):
            act[base + 2 * j + half_block] = value[:, lanes * half_block : lanes * (half_block + 1)]

    def take(base, j):
        return jnp.concatenate([act[base + 2 * j], act[base + 2 * j + 1]], axis=1)

    def forward_block(j, carry):
        slot = j % 2
        cols = pl.ds(pl.multiple_of(j * wide, wide), wide)
        for kind in range(3):
            load(j, kind).wait()
        gate = mm(nb[...], wring[slot, 0])
        raw = mm(nb[...], wring[slot, 1])
        scaled = mm(cot[...], woring[slot], NT)
        for kind in range(3):
            load(j + 2, kind).start()
        x[j] = scaled
        x[each + j] = gate
        x[2 * each + j] = raw
        cv = conv(raw, ik[:, cols], ib[:, cols], kept())
        put(2 * each, j, cv)
        v = cv * sigmoid(cv)
        parts = []
        for k in range(0, HPB, 2):
            vs = (v[:, HEAD_DIM * k : HEAD_DIM * (k + 2)] * steps_of(j, k)).astype(bf16)
            ys = [mm((g[...] * decay_of(j, h)).astype(bf16), vs) for h in (k, k + 1)]
            parts.append(jnp.where(first, ys[0], ys[1]))
        mixed = jnp.concatenate(parts, axis=1) + skipc[:, cols] * v
        put(0, j, mixed)
        gated = mixed * (gate * sigmoid(gate))
        acc[:, 0:1] += jnp.sum(gated * gated, axis=1, keepdims=True)
        acc[:, 1:2] += jnp.sum(scaled * gain[:, cols] * gated, axis=1, keepdims=True)

        @pl.when(edge & (j == 1))
        def _():
            feature1(1, 1).wait_send()
            feature1(1, 0).start()

        @pl.when(hub & (j == 1))
        def _():
            feature1(1, 1).wait_recv()
            feature3(1).start()
            feature2(1).wait_recv()
            spread(1, 1)

        return carry

    lax.fori_loop(0, each, forward_block, 0)
    sums[...] = jnp.transpose(acc[...])[0:8, :]
    started(sum_copy)

    @pl.when(hub)
    def _():
        feature1(1, 0).wait_recv()
        spread(1, 0)

    waited(sum_copy)
    total = jnp.transpose(sums[...] + sumr[0] + sumr[1] + sumr[2])
    acc[:, 0:1] = lax.rsqrt(total[:, 0:1] / (4 * inner) + eps)
    acc[:, 1:2] = acc[:, 0:1] * total[:, 1:2] / (4 * inner)

    def unit_block(j, carry):
        cols = pl.ds(pl.multiple_of(j * wide, wide), wide)
        scaled, gate, mixed = x[j], x[each + j], take(0, j)
        inv_gate, dot = acc[:, 0:1], acc[:, 1:2]
        s = sigmoid(gate)
        gate_act = gate * s
        unit = mixed * gate_act * inv_gate
        weights = gain[:, cols]
        x[j] = (unit * weights).astype(bf16).astype(f32)
        sm[8:9, cols] = jnp.sum(scaled * unit, axis=0, keepdims=True)
        d_gated = inv_gate * (scaled * weights - unit * dot)
        dmb[j] = d_gated * gate_act
        x[each + j] = (d_gated * mixed * s * (1.0 + gate * (1.0 - s))).astype(bf16).astype(f32)

        @pl.when(hub & (j < LEAD2))
        def _():
            p2(j).start()

        @pl.when(edge & (j < 2))
        def _():
            p1(j).start()

        return carry

    lax.fori_loop(0, each, unit_block, 0)

    @pl.when(hub)
    def _():
        feature3(1).wait_recv()
        spread(1, 2)

    def forward_features(f, shards=(1, 0, 2)):
        if not f:
            pl.semaphore_wait(fc_free, 1)
        for shard in shards:
            if not f:
                sibling(f, shard, 0).start()
            across(f, shard).wait_recv()
            sibling(f, shard, 1).start()

    def assemble(f):
        own_rows = (cot if f else nb)[:, pl.ds(near, 2 * part)]
        ft[f, :, 0:count] = own_rows.T
        for shard in (1, 0, 2):
            sibling(f, shard, 0).wait_recv()
            sibling(f, shard, 1).wait_recv()
            for k, ref in enumerate((feature(f, shard), fc.at[0, shard], fx.at[f, shard], fc.at[1, shard])):
                xbr[pl.ds(pl.multiple_of((t ^ k) * piece, piece), piece), :] = ref[...].astype(bf16)
            ft[f, :, count * (shard + 1) : count * (shard + 2)] = xbr[...].T
        if f:
            pl.semaphore_signal(fc_free, inc=1, device_id=(d, t ^ 1), device_id_type=MESH)

    def backward_block(j, carry):
        cols = pl.ds(pl.multiple_of(j * wide, wide), wide)
        cv, dm = take(2 * each, j), dmb[j]
        s = sigmoid(cv)
        v = cv * s
        within = take(0, j) - skipc[:, cols] * v
        us, vss, dys, stepm = [], [], [], []
        for k in range(0, HPB, 2):
            lane = slice(HEAD_DIM * k, HEAD_DIM * (k + 2))
            steps = steps_of(j, k)
            vs = (v[:, lane] * steps).astype(bf16)
            dy = dm[:, lane].astype(bf16)
            both = []
            for h in (k, k + 1):
                ratio = decay_of(j, h)
                both.append(mm((g[...] * ratio).astype(bf16), dy, TN))
                part_of = first if h == k else jnp.logical_not(first)
                dg[...] += ratio * mm(jnp.where(part_of, dy, jnp.zeros_like(dy)), vs, NT)
            us.append(jnp.where(first, both[0], both[1]))
            vss.append(vs.astype(f32))
            dys.append(dy.astype(f32))
            stepm.append(steps)
        u, vs, dy, steps = (jnp.concatenate(p, axis=1) for p in (us, vss, dys, stepm))
        c0 = lax.broadcasted_iota(jnp.int32, (wide, 128), 0) // HEAD_DIM
        l0 = lax.broadcasted_iota(jnp.int32, (wide, 128), 1)
        pick = (l0 == c0 + HPB * j).astype(f32)
        dlogs[...] += mm(dy * within - vs * u, pick, NN, HIGH)
        dstep[...] += mm(v * u, pick, NN, HIGH)
        per_lane = jnp.sum(dm * v, axis=0, keepdims=True)
        hsum[...] += mm(jnp.broadcast_to(per_lane, (8, wide)), pick, NN, HIGH)
        dc = (steps * u + skipc[:, cols] * dm) * (s * (1.0 + cv * (1.0 - s)))
        du, rows = conv_back(dc, x[2 * each + j], ik[:, cols], kept())
        x[2 * each + j] = du.astype(bf16).astype(f32)
        sm[0:5, cols] = jnp.concatenate(rows, axis=0)
        return carry

    def backward_end():
        mask = (addm[...] > -1.0).astype(f32)
        q = mm(mask, dlogs[...], TN, HIGH)
        raw = sraw[...]
        step = softplus(raw)
        rate = -jnp.exp(heads_in[8:9, :])
        draw = (dstep[...] + rate * q) * sigmoid(raw)
        dstep[...] = draw.astype(bf16).astype(f32)
        sm[15:16, 0:128] = jnp.sum(draw, axis=0, keepdims=True)
        sm[15:16, 128:256] = rate * jnp.sum(step * q, axis=0, keepdims=True)
        sm[15:16, 256:384] = hsum[0:1, :]
        d_b = mm(dg[...], sact[:, STATE:], TN, HIGH)
        d_c = mm(dg[...], sact[:, :STATE], NN, HIGH)
        both = jnp.concatenate([d_b, d_c], axis=1)
        for i in range(4):
            dstate[i] = both[:, span * i : span * (i + 1)]
        started(state_copy)

    def slab(ref):
        out = None
        for i in range(4):
            one = jnp.where(t == i, ref[:, span * i : span * (i + 1)], 0.0)
            out = one if out is None else out + one
        return out

    def states():
        waited(state_copy)
        total = dstate[t] + dsr[0] + dsr[1] + dsr[2]
        u, kernel = slab(state_raw), slab(sk)
        cv = conv(u, kernel, slab(sb), kept())
        s = sigmoid(cv)
        du, rows = conv_back(total * (s * (1.0 + cv * (1.0 - s))), u, kernel, kept())
        ex[:, 0:span] = du.astype(bf16).astype(f32)
        ex[:, span : 2 * span] = dstep[:, 0:span]
        srr[t] = jnp.concatenate(rows + [jnp.zeros((3, span), f32)], axis=0)
        started(row_copy)

        @pl.when(hub)
        def _():
            p2x().start()

        @pl.when(edge)
        def _():
            p1x().start()

    def out_parts():
        for c in range(each):
            n = each + c
            load(n, 2).wait()
            xc = x[c].astype(bf16)
            for i in range(4):
                one = mm(xc, woring[n % 2, :, share * i : share * (i + 1)])
                po[i] = one if c == 0 else po[i] + one
            if c + 2 < each:
                load(n + 2, 2).start()
        for n in range(2):
            out_near(n).start()

    def out_across():
        for n in range(2):
            out_near(n).wait()
        po[t ^ 2] = po[t ^ 2] + por[1]
        out_far().start()

    def out_sum():
        out_far().wait()
        hidden = xin[:, pl.ds(my_share, share)].astype(f32)
        out_ref[...] = (po[t] + por[0] + por[2] + hidden).astype(bf16)

    def in_parts():
        lane = lax.broadcasted_iota(jnp.int32, (count, 4 * span), 1) // span
        own_state = ex[:, 0:span]
        states4 = jnp.where(lane == t, jnp.concatenate([own_state] * 4, axis=1), 0.0).astype(bf16)
        steps_back = dstep[:, 0:heads].astype(bf16)
        for i in range(4 * tiles):
            rows = slice(lanes * i, lanes * (i + 1))
            act[i] = mm(states4, wst[rows, :], NT) + mm(steps_back, ws[:, rows])
        for c in range(each):
            n = each + c
            load(n, 0).wait()
            load(n, 1).wait()
            gc, ic = x[each + c].astype(bf16), x[2 * each + c].astype(bf16)
            for i in range(2 * tiles):
                rows = slice(2 * lanes * i, 2 * lanes * (i + 1))
                one = mm(gc, wring[n % 2, 0, rows, :], NT) + mm(ic, wring[n % 2, 1, rows, :], NT)
                act[2 * i] = act[2 * i] + one[:, 0:lanes]
                act[2 * i + 1] = act[2 * i + 1] + one[:, lanes:]
            if c + 2 < each:
                load(n + 2, 0).start()
                load(n + 2, 1).start()
        for n in range(2):
            in_near(n).start()

    def in_across():
        for n in range(2):
            in_near(n).wait()
        for i in range(tiles):
            act[tiles * (t ^ 2) + i] = act[tiles * (t ^ 2) + i] + pir[1, i]
        in_far().start()

    def normed():
        return xin[:, pl.ds(my_share, share)].astype(f32) * inv[:, 0:1]

    def in_sum():
        in_far().wait()
        for i in range(tiles):
            po[0, :, lanes * i : lanes * (i + 1)] = act[tiles * t + i] + pir[0, i] + pir[2, i]
        d_normed = po[0]
        dot = jnp.sum(d_normed * gain_in[:, pl.ds(my_share, share)] * normed(), axis=1, keepdims=True)
        dots[...] = jnp.transpose(jnp.broadcast_to(dot, (count, 128)))[0:8, :]
        started(dot_copy)

    def finish():
        waited(dot_copy)
        waited(row_copy)
        d_normed, n = po[0], normed()
        dot = jnp.transpose(dots[...] + dotr[0] + dotr[1] + dotr[2])[:, 0:1] / width
        d_hat = d_normed * gain_in[:, pl.ds(my_share, share)]
        din_ref[...] = inv[:, 0:1] * (d_hat - n * dot) + cot[:, pl.ds(my_share, share)].astype(f32)
        sm[9:10, 0:share] = jnp.sum(d_normed * n, axis=0, keepdims=True)
        for i in range(4):
            sm[10:15, span * i : span * (i + 1)] = srr[i][0:5, :]
        small_copy(0).start()

    def small(k):
        small_copy(k).wait()
        sm[...] = sm[...] + smr[k]
        if k < 2:
            small_copy(k + 1).start()
        else:
            smalls_ref[...] = sm[...]

    def extra_hub():
        p2x().wait_recv()
        p3x().wait_recv()
        for k, ref in enumerate((ex, exr.at[0], exr.at[1], exr.at[2])):
            xb[k * count : (k + 1) * count, 0:128] = ref[...].astype(bf16)
        rx[0] = mm(ft[0, pl.ds(pair_part, part), :], xb[:, 0:128])
        rx[1] = mm(ft[0, pl.ds(mine_part, part), :], xb[:, 0:128])
        e_x().start()
        yx_hub().start()

    def extra_spread(rows):
        exg[t] = rows + yrx[...]
        step_out[...] = jnp.transpose(exg[t])[span : span + heads, :]
        started(extra_copy)

    def extra_end():
        waited(extra_copy)
        for i in range(4):
            state_out[:, span * i : span * (i + 1)] = exg[i, :, 0:span]

    def process(q):
        p2(q).wait_recv()
        p3(q).wait_recv()
        p3(q).wait_send()

        @pl.when(q >= 2)
        def _():
            e(q - 2).wait_send()
            ya(q - 2, 0).wait_send()
            ya(q - 2, 1).wait_send()
            yb_hub(q - 2).wait_send()

        xb[0:count, :] = x[q].astype(bf16)
        xb[count:, :] = big[q % RING].astype(bf16)

        @pl.when(q + RING < chunks)
        def _():
            pl.semaphore_signal(credit, inc=1, device_id=(peer, t), device_id_type=MESH)

        family = jnp.where(q < each, 1, 0)
        slot = q % 2
        r[slot, 0] = mm(ft[family, pl.ds(pair_part, part), :], xb[...])
        e(q).start()
        ya(q, 0).start()
        r[slot, 1] = mm(ft[family, pl.ds(mine_part, part), :], xb[...])
        ya(q, 1).start()
        yb_hub(q).start()

    def stored(q, k):
        at = pl.multiple_of((q % each) * wide, wide)
        out = (turned_out, gate_out, inner_out)[k]
        return pltpu.make_async_copy(fin.at[q % 2], out.at[:, pl.ds(at, wide)], fins.at[q])

    def store(q, left, right):
        slot = q % 2
        for k in range(3):
            @pl.when((q >= k * each + 2) & (q < (k + 1) * each + 2))
            def _():
                stored(q - 2, k).wait()

        fin[slot, :, 0:lanes] = left
        fin[slot, :, lanes:] = right

        for k in range(3):
            @pl.when((q >= k * each) & (q < (k + 1) * each))
            def _():
                stored(q, k).start()

    def finalize_hub(q):
        slot = q % 2
        ya(q, 0).wait_recv()
        ya(q, 1).wait_recv()
        yb_hub(q).wait_recv()

        @pl.when(q >= 2)
        def _():
            fa(q - 2).wait_send()

        got = yra.at[q % RING]
        ea[slot] = r[slot, 0, pl.ds(mine, own), 0:lanes] + got[0]
        fa(q).start()
        store(
            q,
            r[slot, 1, pl.ds(mine, own), 0:lanes] + got[1],
            r[slot, 1, pl.ds(mine, own), lanes:] + yrb[q % LEAD],
        )

    def finalize_edge(q):
        yb_edge(q).wait_recv()
        fa(q).wait_recv()
        store(q, yra[q % RING, 0], big[q % RING, pl.ds(mine, own), 0:lanes] + yrb[q % LEAD])

    pieces = {
        1: backward_end, 2: out_parts, 3: [states, out_across], 4: in_parts, 5: out_sum, 6: in_across, 8: in_sum,
        9: finish, 10: lambda: small(0), 12: lambda: small(1), 15: lambda: small(2), 14: extra_end,
    }

    lax.fori_loop(0, 2, backward_block, 0)

    @pl.when(hub)
    def _():
        p1(0).wait_recv()
        p3(0).start()
        p2(LEAD2).start()
        forward_features(1, (1, 0))

    @pl.when(edge)
    def _():
        p1(0).wait_send()
        p1(2).start()

    lax.fori_loop(2, each, backward_block, 0)

    @pl.when(hub)
    def _():
        forward_features(1, (2,))
        assemble(1)

    @pl.when(edge)
    def _():
        for n in range(3, LEAD):
            p1(n - 2).wait_send()
            p1(n).start()
        feature1(0, 1).start()
        feature1(0, 0).start()

    def body(q, carry):
        @pl.when(hub)
        def _():
            @pl.when((q >= 1) & (q < chunks))
            def _():
                p1(q).wait_recv()
                p3(q).start()

            @pl.when((q >= 1) & (q + LEAD2 < chunks))
            def _():
                @pl.when(q + LEAD2 >= RING)
                def _():
                    pl.semaphore_wait(credit, 1)

                p2(q + LEAD2).start()

            @pl.when((q >= 1) & (q <= chunks))
            def _():
                process(q - 1)

            @pl.when(q >= 2)
            def _():
                finalize_hub(q - 2)

            @pl.when(q == 2)
            def _():
                feature1(0, 1).wait_recv()
                feature3(0).start()
                feature1(0, 0).wait_recv()
                spread(0, 0)
                feature2(0).wait_recv()
                spread(0, 1)

            @pl.when(q == 3)
            def _():
                feature3(0).wait_recv()
                spread(0, 2)

            @pl.when(q == 4)
            def _():
                forward_features(0)

            @pl.when(q == 5)
            def _():
                assemble(0)

            @pl.when(q == 7)
            def _():
                p1x().wait_recv()
                p3x().start()

            @pl.when(q == 8)
            def _():
                extra_hub()

            @pl.when(q == 11)
            def _():
                yx_hub().wait_recv()
                extra_spread(rx[1, pl.ds(mine, own), :])

        for at, jobs in pieces.items():
            for job in jobs if isinstance(jobs, list) else [jobs]:
                pl.when(q == at)(job)

        @pl.when(edge)
        def _():
            @pl.when(q < chunks)
            def _():
                e(q).wait_recv()
                yb_edge(q).start()

            @pl.when(q + LEAD < chunks)
            def _():
                @pl.when(q >= 2)
                def _():
                    yb_edge(q - 2).wait_send()

                p1(q + LEAD).start()

            @pl.when((q >= 1) & (q <= chunks))
            def _():
                finalize_edge(q - 1)

            @pl.when(q == 9)
            def _():
                e_x().wait_recv()
                yx_edge().start()

            @pl.when(q == 11)
            def _():
                yx_edge().wait_recv()
                extra_spread(exe[pl.ds(mine, own), :])

        return carry

    lax.fori_loop(0, chunks + 2, body, 0)

    stored(chunks - 2, 2).wait()
    stored(chunks - 1, 2).wait()

    @pl.when(hub)
    def _():
        def drain(q, carry):
            p2(q).wait_send()
            return carry

        lax.fori_loop(0, chunks, drain, 0)
        for q in (chunks - 2, chunks - 1):
            e(q).wait_send()
            ya(q, 0).wait_send()
            ya(q, 1).wait_send()
            yb_hub(q).wait_send()
            fa(q).wait_send()
        for f in range(2):
            feature2(f).wait_send()
            feature3(f).wait_send()
            for shard in range(3):
                across(f, shard).wait_send()
                sibling(f, shard, 0).wait_send()
                sibling(f, shard, 1).wait_send()
        p2x().wait_send()
        p3x().wait_send()
        e_x().wait_send()
        yx_hub().wait_send()

    @pl.when(edge)
    def _():
        def drain(q, carry):
            p1(q).wait_send()
            return carry

        lax.fori_loop(LEAD - 2, chunks, drain, 0)
        for q in range(chunks - LEAD - 2, chunks):
            yb_edge(q).wait_send()
        feature1(1, 0).wait_send()
        feature1(0, 0).wait_send()
        feature1(0, 1).wait_send()
        p1x().wait_send()
        yx_edge().wait_send()


def outputs_kernel(
    smalls, a, b, c, d, e, f, g,
    norm_gain, inner_kernel, inner_bias, state_kernel_out, state_bias, step_bias, decay, skip, gate_gain,
    ao, bo, co, do, eo, fo, go, at_, bt, ct, dt, et, ft, gt, loads, stores,
):
    through = list(zip((a, b, c, d, e, f, g), (at_, bt, ct, dt, et, ft, gt), (ao, bo, co, do, eo, fo, go)))
    load = lambda n: pltpu.make_async_copy(through[n][0], through[n][1], loads.at[n])
    keep = lambda n: pltpu.make_async_copy(through[n][1], through[n][2], stores.at[n])
    for n in range(len(through)):
        load(n).start()
    for ref, at, lane in (
        (norm_gain, 9, 0), (inner_bias, CONV, 0), (state_bias, 10 + CONV, 0), (step_bias, 15, 0), (decay, 15, 128),
        (skip, 15, 256), (gate_gain, 8, 0),
    ):
        ref[...] = smalls[at : at + 1, lane : lane + ref.shape[0]].reshape(ref.shape)
    inner_kernel[...] = smalls[0:CONV, :]
    state_kernel_out[...] = smalls[10 : 10 + CONV, 0 : state_kernel_out.shape[1]]
    for n in range(len(through)):
        load(n).wait()
        keep(n).start()
    for n in range(len(through)):
        keep(n).wait()


def whole(shape):
    return pl.BlockSpec(shape, lambda *_: (0,) * len(shape))


def columns(rows):
    return pl.BlockSpec((rows, BLK), lambda j, *_: (0, j))


SMEM = pl.BlockSpec(memory_space=pltpu.SMEM)
VM = pltpu.CompilerParams(vmem_limit_bytes=56 << 20)
VMS = pltpu.CompilerParams(vmem_limit_bytes=56 << 20, dimension_semantics=("arbitrary",))


def struct(shape, dtype=f32):
    return jax.ShapeDtypeStruct(shape, dtype)


def cost(flops, moved):
    return pl.CostEstimate(flops=int(flops), bytes_accessed=int(moved), transcendentals=0)


def on_device(
    block_input, cotangent, seq_lengths, norm_gain, gate_weight, inner_weight, step_weight, state_weight,
    inner_kernel, inner_bias, state_kernel_, state_bias, step_bias, decay_log, skip_scale, gate_gain, output_weight,
):
    parts = lax.axis_size("tensor")
    shards = lax.axis_size("dp")
    t = lax.axis_index("tensor")
    count, width = block_input.shape
    inner = gate_weight.shape[1]
    heads = step_bias.shape[0]
    share = width // parts
    span = 2 * STATE // parts
    steps = inner // BLK
    pad = ((0, 0), (0, 128 - heads))
    row = lambda x: x.reshape(1, -1)

    def swap(x, k):
        return lax.ppermute(x, "tensor", [(i, i ^ k) for i in range(parts)])

    chunks = 3 * steps
    slab = lambda x, size: lax.dynamic_slice_in_dim(x, t * size, size, x.ndim - 1)
    if shards == 8 and parts == 4:
        own, half_blk, piece, near = width // 8, BLK // 2, count // parts, width // 2
        dma, v = pltpu.SemaphoreType.DMA, lambda *shape: pltpu.VMEM(shape, f32)
        vb = lambda *shape: pltpu.VMEM(shape, bf16)
        vmem, hbm = pl.BlockSpec(memory_space=pltpu.VMEM), pl.BlockSpec(memory_space=pl.ANY)
        scratch = [
            v(chunks, count, BLK), v(4 * steps, count, half_blk), v(steps, count, BLK), vb(count, width),
            v(count, 128), v(1, width), v(1, inner), v(1, 2 * STATE), v(24, 128), v(1, inner), v(1, inner), v(2, piece, near), v(2, piece, width), v(2, piece, near), v(2, piece, near),
            v(2, 3, piece, near), v(2, 3, piece, near), vb(2, near, 4 * count), v(RING, 3 * count, BLK),
            v(RING, 2, own, half_blk), v(LEAD, own, half_blk), v(2, 2, 2 * own, BLK), v(2, own, half_blk), v(2, own, BLK),
            vb(4 * count, BLK), vb(count, near), vb(2, 2, width, BLK), vb(2, BLK, width),
            v(4, count, share), v(3, count, share), v(3, share // half_blk, count, half_blk),
            v(count, count), v(count, count), v(steps, count, 128), v(128, count), v(count, 2 * STATE), v(count, 2 * STATE),
            v(count, 128), v(count, 128), v(count, count), v(count, 128), v(count, 128), v(8, 128), v(count, 128),
            v(8, count), v(3, 8, count), v(4, count, span), v(3, count, span), v(4, 8, span), v(16, inner), v(3, 16, inner),
            v(count, 128), v(3, count, 128), v(2, 2 * own, 128), v(2 * own, 128), v(own, 128), v(4, own, 128),
            v(8, count), v(3, 8, count),
        ]
        scratch += [dma((chunks,))] * 8 + [dma((chunks, 2))] * 2 + [dma((chunks,))] * 5 + [dma((3, 2))] + [dma((3,))] * 14
        scratch += [dma((4,))] * 2 + [dma((1,))] * 2 + [dma((3,))] * 2 + [dma((2, 2))] * 2 + [dma((2,))] * 4 + [dma((2, 3))] * 2
        scratch += [dma((2, 2, 3))] * 2 + [pltpu.SemaphoreType.REGULAR] * 2
        shapes = [
            struct((count, share), bf16), struct((count, share)), struct((own, inner)), struct((own, inner)),
            struct((own, 2 * STATE)), struct((heads, own)), struct((own, inner)),
        ]
        *large, smalls = pl.pallas_call(
            layer_kernel,
            in_specs=[SMEM] + [vmem] * 13 + [hbm] * 3,
            out_specs=[vmem, vmem, hbm, hbm, vmem, vmem, hbm, vmem],
            out_shape=shapes + [struct((16, inner))],
            scratch_shapes=scratch,
            compiler_params=pltpu.CompilerParams(collective_id=1, has_side_effects=True, vmem_limit_bytes=VMEM_LIMIT),
            name="layer",
        )(
            seq_lengths, block_input, cotangent, norm_gain, step_weight.T, state_weight, inner_kernel, inner_bias,
            state_kernel_, state_bias, step_bias, decay_log, skip_scale, gate_gain, gate_weight, inner_weight, output_weight,
        )
        cut = [
            struct((share,)), struct((CONV, inner)), struct((inner,)), struct((CONV, 2 * STATE)), struct((2 * STATE,)),
            struct((heads,)), struct((heads,)), struct((heads,)), struct((inner,)),
        ]
        *smalls, out, into, gate_grad, inner_grad, state_grad, step_grad, output_grad = pl.pallas_call(
            outputs_kernel,
            in_specs=[vmem] + [hbm] * 7,
            out_specs=[vmem] * 9 + [hbm] * 7,
            out_shape=cut + shapes,
            scratch_shapes=[pltpu.VMEM(a.shape, a.dtype) for a in shapes] + [dma((7,)), dma((7,))],
            compiler_params=VM,
            name="outputs",
        )(smalls, *large)
        return (
            out, into, smalls[0], gate_grad, inner_grad, step_grad.T, state_grad, *smalls[1:9], output_grad.T,
        )

    padded_step = jnp.pad(step_weight, pad)
    stepb, decay = jnp.pad(row(step_bias), pad), jnp.pad(row(decay_log), pad)
    skipc = jnp.repeat(skip_scale, HEAD_DIM).reshape(1, -1)
    ik, ib, gain = inner_kernel, row(inner_bias), row(gate_gain)
    full = struct((count, inner))
    nb, inv = pl.pallas_call(
        norm_kernel,
        out_shape=(struct((count, width), bf16), struct((count, 128))),
        compiler_params=VM,
        name="norm_in",
    )(block_input, row(norm_gain))

    graw, iraw, cv, mixed, scaled, sums, sraw, sact, state_raw, hc, lsr, addm, g, keep = pl.pallas_call(
        forward_kernel,
        grid=(steps,),
        in_specs=[
            SMEM, whole((count, width)), whole((count, width)), columns(width), columns(width),
            pl.BlockSpec((BLK, width), lambda j: (j, 0)), whole((width, 128)), whole((width, 2 * STATE)),
            columns(CONV), columns(1), whole((CONV, 2 * STATE)), whole((1, 2 * STATE)), whole((1, 128)), whole((1, 128)),
            columns(1), columns(1),
        ],
        out_specs=(
            [columns(count)] * 5
            + [whole((8, count)), whole((count, 128)), whole((count, 2 * STATE)), whole((count, 2 * STATE)),
               whole((steps, count, 128)), whole((128, count)), whole((count, count)), whole((count, count)),
               whole((count, 128))]
        ),
        out_shape=(
            [full] * 5
            + [struct((8, count)), struct((count, 128)), struct((count, 2 * STATE)), struct((count, 2 * STATE)),
               struct((steps, count, 128)), struct((128, count)), struct((count, count)), struct((count, count)),
               struct((count, 128))]
        ),
        scratch_shapes=[pltpu.VMEM((count, 128), f32)],
        compiler_params=VMS,
        cost_estimate=cost(6 * count * width * inner, 6 * width * inner + 20 * count * inner),
        name="forward",
    )(
        seq_lengths, nb, cotangent, gate_weight, inner_weight, output_weight, padded_step, state_weight, ik, ib,
        state_kernel_, row(state_bias), stepb, decay, skipc, gain,
    )

    all_sums = jnp.stack([sums] + [swap(sums, k) for k in range(1, parts)])
    x, dm, gg = pl.pallas_call(
        partial(unit_kernel, float(inner * parts)),
        grid=(steps,),
        in_specs=[whole((parts, 8, count)), columns(count), columns(count), columns(count), columns(1)],
        out_specs=[pl.BlockSpec((2, 1, count, BLK), lambda j: (0, j, 0, 0)), columns(count), columns(8)],
        out_shape=[struct((3, steps, count, BLK)), full, struct((8, inner))],
        compiler_params=VMS,
        cost_estimate=cost(0, 24 * count * inner),
        name="unit",
    )(all_sums, graw, mixed, scaled, gain)

    x, rows, sback, hrows, dstate = pl.pallas_call(
        backward_kernel,
        grid=(steps,),
        in_specs=[
            SMEM, columns(count), columns(count), columns(count), columns(count),
            pl.BlockSpec((1, count, 128), lambda j: (j, 0, 0)), whole((128, count)), whole((count, count)),
            whole((count, count)), whole((count, 128)), whole((count, 2 * STATE)), columns(CONV), columns(1), whole((1, 128)),
            pl.BlockSpec(memory_space=pl.ANY),
        ],
        input_output_aliases={14: 0},
        out_specs=[pl.BlockSpec((1, 1, count, BLK), lambda j: (2, j, 0, 0)), columns(8), whole((count, 128)), whole((8, 128)), whole((parts, count, span))],
        out_shape=[struct((3, steps, count, BLK)), struct((8, inner)), struct((count, 128)), struct((8, 128)), struct((parts, count, span))],
        scratch_shapes=[pltpu.VMEM((count, count), f32), pltpu.VMEM((count, 128), f32), pltpu.VMEM((count, 128), f32)],
        compiler_params=VMS,
        cost_estimate=cost(40 * count * count * inner // 64 * 4, 24 * count * inner),
        name="backward",
    )(seq_lengths, dm, cv, iraw, mixed, hc, lsr, addm, g, sraw, sact, ik, skipc, decay, x)

    uo, gb, back = (jnp.swapaxes(x[i], 0, 1).reshape(count, inner) for i in range(3))

    def to_parts(x, axis):
        size = x.shape[axis] // parts
        block = lambda i: lax.dynamic_slice_in_dim(x, i * size, size, axis)
        got = [swap(block(t ^ k), k) for k in range(1, parts)]
        return [block(t)] + got

    def from_parts(x):
        got = jnp.stack([x] + [swap(x, k) for k in range(1, parts)])
        return jnp.stack([lax.dynamic_index_in_dim(got, t ^ i, 0, False) for i in range(parts)])

    state_parts = jnp.concatenate(to_parts(dstate, 0), axis=0)
    sq, srows = pl.pallas_call(
        state_kernel,
        in_specs=[SMEM] + [pl.BlockSpec(memory_space=pltpu.VMEM)] * 4,
        out_shape=(struct((count, span)), struct((8, span))),
        compiler_params=VM,
        name="state_back",
    )(seq_lengths, state_parts, slab(state_raw, span), slab(state_kernel_, span), row(slab(state_bias, span)))

    hidden = slab(block_input, share).astype(f32)
    cot_share = slab(cotangent, share).astype(f32)
    out_parts = to_parts(mm(uo.astype(bf16), output_weight), 1)
    block_output = (sum(out_parts[1:], out_parts[0]) + hidden).astype(bf16)

    gbb, ibb, sbb, qb = (x.astype(bf16) for x in (gb, back, sback[:, :heads], sq))
    partial_in = (
        mm(gbb, gate_weight, NT) + mm(ibb, inner_weight, NT) + mm(sbb, step_weight, NT)
        + mm(qb, slab(state_weight, span), NT)
    )
    in_parts = to_parts(partial_in, 1)
    d_normed = sum(in_parts[1:], in_parts[0])
    inv_in = inv[:, 0:1]
    normed = hidden * inv_in
    gain_share = row(slab(norm_gain, share))
    d_hat = d_normed * gain_share
    dot = jnp.sum(d_hat * normed, axis=1).reshape(-1, 128)
    dot = sum((swap(dot, k) for k in range(1, parts)), dot).reshape(-1, 1) / width
    input_gradient = inv_in * (d_hat - normed * dot) + cot_share
    norm_gain_grad = jnp.sum(d_normed * normed, axis=0)

    extra = jnp.concatenate([sq, sback[:, :heads], jnp.zeros((count, 128 - span - heads), f32)], axis=1)

    def scatter(a, b):
        return lax.psum_scatter(mm(a, b.astype(bf16), TN), "dp", scatter_dimension=0, tiled=True)

    output_grad = scatter(cotangent, uo).T
    gate_grad, inner_grad, extra_grad = scatter(nb, gb), scatter(nb, back), scatter(nb, extra)

    def over_dp(x):
        return lax.psum(x, "dp")

    step_grad = extra_grad[:, span : span + heads]
    state_grad = jnp.swapaxes(from_parts(extra_grad[:, :span]), 0, 1).reshape(-1, 2 * STATE)
    misc = jnp.concatenate([hrows[0], hrows[1], srows[: CONV + 1].reshape(-1), norm_gain_grad])
    misc = jnp.pad(misc, (0, -misc.shape[0] % 1024)).reshape(8, -1)
    smalls = over_dp(jnp.concatenate([rows, gg], axis=0))
    misc = over_dp(misc).reshape(-1)
    step_bias_grad, decay_grad = misc[:heads], misc[128 : 128 + heads]
    state_rows = from_parts(misc[256 : 256 + (CONV + 1) * span].reshape(CONV + 1, span))
    state_rows = jnp.swapaxes(state_rows, 0, 1).reshape(CONV + 1, 2 * STATE)
    at = 256 + (CONV + 1) * span
    skip_grad = jnp.sum(smalls[CONV + 1].reshape(heads, HEAD_DIM), axis=1)
    return (
        block_output,
        input_gradient,
        misc[at : at + share],
        gate_grad,
        inner_grad,
        step_grad,
        state_grad,
        smalls[:CONV],
        smalls[CONV],
        state_rows[:CONV],
        state_rows[CONV],
        step_bias_grad,
        decay_grad,
        skip_grad,
        smalls[8],
        output_grad,
    )


def solution(mesh):
    return jax.shard_map(
        on_device,
        mesh=mesh,
        in_specs=(
            P("dp", None), P("dp", None), P("dp", None), P(), P(None, "tensor"), P(None, "tensor"), P(None, "tensor"), P(),
            P(None, "tensor"), P("tensor"), P(), P(), P("tensor"), P("tensor"), P("tensor"), P("tensor"), P("tensor", None),
        ),
        out_specs=(
            P("dp", "tensor"), P("dp", "tensor"), P("tensor"), P("dp", "tensor"), P("dp", "tensor"), P("dp", "tensor"),
            P("dp", None), P(None, "tensor"), P("tensor"), P(), P(), P("tensor"), P("tensor"), P("tensor"), P("tensor"),
            P("tensor", "dp"),
        ),
        check_vma=False,
    )
```

```python
from functools import partial

import jax
import jax.numpy as jnp
from jax import lax
from jax.experimental import pallas as pl
from jax.experimental.pallas import tpu as pltpu
from jax.sharding import PartitionSpec as P

HEAD_DIM = 64
STATE = 128
CONV = 4
BLK = 256
HPB = BLK // HEAD_DIM
eps = 1e-05
NEG = -1e30
f32 = jnp.float32
bf16 = jnp.bfloat16
HIGH = lax.Precision.HIGHEST
NN = (((1,), (0,)), ((), ()))
NT = (((1,), (1,)), ((), ()))
TN = (((0,), (0,)), ((), ()))


def mm(a, b, dims=NN, precision=None):
    return lax.dot_general(a, b, dims, precision=precision, preferred_element_type=f32)


def sigmoid(x):
    return 1.0 / (1.0 + jnp.exp(-x))


def softplus(x):
    return jnp.maximum(x, 0.0) + jnp.log1p(jnp.exp(-jnp.abs(x)))


def seg_of(places, lengths):
    total = jnp.zeros(places.shape, jnp.int32)
    end = jnp.int32(0)
    for s in range(lengths.shape[1]):
        end = end + lengths[0, s]
        total = total + (places >= end).astype(jnp.int32)
    return total


def keeps(lengths, count):
    t = lax.broadcasted_iota(jnp.int32, (count, 1), 0)
    own = seg_of(t, lengths)
    out = [None]
    for back in range(1, CONV):
        out.append(((seg_of(t - back, lengths) == own) & (t >= back)).astype(f32))
    return out


def down(x, back):
    return pltpu.roll(x, back, 0)


def up(x, back):
    return pltpu.roll(x, x.shape[0] - back, 0)


def conv(u, kernel, bias, keep):
    out = bias + kernel[CONV - 1 : CONV, :] * u
    for back in range(1, CONV):
        out = out + kernel[CONV - 1 - back : CONV - back, :] * (down(u, back) * keep[back])
    return out


def conv_back(dc, u, kernel, keep):
    du = kernel[CONV - 1 : CONV, :] * dc
    rows = [jnp.sum(dc * u, axis=0, keepdims=True)]
    for back in range(1, CONV):
        kept = dc * keep[back]
        du = du + kernel[CONV - 1 - back : CONV - back, :] * up(kept, back)
        rows.append(jnp.sum(kept * down(u, back), axis=0, keepdims=True))
    return du, rows[::-1] + [jnp.sum(dc, axis=0, keepdims=True)]


def lanes_first(shape):
    return lax.broadcasted_iota(jnp.int32, shape, 1) < HEAD_DIM


def norm_kernel(x_ref, gain_ref, nb_ref, inv_ref):
    x = x_ref[...].astype(f32)
    inv = lax.rsqrt(jnp.sum(x * x, axis=1, keepdims=True) / x.shape[1] + eps)
    nb_ref[...] = (x * inv * gain_ref[...]).astype(bf16)
    inv_ref[...] = jnp.broadcast_to(inv, inv_ref.shape)


def forward_kernel(
    lengths, nb_ref, cot_ref, wg_ref, wi_ref, wo_ref, ws_ref, wst_ref, ik_ref, ib_ref, sk_ref, sb_ref,
    stepb_ref, decay_ref, skipc_ref, gain_ref,
    graw_ref, iraw_ref, cv_ref, mixed_ref, scaled_ref, sums_ref, sraw_ref, sact_ref, state_ref, hc_ref, lsr_ref,
    addm_ref, g_ref, keep_ref, acc,
):
    j = pl.program_id(0)
    count = nb_ref.shape[0]
    nb = nb_ref[...]

    @pl.when(j == 0)
    def _():
        i0 = lax.broadcasted_iota(jnp.int32, (count, count), 0)
        j0 = lax.broadcasted_iota(jnp.int32, (count, count), 1)
        same = (seg_of(i0, lengths) == seg_of(j0, lengths)) & (j0 <= i0)
        addm_ref[...] = jnp.where(same, 0.0, NEG)
        state = mm(nb, wst_ref[...])
        state_ref[...] = state
        keep = keeps(lengths, count)
        for back in range(1, CONV):
            keep_ref[:, back : back + 1] = keep[back]
        cv = conv(state, sk_ref[...], sb_ref[...], keep)
        act = cv * sigmoid(cv)
        sact_ref[...] = act
        g_ref[...] = mm(act[:, STATE:], act[:, :STATE], NT, HIGH)
        raw = mm(nb, ws_ref[...]) + stepb_ref[...]
        sraw_ref[...] = raw
        step = softplus(raw)
        logs = mm(same.astype(f32), step * (-jnp.exp(decay_ref[...])), NN, HIGH)
        lsr_ref[...] = jnp.transpose(logs)
        for k in range(hc_ref.shape[0]):
            hc_ref[k, :, 0:HPB] = logs[:, HPB * k : HPB * (k + 1)]
            hc_ref[k, :, HPB : 2 * HPB] = step[:, HPB * k : HPB * (k + 1)]
        acc[...] = jnp.zeros_like(acc)

    gate = mm(nb, wg_ref[...])
    inner = mm(nb, wi_ref[...])
    scaled = mm(cot_ref[...], wo_ref[...], NT)
    graw_ref[...] = gate
    iraw_ref[...] = inner
    scaled_ref[...] = scaled
    cv = conv(inner, ik_ref[...], ib_ref[...], keeps(lengths, count))
    cv_ref[...] = cv
    v = cv * sigmoid(cv)
    first = lanes_first((count, 2 * HEAD_DIM))
    addm = addm_ref[...]
    g = g_ref[...]
    parts = []
    for pair in range(BLK // (2 * HEAD_DIM)):
        vp = v[:, 2 * HEAD_DIM * pair : 2 * HEAD_DIM * (pair + 1)]
        k = 2 * pair
        steps = jnp.where(first, hc_ref[j, :, HPB + k : HPB + k + 1], hc_ref[j, :, HPB + k + 1 : HPB + k + 2])
        vs = (vp * steps).astype(bf16)
        ys = []
        for h in (k, k + 1):
            gaps = hc_ref[j, :, h : h + 1] - lsr_ref[pl.ds(HPB * j + h, 1), :] + addm
            ys.append(mm((g * jnp.exp(gaps)).astype(bf16), vs))
        parts.append(jnp.where(first, ys[0], ys[1]))
    mixed = jnp.concatenate(parts, axis=1) + skipc_ref[...] * v
    mixed_ref[...] = mixed
    gated = mixed * (gate * sigmoid(gate))
    acc[:, 0:1] += jnp.sum(gated * gated, axis=1, keepdims=True)
    acc[:, 1:2] += jnp.sum(scaled * gain_ref[...] * gated, axis=1, keepdims=True)

    @pl.when(j == pl.num_programs(0) - 1)
    def _():
        sums_ref[...] = jnp.transpose(acc[...])[0:8, :]


def unit_kernel(width, s_ref, graw_ref, mixed_ref, scaled_ref, gain_ref, x_ref, dm_ref, gg_ref):
    sums = jnp.sum(s_ref[...], axis=0)
    cols = jnp.transpose(sums)
    inv = lax.rsqrt(cols[:, 0:1] / width + eps)
    dot = inv * cols[:, 1:2]
    gate, mixed, scaled, gain = graw_ref[...], mixed_ref[...], scaled_ref[...], gain_ref[...]
    s = sigmoid(gate)
    act = gate * s
    unit = mixed * act * inv
    x_ref[0, 0] = (unit * gain).astype(bf16).astype(f32)
    gg_ref[...] = jnp.broadcast_to(jnp.sum(scaled * unit, axis=0, keepdims=True), gg_ref.shape)
    d_gated = inv * (scaled * gain - unit * (dot / width))
    dm_ref[...] = d_gated * act
    x_ref[1, 0] = (d_gated * mixed * s * (1.0 + gate * (1.0 - s))).astype(bf16).astype(f32)


def backward_kernel(
    lengths, dm_ref, cv_ref, iraw_ref, mixed_ref, hc_ref, lsr_ref, addm_ref, g_ref, sraw_ref, sact_ref,
    ik_ref, skipc_ref, decay_ref, _,
    back_ref, rows_ref, sback_ref, hrows_ref, dstate_ref, dg, dlogs, dstep,
):
    j = pl.program_id(0)
    count = dm_ref.shape[0]

    @pl.when(j == 0)
    def _():
        dg[...] = jnp.zeros_like(dg)
        dlogs[...] = jnp.zeros_like(dlogs)
        dstep[...] = jnp.zeros_like(dstep)

    cv, dm, skipc = cv_ref[...], dm_ref[...], skipc_ref[...]
    s = sigmoid(cv)
    v = cv * s
    within = mixed_ref[...] - skipc * v
    first = lanes_first((count, 2 * HEAD_DIM))
    addm = addm_ref[...]
    g = g_ref[...]
    us, vss, dyb, stepm = [], [], [], []
    total = dg[...]
    for pair in range(BLK // (2 * HEAD_DIM)):
        cols = slice(2 * HEAD_DIM * pair, 2 * HEAD_DIM * (pair + 1))
        k = 2 * pair
        steps = jnp.where(first, hc_ref[0, :, HPB + k : HPB + k + 1], hc_ref[0, :, HPB + k + 1 : HPB + k + 2])
        vs = (v[:, cols] * steps).astype(bf16)
        dy = dm[:, cols].astype(bf16)
        both = []
        for h in (k, k + 1):
            gaps = hc_ref[0, :, h : h + 1] - lsr_ref[pl.ds(HPB * j + h, 1), :] + addm
            decay = jnp.exp(gaps)
            both.append(mm((g * decay).astype(bf16), dy, TN))
            mine = first if h == k else jnp.logical_not(first)
            total = total + decay * mm(jnp.where(mine, dy, jnp.zeros_like(dy)), vs, NT)
        us.append(jnp.where(first, both[0], both[1]))
        vss.append(vs.astype(f32))
        dyb.append(dy.astype(f32))
        stepm.append(steps)
    dg[...] = total
    u = jnp.concatenate(us, axis=1)
    vs = jnp.concatenate(vss, axis=1)
    dy = jnp.concatenate(dyb, axis=1)
    steps = jnp.concatenate(stepm, axis=1)
    c0 = lax.broadcasted_iota(jnp.int32, (BLK, 128), 0) // HEAD_DIM
    l0 = lax.broadcasted_iota(jnp.int32, (BLK, 128), 1)
    pick = (l0 == c0 + HPB * j).astype(f32)
    dlogs[...] += mm(dy * within - vs * u, pick, NN, HIGH)
    dstep[...] += mm(v * u, pick, NN, HIGH)
    dv = steps * u + skipc * dm
    dc = dv * (s * (1.0 + cv * (1.0 - s)))
    du, rows = conv_back(dc, iraw_ref[...], ik_ref[...], keeps(lengths, count))
    back_ref[0, 0] = du.astype(bf16).astype(f32)
    rows_ref[...] = jnp.concatenate(rows + [jnp.sum(dm * v, axis=0, keepdims=True)] + [jnp.zeros((2, BLK), f32)], axis=0)

    @pl.when(j == pl.num_programs(0) - 1)
    def _():
        mask = (addm > -1.0).astype(f32)
        q = mm(mask, dlogs[...], TN, HIGH)
        raw = sraw_ref[...]
        step = softplus(raw)
        rate = -jnp.exp(decay_ref[...])
        draw = (dstep[...] + rate * q) * sigmoid(raw)
        sback_ref[...] = draw.astype(bf16).astype(f32)
        hrows_ref[...] = jnp.concatenate(
            [jnp.sum(draw, axis=0, keepdims=True), rate * jnp.sum(step * q, axis=0, keepdims=True), jnp.zeros((6, 128), f32)],
            axis=0,
        )
        act = sact_ref[...]
        d_b = mm(dg[...], act[:, STATE:], TN, HIGH)
        d_c = mm(dg[...], act[:, :STATE], NN, HIGH)
        both = jnp.concatenate([d_b, d_c], axis=1)
        span = dstate_ref.shape[2]
        for t in range(dstate_ref.shape[0]):
            dstate_ref[t] = both[:, span * t : span * (t + 1)]


def state_kernel(lengths, parts_ref, u_ref, sk_ref, sb_ref, back_ref, rows_ref):
    keep = keeps(lengths, u_ref.shape[0])
    cv = conv(u_ref[...], sk_ref[...], sb_ref[...], keep)
    s = sigmoid(cv)
    dc = jnp.sum(parts_ref[...], axis=0) * (s * (1.0 + cv * (1.0 - s)))
    du, rows = conv_back(dc, u_ref[...], sk_ref[...], keep)
    back_ref[...] = du.astype(bf16).astype(f32)
    rows_ref[...] = jnp.concatenate(rows + [jnp.zeros((3, du.shape[1]), f32)], axis=0)


MESH = pl.DeviceIdType.MESH
RING = 6
VMEM_LIMIT = 64 << 20
LEAD = 4
LEAD2 = 1


def layer_kernel(
    lengths, xin_hbm, cot_hbm, gain_in1, ws, wst_hbm, ik, ib1, sk, sb1, stepb1, decay1, skip1, gain1, wg_hbm, wi_hbm, wo_hbm,
    out_ref, din_ref, gate_out, inner_out, state_out, step_out, turned_out, smalls_ref,
    xin, cot, wst, x, act, dmb, nb, inv, gain_in, ib, sb, heads_in, skipc, gain, fs, f1, f2, f3, fx, fc, ft, big, yra, yrb, r, ea, fin, xb, xbr, wring, woring, po, por, pir, addm, g, hc, lsr, sact, state_raw, sraw, keep_ref, dg, dlogs, dstep, hsum, acc, sums, sumr, dstate, dsr, srr, sm, smr,
    ex, exr, rx, exe, yrx, exg, dots, dotr,
    p1s, p1v, p2s, p2v, p3s, p3v, es, ev, yas, yav, ybs, ybv, fas, fav, fins, wsem, pos, pov, pis, piv,
    dss, dsv, srs, srv, dts, dtv, sus, suv, sms, smv, exs, exv, yxs, yxv, exgs, exgv,
    f1s, f1v, f2s, f2v, f3s, f3v, fxs, fxv, fcs, fcv, early, credit, fc_free,
):
    d, t = lax.axis_index("dp"), lax.axis_index("tensor")
    y, z = d % 2, d // 2
    side, half = z % 2, z // 2
    hub = (z == 1) | (z == 2)
    edge = jnp.logical_not(hub)
    chunks, count, wide = x.shape
    each = chunks // 3
    lanes = wide // 2
    width = xin.shape[1]
    part = width // 4
    own = part // 2
    share = width // 4
    span = dsr.shape[2]
    inner = each * wide
    piece = f1.shape[1]
    pair, peer, line = d ^ 2, d ^ 6, d ^ 1
    mine, other = pl.multiple_of(own * y, own), pl.multiple_of(own * (1 - y), own)
    mine_part, pair_part = pl.multiple_of(part * side, part), pl.multiple_of(part * (1 - side), part)
    near, far = pl.multiple_of(half * 2 * part, 2 * part), pl.multiple_of((1 - half) * 2 * part, 2 * part)
    my_rows = pl.multiple_of(t * piece, piece)
    my_share = pl.multiple_of(t * share, share)

    def send(src, dst, ssem, rsem, dev):
        return pltpu.make_async_remote_copy(
            src_ref=src, dst_ref=dst, send_sem=ssem, recv_sem=rsem, device_id=dev, device_id_type=MESH
        )

    def p1(q):
        return send(x.at[q], big.at[q % RING, pl.ds(0, count)], p1s.at[q], p1v.at[q], (pair, t))

    def p2(q):
        return send(x.at[q], big.at[q % RING, pl.ds(count, count)], p2s.at[q], p2v.at[q], (peer, t))

    def p3(q):
        slot = q % RING
        return send(
            big.at[slot, pl.ds(0, count)], big.at[slot, pl.ds(2 * count, count)], p3s.at[q], p3v.at[q], (peer, t)
        )

    def e(q):
        return send(
            r.at[q % 2, 0, :, pl.ds(lanes, lanes)], big.at[q % RING, pl.ds(0, part), pl.ds(0, lanes)], es.at[q], ev.at[q],
            (pair, t),
        )

    def ya(q, k):
        return send(
            r.at[q % 2, k, pl.ds(other, own), pl.ds(0, lanes)], yra.at[q % RING, k], yas.at[q, k], yav.at[q, k], (line, t)
        )

    def yb_hub(q):
        return send(
            r.at[q % 2, 1, pl.ds(other, own), pl.ds(lanes, lanes)], yrb.at[q % LEAD], ybs.at[q], ybv.at[q], (line, t)
        )

    def yb_edge(q):
        return send(
            big.at[q % RING, pl.ds(other, own), pl.ds(0, lanes)], yrb.at[q % LEAD], ybs.at[q], ybv.at[q], (line, t)
        )

    def fa(q):
        return send(ea.at[q % 2], yra.at[q % RING, 0], fas.at[q], fav.at[q], (pair, t))

    def feature1(f, k):
        half_row = f1.at[f, :, pl.ds((near, far)[k], 2 * part)]
        return send(half_row, half_row, f1s.at[f, k], f1v.at[f, k], (pair, t))

    def feature2(f):
        return send(fs.at[f], f2.at[f], f2s.at[f], f2v.at[f], (peer, t))

    def feature3(f):
        return send(f1.at[f, :, pl.ds(far, 2 * part)], f3.at[f], f3s.at[f], f3v.at[f], (peer, t))

    def feature(f, shard):
        return (f1.at[f, :, pl.ds(near, 2 * part)], f2.at[f], f3.at[f])[shard]

    def across(f, shard):
        return send(feature(f, shard), fx.at[f, shard], fxs.at[f, shard], fxv.at[f, shard], (d, t ^ 2))

    def sibling(f, shard, k):
        src = fx.at[f, shard] if k else feature(f, shard)
        return send(src, fc.at[k, shard], fcs.at[k, f, shard], fcv.at[k, f, shard], (d, t ^ 1))

    def spread(f, shard):
        across(f, shard).start()
        if f:
            sibling(f, shard, 0).start()

    p1x = lambda: send(ex, exr.at[0], exs.at[0], exv.at[0], (pair, t))
    p2x = lambda: send(ex, exr.at[1], exs.at[1], exv.at[1], (peer, t))
    p3x = lambda: send(exr.at[0], exr.at[2], exs.at[2], exv.at[2], (peer, t))
    e_x = lambda: send(rx.at[0], exe, exs.at[3], exv.at[3], (pair, t))
    yx_hub = lambda: send(rx.at[1, pl.ds(other, own)], yrx, yxs.at[0], yxv.at[0], (line, t))
    yx_edge = lambda: send(exe.at[pl.ds(other, own)], yrx, yxs.at[0], yxv.at[0], (line, t))

    def over_tensor(src, dst, ssem, rsem):
        return lambda k: send(src(k), dst(k), ssem.at[k - 1], rsem.at[k - 1], (d, t ^ k))

    sum_copy = over_tensor(lambda k: sums, lambda k: sumr.at[k - 1], sus, suv)
    state_copy = over_tensor(lambda k: dstate.at[t ^ k], lambda k: dsr.at[k - 1], dss, dsv)
    row_copy = over_tensor(lambda k: srr.at[t], lambda k: srr.at[t], srs, srv)
    out_near = lambda n: send(po.at[t ^ (1 + 2 * n)], por.at[n], pos.at[n], pov.at[n], (d, t ^ 1))
    out_far = lambda: send(po.at[t ^ 2], por.at[2], pos.at[2], pov.at[2], (d, t ^ 2))
    tiles = share // lanes
    block = lambda i: act.at[pl.ds(tiles * i, tiles)]
    in_near = lambda n: send(block(t ^ (1 + 2 * n)), pir.at[n], pis.at[n], piv.at[n], (d, t ^ 1))
    in_far = lambda: send(block(t ^ 2), pir.at[2], pis.at[2], piv.at[2], (d, t ^ 2))
    dot_copy = over_tensor(lambda k: dots, lambda k: dotr.at[k - 1], dts, dtv)
    extra_copy = over_tensor(lambda k: exg.at[t], lambda k: exg.at[t], exgs, exgv)
    small_copy = lambda k: send(sm, smr.at[k], sms.at[k], smv.at[k], (d ^ (1 << k), t))

    def started(copy):
        for k in range(1, 4):
            copy(k).start()

    def waited(copy):
        for k in range(1, 4):
            copy(k).wait()

    def load(n, kind):
        at = pl.multiple_of((n % each) * wide, wide)
        if kind == 2:
            return pltpu.make_async_copy(wo_hbm.at[pl.ds(at, wide), :], woring.at[n % 2], wsem.at[kind, n % 2])
        ref = (wg_hbm, wi_hbm)[kind]
        return pltpu.make_async_copy(ref.at[:, pl.ds(at, wide)], wring.at[n % 2, kind], wsem.at[kind, n % 2])

    operand = [
        pltpu.make_async_copy(src, dst, early.at[n])
        for n, (src, dst) in enumerate(((cot_hbm, cot), (xin_hbm, xin), (wst_hbm, wst)))
    ]
    for one in operand:
        one.start()

    barrier = pltpu.get_barrier_semaphore()
    for dev in ((pair, t), (peer, t), (line, t), (d ^ 4, t), (d, t ^ 1), (d, t ^ 2), (d, t ^ 3)):
        pl.semaphore_signal(barrier, inc=1, device_id=dev, device_id_type=MESH)
    pl.semaphore_wait(barrier, 7)

    heads = ws.shape[0]
    gain_in[...] = gain_in1[...].reshape(1, width)
    ib[...] = ib1[...].reshape(1, inner)
    gain[...] = gain1[...].reshape(1, inner)
    sb[...] = sb1[...].reshape(1, 4 * span)
    heads_in[...] = jnp.zeros_like(heads_in)
    for n, ref in enumerate((stepb1, decay1, skip1)):
        heads_in[8 * n : 8 * n + 8, 0:heads] = jnp.broadcast_to(ref[...].reshape(1, heads), (8, heads))
    h0 = lax.broadcasted_iota(jnp.int32, (128, inner), 0)
    spread_heads = (h0 == lax.broadcasted_iota(jnp.int32, (128, inner), 1) // HEAD_DIM).astype(f32)
    skipc[...] = mm(heads_in[16:24, :], spread_heads, NN, HIGH)[0:1, :]
    rate_row = -jnp.exp(heads_in[8:9, :])

    def begin_features(f):
        ref = cot if f else nb

        @pl.when(edge)
        def _():
            f1[f] = ref[pl.ds(my_rows, piece), :].astype(f32)
            if f:
                feature1(f, 1).start()

        @pl.when(hub)
        def _():
            fs[f] = ref[pl.ds(my_rows, piece), pl.ds(far, 2 * part)].astype(f32)
            feature2(f).start()

    operand[0].wait()
    begin_features(1)
    for n in range(2):
        for kind in range(3):
            load(n, kind).start()

    operand[1].wait()
    xv = xin[...].astype(f32)
    scale = lax.rsqrt(jnp.sum(xv * xv, axis=1, keepdims=True) / width + eps)
    nb[...] = (xv * scale * gain_in[...]).astype(bf16)
    inv[...] = jnp.broadcast_to(scale, inv.shape)
    begin_features(0)

    i0 = lax.broadcasted_iota(jnp.int32, (count, count), 0)
    j0 = lax.broadcasted_iota(jnp.int32, (count, count), 1)
    same = (seg_of(i0, lengths) == seg_of(j0, lengths)) & (j0 <= i0)
    addm[...] = jnp.where(same, 0.0, NEG)
    keep = keeps(lengths, count)
    for back in range(1, CONV):
        keep_ref[:, back : back + 1] = keep[back]
    operand[2].wait()
    state = mm(nb[...], wst[...])
    state_raw[...] = state
    cv = conv(state, sk[...], sb[...], keep)
    sact[...] = cv * sigmoid(cv)
    g[...] = mm(sact[:, STATE:], sact[:, :STATE], NT, HIGH)
    sraw[...] = jnp.zeros_like(sraw)
    sraw[:, 0:heads] = mm(nb[...], ws[...], NT) + heads_in[0:1, 0:heads]
    step = softplus(sraw[...])
    logs = mm(same.astype(f32), step * rate_row, NN, HIGH)
    lsr[...] = jnp.transpose(logs)
    for k in range(each):
        hc[k, :, 0:HPB] = logs[:, HPB * k : HPB * (k + 1)]
        hc[k, :, HPB : 2 * HPB] = step[:, HPB * k : HPB * (k + 1)]
    for ref in (acc, dg, dlogs, dstep, hsum, sm):
        ref[...] = jnp.zeros_like(ref)

    first = lanes_first((count, 2 * HEAD_DIM))

    def kept():
        return [None] + [keep_ref[:, b : b + 1] for b in range(1, CONV)]

    def steps_of(j, k):
        return jnp.where(first, hc[j, :, HPB + k : HPB + k + 1], hc[j, :, HPB + k + 1 : HPB + k + 2])

    def decay_of(j, h):
        return jnp.exp(hc[j, :, h : h + 1] - lsr[pl.ds(HPB * j + h, 1), :] + addm[...])

    def put(base, j, value):
        for half_block in range(2):
            act[base + 2 * j + half_block] = value[:, lanes * half_block : lanes * (half_block + 1)]

    def take(base, j):
        return jnp.concatenate([act[base + 2 * j], act[base + 2 * j + 1]], axis=1)

    def forward_block(j, carry):
        slot = j % 2
        cols = pl.ds(pl.multiple_of(j * wide, wide), wide)
        for kind in range(3):
            load(j, kind).wait()
        gate = mm(nb[...], wring[slot, 0])
        raw = mm(nb[...], wring[slot, 1])
        scaled = mm(cot[...], woring[slot], NT)
        for kind in range(3):
            load(j + 2, kind).start()
        x[j] = scaled
        x[each + j] = gate
        x[2 * each + j] = raw
        cv = conv(raw, ik[:, cols], ib[:, cols], kept())
        put(2 * each, j, cv)
        v = cv * sigmoid(cv)
        parts = []
        for k in range(0, HPB, 2):
            vs = (v[:, HEAD_DIM * k : HEAD_DIM * (k + 2)] * steps_of(j, k)).astype(bf16)
            ys = [mm((g[...] * decay_of(j, h)).astype(bf16), vs) for h in (k, k + 1)]
            parts.append(jnp.where(first, ys[0], ys[1]))
        mixed = jnp.concatenate(parts, axis=1) + skipc[:, cols] * v
        put(0, j, mixed)
        gated = mixed * (gate * sigmoid(gate))
        acc[:, 0:1] += jnp.sum(gated * gated, axis=1, keepdims=True)
        acc[:, 1:2] += jnp.sum(scaled * gain[:, cols] * gated, axis=1, keepdims=True)

        @pl.when(edge & (j == 1))
        def _():
            feature1(1, 1).wait_send()
            feature1(1, 0).start()

        @pl.when(hub & (j == 1))
        def _():
            feature1(1, 1).wait_recv()
            feature3(1).start()
            feature2(1).wait_recv()
            spread(1, 1)

        return carry

    lax.fori_loop(0, each, forward_block, 0)
    sums[...] = jnp.transpose(acc[...])[0:8, :]
    started(sum_copy)

    @pl.when(hub)
    def _():
        feature1(1, 0).wait_recv()
        spread(1, 0)

    waited(sum_copy)
    total = jnp.transpose(sums[...] + sumr[0] + sumr[1] + sumr[2])
    acc[:, 0:1] = lax.rsqrt(total[:, 0:1] / (4 * inner) + eps)
    acc[:, 1:2] = acc[:, 0:1] * total[:, 1:2] / (4 * inner)

    def unit_block(j, carry):
        cols = pl.ds(pl.multiple_of(j * wide, wide), wide)
        scaled, gate, mixed = x[j], x[each + j], take(0, j)
        inv_gate, dot = acc[:, 0:1], acc[:, 1:2]
        s = sigmoid(gate)
        gate_act = gate * s
        unit = mixed * gate_act * inv_gate
        weights = gain[:, cols]
        x[j] = (unit * weights).astype(bf16).astype(f32)
        sm[5:6, cols] = jnp.sum(scaled * unit, axis=0, keepdims=True)
        d_gated = inv_gate * (scaled * weights - unit * dot)
        dmb[j] = d_gated * gate_act
        x[each + j] = (d_gated * mixed * s * (1.0 + gate * (1.0 - s))).astype(bf16).astype(f32)

        @pl.when(hub & (j < LEAD2))
        def _():
            p2(j).start()

        @pl.when(edge & (j < 2))
        def _():
            p1(j).start()

        return carry

    lax.fori_loop(0, each, unit_block, 0)

    @pl.when(hub)
    def _():
        feature3(1).wait_recv()
        spread(1, 2)

    def forward_features(f, shards=(1, 0, 2)):
        if not f:
            pl.semaphore_wait(fc_free, 1)
        for shard in shards:
            if not f:
                sibling(f, shard, 0).start()
            across(f, shard).wait_recv()
            sibling(f, shard, 1).start()

    def assemble(f):
        own_rows = (cot if f else nb)[:, pl.ds(near, 2 * part)]
        ft[f, :, 0:count] = own_rows.T
        for shard in (1, 0, 2):
            sibling(f, shard, 0).wait_recv()
            sibling(f, shard, 1).wait_recv()
            for k, ref in enumerate((feature(f, shard), fc.at[0, shard], fx.at[f, shard], fc.at[1, shard])):
                xbr[pl.ds(pl.multiple_of((t ^ k) * piece, piece), piece), :] = ref[...].astype(bf16)
            ft[f, :, count * (shard + 1) : count * (shard + 2)] = xbr[...].T
        if f:
            pl.semaphore_signal(fc_free, inc=1, device_id=(d, t ^ 1), device_id_type=MESH)

    def backward_block(j, carry):
        cols = pl.ds(pl.multiple_of(j * wide, wide), wide)
        cv, dm = take(2 * each, j), dmb[j]
        s = sigmoid(cv)
        v = cv * s
        within = take(0, j) - skipc[:, cols] * v
        us, vss, dys, stepm = [], [], [], []
        for k in range(0, HPB, 2):
            lane = slice(HEAD_DIM * k, HEAD_DIM * (k + 2))
            steps = steps_of(j, k)
            vs = (v[:, lane] * steps).astype(bf16)
            dy = dm[:, lane].astype(bf16)
            both = []
            for h in (k, k + 1):
                ratio = decay_of(j, h)
                both.append(mm((g[...] * ratio).astype(bf16), dy, TN))
                part_of = first if h == k else jnp.logical_not(first)
                dg[...] += ratio * mm(jnp.where(part_of, dy, jnp.zeros_like(dy)), vs, NT)
            us.append(jnp.where(first, both[0], both[1]))
            vss.append(vs.astype(f32))
            dys.append(dy.astype(f32))
            stepm.append(steps)
        u, vs, dy, steps = (jnp.concatenate(p, axis=1) for p in (us, vss, dys, stepm))
        c0 = lax.broadcasted_iota(jnp.int32, (wide, 128), 0) // HEAD_DIM
        l0 = lax.broadcasted_iota(jnp.int32, (wide, 128), 1)
        pick = (l0 == c0 + HPB * j).astype(f32)
        dlogs[...] += mm(dy * within - vs * u, pick, NN, HIGH)
        dstep[...] += mm(v * u, pick, NN, HIGH)
        per_lane = jnp.sum(dm * v, axis=0, keepdims=True)
        hsum[...] += mm(jnp.broadcast_to(per_lane, (8, wide)), pick, NN, HIGH)
        dc = (steps * u + skipc[:, cols] * dm) * (s * (1.0 + cv * (1.0 - s)))
        du, rows = conv_back(dc, x[2 * each + j], ik[:, cols], kept())
        x[2 * each + j] = du.astype(bf16).astype(f32)
        sm[0:5, cols] = jnp.concatenate(rows, axis=0)
        return carry

    def backward_end():
        mask = (addm[...] > -1.0).astype(f32)
        q = mm(mask, dlogs[...], TN, HIGH)
        raw = sraw[...]
        step = softplus(raw)
        rate = -jnp.exp(heads_in[8:9, :])
        draw = (dstep[...] + rate * q) * sigmoid(raw)
        dstep[...] = draw.astype(bf16).astype(f32)
        sm[6:7, share : share + 128] = jnp.sum(draw, axis=0, keepdims=True)
        sm[6:7, share + 128 : share + 256] = rate * jnp.sum(step * q, axis=0, keepdims=True)
        sm[6:7, share + 256 : share + 384] = hsum[0:1, :]
        d_b = mm(dg[...], sact[:, STATE:], TN, HIGH)
        d_c = mm(dg[...], sact[:, :STATE], NN, HIGH)
        both = jnp.concatenate([d_b, d_c], axis=1)
        for i in range(4):
            dstate[i] = both[:, span * i : span * (i + 1)]
        started(state_copy)

    def slab(ref):
        out = None
        for i in range(4):
            one = jnp.where(t == i, ref[:, span * i : span * (i + 1)], 0.0)
            out = one if out is None else out + one
        return out

    def states():
        waited(state_copy)
        total = dstate[t] + dsr[0] + dsr[1] + dsr[2]
        u, kernel = slab(state_raw), slab(sk)
        cv = conv(u, kernel, slab(sb), kept())
        s = sigmoid(cv)
        du, rows = conv_back(total * (s * (1.0 + cv * (1.0 - s))), u, kernel, kept())
        ex[:, 0:span] = du.astype(bf16).astype(f32)
        ex[:, span : 2 * span] = dstep[:, 0:span]
        srr[t] = jnp.concatenate(rows + [jnp.zeros((3, span), f32)], axis=0)
        started(row_copy)

        @pl.when(hub)
        def _():
            p2x().start()

        @pl.when(edge)
        def _():
            p1x().start()

    def out_parts():
        for c in range(each):
            n = each + c
            load(n, 2).wait()
            xc = x[c].astype(bf16)
            for i in range(4):
                one = mm(xc, woring[n % 2, :, share * i : share * (i + 1)])
                po[i] = one if c == 0 else po[i] + one
            if c + 2 < each:
                load(n + 2, 2).start()
        for n in range(2):
            out_near(n).start()

    def out_across():
        for n in range(2):
            out_near(n).wait()
        po[t ^ 2] = po[t ^ 2] + por[1]
        out_far().start()

    def out_sum():
        out_far().wait()
        hidden = xin[:, pl.ds(my_share, share)].astype(f32)
        out_ref[...] = (po[t] + por[0] + por[2] + hidden).astype(bf16)

    def in_parts():
        lane = lax.broadcasted_iota(jnp.int32, (count, 4 * span), 1) // span
        own_state = ex[:, 0:span]
        states4 = jnp.where(lane == t, jnp.concatenate([own_state] * 4, axis=1), 0.0).astype(bf16)
        steps_back = dstep[:, 0:heads].astype(bf16)
        for i in range(4 * tiles):
            rows = slice(lanes * i, lanes * (i + 1))
            act[i] = mm(states4, wst[rows, :], NT) + mm(steps_back, ws[:, rows])
        for c in range(each):
            n = each + c
            load(n, 0).wait()
            load(n, 1).wait()
            gc, ic = x[each + c].astype(bf16), x[2 * each + c].astype(bf16)
            for i in range(2 * tiles):
                rows = slice(2 * lanes * i, 2 * lanes * (i + 1))
                one = mm(gc, wring[n % 2, 0, rows, :], NT) + mm(ic, wring[n % 2, 1, rows, :], NT)
                act[2 * i] = act[2 * i] + one[:, 0:lanes]
                act[2 * i + 1] = act[2 * i + 1] + one[:, lanes:]
            if c + 2 < each:
                load(n + 2, 0).start()
                load(n + 2, 1).start()
        for n in range(2):
            in_near(n).start()

    def in_across():
        for n in range(2):
            in_near(n).wait()
        for i in range(tiles):
            act[tiles * (t ^ 2) + i] = act[tiles * (t ^ 2) + i] + pir[1, i]
        in_far().start()

    def normed():
        return xin[:, pl.ds(my_share, share)].astype(f32) * inv[:, 0:1]

    def in_sum():
        in_far().wait()
        for i in range(tiles):
            po[0, :, lanes * i : lanes * (i + 1)] = act[tiles * t + i] + pir[0, i] + pir[2, i]
        d_normed = po[0]
        dot = jnp.sum(d_normed * gain_in[:, pl.ds(my_share, share)] * normed(), axis=1, keepdims=True)
        dots[...] = jnp.transpose(jnp.broadcast_to(dot, (count, 128)))[0:8, :]
        started(dot_copy)

    def finish():
        waited(dot_copy)
        waited(row_copy)
        d_normed, n = po[0], normed()
        dot = jnp.transpose(dots[...] + dotr[0] + dotr[1] + dotr[2])[:, 0:1] / width
        d_hat = d_normed * gain_in[:, pl.ds(my_share, share)]
        din_ref[...] = inv[:, 0:1] * (d_hat - n * dot) + cot[:, pl.ds(my_share, share)].astype(f32)
        sm[6:7, 0:share] = jnp.sum(d_normed * n, axis=0, keepdims=True)
        for i in range(4):
            for n in range(CONV + 1):
                at = 4 * span * n + span * i
                sm[7:8, at : at + span] = srr[i, n : n + 1, :]
        small_copy(0).start()

    def small(k):
        small_copy(k).wait()
        sm[...] = sm[...] + smr[k]
        if k < 2:
            small_copy(k + 1).start()
        else:
            smalls_ref[...] = sm[...]

    def extra_hub():
        p2x().wait_recv()
        p3x().wait_recv()
        for k, ref in enumerate((ex, exr.at[0], exr.at[1], exr.at[2])):
            xb[k * count : (k + 1) * count, 0:128] = ref[...].astype(bf16)
        rx[0] = mm(ft[0, pl.ds(pair_part, part), :], xb[:, 0:128])
        rx[1] = mm(ft[0, pl.ds(mine_part, part), :], xb[:, 0:128])
        e_x().start()
        yx_hub().start()

    def extra_spread(rows):
        exg[t] = rows + yrx[...]
        step_out[...] = jnp.transpose(exg[t])[span : span + heads, :]
        started(extra_copy)

    def extra_end():
        waited(extra_copy)
        for i in range(4):
            state_out[:, span * i : span * (i + 1)] = exg[i, :, 0:span]

    def process(q):
        p2(q).wait_recv()
        p3(q).wait_recv()
        p3(q).wait_send()

        @pl.when(q >= 2)
        def _():
            e(q - 2).wait_send()
            ya(q - 2, 0).wait_send()
            ya(q - 2, 1).wait_send()
            yb_hub(q - 2).wait_send()

        xb[0:count, :] = x[q].astype(bf16)
        xb[count:, :] = big[q % RING].astype(bf16)

        @pl.when(q + RING < chunks)
        def _():
            pl.semaphore_signal(credit, inc=1, device_id=(peer, t), device_id_type=MESH)

        family = jnp.where(q < each, 1, 0)
        slot = q % 2
        r[slot, 0] = mm(ft[family, pl.ds(pair_part, part), :], xb[...])
        e(q).start()
        ya(q, 0).start()
        r[slot, 1] = mm(ft[family, pl.ds(mine_part, part), :], xb[...])
        ya(q, 1).start()
        yb_hub(q).start()

    def stored(q, k):
        at = pl.multiple_of((q % each) * wide, wide)
        out = (turned_out, gate_out, inner_out)[k]
        return pltpu.make_async_copy(fin.at[q % 2], out.at[:, pl.ds(at, wide)], fins.at[q])

    def store(q, left, right):
        slot = q % 2
        for k in range(3):
            @pl.when((q >= k * each + 2) & (q < (k + 1) * each + 2))
            def _():
                stored(q - 2, k).wait()

        fin[slot, :, 0:lanes] = left
        fin[slot, :, lanes:] = right

        for k in range(3):
            @pl.when((q >= k * each) & (q < (k + 1) * each))
            def _():
                stored(q, k).start()

    def finalize_hub(q):
        slot = q % 2
        ya(q, 0).wait_recv()
        ya(q, 1).wait_recv()
        yb_hub(q).wait_recv()

        @pl.when(q >= 2)
        def _():
            fa(q - 2).wait_send()

        got = yra.at[q % RING]
        ea[slot] = r[slot, 0, pl.ds(mine, own), 0:lanes] + got[0]
        fa(q).start()
        store(
            q,
            r[slot, 1, pl.ds(mine, own), 0:lanes] + got[1],
            r[slot, 1, pl.ds(mine, own), lanes:] + yrb[q % LEAD],
        )

    def finalize_edge(q):
        yb_edge(q).wait_recv()
        fa(q).wait_recv()
        store(q, yra[q % RING, 0], big[q % RING, pl.ds(mine, own), 0:lanes] + yrb[q % LEAD])

    pieces = {
        1: backward_end, 2: out_parts, 3: [states, out_across], 4: in_parts, 5: out_sum, 6: in_across, 8: in_sum,
        9: finish, 10: lambda: small(0), 12: lambda: small(1), 15: lambda: small(2), 14: extra_end,
    }

    lax.fori_loop(0, 2, backward_block, 0)

    @pl.when(hub)
    def _():
        p1(0).wait_recv()
        p3(0).start()
        p2(LEAD2).start()
        forward_features(1, (1, 0))

    @pl.when(edge)
    def _():
        p1(0).wait_send()
        p1(2).start()

    lax.fori_loop(2, each, backward_block, 0)

    @pl.when(hub)
    def _():
        forward_features(1, (2,))
        assemble(1)

    @pl.when(edge)
    def _():
        for n in range(3, LEAD):
            p1(n - 2).wait_send()
            p1(n).start()
        feature1(0, 1).start()
        feature1(0, 0).start()

    def body(q, carry):
        @pl.when(hub)
        def _():
            @pl.when((q >= 1) & (q < chunks))
            def _():
                p1(q).wait_recv()
                p3(q).start()

            @pl.when((q >= 1) & (q + LEAD2 < chunks))
            def _():
                @pl.when(q + LEAD2 >= RING)
                def _():
                    pl.semaphore_wait(credit, 1)

                p2(q + LEAD2).start()

            @pl.when((q >= 1) & (q <= chunks))
            def _():
                process(q - 1)

            @pl.when(q >= 2)
            def _():
                finalize_hub(q - 2)

            @pl.when(q == 2)
            def _():
                feature1(0, 1).wait_recv()
                feature3(0).start()
                feature1(0, 0).wait_recv()
                spread(0, 0)
                feature2(0).wait_recv()
                spread(0, 1)

            @pl.when(q == 3)
            def _():
                feature3(0).wait_recv()
                spread(0, 2)

            @pl.when(q == 4)
            def _():
                forward_features(0)

            @pl.when(q == 5)
            def _():
                assemble(0)

            @pl.when(q == 7)
            def _():
                p1x().wait_recv()
                p3x().start()

            @pl.when(q == 8)
            def _():
                extra_hub()

            @pl.when(q == 11)
            def _():
                yx_hub().wait_recv()
                extra_spread(rx[1, pl.ds(mine, own), :])

        for at, jobs in pieces.items():
            for job in jobs if isinstance(jobs, list) else [jobs]:
                pl.when(q == at)(job)

        @pl.when(edge)
        def _():
            @pl.when(q < chunks)
            def _():
                e(q).wait_recv()
                yb_edge(q).start()

            @pl.when(q + LEAD < chunks)
            def _():
                @pl.when(q >= 2)
                def _():
                    yb_edge(q - 2).wait_send()

                p1(q + LEAD).start()

            @pl.when((q >= 1) & (q <= chunks))
            def _():
                finalize_edge(q - 1)

            @pl.when(q == 9)
            def _():
                e_x().wait_recv()
                yx_edge().start()

            @pl.when(q == 11)
            def _():
                yx_edge().wait_recv()
                extra_spread(exe[pl.ds(mine, own), :])

        return carry

    lax.fori_loop(0, chunks + 2, body, 0)

    stored(chunks - 2, 2).wait()
    stored(chunks - 1, 2).wait()

    @pl.when(hub)
    def _():
        def drain(q, carry):
            p2(q).wait_send()
            return carry

        lax.fori_loop(0, chunks, drain, 0)
        for q in (chunks - 2, chunks - 1):
            e(q).wait_send()
            ya(q, 0).wait_send()
            ya(q, 1).wait_send()
            yb_hub(q).wait_send()
            fa(q).wait_send()
        for f in range(2):
            feature2(f).wait_send()
            feature3(f).wait_send()
            for shard in range(3):
                across(f, shard).wait_send()
                sibling(f, shard, 0).wait_send()
                sibling(f, shard, 1).wait_send()
        p2x().wait_send()
        p3x().wait_send()
        e_x().wait_send()
        yx_hub().wait_send()

    @pl.when(edge)
    def _():
        def drain(q, carry):
            p1(q).wait_send()
            return carry

        lax.fori_loop(LEAD - 2, chunks, drain, 0)
        for q in range(chunks - LEAD - 2, chunks):
            yb_edge(q).wait_send()
        feature1(1, 0).wait_send()
        feature1(0, 0).wait_send()
        feature1(0, 1).wait_send()
        p1x().wait_send()
        yx_edge().wait_send()


def outputs_kernel(
    smalls, a, b, c, d, e, f, g,
    norm_gain, inner_kernel, inner_bias, state_kernel_out, state_bias, step_bias, decay, skip, gate_gain,
    ao, bo, co, do, eo, fo, go, at_, bt, ct, dt, et, ft, gt, loads, stores,
):
    through = list(zip((a, b, c, d, e, f, g), (at_, bt, ct, dt, et, ft, gt), (ao, bo, co, do, eo, fo, go)))
    load = lambda n: pltpu.make_async_copy(through[n][0], through[n][1], loads.at[n])
    keep = lambda n: pltpu.make_async_copy(through[n][1], through[n][2], stores.at[n])
    for n in range(len(through)):
        load(n).start()
    for ref, at, lane in (
        (norm_gain, 6, 0), (inner_bias, CONV, 0), (state_bias, 7, CONV * state_bias.shape[0]),
        (step_bias, 6, norm_gain.shape[0]), (decay, 6, norm_gain.shape[0] + 128), (skip, 6, norm_gain.shape[0] + 256),
        (gate_gain, 5, 0),
    ):
        ref[...] = smalls[at : at + 1, lane : lane + ref.shape[0]].reshape(ref.shape)
    inner_kernel[...] = smalls[0:CONV, :]
    for n in range(CONV):
        size = state_kernel_out.shape[1]
        state_kernel_out[n : n + 1, :] = smalls[7:8, size * n : size * (n + 1)]
    for n in range(len(through)):
        load(n).wait()
        keep(n).start()
    for n in range(len(through)):
        keep(n).wait()


def whole(shape):
    return pl.BlockSpec(shape, lambda *_: (0,) * len(shape))


def columns(rows):
    return pl.BlockSpec((rows, BLK), lambda j, *_: (0, j))


SMEM = pl.BlockSpec(memory_space=pltpu.SMEM)
VM = pltpu.CompilerParams(vmem_limit_bytes=56 << 20)
VMS = pltpu.CompilerParams(vmem_limit_bytes=56 << 20, dimension_semantics=("arbitrary",))


def struct(shape, dtype=f32):
    return jax.ShapeDtypeStruct(shape, dtype)


def cost(flops, moved):
    return pl.CostEstimate(flops=int(flops), bytes_accessed=int(moved), transcendentals=0)


def on_device(
    block_input, cotangent, seq_lengths, norm_gain, gate_weight, inner_weight, step_weight, state_weight,
    inner_kernel, inner_bias, state_kernel_, state_bias, step_bias, decay_log, skip_scale, gate_gain, output_weight,
):
    parts = lax.axis_size("tensor")
    shards = lax.axis_size("dp")
    t = lax.axis_index("tensor")
    count, width = block_input.shape
    inner = gate_weight.shape[1]
    heads = step_bias.shape[0]
    share = width // parts
    span = 2 * STATE // parts
    steps = inner // BLK
    pad = ((0, 0), (0, 128 - heads))
    row = lambda x: x.reshape(1, -1)

    def swap(x, k):
        return lax.ppermute(x, "tensor", [(i, i ^ k) for i in range(parts)])

    chunks = 3 * steps
    slab = lambda x, size: lax.dynamic_slice_in_dim(x, t * size, size, x.ndim - 1)
    if shards == 8 and parts == 4:
        own, half_blk, piece, near = width // 8, BLK // 2, count // parts, width // 2
        dma, v = pltpu.SemaphoreType.DMA, lambda *shape: pltpu.VMEM(shape, f32)
        vb = lambda *shape: pltpu.VMEM(shape, bf16)
        vmem, hbm = pl.BlockSpec(memory_space=pltpu.VMEM), pl.BlockSpec(memory_space=pl.ANY)
        scratch = [
            vb(count, width), vb(count, width), vb(width, 2 * STATE), v(chunks, count, BLK), v(4 * steps, count, half_blk), v(steps, count, BLK), vb(count, width),
            v(count, 128), v(1, width), v(1, inner), v(1, 2 * STATE), v(24, 128), v(1, inner), v(1, inner), v(2, piece, near), v(2, piece, width), v(2, piece, near), v(2, piece, near),
            v(2, 3, piece, near), v(2, 3, piece, near), vb(2, near, 4 * count), v(RING, 3 * count, BLK),
            v(RING, 2, own, half_blk), v(LEAD, own, half_blk), v(2, 2, 2 * own, BLK), v(2, own, half_blk), v(2, own, BLK),
            vb(4 * count, BLK), vb(count, near), vb(2, 2, width, BLK), vb(2, BLK, width),
            v(4, count, share), v(3, count, share), v(3, share // half_blk, count, half_blk),
            v(count, count), v(count, count), v(steps, count, 128), v(128, count), v(count, 2 * STATE), v(count, 2 * STATE),
            v(count, 128), v(count, 128), v(count, count), v(count, 128), v(count, 128), v(8, 128), v(count, 128),
            v(8, count), v(3, 8, count), v(4, count, span), v(3, count, span), v(4, 8, span), v(8, inner), v(3, 8, inner),
            v(count, 128), v(3, count, 128), v(2, 2 * own, 128), v(2 * own, 128), v(own, 128), v(4, own, 128),
            v(8, count), v(3, 8, count),
        ]
        scratch += [dma((chunks,))] * 8 + [dma((chunks, 2))] * 2 + [dma((chunks,))] * 5 + [dma((3, 2))] + [dma((3,))] * 14
        scratch += [dma((4,))] * 2 + [dma((1,))] * 2 + [dma((3,))] * 2 + [dma((2, 2))] * 2 + [dma((2,))] * 4 + [dma((2, 3))] * 2
        scratch += [dma((2, 2, 3))] * 2 + [dma((3,))] + [pltpu.SemaphoreType.REGULAR] * 2
        shapes = [
            struct((count, share), bf16), struct((count, share)), struct((own, inner)), struct((own, inner)),
            struct((own, 2 * STATE)), struct((heads, own)), struct((own, inner)),
        ]
        *large, smalls = pl.pallas_call(
            layer_kernel,
            in_specs=[SMEM, hbm, hbm, vmem, vmem, hbm] + [vmem] * 8 + [hbm] * 3,
            out_specs=[vmem, vmem, hbm, hbm, vmem, vmem, hbm, vmem],
            out_shape=shapes + [struct((8, inner))],
            scratch_shapes=scratch,
            compiler_params=pltpu.CompilerParams(collective_id=1, has_side_effects=True, vmem_limit_bytes=VMEM_LIMIT),
            name="layer",
        )(
            seq_lengths, block_input, cotangent, norm_gain, step_weight.T, state_weight, inner_kernel, inner_bias,
            state_kernel_, state_bias, step_bias, decay_log, skip_scale, gate_gain, gate_weight, inner_weight, output_weight,
        )
        cut = [
            struct((share,)), struct((CONV, inner)), struct((inner,)), struct((CONV, 2 * STATE)), struct((2 * STATE,)),
            struct((heads,)), struct((heads,)), struct((heads,)), struct((inner,)),
        ]
        *smalls, out, into, gate_grad, inner_grad, state_grad, step_grad, output_grad = pl.pallas_call(
            outputs_kernel,
            in_specs=[vmem] + [hbm] * 7,
            out_specs=[vmem] * 9 + [hbm] * 7,
            out_shape=cut + shapes,
            scratch_shapes=[pltpu.VMEM(a.shape, a.dtype) for a in shapes] + [dma((7,)), dma((7,))],
            compiler_params=VM,
            name="outputs",
        )(smalls, *large)
        return (
            out, into, smalls[0], gate_grad, inner_grad, step_grad.T, state_grad, *smalls[1:9], output_grad.T,
        )

    padded_step = jnp.pad(step_weight, pad)
    stepb, decay = jnp.pad(row(step_bias), pad), jnp.pad(row(decay_log), pad)
    skipc = jnp.repeat(skip_scale, HEAD_DIM).reshape(1, -1)
    ik, ib, gain = inner_kernel, row(inner_bias), row(gate_gain)
    full = struct((count, inner))
    nb, inv = pl.pallas_call(
        norm_kernel,
        out_shape=(struct((count, width), bf16), struct((count, 128))),
        compiler_params=VM,
        name="norm_in",
    )(block_input, row(norm_gain))

    graw, iraw, cv, mixed, scaled, sums, sraw, sact, state_raw, hc, lsr, addm, g, keep = pl.pallas_call(
        forward_kernel,
        grid=(steps,),
        in_specs=[
            SMEM, whole((count, width)), whole((count, width)), columns(width), columns(width),
            pl.BlockSpec((BLK, width), lambda j: (j, 0)), whole((width, 128)), whole((width, 2 * STATE)),
            columns(CONV), columns(1), whole((CONV, 2 * STATE)), whole((1, 2 * STATE)), whole((1, 128)), whole((1, 128)),
            columns(1), columns(1),
        ],
        out_specs=(
            [columns(count)] * 5
            + [whole((8, count)), whole((count, 128)), whole((count, 2 * STATE)), whole((count, 2 * STATE)),
               whole((steps, count, 128)), whole((128, count)), whole((count, count)), whole((count, count)),
               whole((count, 128))]
        ),
        out_shape=(
            [full] * 5
            + [struct((8, count)), struct((count, 128)), struct((count, 2 * STATE)), struct((count, 2 * STATE)),
               struct((steps, count, 128)), struct((128, count)), struct((count, count)), struct((count, count)),
               struct((count, 128))]
        ),
        scratch_shapes=[pltpu.VMEM((count, 128), f32)],
        compiler_params=VMS,
        cost_estimate=cost(6 * count * width * inner, 6 * width * inner + 20 * count * inner),
        name="forward",
    )(
        seq_lengths, nb, cotangent, gate_weight, inner_weight, output_weight, padded_step, state_weight, ik, ib,
        state_kernel_, row(state_bias), stepb, decay, skipc, gain,
    )

    all_sums = jnp.stack([sums] + [swap(sums, k) for k in range(1, parts)])
    x, dm, gg = pl.pallas_call(
        partial(unit_kernel, float(inner * parts)),
        grid=(steps,),
        in_specs=[whole((parts, 8, count)), columns(count), columns(count), columns(count), columns(1)],
        out_specs=[pl.BlockSpec((2, 1, count, BLK), lambda j: (0, j, 0, 0)), columns(count), columns(8)],
        out_shape=[struct((3, steps, count, BLK)), full, struct((8, inner))],
        compiler_params=VMS,
        cost_estimate=cost(0, 24 * count * inner),
        name="unit",
    )(all_sums, graw, mixed, scaled, gain)

    x, rows, sback, hrows, dstate = pl.pallas_call(
        backward_kernel,
        grid=(steps,),
        in_specs=[
            SMEM, columns(count), columns(count), columns(count), columns(count),
            pl.BlockSpec((1, count, 128), lambda j: (j, 0, 0)), whole((128, count)), whole((count, count)),
            whole((count, count)), whole((count, 128)), whole((count, 2 * STATE)), columns(CONV), columns(1), whole((1, 128)),
            pl.BlockSpec(memory_space=pl.ANY),
        ],
        input_output_aliases={14: 0},
        out_specs=[pl.BlockSpec((1, 1, count, BLK), lambda j: (2, j, 0, 0)), columns(8), whole((count, 128)), whole((8, 128)), whole((parts, count, span))],
        out_shape=[struct((3, steps, count, BLK)), struct((8, inner)), struct((count, 128)), struct((8, 128)), struct((parts, count, span))],
        scratch_shapes=[pltpu.VMEM((count, count), f32), pltpu.VMEM((count, 128), f32), pltpu.VMEM((count, 128), f32)],
        compiler_params=VMS,
        cost_estimate=cost(40 * count * count * inner // 64 * 4, 24 * count * inner),
        name="backward",
    )(seq_lengths, dm, cv, iraw, mixed, hc, lsr, addm, g, sraw, sact, ik, skipc, decay, x)

    uo, gb, back = (jnp.swapaxes(x[i], 0, 1).reshape(count, inner) for i in range(3))

    def to_parts(x, axis):
        size = x.shape[axis] // parts
        block = lambda i: lax.dynamic_slice_in_dim(x, i * size, size, axis)
        got = [swap(block(t ^ k), k) for k in range(1, parts)]
        return [block(t)] + got

    def from_parts(x):
        got = jnp.stack([x] + [swap(x, k) for k in range(1, parts)])
        return jnp.stack([lax.dynamic_index_in_dim(got, t ^ i, 0, False) for i in range(parts)])

    state_parts = jnp.concatenate(to_parts(dstate, 0), axis=0)
    sq, srows = pl.pallas_call(
        state_kernel,
        in_specs=[SMEM] + [pl.BlockSpec(memory_space=pltpu.VMEM)] * 4,
        out_shape=(struct((count, span)), struct((8, span))),
        compiler_params=VM,
        name="state_back",
    )(seq_lengths, state_parts, slab(state_raw, span), slab(state_kernel_, span), row(slab(state_bias, span)))

    hidden = slab(block_input, share).astype(f32)
    cot_share = slab(cotangent, share).astype(f32)
    out_parts = to_parts(mm(uo.astype(bf16), output_weight), 1)
    block_output = (sum(out_parts[1:], out_parts[0]) + hidden).astype(bf16)

    gbb, ibb, sbb, qb = (x.astype(bf16) for x in (gb, back, sback[:, :heads], sq))
    partial_in = (
        mm(gbb, gate_weight, NT) + mm(ibb, inner_weight, NT) + mm(sbb, step_weight, NT)
        + mm(qb, slab(state_weight, span), NT)
    )
    in_parts = to_parts(partial_in, 1)
    d_normed = sum(in_parts[1:], in_parts[0])
    inv_in = inv[:, 0:1]
    normed = hidden * inv_in
    gain_share = row(slab(norm_gain, share))
    d_hat = d_normed * gain_share
    dot = jnp.sum(d_hat * normed, axis=1).reshape(-1, 128)
    dot = sum((swap(dot, k) for k in range(1, parts)), dot).reshape(-1, 1) / width
    input_gradient = inv_in * (d_hat - normed * dot) + cot_share
    norm_gain_grad = jnp.sum(d_normed * normed, axis=0)

    extra = jnp.concatenate([sq, sback[:, :heads], jnp.zeros((count, 128 - span - heads), f32)], axis=1)

    def scatter(a, b):
        return lax.psum_scatter(mm(a, b.astype(bf16), TN), "dp", scatter_dimension=0, tiled=True)

    output_grad = scatter(cotangent, uo).T
    gate_grad, inner_grad, extra_grad = scatter(nb, gb), scatter(nb, back), scatter(nb, extra)

    def over_dp(x):
        return lax.psum(x, "dp")

    step_grad = extra_grad[:, span : span + heads]
    state_grad = jnp.swapaxes(from_parts(extra_grad[:, :span]), 0, 1).reshape(-1, 2 * STATE)
    misc = jnp.concatenate([hrows[0], hrows[1], srows[: CONV + 1].reshape(-1), norm_gain_grad])
    misc = jnp.pad(misc, (0, -misc.shape[0] % 1024)).reshape(8, -1)
    smalls = over_dp(jnp.concatenate([rows, gg], axis=0))
    misc = over_dp(misc).reshape(-1)
    step_bias_grad, decay_grad = misc[:heads], misc[128 : 128 + heads]
    state_rows = from_parts(misc[256 : 256 + (CONV + 1) * span].reshape(CONV + 1, span))
    state_rows = jnp.swapaxes(state_rows, 0, 1).reshape(CONV + 1, 2 * STATE)
    at = 256 + (CONV + 1) * span
    skip_grad = jnp.sum(smalls[CONV + 1].reshape(heads, HEAD_DIM), axis=1)
    return (
        block_output,
        input_gradient,
        misc[at : at + share],
        gate_grad,
        inner_grad,
        step_grad,
        state_grad,
        smalls[:CONV],
        smalls[CONV],
        state_rows[:CONV],
        state_rows[CONV],
        step_bias_grad,
        decay_grad,
        skip_grad,
        smalls[8],
        output_grad,
    )


def solution(mesh):
    return jax.shard_map(
        on_device,
        mesh=mesh,
        in_specs=(
            P("dp", None), P("dp", None), P("dp", None), P(), P(None, "tensor"), P(None, "tensor"), P(None, "tensor"), P(),
            P(None, "tensor"), P("tensor"), P(), P(), P("tensor"), P("tensor"), P("tensor"), P("tensor"), P("tensor", None),
        ),
        out_specs=(
            P("dp", "tensor"), P("dp", "tensor"), P("tensor"), P("dp", "tensor"), P("dp", "tensor"), P("dp", "tensor"),
            P("dp", None), P(None, "tensor"), P("tensor"), P(), P(), P("tensor"), P("tensor"), P("tensor"), P("tensor"),
            P("tensor", "dp"),
        ),
        check_vma=False,
    )
```

```python
from functools import partial

import jax
import jax.numpy as jnp
from jax import lax
from jax.experimental import pallas as pl
from jax.experimental.pallas import tpu as pltpu
from jax.sharding import PartitionSpec as P

HEAD_DIM = 64
STATE = 128
CONV = 4
BLK = 256
HPB = BLK // HEAD_DIM
eps = 1e-05
NEG = -1e30
f32 = jnp.float32
bf16 = jnp.bfloat16
HIGH = lax.Precision.HIGHEST
NN = (((1,), (0,)), ((), ()))
NT = (((1,), (1,)), ((), ()))
TN = (((0,), (0,)), ((), ()))


def mm(a, b, dims=NN, precision=None):
    return lax.dot_general(a, b, dims, precision=precision, preferred_element_type=f32)


def sigmoid(x):
    return 1.0 / (1.0 + jnp.exp(-x))


def softplus(x):
    return jnp.maximum(x, 0.0) + jnp.log1p(jnp.exp(-jnp.abs(x)))


def seg_of(places, lengths):
    total = jnp.zeros(places.shape, jnp.int32)
    end = jnp.int32(0)
    for s in range(lengths.shape[1]):
        end = end + lengths[0, s]
        total = total + (places >= end).astype(jnp.int32)
    return total


def keeps(lengths, count):
    t = lax.broadcasted_iota(jnp.int32, (count, 1), 0)
    own = seg_of(t, lengths)
    out = [None]
    for back in range(1, CONV):
        out.append(((seg_of(t - back, lengths) == own) & (t >= back)).astype(f32))
    return out


def down(x, back):
    return pltpu.roll(x, back, 0)


def up(x, back):
    return pltpu.roll(x, x.shape[0] - back, 0)


def conv(u, kernel, bias, keep):
    out = bias + kernel[CONV - 1 : CONV, :] * u
    for back in range(1, CONV):
        out = out + kernel[CONV - 1 - back : CONV - back, :] * (down(u, back) * keep[back])
    return out


def conv_back(dc, u, kernel, keep):
    du = kernel[CONV - 1 : CONV, :] * dc
    rows = [jnp.sum(dc * u, axis=0, keepdims=True)]
    for back in range(1, CONV):
        kept = dc * keep[back]
        du = du + kernel[CONV - 1 - back : CONV - back, :] * up(kept, back)
        rows.append(jnp.sum(kept * down(u, back), axis=0, keepdims=True))
    return du, rows[::-1] + [jnp.sum(dc, axis=0, keepdims=True)]


def lanes_first(shape):
    return lax.broadcasted_iota(jnp.int32, shape, 1) < HEAD_DIM


def norm_kernel(x_ref, gain_ref, nb_ref, inv_ref):
    x = x_ref[...].astype(f32)
    inv = lax.rsqrt(jnp.sum(x * x, axis=1, keepdims=True) / x.shape[1] + eps)
    nb_ref[...] = (x * inv * gain_ref[...]).astype(bf16)
    inv_ref[...] = jnp.broadcast_to(inv, inv_ref.shape)


def forward_kernel(
    lengths, nb_ref, cot_ref, wg_ref, wi_ref, wo_ref, ws_ref, wst_ref, ik_ref, ib_ref, sk_ref, sb_ref,
    stepb_ref, decay_ref, skipc_ref, gain_ref,
    graw_ref, iraw_ref, cv_ref, mixed_ref, scaled_ref, sums_ref, sraw_ref, sact_ref, state_ref, hc_ref, lsr_ref,
    addm_ref, g_ref, keep_ref, acc,
):
    j = pl.program_id(0)
    count = nb_ref.shape[0]
    nb = nb_ref[...]

    @pl.when(j == 0)
    def _():
        i0 = lax.broadcasted_iota(jnp.int32, (count, count), 0)
        j0 = lax.broadcasted_iota(jnp.int32, (count, count), 1)
        same = (seg_of(i0, lengths) == seg_of(j0, lengths)) & (j0 <= i0)
        addm_ref[...] = jnp.where(same, 0.0, NEG)
        state = mm(nb, wst_ref[...])
        state_ref[...] = state
        keep = keeps(lengths, count)
        for back in range(1, CONV):
            keep_ref[:, back : back + 1] = keep[back]
        cv = conv(state, sk_ref[...], sb_ref[...], keep)
        act = cv * sigmoid(cv)
        sact_ref[...] = act
        g_ref[...] = mm(act[:, STATE:], act[:, :STATE], NT, HIGH)
        raw = mm(nb, ws_ref[...]) + stepb_ref[...]
        sraw_ref[...] = raw
        step = softplus(raw)
        logs = mm(same.astype(f32), step * (-jnp.exp(decay_ref[...])), NN, HIGH)
        lsr_ref[...] = jnp.transpose(logs)
        for k in range(hc_ref.shape[0]):
            hc_ref[k, :, 0:HPB] = logs[:, HPB * k : HPB * (k + 1)]
            hc_ref[k, :, HPB : 2 * HPB] = step[:, HPB * k : HPB * (k + 1)]
        acc[...] = jnp.zeros_like(acc)

    gate = mm(nb, wg_ref[...])
    inner = mm(nb, wi_ref[...])
    scaled = mm(cot_ref[...], wo_ref[...], NT)
    graw_ref[...] = gate
    iraw_ref[...] = inner
    scaled_ref[...] = scaled
    cv = conv(inner, ik_ref[...], ib_ref[...], keeps(lengths, count))
    cv_ref[...] = cv
    v = cv * sigmoid(cv)
    first = lanes_first((count, 2 * HEAD_DIM))
    addm = addm_ref[...]
    g = g_ref[...]
    parts = []
    for pair in range(BLK // (2 * HEAD_DIM)):
        vp = v[:, 2 * HEAD_DIM * pair : 2 * HEAD_DIM * (pair + 1)]
        k = 2 * pair
        steps = jnp.where(first, hc_ref[j, :, HPB + k : HPB + k + 1], hc_ref[j, :, HPB + k + 1 : HPB + k + 2])
        vs = (vp * steps).astype(bf16)
        ys = []
        for h in (k, k + 1):
            gaps = hc_ref[j, :, h : h + 1] - lsr_ref[pl.ds(HPB * j + h, 1), :] + addm
            ys.append(mm((g * jnp.exp(gaps)).astype(bf16), vs))
        parts.append(jnp.where(first, ys[0], ys[1]))
    mixed = jnp.concatenate(parts, axis=1) + skipc_ref[...] * v
    mixed_ref[...] = mixed
    gated = mixed * (gate * sigmoid(gate))
    acc[:, 0:1] += jnp.sum(gated * gated, axis=1, keepdims=True)
    acc[:, 1:2] += jnp.sum(scaled * gain_ref[...] * gated, axis=1, keepdims=True)

    @pl.when(j == pl.num_programs(0) - 1)
    def _():
        sums_ref[...] = jnp.transpose(acc[...])[0:8, :]


def unit_kernel(width, s_ref, graw_ref, mixed_ref, scaled_ref, gain_ref, x_ref, dm_ref, gg_ref):
    sums = jnp.sum(s_ref[...], axis=0)
    cols = jnp.transpose(sums)
    inv = lax.rsqrt(cols[:, 0:1] / width + eps)
    dot = inv * cols[:, 1:2]
    gate, mixed, scaled, gain = graw_ref[...], mixed_ref[...], scaled_ref[...], gain_ref[...]
    s = sigmoid(gate)
    act = gate * s
    unit = mixed * act * inv
    x_ref[0, 0] = (unit * gain).astype(bf16).astype(f32)
    gg_ref[...] = jnp.broadcast_to(jnp.sum(scaled * unit, axis=0, keepdims=True), gg_ref.shape)
    d_gated = inv * (scaled * gain - unit * (dot / width))
    dm_ref[...] = d_gated * act
    x_ref[1, 0] = (d_gated * mixed * s * (1.0 + gate * (1.0 - s))).astype(bf16).astype(f32)


def backward_kernel(
    lengths, dm_ref, cv_ref, iraw_ref, mixed_ref, hc_ref, lsr_ref, addm_ref, g_ref, sraw_ref, sact_ref,
    ik_ref, skipc_ref, decay_ref, _,
    back_ref, rows_ref, sback_ref, hrows_ref, dstate_ref, dg, dlogs, dstep,
):
    j = pl.program_id(0)
    count = dm_ref.shape[0]

    @pl.when(j == 0)
    def _():
        dg[...] = jnp.zeros_like(dg)
        dlogs[...] = jnp.zeros_like(dlogs)
        dstep[...] = jnp.zeros_like(dstep)

    cv, dm, skipc = cv_ref[...], dm_ref[...], skipc_ref[...]
    s = sigmoid(cv)
    v = cv * s
    within = mixed_ref[...] - skipc * v
    first = lanes_first((count, 2 * HEAD_DIM))
    addm = addm_ref[...]
    g = g_ref[...]
    us, vss, dyb, stepm = [], [], [], []
    total = dg[...]
    for pair in range(BLK // (2 * HEAD_DIM)):
        cols = slice(2 * HEAD_DIM * pair, 2 * HEAD_DIM * (pair + 1))
        k = 2 * pair
        steps = jnp.where(first, hc_ref[0, :, HPB + k : HPB + k + 1], hc_ref[0, :, HPB + k + 1 : HPB + k + 2])
        vs = (v[:, cols] * steps).astype(bf16)
        dy = dm[:, cols].astype(bf16)
        both = []
        for h in (k, k + 1):
            gaps = hc_ref[0, :, h : h + 1] - lsr_ref[pl.ds(HPB * j + h, 1), :] + addm
            decay = jnp.exp(gaps)
            both.append(mm((g * decay).astype(bf16), dy, TN))
            mine = first if h == k else jnp.logical_not(first)
            total = total + decay * mm(jnp.where(mine, dy, jnp.zeros_like(dy)), vs, NT)
        us.append(jnp.where(first, both[0], both[1]))
        vss.append(vs.astype(f32))
        dyb.append(dy.astype(f32))
        stepm.append(steps)
    dg[...] = total
    u = jnp.concatenate(us, axis=1)
    vs = jnp.concatenate(vss, axis=1)
    dy = jnp.concatenate(dyb, axis=1)
    steps = jnp.concatenate(stepm, axis=1)
    c0 = lax.broadcasted_iota(jnp.int32, (BLK, 128), 0) // HEAD_DIM
    l0 = lax.broadcasted_iota(jnp.int32, (BLK, 128), 1)
    pick = (l0 == c0 + HPB * j).astype(f32)
    dlogs[...] += mm(dy * within - vs * u, pick, NN, HIGH)
    dstep[...] += mm(v * u, pick, NN, HIGH)
    dv = steps * u + skipc * dm
    dc = dv * (s * (1.0 + cv * (1.0 - s)))
    du, rows = conv_back(dc, iraw_ref[...], ik_ref[...], keeps(lengths, count))
    back_ref[0, 0] = du.astype(bf16).astype(f32)
    rows_ref[...] = jnp.concatenate(rows + [jnp.sum(dm * v, axis=0, keepdims=True)] + [jnp.zeros((2, BLK), f32)], axis=0)

    @pl.when(j == pl.num_programs(0) - 1)
    def _():
        mask = (addm > -1.0).astype(f32)
        q = mm(mask, dlogs[...], TN, HIGH)
        raw = sraw_ref[...]
        step = softplus(raw)
        rate = -jnp.exp(decay_ref[...])
        draw = (dstep[...] + rate * q) * sigmoid(raw)
        sback_ref[...] = draw.astype(bf16).astype(f32)
        hrows_ref[...] = jnp.concatenate(
            [jnp.sum(draw, axis=0, keepdims=True), rate * jnp.sum(step * q, axis=0, keepdims=True), jnp.zeros((6, 128), f32)],
            axis=0,
        )
        act = sact_ref[...]
        d_b = mm(dg[...], act[:, STATE:], TN, HIGH)
        d_c = mm(dg[...], act[:, :STATE], NN, HIGH)
        both = jnp.concatenate([d_b, d_c], axis=1)
        span = dstate_ref.shape[2]
        for t in range(dstate_ref.shape[0]):
            dstate_ref[t] = both[:, span * t : span * (t + 1)]


def state_kernel(lengths, parts_ref, u_ref, sk_ref, sb_ref, back_ref, rows_ref):
    keep = keeps(lengths, u_ref.shape[0])
    cv = conv(u_ref[...], sk_ref[...], sb_ref[...], keep)
    s = sigmoid(cv)
    dc = jnp.sum(parts_ref[...], axis=0) * (s * (1.0 + cv * (1.0 - s)))
    du, rows = conv_back(dc, u_ref[...], sk_ref[...], keep)
    back_ref[...] = du.astype(bf16).astype(f32)
    rows_ref[...] = jnp.concatenate(rows + [jnp.zeros((3, du.shape[1]), f32)], axis=0)


MESH = pl.DeviceIdType.MESH
RING = 6
VMEM_LIMIT = 64 << 20
LEAD = 4
LEAD2 = 1


def layer_kernel(
    lengths, xin_hbm, cot_hbm, gain_in1, ws, wst_hbm, ik, ib1, sk, sb1, stepb1, decay1, skip1, gain1, wg_hbm, wi_hbm, wo_hbm,
    out_ref, din_ref, gate_out, inner_out, state_out, step_out, turned_out, smalls_ref,
    xin, cot, wst, x, act, dmb, nb, inv, gain_in, ib, sb, heads_in, skipc, gain, fs, f1, f2, f3, fx, fc, ft, big, yra, yrb, r, ea, fin, xb, xbr, wring, woring, po, por, pir, addm, g, hc, lsr, sact, state_raw, sraw, keep_ref, dg, dlogs, dstep, hsum, acc, sums, sumr, dstate, dsr, srr, sm, smr,
    ex, ext, exr, rx, exe, yrx, exg, dots, dotr,
    p1s, p1v, p2s, p2v, p3s, p3v, es, ev, yas, yav, ybs, ybv, fas, fav, fins, wsem, pos, pov, pis, piv,
    dss, dsv, srs, srv, dts, dtv, sus, suv, sms, smv, exs, exv, yxs, yxv, exgs, exgv,
    f1s, f1v, f2s, f2v, f3s, f3v, fxs, fxv, fcs, fcv, early, credit, fc_free,
):
    d, t = lax.axis_index("dp"), lax.axis_index("tensor")
    y, z = d % 2, d // 2
    side, half = z % 2, z // 2
    hub = (z == 1) | (z == 2)
    edge = jnp.logical_not(hub)
    chunks, count, wide = x.shape
    each = chunks // 3
    lanes = wide // 2
    width = xin.shape[1]
    part = width // 4
    own = part // 2
    share = width // 4
    span = dsr.shape[2]
    inner = each * wide
    piece = f1.shape[1]
    pair, peer, line = d ^ 2, d ^ 6, d ^ 1
    mine, other = pl.multiple_of(own * y, own), pl.multiple_of(own * (1 - y), own)
    mine_part, pair_part = pl.multiple_of(part * side, part), pl.multiple_of(part * (1 - side), part)
    near, far = pl.multiple_of(half * 2 * part, 2 * part), pl.multiple_of((1 - half) * 2 * part, 2 * part)
    my_rows = pl.multiple_of(t * piece, piece)
    my_share = pl.multiple_of(t * share, share)

    def send(src, dst, ssem, rsem, dev):
        return pltpu.make_async_remote_copy(
            src_ref=src, dst_ref=dst, send_sem=ssem, recv_sem=rsem, device_id=dev, device_id_type=MESH
        )

    def p1(q):
        return send(x.at[q], big.at[q % RING, pl.ds(0, count)], p1s.at[q], p1v.at[q], (pair, t))

    def p2(q):
        return send(x.at[q], big.at[q % RING, pl.ds(count, count)], p2s.at[q], p2v.at[q], (peer, t))

    def p3(q):
        slot = q % RING
        return send(
            big.at[slot, pl.ds(0, count)], big.at[slot, pl.ds(2 * count, count)], p3s.at[q], p3v.at[q], (peer, t)
        )

    def e(q):
        return send(
            r.at[q % 2, 0, :, pl.ds(lanes, lanes)], big.at[q % RING, pl.ds(0, part), pl.ds(0, lanes)], es.at[q], ev.at[q],
            (pair, t),
        )

    def ya(q, k):
        return send(
            r.at[q % 2, k, pl.ds(other, own), pl.ds(0, lanes)], yra.at[q % RING, k], yas.at[q, k], yav.at[q, k], (line, t)
        )

    def yb_hub(q):
        return send(
            r.at[q % 2, 1, pl.ds(other, own), pl.ds(lanes, lanes)], yrb.at[q % LEAD], ybs.at[q], ybv.at[q], (line, t)
        )

    def yb_edge(q):
        return send(
            big.at[q % RING, pl.ds(other, own), pl.ds(0, lanes)], yrb.at[q % LEAD], ybs.at[q], ybv.at[q], (line, t)
        )

    def fa(q):
        return send(ea.at[q % 2], yra.at[q % RING, 0], fas.at[q], fav.at[q], (pair, t))

    def feature1(f, k):
        half_row = f1.at[f, :, pl.ds((near, far)[k], 2 * part)]
        return send(half_row, half_row, f1s.at[f, k], f1v.at[f, k], (pair, t))

    def feature2(f):
        return send(fs.at[f], f2.at[f], f2s.at[f], f2v.at[f], (peer, t))

    def feature3(f):
        return send(f1.at[f, :, pl.ds(far, 2 * part)], f3.at[f], f3s.at[f], f3v.at[f], (peer, t))

    def feature(f, shard):
        return (f1.at[f, :, pl.ds(near, 2 * part)], f2.at[f], f3.at[f])[shard]

    def across(f, shard):
        return send(feature(f, shard), fx.at[f, shard], fxs.at[f, shard], fxv.at[f, shard], (d, t ^ 2))

    def sibling(f, shard, k):
        src = fx.at[f, shard] if k else feature(f, shard)
        return send(src, fc.at[k, shard], fcs.at[k, f, shard], fcv.at[k, f, shard], (d, t ^ 1))

    def spread(f, shard):
        across(f, shard).start()
        if f:
            sibling(f, shard, 0).start()

    used = pl.ds(0, -(-(span + ws.shape[0]) // 8) * 8)
    p1x = lambda: send(ext.at[used], exr.at[0, used], exs.at[0], exv.at[0], (pair, t))
    p2x = lambda: send(ext.at[used], exr.at[1, used], exs.at[1], exv.at[1], (peer, t))
    p3x = lambda: send(exr.at[0, used], exr.at[2, used], exs.at[2], exv.at[2], (peer, t))
    e_x = lambda: send(rx.at[0], exe, exs.at[3], exv.at[3], (pair, t))
    yx_hub = lambda: send(rx.at[1, pl.ds(other, own)], yrx, yxs.at[0], yxv.at[0], (line, t))
    yx_edge = lambda: send(exe.at[pl.ds(other, own)], yrx, yxs.at[0], yxv.at[0], (line, t))

    def over_tensor(src, dst, ssem, rsem):
        return lambda k: send(src(k), dst(k), ssem.at[k - 1], rsem.at[k - 1], (d, t ^ k))

    sum_copy = over_tensor(lambda k: sums, lambda k: sumr.at[k - 1], sus, suv)
    state_copy = over_tensor(lambda k: dstate.at[t ^ k], lambda k: dsr.at[k - 1], dss, dsv)
    row_copy = over_tensor(lambda k: srr.at[t], lambda k: srr.at[t], srs, srv)
    out_near = lambda n: send(po.at[t ^ (1 + 2 * n)], por.at[n], pos.at[n], pov.at[n], (d, t ^ 1))
    out_far = lambda: send(po.at[t ^ 2], por.at[2], pos.at[2], pov.at[2], (d, t ^ 2))
    tiles = share // lanes
    block = lambda i: act.at[pl.ds(tiles * i, tiles)]
    in_near = lambda n: send(block(t ^ (1 + 2 * n)), pir.at[n], pis.at[n], piv.at[n], (d, t ^ 1))
    in_far = lambda: send(block(t ^ 2), pir.at[2], pis.at[2], piv.at[2], (d, t ^ 2))
    dot_copy = over_tensor(lambda k: dots, lambda k: dotr.at[k - 1], dts, dtv)
    extra_copy = over_tensor(lambda k: exg.at[t], lambda k: exg.at[t], exgs, exgv)
    small_copy = lambda k: send(sm, smr.at[k], sms.at[k], smv.at[k], (d ^ (1 << k), t))

    def started(copy):
        for k in range(1, 4):
            copy(k).start()

    def waited(copy):
        for k in range(1, 4):
            copy(k).wait()

    def load(n, kind):
        at = pl.multiple_of((n % each) * wide, wide)
        if kind == 2:
            return pltpu.make_async_copy(wo_hbm.at[pl.ds(at, wide), :], woring.at[n % 2], wsem.at[kind, n % 2])
        ref = (wg_hbm, wi_hbm)[kind]
        return pltpu.make_async_copy(ref.at[:, pl.ds(at, wide)], wring.at[n % 2, kind], wsem.at[kind, n % 2])

    operand = [
        pltpu.make_async_copy(src, dst, early.at[n])
        for n, (src, dst) in enumerate(((cot_hbm, cot), (xin_hbm, xin), (wst_hbm, wst)))
    ]
    for one in operand:
        one.start()

    barrier = pltpu.get_barrier_semaphore()
    for dev in ((pair, t), (peer, t), (line, t), (d ^ 4, t), (d, t ^ 1), (d, t ^ 2), (d, t ^ 3)):
        pl.semaphore_signal(barrier, inc=1, device_id=dev, device_id_type=MESH)
    pl.semaphore_wait(barrier, 7)

    heads = ws.shape[0]
    gain_in[...] = gain_in1[...].reshape(1, width)
    ib[...] = ib1[...].reshape(1, inner)
    gain[...] = gain1[...].reshape(1, inner)
    sb[...] = sb1[...].reshape(1, 4 * span)
    heads_in[...] = jnp.zeros_like(heads_in)
    for n, ref in enumerate((stepb1, decay1, skip1)):
        heads_in[8 * n : 8 * n + 8, 0:heads] = jnp.broadcast_to(ref[...].reshape(1, heads), (8, heads))
    h0 = lax.broadcasted_iota(jnp.int32, (128, inner), 0)
    spread_heads = (h0 == lax.broadcasted_iota(jnp.int32, (128, inner), 1) // HEAD_DIM).astype(f32)
    skipc[...] = mm(heads_in[16:24, :], spread_heads, NN, HIGH)[0:1, :]
    rate_row = -jnp.exp(heads_in[8:9, :])

    def begin_features(f):
        ref = cot if f else nb

        @pl.when(edge)
        def _():
            f1[f] = ref[pl.ds(my_rows, piece), :].astype(f32)
            if f:
                feature1(f, 1).start()

        @pl.when(hub)
        def _():
            fs[f] = ref[pl.ds(my_rows, piece), pl.ds(far, 2 * part)].astype(f32)
            feature2(f).start()

    operand[0].wait()
    begin_features(1)
    for n in range(2):
        for kind in range(3):
            load(n, kind).start()

    operand[1].wait()
    xv = xin[...].astype(f32)
    scale = lax.rsqrt(jnp.sum(xv * xv, axis=1, keepdims=True) / width + eps)
    nb[...] = (xv * scale * gain_in[...]).astype(bf16)
    inv[...] = jnp.broadcast_to(scale, inv.shape)
    begin_features(0)

    i0 = lax.broadcasted_iota(jnp.int32, (count, count), 0)
    j0 = lax.broadcasted_iota(jnp.int32, (count, count), 1)
    same = (seg_of(i0, lengths) == seg_of(j0, lengths)) & (j0 <= i0)
    addm[...] = jnp.where(same, 0.0, NEG)
    keep = keeps(lengths, count)
    for back in range(1, CONV):
        keep_ref[:, back : back + 1] = keep[back]
    operand[2].wait()
    state = mm(nb[...], wst[...])
    state_raw[...] = state
    cv = conv(state, sk[...], sb[...], keep)
    sact[...] = cv * sigmoid(cv)
    g[...] = mm(sact[:, STATE:], sact[:, :STATE], NT, HIGH)
    sraw[...] = jnp.zeros_like(sraw)
    sraw[:, 0:heads] = mm(nb[...], ws[...], NT) + heads_in[0:1, 0:heads]
    step = softplus(sraw[...])
    logs = mm(same.astype(f32), step * rate_row, NN, HIGH)
    lsr[...] = jnp.transpose(logs)
    for k in range(each):
        hc[k, :, 0:HPB] = logs[:, HPB * k : HPB * (k + 1)]
        hc[k, :, HPB : 2 * HPB] = step[:, HPB * k : HPB * (k + 1)]
    for ref in (acc, dg, dlogs, dstep, hsum, sm):
        ref[...] = jnp.zeros_like(ref)
    exr[:, used.size :, :] = jnp.zeros((3, 128 - used.size, count), f32)

    first = lanes_first((count, 2 * HEAD_DIM))

    def kept():
        return [None] + [keep_ref[:, b : b + 1] for b in range(1, CONV)]

    def steps_of(j, k):
        return jnp.where(first, hc[j, :, HPB + k : HPB + k + 1], hc[j, :, HPB + k + 1 : HPB + k + 2])

    def decay_of(j, h):
        return jnp.exp(hc[j, :, h : h + 1] - lsr[pl.ds(HPB * j + h, 1), :] + addm[...])

    def put(base, j, value):
        for half_block in range(2):
            act[base + 2 * j + half_block] = value[:, lanes * half_block : lanes * (half_block + 1)]

    def take(base, j):
        return jnp.concatenate([act[base + 2 * j], act[base + 2 * j + 1]], axis=1)

    def forward_block(j, carry):
        slot = j % 2
        cols = pl.ds(pl.multiple_of(j * wide, wide), wide)
        for kind in range(3):
            load(j, kind).wait()
        gate = mm(nb[...], wring[slot, 0])
        raw = mm(nb[...], wring[slot, 1])
        scaled = mm(cot[...], woring[slot], NT)
        for kind in range(3):
            load(j + 2, kind).start()
        x[j] = scaled
        x[each + j] = gate
        x[2 * each + j] = raw
        cv = conv(raw, ik[:, cols], ib[:, cols], kept())
        put(2 * each, j, cv)
        v = cv * sigmoid(cv)
        parts = []
        for k in range(0, HPB, 2):
            vs = (v[:, HEAD_DIM * k : HEAD_DIM * (k + 2)] * steps_of(j, k)).astype(bf16)
            ys = [mm((g[...] * decay_of(j, h)).astype(bf16), vs) for h in (k, k + 1)]
            parts.append(jnp.where(first, ys[0], ys[1]))
        mixed = jnp.concatenate(parts, axis=1) + skipc[:, cols] * v
        put(0, j, mixed)
        gated = mixed * (gate * sigmoid(gate))
        acc[:, 0:1] += jnp.sum(gated * gated, axis=1, keepdims=True)
        acc[:, 1:2] += jnp.sum(scaled * gain[:, cols] * gated, axis=1, keepdims=True)

        @pl.when(edge & (j == 1))
        def _():
            feature1(1, 1).wait_send()
            feature1(1, 0).start()

        @pl.when(hub & (j == 1))
        def _():
            feature1(1, 1).wait_recv()
            feature3(1).start()
            feature2(1).wait_recv()
            spread(1, 1)

        return carry

    lax.fori_loop(0, each, forward_block, 0)
    sums[...] = jnp.transpose(acc[...])[0:8, :]
    started(sum_copy)

    @pl.when(hub)
    def _():
        feature1(1, 0).wait_recv()
        spread(1, 0)

    waited(sum_copy)
    total = jnp.transpose(sums[...] + sumr[0] + sumr[1] + sumr[2])
    acc[:, 0:1] = lax.rsqrt(total[:, 0:1] / (4 * inner) + eps)
    acc[:, 1:2] = acc[:, 0:1] * total[:, 1:2] / (4 * inner)

    def unit_block(j, carry):
        cols = pl.ds(pl.multiple_of(j * wide, wide), wide)
        scaled, gate, mixed = x[j], x[each + j], take(0, j)
        inv_gate, dot = acc[:, 0:1], acc[:, 1:2]
        s = sigmoid(gate)
        gate_act = gate * s
        unit = mixed * gate_act * inv_gate
        weights = gain[:, cols]
        x[j] = (unit * weights).astype(bf16).astype(f32)
        sm[5:6, cols] = jnp.sum(scaled * unit, axis=0, keepdims=True)
        d_gated = inv_gate * (scaled * weights - unit * dot)
        dmb[j] = d_gated * gate_act
        x[each + j] = (d_gated * mixed * s * (1.0 + gate * (1.0 - s))).astype(bf16).astype(f32)

        @pl.when(hub & (j < LEAD2))
        def _():
            p2(j).start()

        @pl.when(edge & (j < 2))
        def _():
            p1(j).start()

        return carry

    lax.fori_loop(0, each, unit_block, 0)

    @pl.when(hub)
    def _():
        feature3(1).wait_recv()
        spread(1, 2)

    def forward_features(f, shards=(1, 0, 2)):
        if not f:
            pl.semaphore_wait(fc_free, 1)
        for shard in shards:
            if not f:
                sibling(f, shard, 0).start()
            across(f, shard).wait_recv()
            sibling(f, shard, 1).start()

    def assemble(f):
        own_rows = (cot if f else nb)[:, pl.ds(near, 2 * part)]
        ft[f, :, 0:count] = own_rows.T
        for shard in (1, 0, 2):
            sibling(f, shard, 0).wait_recv()
            sibling(f, shard, 1).wait_recv()
            for k, ref in enumerate((feature(f, shard), fc.at[0, shard], fx.at[f, shard], fc.at[1, shard])):
                xbr[pl.ds(pl.multiple_of((t ^ k) * piece, piece), piece), :] = ref[...].astype(bf16)
            ft[f, :, count * (shard + 1) : count * (shard + 2)] = xbr[...].T
        if f:
            pl.semaphore_signal(fc_free, inc=1, device_id=(d, t ^ 1), device_id_type=MESH)

    def backward_block(j, carry):
        cols = pl.ds(pl.multiple_of(j * wide, wide), wide)
        cv, dm = take(2 * each, j), dmb[j]
        s = sigmoid(cv)
        v = cv * s
        within = take(0, j) - skipc[:, cols] * v
        us, vss, dys, stepm = [], [], [], []
        for k in range(0, HPB, 2):
            lane = slice(HEAD_DIM * k, HEAD_DIM * (k + 2))
            steps = steps_of(j, k)
            vs = (v[:, lane] * steps).astype(bf16)
            dy = dm[:, lane].astype(bf16)
            both = []
            for h in (k, k + 1):
                ratio = decay_of(j, h)
                both.append(mm((g[...] * ratio).astype(bf16), dy, TN))
                part_of = first if h == k else jnp.logical_not(first)
                dg[...] += ratio * mm(jnp.where(part_of, dy, jnp.zeros_like(dy)), vs, NT)
            us.append(jnp.where(first, both[0], both[1]))
            vss.append(vs.astype(f32))
            dys.append(dy.astype(f32))
            stepm.append(steps)
        u, vs, dy, steps = (jnp.concatenate(p, axis=1) for p in (us, vss, dys, stepm))
        c0 = lax.broadcasted_iota(jnp.int32, (wide, 128), 0) // HEAD_DIM
        l0 = lax.broadcasted_iota(jnp.int32, (wide, 128), 1)
        pick = (l0 == c0 + HPB * j).astype(f32)
        dlogs[...] += mm(dy * within - vs * u, pick, NN, HIGH)
        dstep[...] += mm(v * u, pick, NN, HIGH)
        per_lane = jnp.sum(dm * v, axis=0, keepdims=True)
        hsum[...] += mm(jnp.broadcast_to(per_lane, (8, wide)), pick, NN, HIGH)
        dc = (steps * u + skipc[:, cols] * dm) * (s * (1.0 + cv * (1.0 - s)))
        du, rows = conv_back(dc, x[2 * each + j], ik[:, cols], kept())
        x[2 * each + j] = du.astype(bf16).astype(f32)
        sm[0:5, cols] = jnp.concatenate(rows, axis=0)
        return carry

    def backward_end():
        mask = (addm[...] > -1.0).astype(f32)
        q = mm(mask, dlogs[...], TN, HIGH)
        raw = sraw[...]
        step = softplus(raw)
        rate = -jnp.exp(heads_in[8:9, :])
        draw = (dstep[...] + rate * q) * sigmoid(raw)
        dstep[...] = draw.astype(bf16).astype(f32)
        sm[6:7, share : share + 128] = jnp.sum(draw, axis=0, keepdims=True)
        sm[6:7, share + 128 : share + 256] = rate * jnp.sum(step * q, axis=0, keepdims=True)
        sm[6:7, share + 256 : share + 384] = hsum[0:1, :]
        d_b = mm(dg[...], sact[:, STATE:], TN, HIGH)
        d_c = mm(dg[...], sact[:, :STATE], NN, HIGH)
        both = jnp.concatenate([d_b, d_c], axis=1)
        for i in range(4):
            dstate[i] = both[:, span * i : span * (i + 1)]
        started(state_copy)

    def slab(ref):
        out = None
        for i in range(4):
            one = jnp.where(t == i, ref[:, span * i : span * (i + 1)], 0.0)
            out = one if out is None else out + one
        return out

    def states():
        waited(state_copy)
        total = dstate[t] + dsr[0] + dsr[1] + dsr[2]
        u, kernel = slab(state_raw), slab(sk)
        cv = conv(u, kernel, slab(sb), kept())
        s = sigmoid(cv)
        du, rows = conv_back(total * (s * (1.0 + cv * (1.0 - s))), u, kernel, kept())
        ex[:, 0:span] = du.astype(bf16).astype(f32)
        ex[:, span : 2 * span] = dstep[:, 0:span]
        ext[...] = jnp.transpose(ex[...])
        srr[t] = jnp.concatenate(rows + [jnp.zeros((3, span), f32)], axis=0)
        started(row_copy)

        @pl.when(hub)
        def _():
            p2x().start()

        @pl.when(edge)
        def _():
            p1x().start()

    def out_parts():
        for c in range(each):
            n = each + c
            load(n, 2).wait()
            xc = x[c].astype(bf16)
            for i in range(4):
                one = mm(xc, woring[n % 2, :, share * i : share * (i + 1)])
                po[i] = one if c == 0 else po[i] + one
            if c + 2 < each:
                load(n + 2, 2).start()
        for n in range(2):
            out_near(n).start()

    def out_across():
        for n in range(2):
            out_near(n).wait()
        po[t ^ 2] = po[t ^ 2] + por[1]
        out_far().start()

    def out_sum():
        out_far().wait()
        hidden = xin[:, pl.ds(my_share, share)].astype(f32)
        out_ref[...] = (po[t] + por[0] + por[2] + hidden).astype(bf16)

    def in_parts():
        lane = lax.broadcasted_iota(jnp.int32, (count, 4 * span), 1) // span
        own_state = ex[:, 0:span]
        states4 = jnp.where(lane == t, jnp.concatenate([own_state] * 4, axis=1), 0.0).astype(bf16)
        steps_back = dstep[:, 0:heads].astype(bf16)
        for i in range(4 * tiles):
            rows = slice(lanes * i, lanes * (i + 1))
            act[i] = mm(states4, wst[rows, :], NT) + mm(steps_back, ws[:, rows])
        for c in range(each):
            n = each + c
            load(n, 0).wait()
            load(n, 1).wait()
            gc, ic = x[each + c].astype(bf16), x[2 * each + c].astype(bf16)
            for i in range(2 * tiles):
                rows = slice(2 * lanes * i, 2 * lanes * (i + 1))
                one = mm(gc, wring[n % 2, 0, rows, :], NT) + mm(ic, wring[n % 2, 1, rows, :], NT)
                act[2 * i] = act[2 * i] + one[:, 0:lanes]
                act[2 * i + 1] = act[2 * i + 1] + one[:, lanes:]
            if c + 2 < each:
                load(n + 2, 0).start()
                load(n + 2, 1).start()
        for n in range(2):
            in_near(n).start()

    def in_across():
        for n in range(2):
            in_near(n).wait()
        for i in range(tiles):
            act[tiles * (t ^ 2) + i] = act[tiles * (t ^ 2) + i] + pir[1, i]
        in_far().start()

    def normed():
        return xin[:, pl.ds(my_share, share)].astype(f32) * inv[:, 0:1]

    def in_sum():
        in_far().wait()
        for i in range(tiles):
            po[0, :, lanes * i : lanes * (i + 1)] = act[tiles * t + i] + pir[0, i] + pir[2, i]
        d_normed = po[0]
        dot = jnp.sum(d_normed * gain_in[:, pl.ds(my_share, share)] * normed(), axis=1, keepdims=True)
        dots[...] = jnp.transpose(jnp.broadcast_to(dot, (count, 128)))[0:8, :]
        started(dot_copy)

    def finish():
        waited(dot_copy)
        waited(row_copy)
        d_normed, n = po[0], normed()
        dot = jnp.transpose(dots[...] + dotr[0] + dotr[1] + dotr[2])[:, 0:1] / width
        d_hat = d_normed * gain_in[:, pl.ds(my_share, share)]
        din_ref[...] = inv[:, 0:1] * (d_hat - n * dot) + cot[:, pl.ds(my_share, share)].astype(f32)
        sm[6:7, 0:share] = jnp.sum(d_normed * n, axis=0, keepdims=True)
        for i in range(4):
            for n in range(CONV + 1):
                at = 4 * span * n + span * i
                sm[7:8, at : at + span] = srr[i, n : n + 1, :]
        small_copy(0).start()

    def small(k):
        small_copy(k).wait()
        sm[...] = sm[...] + smr[k]
        if k < 2:
            small_copy(k + 1).start()
        else:
            smalls_ref[...] = sm[...]

    def extra_hub():
        p2x().wait_recv()
        p3x().wait_recv()
        xb[0:count, 0:128] = ex[...].astype(bf16)
        for k in range(3):
            xb[(k + 1) * count : (k + 2) * count, 0:128] = jnp.transpose(exr[k]).astype(bf16)
        rx[0] = mm(ft[0, pl.ds(pair_part, part), :], xb[:, 0:128])
        rx[1] = mm(ft[0, pl.ds(mine_part, part), :], xb[:, 0:128])
        e_x().start()
        yx_hub().start()

    def extra_spread(rows):
        exg[t] = rows + yrx[...]
        step_out[...] = jnp.transpose(exg[t])[span : span + heads, :]
        started(extra_copy)

    def extra_end():
        waited(extra_copy)
        for i in range(4):
            state_out[:, span * i : span * (i + 1)] = exg[i, :, 0:span]

    def process(q):
        p2(q).wait_recv()
        p3(q).wait_recv()
        p3(q).wait_send()

        @pl.when(q >= 2)
        def _():
            e(q - 2).wait_send()
            ya(q - 2, 0).wait_send()
            ya(q - 2, 1).wait_send()
            yb_hub(q - 2).wait_send()

        xb[0:count, :] = x[q].astype(bf16)
        xb[count:, :] = big[q % RING].astype(bf16)

        @pl.when(q + RING < chunks)
        def _():
            pl.semaphore_signal(credit, inc=1, device_id=(peer, t), device_id_type=MESH)

        family = jnp.where(q < each, 1, 0)
        slot = q % 2
        r[slot, 0] = mm(ft[family, pl.ds(pair_part, part), :], xb[...])
        e(q).start()
        ya(q, 0).start()
        r[slot, 1] = mm(ft[family, pl.ds(mine_part, part), :], xb[...])
        ya(q, 1).start()
        yb_hub(q).start()

    def stored(q, k):
        at = pl.multiple_of((q % each) * wide, wide)
        out = (turned_out, gate_out, inner_out)[k]
        return pltpu.make_async_copy(fin.at[q % 2], out.at[:, pl.ds(at, wide)], fins.at[q])

    def store(q, left, right):
        slot = q % 2
        for k in range(3):
            @pl.when((q >= k * each + 2) & (q < (k + 1) * each + 2))
            def _():
                stored(q - 2, k).wait()

        fin[slot, :, 0:lanes] = left
        fin[slot, :, lanes:] = right

        for k in range(3):
            @pl.when((q >= k * each) & (q < (k + 1) * each))
            def _():
                stored(q, k).start()

    def finalize_hub(q):
        slot = q % 2
        ya(q, 0).wait_recv()
        ya(q, 1).wait_recv()
        yb_hub(q).wait_recv()

        @pl.when(q >= 2)
        def _():
            fa(q - 2).wait_send()

        got = yra.at[q % RING]
        ea[slot] = r[slot, 0, pl.ds(mine, own), 0:lanes] + got[0]
        fa(q).start()
        store(
            q,
            r[slot, 1, pl.ds(mine, own), 0:lanes] + got[1],
            r[slot, 1, pl.ds(mine, own), lanes:] + yrb[q % LEAD],
        )

    def finalize_edge(q):
        yb_edge(q).wait_recv()
        fa(q).wait_recv()
        store(q, yra[q % RING, 0], big[q % RING, pl.ds(mine, own), 0:lanes] + yrb[q % LEAD])

    pieces = {
        1: backward_end, 2: out_parts, 3: [states, out_across], 4: in_parts, 5: out_sum, 6: in_across, 8: in_sum,
        9: finish, 10: lambda: small(0), 12: lambda: small(1), 15: lambda: small(2), 14: extra_end,
    }

    lax.fori_loop(0, 2, backward_block, 0)

    @pl.when(hub)
    def _():
        p1(0).wait_recv()
        p3(0).start()
        p2(LEAD2).start()
        forward_features(1, (1, 0))

    @pl.when(edge)
    def _():
        p1(0).wait_send()
        p1(2).start()

    lax.fori_loop(2, each, backward_block, 0)

    @pl.when(hub)
    def _():
        forward_features(1, (2,))
        assemble(1)

    @pl.when(edge)
    def _():
        for n in range(3, LEAD):
            p1(n - 2).wait_send()
            p1(n).start()
        feature1(0, 1).start()
        feature1(0, 0).start()

    def body(q, carry):
        @pl.when(hub)
        def _():
            @pl.when((q >= 1) & (q < chunks))
            def _():
                p1(q).wait_recv()
                p3(q).start()

            @pl.when((q >= 1) & (q + LEAD2 < chunks))
            def _():
                @pl.when(q + LEAD2 >= RING)
                def _():
                    pl.semaphore_wait(credit, 1)

                p2(q + LEAD2).start()

            @pl.when((q >= 1) & (q <= chunks))
            def _():
                process(q - 1)

            @pl.when(q >= 2)
            def _():
                finalize_hub(q - 2)

            @pl.when(q == 2)
            def _():
                feature1(0, 1).wait_recv()
                feature3(0).start()
                feature1(0, 0).wait_recv()
                spread(0, 0)
                feature2(0).wait_recv()
                spread(0, 1)

            @pl.when(q == 3)
            def _():
                feature3(0).wait_recv()
                spread(0, 2)

            @pl.when(q == 4)
            def _():
                forward_features(0)

            @pl.when(q == 5)
            def _():
                assemble(0)

            @pl.when(q == 7)
            def _():
                p1x().wait_recv()
                p3x().start()

            @pl.when(q == 8)
            def _():
                extra_hub()

            @pl.when(q == 11)
            def _():
                yx_hub().wait_recv()
                extra_spread(rx[1, pl.ds(mine, own), :])

        for at, jobs in pieces.items():
            for job in jobs if isinstance(jobs, list) else [jobs]:
                pl.when(q == at)(job)

        @pl.when(edge)
        def _():
            @pl.when(q < chunks)
            def _():
                e(q).wait_recv()
                yb_edge(q).start()

            @pl.when(q + LEAD < chunks)
            def _():
                @pl.when(q >= 2)
                def _():
                    yb_edge(q - 2).wait_send()

                p1(q + LEAD).start()

            @pl.when((q >= 1) & (q <= chunks))
            def _():
                finalize_edge(q - 1)

            @pl.when(q == 9)
            def _():
                e_x().wait_recv()
                yx_edge().start()

            @pl.when(q == 11)
            def _():
                yx_edge().wait_recv()
                extra_spread(exe[pl.ds(mine, own), :])

        return carry

    lax.fori_loop(0, chunks + 2, body, 0)

    stored(chunks - 2, 2).wait()
    stored(chunks - 1, 2).wait()

    @pl.when(hub)
    def _():
        def drain(q, carry):
            p2(q).wait_send()
            return carry

        lax.fori_loop(0, chunks, drain, 0)
        for q in (chunks - 2, chunks - 1):
            e(q).wait_send()
            ya(q, 0).wait_send()
            ya(q, 1).wait_send()
            yb_hub(q).wait_send()
            fa(q).wait_send()
        for f in range(2):
            feature2(f).wait_send()
            feature3(f).wait_send()
            for shard in range(3):
                across(f, shard).wait_send()
                sibling(f, shard, 0).wait_send()
                sibling(f, shard, 1).wait_send()
        p2x().wait_send()
        p3x().wait_send()
        e_x().wait_send()
        yx_hub().wait_send()

    @pl.when(edge)
    def _():
        def drain(q, carry):
            p1(q).wait_send()
            return carry

        lax.fori_loop(LEAD - 2, chunks, drain, 0)
        for q in range(chunks - LEAD - 2, chunks):
            yb_edge(q).wait_send()
        feature1(1, 0).wait_send()
        feature1(0, 0).wait_send()
        feature1(0, 1).wait_send()
        p1x().wait_send()
        yx_edge().wait_send()


def outputs_kernel(
    smalls, a, b, c, d, e, f, g,
    norm_gain, inner_kernel, inner_bias, state_kernel_out, state_bias, step_bias, decay, skip, gate_gain,
    ao, bo, co, do, eo, fo, go, at_, bt, ct, dt, et, ft, gt, loads, stores,
):
    through = list(zip((a, b, c, d, e, f, g), (at_, bt, ct, dt, et, ft, gt), (ao, bo, co, do, eo, fo, go)))
    load = lambda n: pltpu.make_async_copy(through[n][0], through[n][1], loads.at[n])
    keep = lambda n: pltpu.make_async_copy(through[n][1], through[n][2], stores.at[n])
    for n in range(len(through)):
        load(n).start()
    for ref, at, lane in (
        (norm_gain, 6, 0), (inner_bias, CONV, 0), (state_bias, 7, CONV * state_bias.shape[0]),
        (step_bias, 6, norm_gain.shape[0]), (decay, 6, norm_gain.shape[0] + 128), (skip, 6, norm_gain.shape[0] + 256),
        (gate_gain, 5, 0),
    ):
        ref[...] = smalls[at : at + 1, lane : lane + ref.shape[0]].reshape(ref.shape)
    inner_kernel[...] = smalls[0:CONV, :]
    for n in range(CONV):
        size = state_kernel_out.shape[1]
        state_kernel_out[n : n + 1, :] = smalls[7:8, size * n : size * (n + 1)]
    for n in range(len(through)):
        load(n).wait()
        keep(n).start()
    for n in range(len(through)):
        keep(n).wait()


def whole(shape):
    return pl.BlockSpec(shape, lambda *_: (0,) * len(shape))


def columns(rows):
    return pl.BlockSpec((rows, BLK), lambda j, *_: (0, j))


SMEM = pl.BlockSpec(memory_space=pltpu.SMEM)
VM = pltpu.CompilerParams(vmem_limit_bytes=56 << 20)
VMS = pltpu.CompilerParams(vmem_limit_bytes=56 << 20, dimension_semantics=("arbitrary",))


def struct(shape, dtype=f32):
    return jax.ShapeDtypeStruct(shape, dtype)


def cost(flops, moved):
    return pl.CostEstimate(flops=int(flops), bytes_accessed=int(moved), transcendentals=0)


def on_device(
    block_input, cotangent, seq_lengths, norm_gain, gate_weight, inner_weight, step_weight, state_weight,
    inner_kernel, inner_bias, state_kernel_, state_bias, step_bias, decay_log, skip_scale, gate_gain, output_weight,
):
    parts = lax.axis_size("tensor")
    shards = lax.axis_size("dp")
    t = lax.axis_index("tensor")
    count, width = block_input.shape
    inner = gate_weight.shape[1]
    heads = step_bias.shape[0]
    share = width // parts
    span = 2 * STATE // parts
    steps = inner // BLK
    pad = ((0, 0), (0, 128 - heads))
    row = lambda x: x.reshape(1, -1)

    def swap(x, k):
        return lax.ppermute(x, "tensor", [(i, i ^ k) for i in range(parts)])

    chunks = 3 * steps
    slab = lambda x, size: lax.dynamic_slice_in_dim(x, t * size, size, x.ndim - 1)
    if shards == 8 and parts == 4:
        own, half_blk, piece, near = width // 8, BLK // 2, count // parts, width // 2
        dma, v = pltpu.SemaphoreType.DMA, lambda *shape: pltpu.VMEM(shape, f32)
        vb = lambda *shape: pltpu.VMEM(shape, bf16)
        vmem, hbm = pl.BlockSpec(memory_space=pltpu.VMEM), pl.BlockSpec(memory_space=pl.ANY)
        scratch = [
            vb(count, width), vb(count, width), vb(width, 2 * STATE), v(chunks, count, BLK), v(4 * steps, count, half_blk), v(steps, count, BLK), vb(count, width),
            v(count, 128), v(1, width), v(1, inner), v(1, 2 * STATE), v(24, 128), v(1, inner), v(1, inner), v(2, piece, near), v(2, piece, width), v(2, piece, near), v(2, piece, near),
            v(2, 3, piece, near), v(2, 3, piece, near), vb(2, near, 4 * count), v(RING, 3 * count, BLK),
            v(RING, 2, own, half_blk), v(LEAD, own, half_blk), v(2, 2, 2 * own, BLK), v(2, own, half_blk), v(2, own, BLK),
            vb(4 * count, BLK), vb(count, near), vb(2, 2, width, BLK), vb(2, BLK, width),
            v(4, count, share), v(3, count, share), v(3, share // half_blk, count, half_blk),
            v(count, count), v(count, count), v(steps, count, 128), v(128, count), v(count, 2 * STATE), v(count, 2 * STATE),
            v(count, 128), v(count, 128), v(count, count), v(count, 128), v(count, 128), v(8, 128), v(count, 128),
            v(8, count), v(3, 8, count), v(4, count, span), v(3, count, span), v(4, 8, span), v(8, inner), v(3, 8, inner),
            v(count, 128), v(128, count), v(3, 128, count), v(2, 2 * own, 128), v(2 * own, 128), v(own, 128), v(4, own, 128),
            v(8, count), v(3, 8, count),
        ]
        scratch += [dma((chunks,))] * 8 + [dma((chunks, 2))] * 2 + [dma((chunks,))] * 5 + [dma((3, 2))] + [dma((3,))] * 14
        scratch += [dma((4,))] * 2 + [dma((1,))] * 2 + [dma((3,))] * 2 + [dma((2, 2))] * 2 + [dma((2,))] * 4 + [dma((2, 3))] * 2
        scratch += [dma((2, 2, 3))] * 2 + [dma((3,))] + [pltpu.SemaphoreType.REGULAR] * 2
        shapes = [
            struct((count, share), bf16), struct((count, share)), struct((own, inner)), struct((own, inner)),
            struct((own, 2 * STATE)), struct((heads, own)), struct((own, inner)),
        ]
        *large, smalls = pl.pallas_call(
            layer_kernel,
            in_specs=[SMEM, hbm, hbm, vmem, vmem, hbm] + [vmem] * 8 + [hbm] * 3,
            out_specs=[vmem, vmem, hbm, hbm, vmem, vmem, hbm, vmem],
            out_shape=shapes + [struct((8, inner))],
            scratch_shapes=scratch,
            compiler_params=pltpu.CompilerParams(collective_id=1, has_side_effects=True, vmem_limit_bytes=VMEM_LIMIT),
            name="layer",
        )(
            seq_lengths, block_input, cotangent, norm_gain, step_weight.T, state_weight, inner_kernel, inner_bias,
            state_kernel_, state_bias, step_bias, decay_log, skip_scale, gate_gain, gate_weight, inner_weight, output_weight,
        )
        cut = [
            struct((share,)), struct((CONV, inner)), struct((inner,)), struct((CONV, 2 * STATE)), struct((2 * STATE,)),
            struct((heads,)), struct((heads,)), struct((heads,)), struct((inner,)),
        ]
        *smalls, out, into, gate_grad, inner_grad, state_grad, step_grad, output_grad = pl.pallas_call(
            outputs_kernel,
            in_specs=[vmem] + [hbm] * 7,
            out_specs=[vmem] * 9 + [hbm] * 7,
            out_shape=cut + shapes,
            scratch_shapes=[pltpu.VMEM(a.shape, a.dtype) for a in shapes] + [dma((7,)), dma((7,))],
            compiler_params=VM,
            name="outputs",
        )(smalls, *large)
        return (
            out, into, smalls[0], gate_grad, inner_grad, step_grad.T, state_grad, *smalls[1:9], output_grad.T,
        )

    padded_step = jnp.pad(step_weight, pad)
    stepb, decay = jnp.pad(row(step_bias), pad), jnp.pad(row(decay_log), pad)
    skipc = jnp.repeat(skip_scale, HEAD_DIM).reshape(1, -1)
    ik, ib, gain = inner_kernel, row(inner_bias), row(gate_gain)
    full = struct((count, inner))
    nb, inv = pl.pallas_call(
        norm_kernel,
        out_shape=(struct((count, width), bf16), struct((count, 128))),
        compiler_params=VM,
        name="norm_in",
    )(block_input, row(norm_gain))

    graw, iraw, cv, mixed, scaled, sums, sraw, sact, state_raw, hc, lsr, addm, g, keep = pl.pallas_call(
        forward_kernel,
        grid=(steps,),
        in_specs=[
            SMEM, whole((count, width)), whole((count, width)), columns(width), columns(width),
            pl.BlockSpec((BLK, width), lambda j: (j, 0)), whole((width, 128)), whole((width, 2 * STATE)),
            columns(CONV), columns(1), whole((CONV, 2 * STATE)), whole((1, 2 * STATE)), whole((1, 128)), whole((1, 128)),
            columns(1), columns(1),
        ],
        out_specs=(
            [columns(count)] * 5
            + [whole((8, count)), whole((count, 128)), whole((count, 2 * STATE)), whole((count, 2 * STATE)),
               whole((steps, count, 128)), whole((128, count)), whole((count, count)), whole((count, count)),
               whole((count, 128))]
        ),
        out_shape=(
            [full] * 5
            + [struct((8, count)), struct((count, 128)), struct((count, 2 * STATE)), struct((count, 2 * STATE)),
               struct((steps, count, 128)), struct((128, count)), struct((count, count)), struct((count, count)),
               struct((count, 128))]
        ),
        scratch_shapes=[pltpu.VMEM((count, 128), f32)],
        compiler_params=VMS,
        cost_estimate=cost(6 * count * width * inner, 6 * width * inner + 20 * count * inner),
        name="forward",
    )(
        seq_lengths, nb, cotangent, gate_weight, inner_weight, output_weight, padded_step, state_weight, ik, ib,
        state_kernel_, row(state_bias), stepb, decay, skipc, gain,
    )

    all_sums = jnp.stack([sums] + [swap(sums, k) for k in range(1, parts)])
    x, dm, gg = pl.pallas_call(
        partial(unit_kernel, float(inner * parts)),
        grid=(steps,),
        in_specs=[whole((parts, 8, count)), columns(count), columns(count), columns(count), columns(1)],
        out_specs=[pl.BlockSpec((2, 1, count, BLK), lambda j: (0, j, 0, 0)), columns(count), columns(8)],
        out_shape=[struct((3, steps, count, BLK)), full, struct((8, inner))],
        compiler_params=VMS,
        cost_estimate=cost(0, 24 * count * inner),
        name="unit",
    )(all_sums, graw, mixed, scaled, gain)

    x, rows, sback, hrows, dstate = pl.pallas_call(
        backward_kernel,
        grid=(steps,),
        in_specs=[
            SMEM, columns(count), columns(count), columns(count), columns(count),
            pl.BlockSpec((1, count, 128), lambda j: (j, 0, 0)), whole((128, count)), whole((count, count)),
            whole((count, count)), whole((count, 128)), whole((count, 2 * STATE)), columns(CONV), columns(1), whole((1, 128)),
            pl.BlockSpec(memory_space=pl.ANY),
        ],
        input_output_aliases={14: 0},
        out_specs=[pl.BlockSpec((1, 1, count, BLK), lambda j: (2, j, 0, 0)), columns(8), whole((count, 128)), whole((8, 128)), whole((parts, count, span))],
        out_shape=[struct((3, steps, count, BLK)), struct((8, inner)), struct((count, 128)), struct((8, 128)), struct((parts, count, span))],
        scratch_shapes=[pltpu.VMEM((count, count), f32), pltpu.VMEM((count, 128), f32), pltpu.VMEM((count, 128), f32)],
        compiler_params=VMS,
        cost_estimate=cost(40 * count * count * inner // 64 * 4, 24 * count * inner),
        name="backward",
    )(seq_lengths, dm, cv, iraw, mixed, hc, lsr, addm, g, sraw, sact, ik, skipc, decay, x)

    uo, gb, back = (jnp.swapaxes(x[i], 0, 1).reshape(count, inner) for i in range(3))

    def to_parts(x, axis):
        size = x.shape[axis] // parts
        block = lambda i: lax.dynamic_slice_in_dim(x, i * size, size, axis)
        got = [swap(block(t ^ k), k) for k in range(1, parts)]
        return [block(t)] + got

    def from_parts(x):
        got = jnp.stack([x] + [swap(x, k) for k in range(1, parts)])
        return jnp.stack([lax.dynamic_index_in_dim(got, t ^ i, 0, False) for i in range(parts)])

    state_parts = jnp.concatenate(to_parts(dstate, 0), axis=0)
    sq, srows = pl.pallas_call(
        state_kernel,
        in_specs=[SMEM] + [pl.BlockSpec(memory_space=pltpu.VMEM)] * 4,
        out_shape=(struct((count, span)), struct((8, span))),
        compiler_params=VM,
        name="state_back",
    )(seq_lengths, state_parts, slab(state_raw, span), slab(state_kernel_, span), row(slab(state_bias, span)))

    hidden = slab(block_input, share).astype(f32)
    cot_share = slab(cotangent, share).astype(f32)
    out_parts = to_parts(mm(uo.astype(bf16), output_weight), 1)
    block_output = (sum(out_parts[1:], out_parts[0]) + hidden).astype(bf16)

    gbb, ibb, sbb, qb = (x.astype(bf16) for x in (gb, back, sback[:, :heads], sq))
    partial_in = (
        mm(gbb, gate_weight, NT) + mm(ibb, inner_weight, NT) + mm(sbb, step_weight, NT)
        + mm(qb, slab(state_weight, span), NT)
    )
    in_parts = to_parts(partial_in, 1)
    d_normed = sum(in_parts[1:], in_parts[0])
    inv_in = inv[:, 0:1]
    normed = hidden * inv_in
    gain_share = row(slab(norm_gain, share))
    d_hat = d_normed * gain_share
    dot = jnp.sum(d_hat * normed, axis=1).reshape(-1, 128)
    dot = sum((swap(dot, k) for k in range(1, parts)), dot).reshape(-1, 1) / width
    input_gradient = inv_in * (d_hat - normed * dot) + cot_share
    norm_gain_grad = jnp.sum(d_normed * normed, axis=0)

    extra = jnp.concatenate([sq, sback[:, :heads], jnp.zeros((count, 128 - span - heads), f32)], axis=1)

    def scatter(a, b):
        return lax.psum_scatter(mm(a, b.astype(bf16), TN), "dp", scatter_dimension=0, tiled=True)

    output_grad = scatter(cotangent, uo).T
    gate_grad, inner_grad, extra_grad = scatter(nb, gb), scatter(nb, back), scatter(nb, extra)

    def over_dp(x):
        return lax.psum(x, "dp")

    step_grad = extra_grad[:, span : span + heads]
    state_grad = jnp.swapaxes(from_parts(extra_grad[:, :span]), 0, 1).reshape(-1, 2 * STATE)
    misc = jnp.concatenate([hrows[0], hrows[1], srows[: CONV + 1].reshape(-1), norm_gain_grad])
    misc = jnp.pad(misc, (0, -misc.shape[0] % 1024)).reshape(8, -1)
    smalls = over_dp(jnp.concatenate([rows, gg], axis=0))
    misc = over_dp(misc).reshape(-1)
    step_bias_grad, decay_grad = misc[:heads], misc[128 : 128 + heads]
    state_rows = from_parts(misc[256 : 256 + (CONV + 1) * span].reshape(CONV + 1, span))
    state_rows = jnp.swapaxes(state_rows, 0, 1).reshape(CONV + 1, 2 * STATE)
    at = 256 + (CONV + 1) * span
    skip_grad = jnp.sum(smalls[CONV + 1].reshape(heads, HEAD_DIM), axis=1)
    return (
        block_output,
        input_gradient,
        misc[at : at + share],
        gate_grad,
        inner_grad,
        step_grad,
        state_grad,
        smalls[:CONV],
        smalls[CONV],
        state_rows[:CONV],
        state_rows[CONV],
        step_bias_grad,
        decay_grad,
        skip_grad,
        smalls[8],
        output_grad,
    )


def solution(mesh):
    return jax.shard_map(
        on_device,
        mesh=mesh,
        in_specs=(
            P("dp", None), P("dp", None), P("dp", None), P(), P(None, "tensor"), P(None, "tensor"), P(None, "tensor"), P(),
            P(None, "tensor"), P("tensor"), P(), P(), P("tensor"), P("tensor"), P("tensor"), P("tensor"), P("tensor", None),
        ),
        out_specs=(
            P("dp", "tensor"), P("dp", "tensor"), P("tensor"), P("dp", "tensor"), P("dp", "tensor"), P("dp", "tensor"),
            P("dp", None), P(None, "tensor"), P("tensor"), P(), P(), P("tensor"), P("tensor"), P("tensor"), P("tensor"),
            P("tensor", "dp"),
        ),
        check_vma=False,
    )
```
